32 devices in a mesh: dp: 16 (over z, y, x), mp: 2 (over core).
Axes of the slice: x: 2, y: 2, z: 4, core: 2. Of those that a mesh axis runs over, the one named last changes fastest.
Arguments:
- inputs: bfloat16 [16, 1024, 768], P('dp', 'mp'), may hold values from -6 to 6
- grad_out: bfloat16 [16, 1024, 768], P('dp', 'mp'), may hold values from -6 to 6
- lengths: int32 [16], P('dp'), may hold values from 512 to 1024, as said below
- rand_blocks: int32 [16, 16, 3], P('dp', 'mp'), may hold values from 0 to 15, as said below
- w_query: bfloat16 [768, 768], replicated, may hold values from -0.3125 to 0.3125
- b_query: bfloat16 [768], replicated, may hold values from -1.5 to 1.5
- w_key: bfloat16 [768, 768], replicated, may hold values from -0.3125 to 0.3125
- w_value: bfloat16 [768, 768], replicated, may hold values from -0.21875 to 0.21875
- b_value: bfloat16 [768], replicated, may hold values from -0.5 to 0.5
- w_output: bfloat16 [768, 768], replicated, may hold values from -1.75 to 1.75
- b_output: bfloat16 [768], replicated, may hold values from -1.5 to 1.5
- gain_one: bfloat16 [768], replicated, may hold values from 0.099609375 to 1.8984375
- shift_one: bfloat16 [768], replicated, may hold values from -1.5 to 1.5
- w_in: bfloat16 [768, 3072], P(None, 'mp'), may hold values from -0.21875 to 0.21875
- b_in: bfloat16 [3072], P('mp'), may hold values from -1.5 to 1.5
- w_out: bfloat16 [768, 3072], P(None, 'mp'), may hold values from -0.109375 to 0.109375
- b_out: bfloat16 [768], replicated, may hold values from -1.5 to 1.5
- gain_two: bfloat16 [768], replicated, may hold values from 0.099609375 to 1.8984375
- shift_two: bfloat16 [768], replicated, may hold values from -1.5 to 1.5
Outputs:
- output: bfloat16 [16, 1024, 768], P('dp', 'mp')
- input_grad: float32 [16, 1024, 768], P('dp', 'mp')
- w_query_grad: float32 [768, 768], P('dp', 'mp')
- b_query_grad: float32 [768], P('dp')
- w_key_grad: float32 [768, 768], P('dp', 'mp')
- w_value_grad: float32 [768, 768], P('dp', 'mp')
- b_value_grad: float32 [768], P('dp')
- w_output_grad: float32 [768, 768], P('dp', 'mp')
- b_output_grad: float32 [768], P('dp')
- gain_one_grad: float32 [768], P('dp')
- shift_one_grad: float32 [768], P('dp')
- w_in_grad: float32 [768, 3072], P('dp', 'mp')
- b_in_grad: float32 [3072], P('dp')
- w_out_grad: float32 [768, 3072], P('dp', 'mp')
- b_out_grad: float32 [768], P('dp')
- gain_two_grad: float32 [768], P('dp')
- shift_two_grad: float32 [768], P('dp')
The draws below stay inside these ranges and needn't reach their ends.
Inputs may be any that keep to these rules, and one draw needn't show every extreme that they name: Positions below lengths[s] of sequence s are real tokens, the rest padding; some sequence has 1024 real tokens and some has 512. rand_blocks[s, i, j] lies below ceil(lengths[s] / 64).
All inputs are finite; a program needn't handle non-finite values.
Results may differ from the reference program's by a relative error of at most 0.02.
Values may be sent and summed in bfloat16 or wider, within the bound.
A program may use at most 256 MiB of HBM per device.

```python
import jax
import jax.numpy as jnp
from jax import lax

HEADS = 12
HD = 64
D = 768
FF = 3072
BLK = 64
RND = 3
SEQ_LEN = 1024
SEQS = 16
NB = 16


def sequence_lengths(key):
    drawn = jax.random.randint(jax.random.fold_in(key, 11), (SEQS,), 8 * BLK, SEQ_LEN + 1, dtype=jnp.int32)
    longest = jax.random.randint(jax.random.fold_in(key, 12), (), 0, SEQS, dtype=jnp.int32)
    order = jnp.arange(SEQS, dtype=jnp.int32)
    drawn = jnp.where(order == longest, SEQ_LEN, drawn)
    return jnp.where(order == (longest + 1) % SEQS, 8 * BLK, drawn).astype(jnp.int32)


def draw_lengths(key, part):
    return sequence_lengths(key)


def draw_rand_blocks(key, part):
    seq_lengths = sequence_lengths(key)
    counts = (seq_lengths + BLK - 1) // BLK
    picks = jax.random.randint(jax.random.fold_in(key, 13), (SEQS, NB, RND), 0, counts[:, None, None], dtype=jnp.int32)
    forced = (seq_lengths == SEQ_LEN)[:, None, None] & (jnp.arange(NB)[None, :, None] == 0) & (jnp.arange(RND)[None, None, :] == 0)
    return jnp.where(forced, NB - 1, picks).astype(jnp.int32)


def raised(values, own_key, source, target, parts, factor):
    def block_of(axis_at):
        return (jnp.arange(values.shape[axis_at]) // (values.shape[axis_at] // parts)).reshape((-1,) + (1,) * (values.ndim - 1 - axis_at))

    one_side = jax.random.permutation(own_key, parts)[block_of(target)]
    other_side = (block_of(target) + parts // 2) % parts
    return jnp.where((block_of(source) == one_side) | (block_of(source) == other_side), factor * values, values)


def levels(stream_key, shape, cuts, low, top_value):
    def one(axis_at, shards_of):
        draws = jax.random.uniform(jax.random.fold_in(jax.random.fold_in(stream_key, 6), axis_at), (shards_of,), jnp.float32, low / len(cuts), top_value / len(cuts))
        return jnp.repeat(jnp.exp(draws), shape[axis_at] // shards_of).reshape((-1,) + (1,) * (len(shape) - axis_at - 1))

    gain = one(*cuts[0])
    for cut in cuts[1:]:
        gain = gain * one(*cut)
    return gain


def normal_values(key, shape, spread, reach, pieces=(), held_as=jnp.bfloat16):
    factor_of = levels(key, shape, pieces, -0.22, 0.18) if pieces else 1.0
    values = jax.random.normal(key, shape, jnp.float32) * spread * factor_of
    return jnp.minimum(jnp.maximum(values, -reach), reach).astype(held_as)


def heavy_noise(stream_key, extent, scale, bound, shards, heavy, kind=jnp.bfloat16):
    entries = scale * jax.random.normal(stream_key, extent, jnp.float32)
    if shards:
        entries = entries * levels(stream_key, extent, shards, -0.22, 0.18)
    return jnp.clip(raised(entries, jax.random.fold_in(stream_key, 3), *heavy), -bound, bound).astype(kind)


def setup_inputs(seed: int = 0) -> dict:
    streams_of = jax.random.split(jax.random.key(seed), 20)
    return {
        "inputs": normal_values(streams_of[0], (SEQS, SEQ_LEN, D), 1.0, 6.0, ((0, 16), (1, 2))),
        "grad_out": heavy_noise(streams_of[1], (SEQS, SEQ_LEN, D), 1.0, 6.0, ((0, 16), (1, 2)), (0, 2, 16, 2.0)),
        "lengths": draw_lengths(jax.random.fold_in(streams_of[19], 71), 0),
        "rand_blocks": draw_rand_blocks(jax.random.fold_in(streams_of[19], 71), 0),
        "w_query": normal_values(streams_of[4], (D, D), (D // 2) ** -0.5, 0.3125),
        "b_query": normal_values(streams_of[5], (D,), 0.3, 1.5),
        "w_key": normal_values(streams_of[6], (D, D), (D // 2) ** -0.5, 0.3125),
        "w_value": normal_values(streams_of[7], (D, D), D ** -0.5, 0.21875),
        "b_value": normal_values(streams_of[8], (D,), 0.1, 0.5),
        "w_output": normal_values(streams_of[9], (D, D), (D // 64) ** -0.5, 1.75),
        "b_output": normal_values(streams_of[10], (D,), 0.3, 1.5),
        "gain_one": jnp.clip(1.0 + 0.18 * jax.random.normal(streams_of[11], (D,), jnp.float32), 0.099609375, 1.8984375).astype(jnp.bfloat16),
        "shift_one": normal_values(streams_of[12], (D,), 0.3, 1.5),
        "w_in": normal_values(streams_of[13], (D, FF), D ** -0.5, 0.21875, ((1, 2),)),
        "b_in": normal_values(streams_of[14], (FF,), 0.3, 1.5, ((0, 2),)),
        "w_out": normal_values(streams_of[15], (D, FF), FF ** -0.5, 0.109375, ((1, 2),)),
        "b_out": normal_values(streams_of[16], (D,), 0.3, 1.5),
        "gain_two": jnp.clip(1.0 + 0.18 * jax.random.normal(streams_of[17], (D,), jnp.float32), 0.099609375, 1.8984375).astype(jnp.bfloat16),
        "shift_two": normal_values(streams_of[18], (D,), 0.3, 1.5),
    }


@jax.custom_vjp
def low(v):
    return lax.optimization_barrier(v.astype(jnp.bfloat16)).astype(jnp.float32)

@jax.custom_vjp
def low_back(v):
    return v

def low_keep(v):
    return (low(v), None)

def low_pass(kept, grad):
    return (grad,)

def back_keep(v):
    return (v, None)

def back_low(kept, grad):
    return (low(grad),)
low.defvjp(low_keep, low_pass)
low_back.defvjp(back_keep, back_low)
highest = lax.Precision.HIGHEST
negative_fill = -1000000000.0
norm_epsilon = 1e-12

def layer_norm(features, norm_gain, norm_shift):
    row_mean = lax.optimization_barrier(jnp.mean(features, axis=-1, keepdims=True))
    centered = features - row_mean
    variance = lax.optimization_barrier(jnp.mean(centered * centered, axis=-1, keepdims=True))
    return centered * lax.rsqrt(variance + norm_epsilon) * norm_gain + norm_shift

def slot_table(first_block, rand_rows, length):
    block_ids = first_block + jnp.arange(rand_rows.shape[0], dtype=jnp.int32)
    valid_blocks = (length + BLK - 1) // BLK
    column = block_ids[:, None]
    columns = jnp.concatenate([column - 1, column, column + 1, rand_rows, jnp.zeros_like(column), jnp.zeros_like(column) + valid_blocks - 1], axis=1)
    in_range = (columns >= 0) & (columns < valid_blocks)
    slot_ids = jnp.arange(columns.shape[1], dtype=jnp.int32)
    earlier = slot_ids[None, :] < slot_ids[:, None]
    repeated = jnp.any((columns[:, :, None] == columns[:, None, :]) & earlier[None, :, :] & in_range[:, None, :], axis=2)
    return (jnp.clip(columns, 0, NB - 1), in_range & jnp.logical_not(repeated))

def slot_mask(slot_blocks, slot_valid, length):
    positions = slot_blocks[:, :, None] * BLK + jnp.arange(BLK, dtype=jnp.int32)
    allowed = slot_valid[:, :, None] & (positions < length)
    return allowed.reshape(slot_blocks.shape[0], 1, 1, -1)

def gather_slots(whole_rows, slot_blocks):
    picked = whole_rows.reshape(NB, BLK, whole_rows.shape[1])[slot_blocks]
    return picked.reshape(slot_blocks.shape[0], slot_blocks.shape[1] * BLK, HEADS, HD)

def masked_softmax(scores, allowed):
    masked = jnp.where(allowed, scores, negative_fill)
    top_score = lax.optimization_barrier(jnp.max(masked, axis=-1, keepdims=True))
    log_sum = top_score + jnp.log(lax.optimization_barrier(jnp.sum(jnp.exp(masked - top_score), axis=-1, keepdims=True)))
    return jnp.exp(masked - log_sum)

def attention(query, keys, values, length, rand_rows):
    score_scale = HD ** (-0.5)
    slot_blocks, slot_valid = slot_table(0, rand_rows, length)
    allowed = slot_mask(slot_blocks, slot_valid, length)
    query_blocks = query.reshape(NB, BLK, HEADS, HD)
    scores = low_back(jnp.einsum('nqhd,nkhd->nhqk', query_blocks, gather_slots(keys, slot_blocks), precision=highest) * score_scale)
    attended = jnp.einsum('nhqk,nkhd->nqhd', low(masked_softmax(scores, allowed)), gather_slots(values, slot_blocks), precision=highest).reshape(SEQ_LEN, -1)
    last_block = (length + BLK - 1) // BLK - 1
    key_live = (jnp.arange(SEQ_LEN, dtype=jnp.int32) < length)[None, None, :]
    row_blocks = jnp.arange(SEQ_LEN, dtype=jnp.int32) // BLK
    key_heads = keys.reshape(SEQ_LEN, HEADS, HD)
    value_heads = values.reshape(SEQ_LEN, HEADS, HD)
    for target_block in (jnp.zeros_like(last_block), last_block):
        query_rows = lax.dynamic_slice_in_dim(query, target_block * BLK, BLK, 0).reshape(BLK, HEADS, HD)
        global_scores = low_back(jnp.einsum('qhd,khd->hqk', query_rows, key_heads, precision=highest) * score_scale)
        out_rows = jnp.einsum('hqk,khd->qhd', low(masked_softmax(global_scores, key_live)), value_heads, precision=highest).reshape(BLK, -1)
        attended = jnp.where((row_blocks == target_block)[:, None], jnp.tile(out_rows, (NB, 1)), attended)
    return attended

def forward(params, inputs, length, rand_rows):
    w_query, b_query, w_key, w_value, b_value, w_output, b_output, gain_one, shift_one, w_in, b_in, w_out, b_out, gain_two, shift_two = params
    query = low(low_back(jnp.dot(inputs, w_query, precision=highest) + b_query))
    keys = low(low_back(jnp.dot(inputs, w_key, precision=highest)))
    values = low(low_back(jnp.dot(inputs, w_value, precision=highest) + b_value))
    attended = attention(query, keys, values, length, rand_rows)
    branch = low_back(jnp.dot(low(low_back(attended)), w_output, precision=highest) + b_output)
    first = layer_norm(inputs + branch, gain_one, shift_one)
    hidden = jnp.dot(low(first), w_in, precision=highest) + b_in
    active = low(jax.nn.gelu(low_back(hidden), approximate=True))
    feed = low_back(jnp.dot(active, w_out.T, precision=highest) + b_out)
    return layer_norm(first + feed, gain_two, shift_two)

def reference(inputs, grad_out, lengths, rand_blocks, w_query, b_query, w_key, w_value, b_value, w_output, b_output, gain_one, shift_one, w_in, b_in, w_out, b_out, gain_two, shift_two):
    params = tuple((item.astype(jnp.float32) for item in (w_query, b_query, w_key, w_value, b_value, w_output, b_output, gain_one, shift_one, w_in, b_in, w_out, b_out, gain_two, shift_two)))

    def one_sequence(running, seq_items):
        seq_in, seq_grad, length, rand_rows = seq_items

        def local_layer(params_now, inputs_now):
            return forward(params_now, inputs_now, length, rand_rows)
        result, pullback = jax.vjp(local_layer, params, seq_in.astype(jnp.float32))
        param_grads, input_grad = pullback(seq_grad.astype(jnp.float32))
        running = jax.tree.map(lambda total_now, addend: total_now + addend, running, param_grads)
        return (running, (result.astype(jnp.bfloat16), input_grad))
    starting = tuple((jnp.zeros_like(item) for item in params))
    totals, (outputs, input_grads) = lax.scan(one_sequence, starting, (inputs, grad_out, lengths, rand_blocks))
    return (outputs, input_grads, totals[0], totals[1], totals[2], totals[3], totals[4], totals[5], totals[6], totals[7], totals[8], totals[9], totals[10], totals[11], totals[12], totals[13], totals[14])
```

```python
import functools

import jax
import jax.numpy as jnp
from jax import lax
from jax.experimental import pallas as pl
from jax.experimental.pallas import tpu as pltpu
from jax.sharding import PartitionSpec as P

HEADS = 12
HD = 64
FF = 3072
BLK = 64
NB = 16


negative_fill = -1000000000.0
norm_epsilon = 1e-12


F32 = jnp.float32
BF16 = jnp.bfloat16
NN = (((1,), (0,)), ((), ()))
NT = (((1,), (1,)), ((), ()))
TN = (((0,), (0,)), ((), ()))


def mm(a, b, dims=NN):
    return lax.dot_general(a, b, dims, preferred_element_type=F32)


def params(mib=56):
    return pltpu.CompilerParams(vmem_limit_bytes=mib << 20)


def cost(flops, nbytes, trans=0):
    return pl.CostEstimate(flops=int(flops), bytes_accessed=int(nbytes), transcendentals=int(trans))


def shape(dims, dtype):
    return jax.ShapeDtypeStruct(dims, dtype)


def row_stats(u):
    mean = jnp.mean(u, axis=-1, keepdims=True)
    cen = u - mean
    var = jnp.mean(cen * cen, axis=-1, keepdims=True)
    rs = lax.rsqrt(var + norm_epsilon)
    return cen * rs, rs


def attn_fwd_body(sc, xo, xt, wq, wk, wv, bq, bv, rand, q_o, k_o, v_o, p_o, ao, at, bias):
    half = xo.shape[0]
    rows = 2 * half
    nb = rows // BLK
    tile = 256

    @pl.when(pl.program_id(0) == 0)
    def _():
        c = sc[0]
        ln = sc[1]
        last = (ln + BLK - 1) // BLK - 1
        lb = lax.broadcasted_iota(jnp.int32, (nb, rows), 0)
        kp = lax.broadcasted_iota(jnp.int32, (nb, rows), 1)
        qb = jnp.where(lb < nb // 2, lb + (nb // 2) * c, lb - (nb // 2) * c)
        kpos = jnp.where(kp < half, kp + half * c, kp - half * c)
        kb = kpos // BLK
        ok = (jnp.abs(kb - qb) <= 1) | (kb == 0) | (kb == last)
        for j in range(rand.shape[1]):
            ok = ok | (kb == rand[:, j : j + 1])
        ok = ok | (qb == 0) | (qb == last)
        ok = ok & (kpos < ln)
        table = jnp.where(ok, 0.0, -1e30).astype(F32)
        for b in range(nb):
            bias[b] = jnp.broadcast_to(table[b : b + 1, :], (8, rows))

    for i, xr in enumerate((xo, xt)):
        rs = slice(i * half, (i + 1) * half)
        q_o[rs, :] = (mm(xr[...], wq[...]) + bq[...].astype(F32)).astype(BF16)
        k_o[rs, :] = mm(xr[...], wk[...]).astype(BF16)
        v_o[rs, :] = (mm(xr[...], wv[...]) + bv[...].astype(F32)).astype(BF16)

    lane = lax.broadcasted_iota(jnp.int32, (tile, 2 * HD), 1)
    low = lane < HD
    for i, a_ref in enumerate((ao, at)):

        def step(t, carry, i=i, a_ref=a_ref):
            r0 = pl.multiple_of(i * half + t * tile, tile)
            q = q_o[pl.ds(r0, tile), :] * BF16(HD**-0.5)
            outs = []
            for h in range(2):
                qh = jnp.where(low if h == 0 else ~low, q, BF16(0))
                s = mm(qh, k_o[...], NT)
                s = s.reshape(tile // BLK, BLK // 8, 8, rows)
                s = s + bias[pl.ds(r0 // BLK, tile // BLK)][:, None]
                s = s.reshape(tile, rows)
                e = jnp.exp(s - jnp.max(s, axis=-1, keepdims=True))
                p = (e * (1.0 / jnp.sum(e, axis=-1, keepdims=True))).astype(BF16)
                p_o[h, pl.ds(r0, tile), :] = p
                outs.append(mm(p, v_o[...]))
            a = jnp.where(low, outs[0], outs[1]).astype(BF16)
            a_ref[pl.ds(pl.multiple_of(t * tile, tile), tile), :] = a
            return carry

        lax.fori_loop(0, half // tile, step, 0)


def attn_fwd(sc, xo, xt, wq, wk, wv, bq, bv, rand):
    half, width = xo.shape
    rows = 2 * half
    pairs = HEADS // 4
    pw = 2 * HD
    whole = lambda a: pl.BlockSpec(a.shape, lambda p, s: (0,) * a.ndim)
    wspec = pl.BlockSpec((width, pw), lambda p, s: (0, s[0] * pairs + p))
    bspec = pl.BlockSpec((1, pw), lambda p, s: (0, s[0] * pairs + p))
    ospec = lambda r: pl.BlockSpec((r, pw), lambda p, s: (0, p))
    return pl.pallas_call(
        attn_fwd_body,
        grid_spec=pltpu.PrefetchScalarGridSpec(
            num_scalar_prefetch=1,
            grid=(pairs,),
            in_specs=[whole(xo), whole(xt), wspec, wspec, wspec, bspec, bspec, whole(rand)],
            out_specs=[ospec(rows)] * 3
            + [pl.BlockSpec((2, rows, rows), lambda p, s: (p, 0, 0))]
            + [ospec(half)] * 2,
            scratch_shapes=[pltpu.VMEM((rows // BLK, 8, rows), F32)],
        ),
        out_shape=[shape((rows, pairs * pw), BF16)] * 3
        + [shape((2 * pairs, rows, rows), BF16)]
        + [shape((half, pairs * pw), BF16)] * 2,
        compiler_params=params(),
        cost_estimate=cost(20e9, 20e6, 6 * rows * rows),
        name="attn_fwd",
    )(sc, xo, xt, wq, wk, wv, bq, bv, rand)


def attn_bwd_body(
    sc, xo, xt, wq, wk, wv, q_i, k_i, v_i, p_i, ao, at, go, gt,
    wg, bqg, bvg, igo, igt, g_s, gT, qT, dkT, dvT, dqkv, wcat, xT, acc,
):
    half = xo.shape[0]
    rows = 2 * half
    pw = 2 * HD
    tile = 256
    step_id = pl.program_id(0)

    @pl.when(step_id == 0)
    def _():
        xT[:, :half] = xo[...].T
        xT[:, half:] = xt[...].T

    for i, w in enumerate((wq, wk, wv)):
        wcat[:, i * pw : (i + 1) * pw] = w[...]
    g_s[:half, :] = go[...]
    g_s[half:, :] = gt[...]
    gT[...] = g_s[...].T
    qT[...] = q_i[...].T
    dkT[...] = jnp.zeros_like(dkT)
    dvT[...] = jnp.zeros_like(dvT)
    lane = lax.broadcasted_iota(jnp.int32, (tile, pw), 1)
    low = lane < HD

    for i, a_ref in enumerate((ao, at)):

        def step(t, carry, i=i, a_ref=a_ref):
            r0 = pl.multiple_of(i * half + t * tile, tile)
            a0 = pl.multiple_of(t * tile, tile)
            g = g_s[pl.ds(r0, tile), :]
            ga = g.astype(F32) * a_ref[pl.ds(a0, tile), :].astype(F32)
            outs = []
            for h in range(2):
                mine = low if h == 0 else ~low
                hs = slice(h * HD, (h + 1) * HD)
                dp = mm(jnp.where(mine, g, BF16(0)), v_i[...], NT)
                delta = jnp.sum(jnp.where(mine, ga, 0.0), axis=-1, keepdims=True)
                p = p_i[h, pl.ds(r0, tile), :]
                ds = (p.astype(F32) * (dp - delta)).astype(BF16)
                outs.append(mm(ds, k_i[...]))
                dvT[hs, :] += mm(gT[hs, pl.ds(r0, tile)], p)
                dkT[hs, :] += mm(qT[hs, pl.ds(r0, tile)], ds)
            dq = jnp.where(low, outs[0], outs[1]) * HD**-0.5
            dqkv[pl.ds(r0, tile), 0:pw] = dq.astype(BF16)
            return carry

        lax.fori_loop(0, half // tile, step, 0)

    dqkv[:, pw : 2 * pw] = (dkT[...].T * HD**-0.5).astype(BF16)
    dqkv[:, 2 * pw : 3 * pw] = dvT[...].T.astype(BF16)
    d = dqkv[...]
    wg[...] = mm(xT[...], d).astype(BF16)
    bqg[...] = jnp.sum(d[:, 0:pw].astype(F32), axis=0, keepdims=True)
    bvg[...] = jnp.sum(d[:, 2 * pw :].astype(F32), axis=0, keepdims=True)
    part = mm(d, wcat[...], NT)

    @pl.when(step_id == 0)
    def _():
        acc[...] = part

    @pl.when((step_id > 0) & (step_id < pl.num_programs(0) - 1))
    def _():
        acc[...] += part

    @pl.when(step_id == pl.num_programs(0) - 1)
    def _():
        total = acc[...] + part
        igo[...] = total[:half]
        igt[...] = total[half:].astype(BF16)


def attn_bwd(sc, xo, xt, wq, wk, wv, q, k, v, probs, ao, at, go, gt):
    half, width = xo.shape
    rows = 2 * half
    pairs = HEADS // 4
    pw = 2 * HD
    whole = lambda a: pl.BlockSpec(a.shape, lambda p, s: (0,) * a.ndim)
    wspec = pl.BlockSpec((width, pw), lambda p, s: (0, s[0] * pairs + p))
    col = lambda r, w: pl.BlockSpec((r, w), lambda p, s: (0, p))
    return pl.pallas_call(
        attn_bwd_body,
        grid_spec=pltpu.PrefetchScalarGridSpec(
            num_scalar_prefetch=1,
            grid=(pairs,),
            in_specs=[whole(xo), whole(xt), wspec, wspec, wspec]
            + [col(rows, pw)] * 3
            + [pl.BlockSpec((2, rows, rows), lambda p, s: (p, 0, 0))]
            + [col(half, pw)] * 4,
            out_specs=[col(width, 3 * pw), col(1, pw), col(1, pw)]
            + [pl.BlockSpec((half, width), lambda p, s: (0, 0))] * 2,
            scratch_shapes=[
                pltpu.VMEM((rows, pw), BF16),
                pltpu.VMEM((pw, rows), BF16),
                pltpu.VMEM((pw, rows), BF16),
                pltpu.VMEM((pw, rows), F32),
                pltpu.VMEM((pw, rows), F32),
                pltpu.VMEM((rows, 3 * pw), BF16),
                pltpu.VMEM((width, 3 * pw), BF16),
                pltpu.VMEM((width, rows), BF16),
                pltpu.VMEM((rows, width), F32),
            ],
        ),
        out_shape=[
            shape((width, 3 * pw * pairs), BF16),
            shape((1, pw * pairs), F32),
            shape((1, pw * pairs), F32),
            shape((half, width), F32),
            shape((half, width), BF16),
        ],
        compiler_params=params(),
        cost_estimate=cost(40e9, 20e6),
        name="attn_bwd",
    )(sc, xo, xt, wq, wk, wv, q, k, v, probs, ao, at, go, gt)


def proj_body(sc, a0, a1, x, w0, w1, b, g, s, u_o, f_o, fl_o):
    u = x[...].astype(F32) + (mm(a0[...], w0[...]) + mm(a1[...], w1[...])) + b[...].astype(F32)
    n, _ = row_stats(u)
    first = n * g[...].astype(F32) + s[...].astype(F32)
    u_o[...] = u
    f_o[...] = first
    fl_o[...] = first.astype(BF16)


def proj_norm(sc, a_own, a_got, x, w_output, b, g, s):
    rows, width = x.shape
    t = 256
    row = lambda w: pl.BlockSpec((t, w), lambda i, c: (i, 0))
    vec = pl.BlockSpec((1, width), lambda i, c: (0, 0))
    return pl.pallas_call(
        proj_body,
        grid_spec=pltpu.PrefetchScalarGridSpec(
            num_scalar_prefetch=1,
            grid=(rows // t,),
            in_specs=[
                row(width // 2),
                row(width // 2),
                row(width),
                pl.BlockSpec((width // 2, width), lambda i, c: (c[0], 0)),
                pl.BlockSpec((width // 2, width), lambda i, c: (1 - c[0], 0)),
                vec,
                vec,
                vec,
            ],
            out_specs=[row(width)] * 3,
        ),
        out_shape=[shape((rows, width), F32), shape((rows, width), F32), shape((rows, width), BF16)],
        compiler_params=params(),
        cost_estimate=cost(2 * rows * width * width, 8e6),
        name="proj_norm",
    )(sc, a_own, a_got, x, w_output, w_output, b, g, s)


def norm_one_back_body(sc, gtwo, p0, p1, u, g, w0, w1, gs_o, gb_o, ga0, ga1, gg, sg, bg):
    e = gtwo[...] + p0[...] + p1[...].astype(F32)
    n, rs = row_stats(u[...])
    eg = e * g[...].astype(F32)
    d = (eg - jnp.mean(eg, -1, keepdims=True) - n * jnp.mean(eg * n, -1, keepdims=True)) * rs
    low = d.astype(BF16)
    gs_o[...] = d
    gb_o[...] = low
    ga0[...] = mm(low, w0[...], NT).astype(BF16)
    ga1[...] = mm(low, w1[...], NT).astype(BF16)

    @pl.when(pl.program_id(0) == 0)
    def _():
        gg[...] = jnp.zeros_like(gg)
        sg[...] = jnp.zeros_like(sg)
        bg[...] = jnp.zeros_like(bg)

    gg[...] += jnp.sum(e * n, 0, keepdims=True)
    sg[...] += jnp.sum(e, 0, keepdims=True)
    bg[...] += jnp.sum(low.astype(F32), 0, keepdims=True)


def norm_one_back(sc, gtwo, p0, p1, u, g, w_output):
    rows, width = u.shape
    t = 256
    row = lambda w: pl.BlockSpec((t, w), lambda i, c: (i, 0))
    vec = pl.BlockSpec((1, width), lambda i, c: (0, 0))
    return pl.pallas_call(
        norm_one_back_body,
        grid_spec=pltpu.PrefetchScalarGridSpec(
            num_scalar_prefetch=1,
            grid=(rows // t,),
            in_specs=[row(width)] * 4
            + [
                vec,
                pl.BlockSpec((width // 2, width), lambda i, c: (c[0], 0)),
                pl.BlockSpec((width // 2, width), lambda i, c: (1 - c[0], 0)),
            ],
            out_specs=[row(width)] * 2 + [row(width // 2)] * 2 + [vec] * 3,
        ),
        out_shape=[shape((rows, width), F32), shape((rows, width), BF16)]
        + [shape((rows, width // 2), BF16)] * 2
        + [shape((1, width), F32)] * 3,
        compiler_params=params(),
        cost_estimate=cost(2 * rows * width * width, 10e6),
        name="norm_one_back",
    )(sc, gtwo, p0, p1, u, g, w_output, w_output)


def w_output_body(sc, a0, a1, keep_cols, send_cols, keep, send):
    for i, a in enumerate((a0, a1)):

        @pl.when(pl.program_id(0) == i)
        def _(a=a):
            keep[...] = mm(a[...], keep_cols[...], TN)
            send[...] = mm(a[...], send_cols[...], TN).astype(BF16)


def w_output_grad(sc, a_own, a_got, gb):
    rows, width = gb.shape
    hw = width // 2
    whole = pl.BlockSpec((rows, hw), lambda i, c: (0, 0))
    out = pl.BlockSpec((hw, hw), lambda i, c: (i + c[0] - 2 * i * c[0], 0))
    return pl.pallas_call(
        w_output_body,
        grid_spec=pltpu.PrefetchScalarGridSpec(
            num_scalar_prefetch=1,
            grid=(2,),
            in_specs=[
                whole,
                whole,
                pl.BlockSpec((rows, hw), lambda i, c: (0, c[0])),
                pl.BlockSpec((rows, hw), lambda i, c: (0, 1 - c[0])),
            ],
            out_specs=[out, out],
        ),
        out_shape=[shape((width, hw), F32), shape((width, hw), BF16)],
        compiler_params=params(),
        cost_estimate=cost(2 * rows * width * width, 5e6),
        name="w_output_grad",
    )(sc, a_own, a_got, gb, gb)


def ffn_fwd_body(x, w_in, b_in, w_out, act_o, slope_o, feed_o):
    v = mm(x[...], w_in[...]) + b_in[...].astype(F32)
    k0 = 0.7978845608028654
    k1 = 0.044715
    v2 = v * v
    t = jnp.tanh(v * (k0 + (k0 * k1) * v2))
    hp = 0.5 * t + 0.5
    act = (v * hp).astype(BF16)
    slope = hp + (0.5 * v) * (1.0 - t * t) * (k0 + (3 * k0 * k1) * v2)
    act_o[...] = act
    slope_o[...] = slope.astype(BF16)
    feed_o[...] = mm(act, w_out[...], NT).astype(feed_o.dtype)


def ffn_fwd(x, w_in, b_in, w_out, dtype):
    rows, width = x.shape
    ff = w_in.shape[1]
    t = 256
    whole = lambda a: pl.BlockSpec(a.shape, lambda i: (0, 0))
    row = lambda w: pl.BlockSpec((t, w), lambda i: (i, 0))
    return pl.pallas_call(
        ffn_fwd_body,
        grid=(rows // t,),
        in_specs=[row(width), whole(w_in), whole(b_in), whole(w_out)],
        out_specs=[row(ff), row(ff), row(width)],
        out_shape=[shape((rows, ff), BF16)] * 2 + [shape((rows, width), dtype)],
        compiler_params=params(),
        cost_estimate=cost(4 * rows * width * ff, 8e6, rows * ff),
        name="ffn_fwd",
    )(x, w_in, b_in, w_out)


def norm_two_body(first, f0, f1, b, g, s, go, out_o, gtwo_o, gf_o, gg, sg, bg):
    u = first[...] + (f0[...] + f1[...].astype(F32)) + b[...].astype(F32)
    n, rs = row_stats(u)
    gain = g[...].astype(F32)
    out_o[...] = (n * gain + s[...].astype(F32)).astype(BF16)
    e = go[...].astype(F32)
    eg = e * gain
    d = (eg - jnp.mean(eg, -1, keepdims=True) - n * jnp.mean(eg * n, -1, keepdims=True)) * rs
    low = d.astype(BF16)
    gtwo_o[...] = d
    gf_o[...] = low

    @pl.when(pl.program_id(0) == 0)
    def _():
        gg[...] = jnp.zeros_like(gg)
        sg[...] = jnp.zeros_like(sg)
        bg[...] = jnp.zeros_like(bg)

    gg[...] += jnp.sum(e * n, 0, keepdims=True)
    sg[...] += jnp.sum(e, 0, keepdims=True)
    bg[...] += jnp.sum(low.astype(F32), 0, keepdims=True)


def norm_two(first, f0, f1, b, g, s, go):
    rows, width = first.shape
    t = 256
    row = pl.BlockSpec((t, width), lambda i: (i, 0))
    vec = pl.BlockSpec((1, width), lambda i: (0, 0))
    return pl.pallas_call(
        norm_two_body,
        grid=(rows // t,),
        in_specs=[row] * 3 + [vec] * 3 + [row],
        out_specs=[row] * 3 + [vec] * 3,
        out_shape=[
            shape((rows, width), BF16),
            shape((rows, width), F32),
            shape((rows, width), BF16),
        ]
        + [shape((1, width), F32)] * 3,
        compiler_params=params(),
        cost_estimate=cost(30 * rows * width, 8e6),
        name="norm_two",
    )(first, f0, f1, b, g, s, go)


def ffn_bwd_body(gf, slope, w_in, w_out, gh_o, part_o, bg):
    gh = (mm(gf[...], w_out[...]) * slope[...].astype(F32)).astype(BF16)
    gh_o[...] = gh
    part_o[...] = mm(gh, w_in[...], NT).astype(part_o.dtype)

    @pl.when(pl.program_id(0) == 0)
    def _():
        bg[...] = jnp.zeros_like(bg)

    bg[...] += jnp.sum(gh.astype(F32), 0, keepdims=True)


def ffn_bwd(gf, slope, w_in, w_out, dtype):
    rows, width = gf.shape
    ff = w_in.shape[1]
    t = 256
    whole = lambda a: pl.BlockSpec(a.shape, lambda i: (0, 0))
    row = lambda w: pl.BlockSpec((t, w), lambda i: (i, 0))
    return pl.pallas_call(
        ffn_bwd_body,
        grid=(rows // t,),
        in_specs=[row(width), row(ff), whole(w_in), whole(w_out)],
        out_specs=[row(ff), row(width), pl.BlockSpec((1, ff), lambda i: (0, 0))],
        out_shape=[shape((rows, ff), BF16), shape((rows, width), dtype), shape((1, ff), F32)],
        compiler_params=params(),
        cost_estimate=cost(4 * rows * width * ff, 8e6),
        name="ffn_bwd",
    )(gf, slope, w_in, w_out)


def ffn_weights_body(a0, a1, b0, b1, out):
    out[...] = (mm(a0[...], b0[...], TN) + mm(a1[...], b1[...], TN)).astype(BF16)


def ffn_weights(a0, a1, b0, b1):
    rows, width = a0.shape
    ff = b0.shape[1]
    t = 256
    whole = pl.BlockSpec((rows, ff), lambda i: (0, 0))
    lhs = pl.BlockSpec((rows, t), lambda i: (0, i))
    return pl.pallas_call(
        ffn_weights_body,
        grid=(width // t,),
        in_specs=[lhs, lhs, whole, whole],
        out_specs=pl.BlockSpec((t, ff), lambda i: (i, 0)),
        out_shape=shape((width, ff), BF16),
        compiler_params=params(),
        cost_estimate=cost(4 * rows * width * ff, 8e6),
        name="ffn_weights",
    )(a0, a1, b0, b1)


def pick(a, index, axis):
    return lax.dynamic_index_in_dim(a, index, axis, keepdims=False)


def halve(parts, size, bit_axis, stride):
    me = lax.axis_index("dp")
    mine = (me // stride) % 2
    pairs = [(i, i ^ stride) for i in range(size)]
    got = lax.ppermute(pick(parts, 1 - mine, bit_axis), "dp", pairs)
    return (pick(parts, mine, bit_axis).astype(F32) + got.astype(F32)).astype(parts.dtype)


def sum_rest(parts, size):
    groups = size // 4
    me = lax.axis_index("dp")
    high = me // 4
    total = pick(parts, high, 0).astype(F32)
    for s in range(1, groups):
        perm = [(i, (i + 4 * s) % size) for i in range(size)]
        got = lax.ppermute(pick(parts, (high + s) % groups, 0), "dp", perm)
        total = total + got.astype(F32)
    return total


def sum_sequences(grad, size, x_first):
    rows = grad.shape[0]
    parts = grad.reshape(size // 4, 2, 2, rows // size, grad.shape[1])
    if x_first:
        parts = halve(parts, size, 2, 1)
        parts = halve(parts, size, 1, 2)
    else:
        parts = halve(parts, size, 1, 2)
        parts = halve(parts, size, 1, 1)
    return sum_rest(parts, size)


def local_pair(
    dp_size, inputs, grad_out, lengths, rand_blocks, w_query, b_query, w_key, w_value, b_value,
    w_output, b_output, gain_one, shift_one, w_in, b_in, w_out, b_out, gain_two, shift_two,
):
    core = lax.axis_index("mp").astype(jnp.int32)
    swap = lambda a: lax.ppermute(a, "mp", [(0, 1), (1, 0)])
    vec = lambda a: a.reshape(1, -1)
    x = inputs[0]
    half, width = x.shape
    x_got = swap(x)
    rand = jnp.concatenate([rand_blocks[0], swap(rand_blocks[0])], axis=0)
    sc = jnp.stack([core, lengths[0]])
    q, k, v, probs, a_own, a_send = attn_fwd(
        sc, x, x_got, w_query, w_key, w_value, vec(b_query), vec(b_value), rand
    )
    a_got = swap(a_send)
    u_one, first, first_low = proj_norm(
        sc, a_own, a_got, x, w_output, vec(b_output), vec(gain_one), vec(shift_one)
    )
    first_got = swap(first_low)
    act0, slope0, feed0 = ffn_fwd(first_low, w_in, vec(b_in), w_out, F32)
    act1, slope1, feed1 = ffn_fwd(first_got, w_in, vec(b_in), w_out, BF16)
    out, grad_two, grad_feed, gain_two_g, shift_two_g, b_out_g = norm_two(
        first, feed0, swap(feed1), vec(b_out), vec(gain_two), vec(shift_two), grad_out[0]
    )
    gf_got = swap(grad_feed)
    gh0, part0, bi0 = ffn_bwd(grad_feed, slope0, w_in, w_out, F32)
    gh1, part1, bi1 = ffn_bwd(gf_got, slope1, w_in, w_out, BF16)
    part_got = swap(part1)
    w_out_g = ffn_weights(grad_feed, gf_got, act0, act1)
    w_in_g = ffn_weights(first_low, first_got, gh0, gh1)
    gsum, gb, ga0, ga1, gain_one_g, shift_one_g, b_output_g = norm_one_back(
        sc, grad_two, part0, part_got, u_one, vec(gain_one), w_output
    )
    ga_got = swap(ga1)
    wo_keep, wo_send = w_output_grad(sc, a_own, a_got, gb)
    w_output_g = (wo_keep + swap(wo_send).astype(F32)).astype(BF16)
    wqkv_g, bq_g, bv_g, ig_own, ig_send = attn_bwd(
        sc, x, x_got, w_query, w_key, w_value, q, k, v, probs, a_own, a_send, ga0, ga_got
    )
    input_grad = gsum + (ig_own + swap(ig_send).astype(F32))

    def spread(part, total):
        return lax.dynamic_update_slice(
            jnp.zeros((1, total), F32), part, (jnp.int32(0), core * part.shape[1])
        )

    ff_all = 2 * w_in.shape[1]
    vectors = [
        spread(bq_g, width), spread(bv_g, width), b_output_g, gain_one_g, shift_one_g, b_out_g,
        gain_two_g, shift_two_g, spread(bi0 + bi1, ff_all),
    ]
    table = jnp.concatenate([a.reshape(dp_size, -1) for a in vectors], axis=1)
    table = table + swap(table)
    rows = width // dp_size
    lanes = 2 * HD
    table = jnp.pad(table, ((0, 0), (0, rows * lanes - table.shape[1])))
    table = table.astype(BF16).reshape(width, lanes)

    cut = 2 * width // 2
    late = jnp.concatenate([wqkv_g[:, cut:], w_output_g, table], axis=1)
    out_part = sum_sequences(w_out_g, dp_size, True)
    in_part = sum_sequences(w_in_g, dp_size, False)
    early_part = sum_sequences(wqkv_g[:, :cut], dp_size, True)
    late_part = sum_sequences(late, dp_size, False)

    qkv = jnp.concatenate([early_part, late_part[:, : wqkv_g.shape[1] - cut]], axis=1)
    qkv = qkv.reshape(rows, HEADS // 4, 3, 2 * HD)
    wq_p, wk_p, wv_p = (qkv[:, :, i].reshape(rows, width // 2) for i in range(3))
    wo_p = late_part[:, wqkv_g.shape[1] - cut :][:, : width // 2]
    flat = late_part[:, wqkv_g.shape[1] - cut + width // 2 :].reshape(-1)
    vs = [flat[i * rows : (i + 1) * rows] for i in range(8)]
    bi_p = flat[8 * rows : 8 * rows + ff_all // dp_size]
    return (
        out[None], input_grad[None], wq_p, vs[0], wk_p, wv_p, vs[1], wo_p, vs[2], vs[3], vs[4],
        in_part, bi_p, out_part, vs[5], vs[6], vs[7],
    )


def layer_norm(features, norm_gain, norm_shift):
    row_mean = jnp.mean(features, axis=-1, keepdims=True)
    centered = features - row_mean
    variance = jnp.mean(centered * centered, axis=-1, keepdims=True)
    return centered * lax.rsqrt(variance + norm_epsilon) * norm_gain + norm_shift


def gelu_tanh(features):
    return jax.nn.gelu(features, approximate=True)


def slot_table_ids(block_ids, rand_rows, length):
    valid_blocks = (length + BLK - 1) // BLK
    column = block_ids[:, None]
    columns = jnp.concatenate(
        [
            column - 1,
            column,
            column + 1,
            rand_rows,
            jnp.zeros_like(column),
            jnp.zeros_like(column) + valid_blocks - 1,
        ],
        axis=1,
    )
    in_range = (columns >= 0) & (columns < valid_blocks)
    slot_ids = jnp.arange(columns.shape[1], dtype=jnp.int32)
    earlier = slot_ids[None, :] < slot_ids[:, None]
    repeated = jnp.any(
        (columns[:, :, None] == columns[:, None, :]) & earlier[None, :, :] & in_range[:, None, :],
        axis=2,
    )
    return (jnp.clip(columns, 0, NB - 1), in_range & jnp.logical_not(repeated))


def slot_table(first_block, rand_rows, length):
    block_ids = first_block + jnp.arange(rand_rows.shape[0], dtype=jnp.int32)
    return slot_table_ids(block_ids, rand_rows, length)


def slot_mask(slot_blocks, slot_valid, length):
    positions = slot_blocks[:, :, None] * BLK + jnp.arange(BLK, dtype=jnp.int32)
    allowed = slot_valid[:, :, None] & (positions < length)
    return allowed.reshape(slot_blocks.shape[0], 1, 1, -1)


def gather_slots(whole_rows, slot_blocks):
    picked = whole_rows.reshape(NB, BLK, whole_rows.shape[1])[slot_blocks]
    return picked.reshape(slot_blocks.shape[0], slot_blocks.shape[1] * BLK, HEADS, HD)


def log_total(scores, allowed):
    masked = jnp.where(allowed, scores, negative_fill)
    top_score = jnp.max(masked, axis=-1, keepdims=True)
    return top_score + jnp.log(jnp.sum(jnp.exp(masked - top_score), axis=-1, keepdims=True))


def exp_probs(scores, allowed, totals):
    return jnp.exp(jnp.where(allowed, scores, negative_fill) - totals)


def global_targets(length, device, local_blocks):
    last_block = (length + BLK - 1) // BLK - 1
    targets = []
    for target_block in (jnp.zeros_like(last_block), last_block):
        is_owner = target_block // local_blocks == device
        local_block = jnp.clip(target_block - device * local_blocks, 0, local_blocks - 1)
        targets.append((is_owner, local_block))
    return targets


def global_scores(query_rows, key_one, length):
    scores = jnp.einsum(
        "qhd,khd->hqk",
        query_rows.reshape(BLK, HEADS, HD),
        key_one.reshape(-1, HEADS, HD),
        preferred_element_type=jnp.float32,
    ) * HD ** (-0.5)
    allowed = (jnp.arange(key_one.shape[0], dtype=jnp.int32) < length)[None, None, :]
    return (scores, allowed)


def global_forward(query_rows, key_one, value_one, length):
    scores, allowed = global_scores(query_rows, key_one, length)
    totals = log_total(scores, allowed)
    weighting = exp_probs(scores, allowed, totals).astype(jnp.bfloat16)
    out_rows = jnp.einsum(
        "hqk,khd->qhd",
        weighting,
        value_one.reshape(-1, HEADS, HD),
        preferred_element_type=jnp.float32,
    )
    return (out_rows.reshape(BLK, -1), totals)


def global_skip(query_rows, key_one, value_one, length):
    return (jnp.zeros((BLK, HEADS * HD), jnp.float32), jnp.zeros((HEADS, BLK, 1), jnp.float32))


def global_backward(query_rows, grad_rows, key_one, value_one, length, row_totals):
    score_scale = HD ** (-0.5)
    scores, allowed = global_scores(query_rows, key_one, length)
    exact_probs = exp_probs(scores, allowed, row_totals)
    grad_heads = grad_rows.reshape(BLK, HEADS, HD)
    grad_weights = jnp.einsum(
        "qhd,khd->hqk",
        grad_heads,
        value_one.reshape(-1, HEADS, HD),
        preferred_element_type=jnp.float32,
    )
    delta_sum = jnp.sum(exact_probs * grad_weights, axis=-1, keepdims=True)
    grad_scores = (exact_probs * (grad_weights - delta_sum)).astype(jnp.bfloat16)
    grad_query = (
        jnp.einsum(
            "hqk,khd->qhd",
            grad_scores,
            key_one.reshape(-1, HEADS, HD),
            preferred_element_type=jnp.float32,
        )
        * score_scale
    )
    grad_keys = (
        jnp.einsum(
            "hqk,qhd->khd",
            grad_scores,
            query_rows.reshape(BLK, HEADS, HD),
            preferred_element_type=jnp.float32,
        )
        * score_scale
    )
    grad_values = jnp.einsum(
        "hqk,qhd->khd",
        exact_probs.astype(jnp.bfloat16),
        grad_heads,
        preferred_element_type=jnp.float32,
    )
    return (
        grad_query.reshape(BLK, -1),
        grad_keys.reshape(key_one.shape[0], -1),
        grad_values.reshape(key_one.shape[0], -1),
    )


def global_back_skip(query_rows, grad_rows, key_one, value_one, length, row_totals):
    key_zeros = jnp.zeros(key_one.shape, jnp.float32)
    return (jnp.zeros((BLK, key_one.shape[1]), jnp.float32), key_zeros, key_zeros)


def attend_forward(query_one, key_one, value_one, length, rand_rows, device):
    local_blocks = rand_rows.shape[0]
    slot_blocks, slot_valid = slot_table(device * local_blocks, rand_rows, length)
    allowed = slot_mask(slot_blocks, slot_valid, length)
    query_blocks = query_one.reshape(local_blocks, BLK, HEADS, HD)
    scores = jnp.einsum(
        "nqhd,nkhd->nhqk",
        query_blocks,
        gather_slots(key_one, slot_blocks),
        preferred_element_type=jnp.float32,
    ) * HD ** (-0.5)
    totals = log_total(scores, allowed)
    weighting = exp_probs(scores, allowed, totals).astype(jnp.bfloat16)
    attended = jnp.einsum(
        "nhqk,nkhd->nqhd",
        weighting,
        gather_slots(value_one, slot_blocks),
        preferred_element_type=jnp.float32,
    ).reshape(query_one.shape[0], -1)
    global_totals = []
    for is_owner, local_block in global_targets(length, device, local_blocks):
        query_rows = lax.dynamic_slice_in_dim(query_one, local_block * BLK, BLK, 0)
        out_rows, row_totals = lax.cond(
            is_owner, global_forward, global_skip, query_rows, key_one, value_one, length
        )
        updated = lax.dynamic_update_slice_in_dim(attended, out_rows, local_block * BLK, 0)
        attended = jnp.where(is_owner, updated, attended)
        global_totals.append(row_totals)
    return (attended, totals, global_totals[0], global_totals[1])


def attend_backward(
    query_one,
    key_one,
    value_one,
    length,
    rand_rows,
    totals,
    first_totals,
    last_totals,
    grad_one,
    device,
):
    score_scale = HD ** (-0.5)
    local_blocks = rand_rows.shape[0]
    first_block = device * local_blocks
    slot_blocks, slot_valid = slot_table(first_block, rand_rows, length)
    allowed = slot_mask(slot_blocks, slot_valid, length)
    query_blocks = query_one.reshape(local_blocks, BLK, HEADS, HD)
    key_slots = gather_slots(key_one, slot_blocks)
    value_slots = gather_slots(value_one, slot_blocks)
    scores = (
        jnp.einsum("nqhd,nkhd->nhqk", query_blocks, key_slots, preferred_element_type=jnp.float32)
        * score_scale
    )
    exact_probs = exp_probs(scores, allowed, totals)
    last_block = (length + BLK - 1) // BLK - 1
    row_blocks = first_block + jnp.arange(query_one.shape[0], dtype=jnp.int32) // BLK
    is_global = (row_blocks == 0) | (row_blocks == last_block)
    grad_sparse = jnp.where(is_global[:, None], jnp.zeros_like(grad_one), grad_one)
    grad_heads = grad_sparse.reshape(local_blocks, BLK, HEADS, HD)
    grad_weights = jnp.einsum(
        "nqhd,nkhd->nhqk", grad_heads, value_slots, preferred_element_type=jnp.float32
    )
    delta_sum = jnp.sum(exact_probs * grad_weights, axis=-1, keepdims=True)
    grad_scores = (exact_probs * (grad_weights - delta_sum)).astype(jnp.bfloat16)
    grad_query = (
        jnp.einsum(
            "nhqk,nkhd->nqhd", grad_scores, key_slots, preferred_element_type=jnp.float32
        ).reshape(query_one.shape[0], -1)
        * score_scale
    )
    grad_key_slots = (
        jnp.einsum("nhqk,nqhd->nkhd", grad_scores, query_blocks, preferred_element_type=jnp.float32)
        * score_scale
    )
    grad_value_slots = jnp.einsum(
        "nhqk,nqhd->nkhd",
        exact_probs.astype(jnp.bfloat16),
        grad_heads,
        preferred_element_type=jnp.float32,
    )
    flat_ids = slot_blocks.reshape(-1)
    slot_width = BLK * query_one.shape[1]
    grad_keys = jax.ops.segment_sum(
        grad_key_slots.reshape(-1, slot_width), flat_ids, num_segments=NB
    ).reshape(-1, query_one.shape[1])
    grad_values = jax.ops.segment_sum(
        grad_value_slots.reshape(-1, slot_width), flat_ids, num_segments=NB
    ).reshape(-1, query_one.shape[1])
    for (is_owner, local_block), row_totals in zip(
        global_targets(length, device, local_blocks), (first_totals, last_totals)
    ):
        query_rows = lax.dynamic_slice_in_dim(query_one, local_block * BLK, BLK, 0)
        grad_rows = lax.dynamic_slice_in_dim(grad_one, local_block * BLK, BLK, 0)
        query_add, key_add, value_add = lax.cond(
            is_owner,
            global_backward,
            global_back_skip,
            query_rows,
            grad_rows,
            key_one,
            value_one,
            length,
            row_totals,
        )
        current = lax.dynamic_slice_in_dim(grad_query, local_block * BLK, BLK, 0)
        grad_query = lax.dynamic_update_slice_in_dim(
            grad_query, current + query_add, local_block * BLK, 0
        )
        grad_keys = grad_keys + key_add
        grad_values = grad_values + value_add
    return (grad_query, grad_keys, grad_values)


def local(
    inputs,
    grad_out,
    lengths,
    rand_blocks,
    w_query,
    b_query,
    w_key,
    w_value,
    b_value,
    w_output,
    b_output,
    gain_one,
    shift_one,
    w_in,
    b_in,
    w_out,
    b_out,
    gain_two,
    shift_two,
):
    device = lax.axis_index("mp")
    seq_count, local_rows, width = inputs.shape
    flat_in = inputs.reshape(-1, width)
    query = (jnp.dot(flat_in, w_query, preferred_element_type=jnp.float32) + b_query).astype(
        jnp.bfloat16
    )
    keys = jnp.dot(flat_in, w_key, preferred_element_type=jnp.float32).astype(jnp.bfloat16)
    values = (jnp.dot(flat_in, w_value, preferred_element_type=jnp.float32) + b_value).astype(
        jnp.bfloat16
    )
    key_all, value_all = (
        lax.all_gather(keys.reshape(seq_count, local_rows, width), "mp", axis=1, tiled=True),
        lax.all_gather(values.reshape(seq_count, local_rows, width), "mp", axis=1, tiled=True),
    )
    query_seq = query.reshape(seq_count, local_rows, width)

    def forward_item(seq_items):
        query_one, key_one, value_one, length, rand_rows = seq_items
        return attend_forward(query_one, key_one, value_one, length, rand_rows, device)

    attended, totals, first_totals, last_totals = lax.map(
        forward_item, (query_seq, key_all, value_all, lengths, rand_blocks)
    )
    attended_low = attended.reshape(-1, width).astype(jnp.bfloat16)
    summed_one = (
        flat_in.astype(jnp.float32)
        + jnp.dot(attended_low, w_output, preferred_element_type=jnp.float32)
        + b_output
    )
    first, norm_one_back = jax.vjp(
        layer_norm, summed_one, gain_one.astype(jnp.float32), shift_one.astype(jnp.float32)
    )
    first_low = first.astype(jnp.bfloat16)
    rows_all = lax.all_gather(first_low, "mp", axis=0, tiled=True)
    hidden = jnp.dot(rows_all, w_in, preferred_element_type=jnp.float32) + b_in
    active_full, gelu_back = jax.vjp(gelu_tanh, hidden)
    active = active_full.astype(jnp.bfloat16)
    feed = lax.psum_scatter(
        jnp.einsum(
            "rf,df->rd",
            lax.slice_in_dim(active, 0, first_low.shape[0] * lax.axis_size("mp"), axis=0),
            w_out,
            preferred_element_type=jnp.float32,
        ),
        "mp",
        scatter_dimension=0,
        tiled=True,
    )
    summed_two = first + feed + b_out
    output, norm_two_back = jax.vjp(
        layer_norm, summed_two, gain_two.astype(jnp.float32), shift_two.astype(jnp.float32)
    )
    grad_two, gain_two_grad, shift_two_grad = norm_two_back(
        grad_out.reshape(-1, width).astype(jnp.float32)
    )
    grad_feed = grad_two.astype(jnp.bfloat16)
    b_out_grad = jnp.sum(grad_feed, axis=0, dtype=jnp.float32)
    grads_all = lax.all_gather(grad_feed, "mp", axis=0, tiled=True)
    w_out_grad = jnp.einsum("rd,rf->df", grads_all, active, preferred_element_type=jnp.float32)
    grad_hidden = gelu_back(jnp.dot(grads_all, w_out, preferred_element_type=jnp.float32))[
        0
    ].astype(jnp.bfloat16)
    w_in_grad = jnp.einsum("rd,rf->df", rows_all, grad_hidden, preferred_element_type=jnp.float32)
    grad_first = grad_two + lax.psum_scatter(
        jnp.einsum(
            "rf,df->rd",
            lax.slice_in_dim(grad_hidden, 0, grad_feed.shape[0] * lax.axis_size("mp"), axis=0),
            w_in,
            preferred_element_type=jnp.float32,
        ),
        "mp",
        scatter_dimension=0,
        tiled=True,
    )
    b_in_grad = lax.dynamic_update_slice_in_dim(
        jnp.zeros((FF,), jnp.float32),
        jnp.sum(grad_hidden, axis=0, dtype=jnp.float32),
        device * w_in.shape[1],
        0,
    )
    grad_sum_one, gain_one_grad, shift_one_grad = norm_one_back(grad_first)
    grad_branch = grad_sum_one.astype(jnp.bfloat16)
    b_output_grad = jnp.sum(grad_branch, axis=0, dtype=jnp.float32)
    w_output_grad = jnp.einsum(
        "rd,re->de", attended_low, grad_branch, preferred_element_type=jnp.float32
    )
    grad_attended = (
        jnp.einsum("re,de->rd", grad_branch, w_output, preferred_element_type=jnp.float32)
        .astype(jnp.bfloat16)
        .reshape(seq_count, local_rows, width)
    )

    def backward_item(seq_items):
        (
            query_one,
            key_one,
            value_one,
            length,
            rand_rows,
            sparse_totals,
            first_one,
            last_one,
            grad_one,
        ) = seq_items
        return attend_backward(
            query_one,
            key_one,
            value_one,
            length,
            rand_rows,
            sparse_totals,
            first_one,
            last_one,
            grad_one,
            device,
        )

    grad_query, grad_keys, grad_values = lax.map(
        backward_item,
        (
            query_seq,
            key_all,
            value_all,
            lengths,
            rand_blocks,
            totals,
            first_totals,
            last_totals,
            grad_attended,
        ),
    )
    key_sums, value_sums = (
        lax.psum_scatter(
            grad_keys.astype(jnp.bfloat16), "mp", scatter_dimension=1, tiled=True
        ).astype(jnp.float32),
        lax.psum_scatter(
            grad_values.astype(jnp.bfloat16), "mp", scatter_dimension=1, tiled=True
        ).astype(jnp.float32),
    )
    grad_q_low = grad_query.reshape(-1, width).astype(jnp.bfloat16)
    grad_k_low = key_sums.reshape(-1, width).astype(jnp.bfloat16)
    grad_v_low = value_sums.reshape(-1, width).astype(jnp.bfloat16)
    input_grad = grad_sum_one + jnp.einsum(
        "re,de->rd", grad_q_low, w_query, preferred_element_type=jnp.float32
    )
    input_grad = input_grad + jnp.einsum(
        "re,de->rd", grad_k_low, w_key, preferred_element_type=jnp.float32
    )
    input_grad = input_grad + jnp.einsum(
        "re,de->rd", grad_v_low, w_value, preferred_element_type=jnp.float32
    )
    w_query_grad = jnp.einsum("rd,re->de", flat_in, grad_q_low, preferred_element_type=jnp.float32)
    w_key_grad = jnp.einsum("rd,re->de", flat_in, grad_k_low, preferred_element_type=jnp.float32)
    w_value_grad = jnp.einsum("rd,re->de", flat_in, grad_v_low, preferred_element_type=jnp.float32)
    b_query_grad = jnp.sum(grad_q_low, axis=0, dtype=jnp.float32)
    b_value_grad = jnp.sum(grad_v_low, axis=0, dtype=jnp.float32)
    reduced = (
        lax.psum_scatter(
            w_query_grad.astype(jnp.bfloat16), "dp", scatter_dimension=0, tiled=True
        ).astype(jnp.float32),
        lax.psum_scatter(
            w_key_grad.astype(jnp.bfloat16), "dp", scatter_dimension=0, tiled=True
        ).astype(jnp.float32),
        lax.psum_scatter(
            w_value_grad.astype(jnp.bfloat16), "dp", scatter_dimension=0, tiled=True
        ).astype(jnp.float32),
        lax.psum_scatter(
            w_output_grad.astype(jnp.bfloat16), "dp", scatter_dimension=0, tiled=True
        ).astype(jnp.float32),
        lax.psum_scatter(
            w_in_grad.astype(jnp.bfloat16), "dp", scatter_dimension=0, tiled=True
        ).astype(jnp.float32),
        lax.psum_scatter(
            w_out_grad.astype(jnp.bfloat16), "dp", scatter_dimension=0, tiled=True
        ).astype(jnp.float32),
        lax.psum_scatter(
            b_query_grad.astype(jnp.bfloat16), "dp", scatter_dimension=0, tiled=True
        ).astype(jnp.float32),
        lax.psum_scatter(
            b_value_grad.astype(jnp.bfloat16), "dp", scatter_dimension=0, tiled=True
        ).astype(jnp.float32),
        lax.psum_scatter(
            b_output_grad.astype(jnp.bfloat16), "dp", scatter_dimension=0, tiled=True
        ).astype(jnp.float32),
        lax.psum_scatter(
            gain_one_grad.astype(jnp.bfloat16), "dp", scatter_dimension=0, tiled=True
        ).astype(jnp.float32),
        lax.psum_scatter(
            shift_one_grad.astype(jnp.bfloat16), "dp", scatter_dimension=0, tiled=True
        ).astype(jnp.float32),
        lax.psum_scatter(
            b_in_grad.astype(jnp.bfloat16), "dp", scatter_dimension=0, tiled=True
        ).astype(jnp.float32),
        lax.psum_scatter(
            b_out_grad.astype(jnp.bfloat16), "dp", scatter_dimension=0, tiled=True
        ).astype(jnp.float32),
        lax.psum_scatter(
            gain_two_grad.astype(jnp.bfloat16), "dp", scatter_dimension=0, tiled=True
        ).astype(jnp.float32),
        lax.psum_scatter(
            shift_two_grad.astype(jnp.bfloat16), "dp", scatter_dimension=0, tiled=True
        ).astype(jnp.float32),
    )
    query_part, key_part_out, value_part, output_part = (
        lax.psum_scatter(
            reduced[0].astype(jnp.bfloat16), "mp", scatter_dimension=1, tiled=True
        ).astype(jnp.float32),
        lax.psum_scatter(
            reduced[1].astype(jnp.bfloat16), "mp", scatter_dimension=1, tiled=True
        ).astype(jnp.float32),
        lax.psum_scatter(
            reduced[2].astype(jnp.bfloat16), "mp", scatter_dimension=1, tiled=True
        ).astype(jnp.float32),
        lax.psum_scatter(
            reduced[3].astype(jnp.bfloat16), "mp", scatter_dimension=1, tiled=True
        ).astype(jnp.float32),
    )
    in_part = reduced[4]
    out_part = reduced[5]
    vectors = lax.psum(
        (
            reduced[6],
            reduced[7],
            reduced[8],
            reduced[9],
            reduced[10],
            reduced[11],
            reduced[12],
            reduced[13],
            reduced[14],
        ),
        "mp",
    )
    return (
        output.astype(jnp.bfloat16).reshape(seq_count, local_rows, width),
        input_grad.reshape(seq_count, local_rows, width),
        query_part,
        vectors[0],
        key_part_out,
        value_part,
        vectors[1],
        output_part,
        vectors[2],
        vectors[3],
        vectors[4],
        in_part,
        vectors[5],
        out_part,
        vectors[6],
        vectors[7],
        vectors[8],
    )


def solution(mesh):
    in_specs = (
        P("dp", "mp", None),
        P("dp", "mp", None),
        P("dp"),
        P("dp", "mp", None),
        P(),
        P(),
        P(),
        P(),
        P(),
        P(),
        P(),
        P(),
        P(),
        P(None, "mp"),
        P("mp"),
        P(None, "mp"),
        P(),
        P(),
        P(),
    )
    out_specs = (
        P("dp", "mp", None),
        P("dp", "mp", None),
        P("dp", "mp"),
        P("dp"),
        P("dp", "mp"),
        P("dp", "mp"),
        P("dp"),
        P("dp", "mp"),
        P("dp"),
        P("dp"),
        P("dp"),
        P("dp", "mp"),
        P("dp"),
        P("dp", "mp"),
        P("dp"),
        P("dp"),
        P("dp"),
    )
    sizes = dict(mesh.shape)
    if sizes["mp"] == 2 and sizes["dp"] % 4 == 0:
        local_fn = functools.partial(local_pair, sizes["dp"])
    else:
        local_fn = local
    return jax.shard_map(local_fn, mesh=mesh, in_specs=in_specs, out_specs=out_specs, check_vma=False)
```

```python
import functools

import jax
import jax.numpy as jnp
from jax import lax
from jax.experimental import pallas as pl
from jax.experimental.pallas import tpu as pltpu
from jax.sharding import PartitionSpec as P

HEADS = 12
HD = 64
FF = 3072
BLK = 64
NB = 16


negative_fill = -1000000000.0
norm_epsilon = 1e-12


F32 = jnp.float32
BF16 = jnp.bfloat16
NN = (((1,), (0,)), ((), ()))
NT = (((1,), (1,)), ((), ()))
TN = (((0,), (0,)), ((), ()))


def mm(a, b, dims=NN):
    return lax.dot_general(a, b, dims, preferred_element_type=F32)


def params(mib=56):
    return pltpu.CompilerParams(vmem_limit_bytes=mib << 20)


def cost(flops, nbytes, trans=0):
    return pl.CostEstimate(flops=int(flops), bytes_accessed=int(nbytes), transcendentals=int(trans))


def shape(dims, dtype):
    return jax.ShapeDtypeStruct(dims, dtype)


def row_stats(u):
    mean = jnp.mean(u, axis=-1, keepdims=True)
    cen = u - mean
    var = jnp.mean(cen * cen, axis=-1, keepdims=True)
    rs = lax.rsqrt(var + norm_epsilon)
    return cen * rs, rs


def attn_fwd_body(sc, xo, xt, wq, wk, wv, bq, bv, rand, q_o, k_o, v_o, p_o, ao, at, bias):
    half = xo.shape[0]
    rows = 2 * half
    nb = rows // BLK
    tile = 256

    @pl.when(pl.program_id(0) == 0)
    def _():
        c = sc[0]
        ln = sc[1]
        last = (ln + BLK - 1) // BLK - 1
        lb = lax.broadcasted_iota(jnp.int32, (nb, rows), 0)
        kp = lax.broadcasted_iota(jnp.int32, (nb, rows), 1)
        qb = jnp.where(lb < nb // 2, lb + (nb // 2) * c, lb - (nb // 2) * c)
        kpos = jnp.where(kp < half, kp + half * c, kp - half * c)
        kb = kpos // BLK
        ok = (jnp.abs(kb - qb) <= 1) | (kb == 0) | (kb == last)
        for j in range(rand.shape[1]):
            ok = ok | (kb == rand[:, j : j + 1])
        ok = ok | (qb == 0) | (qb == last)
        ok = ok & (kpos < ln)
        table = jnp.where(ok, 0.0, -1e30).astype(F32)
        for b in range(nb):
            bias[b] = jnp.broadcast_to(table[b : b + 1, :], (8, rows))

    for i, xr in enumerate((xo, xt)):
        rs = slice(i * half, (i + 1) * half)
        q_o[rs, :] = (mm(xr[...], wq[...]) + bq[...].astype(F32)).astype(BF16)
        k_o[rs, :] = mm(xr[...], wk[...]).astype(BF16)
        v_o[rs, :] = (mm(xr[...], wv[...]) + bv[...].astype(F32)).astype(BF16)

    lane = lax.broadcasted_iota(jnp.int32, (tile, 2 * HD), 1)
    low = lane < HD
    for i, a_ref in enumerate((ao, at)):

        def step(t, carry, i=i, a_ref=a_ref):
            r0 = pl.multiple_of(i * half + t * tile, tile)
            q = q_o[pl.ds(r0, tile), :] * BF16(HD**-0.5)
            outs = []
            for h in range(2):
                qh = jnp.where(low if h == 0 else ~low, q, BF16(0))
                s = mm(qh, k_o[...], NT)
                s = s.reshape(tile // BLK, BLK // 8, 8, rows)
                s = s + bias[pl.ds(r0 // BLK, tile // BLK)][:, None]
                s = s.reshape(tile, rows)
                e = jnp.exp(s - jnp.max(s, axis=-1, keepdims=True))
                p = (e * (1.0 / jnp.sum(e, axis=-1, keepdims=True))).astype(BF16)
                p_o[h, pl.ds(r0, tile), :] = p
                outs.append(mm(p, v_o[...]))
            a = jnp.where(low, outs[0], outs[1]).astype(BF16)
            a_ref[pl.ds(pl.multiple_of(t * tile, tile), tile), :] = a
            return carry

        lax.fori_loop(0, half // tile, step, 0)


def attn_fwd(sc, xo, xt, wq, wk, wv, bq, bv, rand):
    half, width = xo.shape
    rows = 2 * half
    pairs = HEADS // 4
    pw = 2 * HD
    whole = lambda a: pl.BlockSpec(a.shape, lambda p, s: (0,) * a.ndim)
    wspec = pl.BlockSpec((width, pw), lambda p, s: (0, s[0] * pairs + p))
    bspec = pl.BlockSpec((1, pw), lambda p, s: (0, s[0] * pairs + p))
    ospec = lambda r: pl.BlockSpec((r, pw), lambda p, s: (0, p))
    return pl.pallas_call(
        attn_fwd_body,
        grid_spec=pltpu.PrefetchScalarGridSpec(
            num_scalar_prefetch=1,
            grid=(pairs,),
            in_specs=[whole(xo), whole(xt), wspec, wspec, wspec, bspec, bspec, whole(rand)],
            out_specs=[ospec(rows)] * 3
            + [pl.BlockSpec((2, rows, rows), lambda p, s: (p, 0, 0))]
            + [ospec(half)] * 2,
            scratch_shapes=[pltpu.VMEM((rows // BLK, 8, rows), F32)],
        ),
        out_shape=[shape((rows, pairs * pw), BF16)] * 3
        + [shape((2 * pairs, rows, rows), BF16)]
        + [shape((half, pairs * pw), BF16)] * 2,
        compiler_params=params(),
        cost_estimate=cost(20e9, 20e6, 6 * rows * rows),
        name="attn_fwd",
    )(sc, xo, xt, wq, wk, wv, bq, bv, rand)


def attn_bwd_body(
    sc, xo, xt, wq, wk, wv, q_i, k_i, v_i, p_i, ao, at, go, gt,
    wg, bqg, bvg, igo, igt, g_s, gT, qT, dkT, dvT, dqkv, wcat, xT, acc,
):
    half = xo.shape[0]
    rows = 2 * half
    pw = 2 * HD
    tile = 256
    step_id = pl.program_id(0)

    @pl.when(step_id == 0)
    def _():
        xT[:, :half] = xo[...].T
        xT[:, half:] = xt[...].T

    for i, w in enumerate((wq, wk, wv)):
        wcat[:, i * pw : (i + 1) * pw] = w[...]
    g_s[:half, :] = go[...]
    g_s[half:, :] = gt[...]
    gT[...] = g_s[...].T
    qT[...] = q_i[...].T
    dkT[...] = jnp.zeros_like(dkT)
    dvT[...] = jnp.zeros_like(dvT)
    lane = lax.broadcasted_iota(jnp.int32, (tile, pw), 1)
    low = lane < HD

    for i, a_ref in enumerate((ao, at)):

        def step(t, carry, i=i, a_ref=a_ref):
            r0 = pl.multiple_of(i * half + t * tile, tile)
            a0 = pl.multiple_of(t * tile, tile)
            g = g_s[pl.ds(r0, tile), :]
            ga = g.astype(F32) * a_ref[pl.ds(a0, tile), :].astype(F32)
            outs = []
            for h in range(2):
                mine = low if h == 0 else ~low
                hs = slice(h * HD, (h + 1) * HD)
                dp = mm(jnp.where(mine, g, BF16(0)), v_i[...], NT)
                delta = jnp.sum(jnp.where(mine, ga, 0.0), axis=-1, keepdims=True)
                p = p_i[h, pl.ds(r0, tile), :]
                ds = (p.astype(F32) * (dp - delta)).astype(BF16)
                outs.append(mm(ds, k_i[...]))
                dvT[hs, :] += mm(gT[hs, pl.ds(r0, tile)], p)
                dkT[hs, :] += mm(qT[hs, pl.ds(r0, tile)], ds)
            dq = jnp.where(low, outs[0], outs[1]) * HD**-0.5
            dqkv[pl.ds(r0, tile), 0:pw] = dq.astype(BF16)
            return carry

        lax.fori_loop(0, half // tile, step, 0)

    dqkv[:, pw : 2 * pw] = (dkT[...].T * HD**-0.5).astype(BF16)
    dqkv[:, 2 * pw : 3 * pw] = dvT[...].T.astype(BF16)
    d = dqkv[...]
    wg[...] = mm(xT[...], d).astype(BF16)
    bqg[...] = jnp.sum(d[:, 0:pw].astype(F32), axis=0, keepdims=True)
    bvg[...] = jnp.sum(d[:, 2 * pw :].astype(F32), axis=0, keepdims=True)
    part = mm(d, wcat[...], NT)

    @pl.when(step_id == 0)
    def _():
        acc[...] = part

    @pl.when((step_id > 0) & (step_id < pl.num_programs(0) - 1))
    def _():
        acc[...] += part

    @pl.when(step_id == pl.num_programs(0) - 1)
    def _():
        total = acc[...] + part
        igo[...] = total[:half]
        igt[...] = total[half:].astype(BF16)


def attn_bwd(sc, xo, xt, wq, wk, wv, q, k, v, probs, ao, at, go, gt):
    half, width = xo.shape
    rows = 2 * half
    pairs = HEADS // 4
    pw = 2 * HD
    whole = lambda a: pl.BlockSpec(a.shape, lambda p, s: (0,) * a.ndim)
    wspec = pl.BlockSpec((width, pw), lambda p, s: (0, s[0] * pairs + p))
    col = lambda r, w: pl.BlockSpec((r, w), lambda p, s: (0, p))
    return pl.pallas_call(
        attn_bwd_body,
        grid_spec=pltpu.PrefetchScalarGridSpec(
            num_scalar_prefetch=1,
            grid=(pairs,),
            in_specs=[whole(xo), whole(xt), wspec, wspec, wspec]
            + [col(rows, pw)] * 3
            + [pl.BlockSpec((2, rows, rows), lambda p, s: (p, 0, 0))]
            + [col(half, pw)] * 4,
            out_specs=[col(width, 3 * pw), col(1, pw), col(1, pw)]
            + [pl.BlockSpec((half, width), lambda p, s: (0, 0))] * 2,
            scratch_shapes=[
                pltpu.VMEM((rows, pw), BF16),
                pltpu.VMEM((pw, rows), BF16),
                pltpu.VMEM((pw, rows), BF16),
                pltpu.VMEM((pw, rows), F32),
                pltpu.VMEM((pw, rows), F32),
                pltpu.VMEM((rows, 3 * pw), BF16),
                pltpu.VMEM((width, 3 * pw), BF16),
                pltpu.VMEM((width, rows), BF16),
                pltpu.VMEM((rows, width), F32),
            ],
        ),
        out_shape=[
            shape((width, 3 * pw * pairs), BF16),
            shape((1, pw * pairs), F32),
            shape((1, pw * pairs), F32),
            shape((half, width), F32),
            shape((half, width), BF16),
        ],
        compiler_params=params(),
        cost_estimate=cost(40e9, 20e6),
        name="attn_bwd",
    )(sc, xo, xt, wq, wk, wv, q, k, v, probs, ao, at, go, gt)


def partner_copy(src, dst, send, recv, me):
    return pltpu.make_async_remote_copy(
        src_ref=src, dst_ref=dst, send_sem=send, recv_sem=recv,
        device_id={"mp": 1 - me}, device_id_type=pl.DeviceIdType.MESH,
    )


def gelu_and_slope(v):
    k0 = 0.7978845608028654
    k1 = 0.044715
    v2 = v * v
    t = jnp.tanh(v * (k0 + (k0 * k1) * v2))
    hp = 0.5 * t + 0.5
    return v * hp, hp + (0.5 * v) * (1.0 - t * t) * (k0 + (3 * k0 * k1) * v2)


def norm_back(e, n, rs, gain):
    eg = e * gain
    return (eg - jnp.mean(eg, -1, keepdims=True) - n * jnp.mean(eg * n, -1, keepdims=True)) * rs


def middle_body(
    a_own, a_send, x, gout, b_output, gain1, shift1, b_in, b_out, gain2, shift2,
    w_o_h, w_in_h, w_out_h,
    out_o, gsum_o, ga_o, gat_o, wout_g, win_g, wo_g, vec_o, bi_o,
    a_got, fl, feed_s, feed_g, gf, part_s, part_g, gat_s, gb, wo_s, wo_r, vec_s, vec_r, bi_s,
    w_o, w_in, w_out, act, slope, gh, u_s, first_s, own_s, gtwo_s,
    load_sem, send_sem, recv_sem,
):
    me = lax.axis_index("mp")
    half, width = x.shape
    hw = width // 2
    tile = 256
    tiles = half // tile
    barrier = pltpu.get_barrier_semaphore()
    pl.semaphore_signal(
        barrier, inc=1, device_id={"mp": 1 - me}, device_id_type=pl.DeviceIdType.MESH
    )
    loads = []
    for i, (src, dst) in enumerate(((w_o_h, w_o), (w_in_h, w_in), (w_out_h, w_out))):
        loads.append(pltpu.make_async_copy(src, dst, load_sem.at[i]))
        loads[-1].start()
    pl.semaphore_wait(barrier, 1)

    def copy(src, dst, i):
        return partner_copy(src, dst, send_sem.at[i], recv_sem.at[i], me)

    a_copy = copy(a_send, a_got, 0)
    a_copy.start()
    loads[0].wait()
    a_copy.wait_recv()

    def rows(t):
        return pl.ds(pl.multiple_of(t * tile, tile), tile)

    def fl_copy(t):
        return copy(fl.at[0, rows(t)], fl.at[1, rows(t)], 1 + t)

    def feed_copy(t):
        return copy(feed_s.at[rows(t)], feed_g.at[rows(t)], 3 + t)

    def gf_copy(t):
        return copy(gf.at[0, rows(t)], gf.at[1, rows(t)], 5 + t)

    def part_copy(t):
        return copy(part_s.at[rows(t)], part_g.at[rows(t)], 7 + t)

    def ga_copy(t):
        return copy(gat_s.at[rows(t)], gat_o.at[rows(t)], 9 + t)

    own_o = pl.ds(pl.multiple_of(me * hw, hw), hw)
    got_o = pl.ds(pl.multiple_of((1 - me) * hw, hw), hw)

    def project(t, carry):
        r = rows(t)
        u = x[r, :].astype(F32) + (
            mm(a_own[r, :], w_o[own_o, :]) + mm(a_got[r, :], w_o[got_o, :])
        ) + b_output[...].astype(F32)
        n, _ = row_stats(u)
        first = n * gain1[...].astype(F32) + shift1[...].astype(F32)
        u_s[r, :] = u
        first_s[r, :] = first
        fl[0, r, :] = first.astype(BF16)
        fl_copy(t).start()
        return carry

    lax.fori_loop(0, tiles, project, 0)
    loads[1].wait()
    loads[2].wait()

    def feed_forward(i, t):
        r = rows(t)
        v = mm(fl[i, r, :], w_in[...]) + b_in[...].astype(F32)
        a, s = gelu_and_slope(v)
        a = a.astype(BF16)
        act[i, r, :] = a
        slope[i, r, :] = s.astype(BF16)
        return mm(a, w_out[...], NT)

    def forward_own(t, carry):
        own_s[rows(t), :] = feed_forward(0, t)
        return carry

    def forward_got(t, carry):
        fl_copy(t).wait_recv()
        feed_s[rows(t), :] = feed_forward(1, t).astype(BF16)
        feed_copy(t).start()
        return carry

    lax.fori_loop(0, tiles, forward_own, 0)
    lax.fori_loop(0, tiles, forward_got, 0)

    vec_s[...] = jnp.zeros_like(vec_s)

    def add_vec(i, value):
        vec_s[i : i + 1, :] += jnp.sum(value, 0, keepdims=True)

    def second_norm(t, carry):
        r = rows(t)
        feed_copy(t).wait_recv()
        u = first_s[r, :] + (own_s[r, :] + feed_g[r, :].astype(F32)) + b_out[...].astype(F32)
        n, rs = row_stats(u)
        gain = gain2[...].astype(F32)
        out_o[r, :] = (n * gain + shift2[...].astype(F32)).astype(BF16)
        e = gout[r, :].astype(F32)
        d = norm_back(e, n, rs, gain)
        low = d.astype(BF16)
        gtwo_s[r, :] = d
        gf[0, r, :] = low
        gf_copy(t).start()
        add_vec(4, e * n)
        add_vec(5, e)
        add_vec(3, low.astype(F32))
        return carry

    lax.fori_loop(0, tiles, second_norm, 0)
    bi_s[...] = jnp.zeros_like(bi_s)

    def feed_back(i, t):
        r = rows(t)
        g = (mm(gf[i, r, :], w_out[...]) * slope[i, r, :].astype(F32)).astype(BF16)
        gh[i, r, :] = g
        bi_s[0:1, :] += jnp.sum(g.astype(F32), 0, keepdims=True)
        return mm(g, w_in[...], NT)

    def back_own(t, carry):
        own_s[rows(t), :] = feed_back(0, t)
        return carry

    def back_got(t, carry):
        gf_copy(t).wait_recv()
        part_s[rows(t), :] = feed_back(1, t).astype(BF16)
        part_copy(t).start()
        return carry

    lax.fori_loop(0, tiles, back_own, 0)
    lax.fori_loop(0, tiles, back_got, 0)

    def weights(out, lhs, rhs):
        def step(j, carry):
            c = pl.ds(pl.multiple_of(j * tile, tile), tile)
            out[c, :] = (
                mm(lhs[0, :, c], rhs[0], TN) + mm(lhs[1, :, c], rhs[1], TN)
            ).astype(BF16)
            return carry

        lax.fori_loop(0, width // tile, step, 0)

    weights(wout_g, gf, act)
    weights(win_g, fl, gh)

    def first_norm(t, carry):
        r = rows(t)
        part_copy(t).wait_recv()
        e = gtwo_s[r, :] + own_s[r, :] + part_g[r, :].astype(F32)
        n, rs = row_stats(u_s[r, :])
        d = norm_back(e, n, rs, gain1[...].astype(F32))
        low = d.astype(BF16)
        gsum_o[r, :] = d
        gb[r, :] = low
        gat_s[r, :] = mm(low, w_o[got_o, :], NT).astype(BF16)
        ga_copy(t).start()
        ga_o[r, :] = mm(low, w_o[own_o, :], NT).astype(BF16)
        add_vec(1, e * n)
        add_vec(2, e)
        add_vec(0, low.astype(F32))
        return carry

    lax.fori_loop(0, tiles, first_norm, 0)
    vec_copy = copy(vec_s, vec_r, 11)
    vec_copy.start()
    bi_copy = copy(bi_s, bi_o.at[1], 12)
    bi_copy.start()
    cols_own = own_o
    cols_got = got_o
    wo_s[own_o, :] = mm(a_own[...], gb[:, cols_got], TN).astype(BF16)
    wo_s[got_o, :] = mm(a_got[...], gb[:, cols_got], TN).astype(BF16)
    wo_copy = copy(wo_s, wo_r, 13)
    wo_copy.start()
    own_part = mm(a_own[...], gb[:, cols_own], TN)
    got_part = mm(a_got[...], gb[:, cols_own], TN)
    bi_o[0] = bi_s[...]
    wo_copy.wait_recv()
    wo_g[own_o, :] = (own_part + wo_r[own_o, :].astype(F32)).astype(BF16)
    wo_g[got_o, :] = (got_part + wo_r[got_o, :].astype(F32)).astype(BF16)
    vec_copy.wait_recv()
    vec_o[...] = vec_s[...] + vec_r[...]
    bi_copy.wait_recv()

    def finish(t, carry):
        ga_copy(t).wait_recv()
        fl_copy(t).wait_send()
        feed_copy(t).wait_send()
        gf_copy(t).wait_send()
        part_copy(t).wait_send()
        ga_copy(t).wait_send()
        return carry

    lax.fori_loop(0, tiles, finish, 0)
    a_copy.wait_send()
    vec_copy.wait_send()
    bi_copy.wait_send()
    wo_copy.wait_send()


def middle(a_own, a_send, x, gout, b_output, gain1, shift1, b_in, b_out, gain2, shift2, w_o, w_in, w_out):
    half, width = x.shape
    hw = width // 2
    ff = w_in.shape[1]
    vm = pl.BlockSpec(memory_space=pltpu.VMEM)
    hbm = pl.BlockSpec(memory_space=pl.ANY)
    V = pltpu.VMEM
    return pl.pallas_call(
        middle_body,
        in_specs=[vm] * 11 + [hbm] * 3,
        out_specs=[vm] * 9,
        out_shape=[
            shape((half, width), BF16),
            shape((half, width), F32),
            shape((half, hw), BF16),
            shape((half, hw), BF16),
            shape((width, ff), BF16),
            shape((width, ff), BF16),
            shape((width, hw), BF16),
            shape((8, width), F32),
            shape((2, 8, ff), F32),
        ],
        scratch_shapes=[
            V((half, hw), BF16),
            V((2, half, width), BF16),
            V((half, width), BF16),
            V((half, width), BF16),
            V((2, half, width), BF16),
            V((half, width), BF16),
            V((half, width), BF16),
            V((half, hw), BF16),
            V((half, width), BF16),
            V((width, hw), BF16),
            V((width, hw), BF16),
            V((8, width), F32),
            V((8, width), F32),
            V((8, ff), F32),
            V((width, width), BF16),
            V((width, ff), BF16),
            V((width, ff), BF16),
            V((2, half, ff), BF16),
            V((2, half, ff), BF16),
            V((2, half, ff), BF16),
            V((half, width), F32),
            V((half, width), F32),
            V((half, width), F32),
            V((half, width), F32),
            pltpu.SemaphoreType.DMA((3,)),
            pltpu.SemaphoreType.DMA((14,)),
            pltpu.SemaphoreType.DMA((14,)),
        ],
        compiler_params=pltpu.CompilerParams(
            vmem_limit_bytes=60 << 20, collective_id=1, has_side_effects=True
        ),
        cost_estimate=cost(17e9, 20e6),
        name="middle",
    )(a_own, a_send, x, gout, b_output, gain1, shift1, b_in, b_out, gain2, shift2, w_o, w_in, w_out)


def pick(a, index, axis):
    return lax.dynamic_index_in_dim(a, index, axis, keepdims=False)


def halve(parts, size, bit_axis, stride):
    me = lax.axis_index("dp")
    mine = (me // stride) % 2
    pairs = [(i, i ^ stride) for i in range(size)]
    got = lax.ppermute(pick(parts, 1 - mine, bit_axis), "dp", pairs)
    return (pick(parts, mine, bit_axis).astype(F32) + got.astype(F32)).astype(parts.dtype)


def sum_rest(parts, size):
    groups = size // 4
    me = lax.axis_index("dp")
    high = me // 4
    total = pick(parts, high, 0).astype(F32)
    for s in range(1, groups):
        perm = [(i, (i + 4 * s) % size) for i in range(size)]
        got = lax.ppermute(pick(parts, (high + s) % groups, 0), "dp", perm)
        total = total + got.astype(F32)
    return total


def sum_sequences(grad, size, x_first):
    rows = grad.shape[0]
    parts = grad.reshape(size // 4, 2, 2, rows // size, grad.shape[1])
    if x_first:
        parts = halve(parts, size, 2, 1)
        parts = halve(parts, size, 1, 2)
    else:
        parts = halve(parts, size, 1, 2)
        parts = halve(parts, size, 1, 1)
    return sum_rest(parts, size)


def local_pair(
    dp_size, inputs, grad_out, lengths, rand_blocks, w_query, b_query, w_key, w_value, b_value,
    w_output, b_output, gain_one, shift_one, w_in, b_in, w_out, b_out, gain_two, shift_two,
):
    core = lax.axis_index("mp").astype(jnp.int32)
    swap = lambda a: lax.ppermute(a, "mp", [(0, 1), (1, 0)])
    vec = lambda a: a.reshape(1, -1)
    x = inputs[0]
    half, width = x.shape
    x_got = swap(x)
    rand = jnp.concatenate([rand_blocks[0], swap(rand_blocks[0])], axis=0)
    sc = jnp.stack([core, lengths[0]])
    q, k, v, probs, a_own, a_send = attn_fwd(
        sc, x, x_got, w_query, w_key, w_value, vec(b_query), vec(b_value), rand
    )
    out, gsum, ga0, ga_got, w_out_g, w_in_g, w_output_g, vec_g, bi_g = middle(
        a_own, a_send, x, grad_out[0], vec(b_output), vec(gain_one), vec(shift_one), vec(b_in),
        vec(b_out), vec(gain_two), vec(shift_two), w_output, w_in, w_out,
    )
    wqkv_g, bq_g, bv_g, ig_own, ig_send = attn_bwd(
        sc, x, x_got, w_query, w_key, w_value, q, k, v, probs, a_own, a_send, ga0, ga_got
    )
    input_grad = gsum + (ig_own + swap(ig_send).astype(F32))

    def spread(part, total):
        return lax.dynamic_update_slice(
            jnp.zeros((1, total), F32), part, (jnp.int32(0), core * part.shape[1])
        )

    ff_all = 2 * w_in.shape[1]
    bqv = jnp.concatenate([spread(bq_g, width), spread(bv_g, width)], axis=0)
    bqv = bqv + swap(bqv)
    bi_all = jnp.where(core == 0, bi_g[:, 0], bi_g[::-1, 0]).reshape(dp_size, -1)
    eight = jnp.concatenate([bqv, vec_g[:6]], axis=0).reshape(8, dp_size, -1)
    table = jnp.concatenate([eight.transpose(1, 0, 2).reshape(dp_size, -1), bi_all], axis=1)
    rows = width // dp_size
    lanes = 2 * HD
    table = jnp.pad(table, ((0, 0), (0, rows * lanes - table.shape[1])))
    table = table.astype(BF16).reshape(width, lanes)

    cut = 2 * width // 2
    late = jnp.concatenate([wqkv_g[:, cut:], w_output_g, table], axis=1)
    out_part = sum_sequences(w_out_g, dp_size, True)
    in_part = sum_sequences(w_in_g, dp_size, False)
    early_part = sum_sequences(wqkv_g[:, :cut], dp_size, True)
    late_part = sum_sequences(late, dp_size, False)

    qkv = jnp.concatenate([early_part, late_part[:, : wqkv_g.shape[1] - cut]], axis=1)
    qkv = qkv.reshape(rows, HEADS // 4, 3, 2 * HD)
    wq_p, wk_p, wv_p = (qkv[:, :, i].reshape(rows, width // 2) for i in range(3))
    wo_p = late_part[:, wqkv_g.shape[1] - cut :][:, : width // 2]
    flat = late_part[:, wqkv_g.shape[1] - cut + width // 2 :].reshape(-1)
    vs = [flat[i * rows : (i + 1) * rows] for i in range(8)]
    bi_p = flat[8 * rows : 8 * rows + ff_all // dp_size]
    return (
        out[None], input_grad[None], wq_p, vs[0], wk_p, wv_p, vs[1], wo_p, vs[2], vs[3], vs[4],
        in_part, bi_p, out_part, vs[5], vs[6], vs[7],
    )


def layer_norm(features, norm_gain, norm_shift):
    row_mean = jnp.mean(features, axis=-1, keepdims=True)
    centered = features - row_mean
    variance = jnp.mean(centered * centered, axis=-1, keepdims=True)
    return centered * lax.rsqrt(variance + norm_epsilon) * norm_gain + norm_shift


def gelu_tanh(features):
    return jax.nn.gelu(features, approximate=True)


def slot_table_ids(block_ids, rand_rows, length):
    valid_blocks = (length + BLK - 1) // BLK
    column = block_ids[:, None]
    columns = jnp.concatenate(
        [
            column - 1,
            column,
            column + 1,
            rand_rows,
            jnp.zeros_like(column),
            jnp.zeros_like(column) + valid_blocks - 1,
        ],
        axis=1,
    )
    in_range = (columns >= 0) & (columns < valid_blocks)
    slot_ids = jnp.arange(columns.shape[1], dtype=jnp.int32)
    earlier = slot_ids[None, :] < slot_ids[:, None]
    repeated = jnp.any(
        (columns[:, :, None] == columns[:, None, :]) & earlier[None, :, :] & in_range[:, None, :],
        axis=2,
    )
    return (jnp.clip(columns, 0, NB - 1), in_range & jnp.logical_not(repeated))


def slot_table(first_block, rand_rows, length):
    block_ids = first_block + jnp.arange(rand_rows.shape[0], dtype=jnp.int32)
    return slot_table_ids(block_ids, rand_rows, length)


def slot_mask(slot_blocks, slot_valid, length):
    positions = slot_blocks[:, :, None] * BLK + jnp.arange(BLK, dtype=jnp.int32)
    allowed = slot_valid[:, :, None] & (positions < length)
    return allowed.reshape(slot_blocks.shape[0], 1, 1, -1)


def gather_slots(whole_rows, slot_blocks):
    picked = whole_rows.reshape(NB, BLK, whole_rows.shape[1])[slot_blocks]
    return picked.reshape(slot_blocks.shape[0], slot_blocks.shape[1] * BLK, HEADS, HD)


def log_total(scores, allowed):
    masked = jnp.where(allowed, scores, negative_fill)
    top_score = jnp.max(masked, axis=-1, keepdims=True)
    return top_score + jnp.log(jnp.sum(jnp.exp(masked - top_score), axis=-1, keepdims=True))


def exp_probs(scores, allowed, totals):
    return jnp.exp(jnp.where(allowed, scores, negative_fill) - totals)


def global_targets(length, device, local_blocks):
    last_block = (length + BLK - 1) // BLK - 1
    targets = []
    for target_block in (jnp.zeros_like(last_block), last_block):
        is_owner = target_block // local_blocks == device
        local_block = jnp.clip(target_block - device * local_blocks, 0, local_blocks - 1)
        targets.append((is_owner, local_block))
    return targets


def global_scores(query_rows, key_one, length):
    scores = jnp.einsum(
        "qhd,khd->hqk",
        query_rows.reshape(BLK, HEADS, HD),
        key_one.reshape(-1, HEADS, HD),
        preferred_element_type=jnp.float32,
    ) * HD ** (-0.5)
    allowed = (jnp.arange(key_one.shape[0], dtype=jnp.int32) < length)[None, None, :]
    return (scores, allowed)


def global_forward(query_rows, key_one, value_one, length):
    scores, allowed = global_scores(query_rows, key_one, length)
    totals = log_total(scores, allowed)
    weighting = exp_probs(scores, allowed, totals).astype(jnp.bfloat16)
    out_rows = jnp.einsum(
        "hqk,khd->qhd",
        weighting,
        value_one.reshape(-1, HEADS, HD),
        preferred_element_type=jnp.float32,
    )
    return (out_rows.reshape(BLK, -1), totals)


def global_skip(query_rows, key_one, value_one, length):
    return (jnp.zeros((BLK, HEADS * HD), jnp.float32), jnp.zeros((HEADS, BLK, 1), jnp.float32))


def global_backward(query_rows, grad_rows, key_one, value_one, length, row_totals):
    score_scale = HD ** (-0.5)
    scores, allowed = global_scores(query_rows, key_one, length)
    exact_probs = exp_probs(scores, allowed, row_totals)
    grad_heads = grad_rows.reshape(BLK, HEADS, HD)
    grad_weights = jnp.einsum(
        "qhd,khd->hqk",
        grad_heads,
        value_one.reshape(-1, HEADS, HD),
        preferred_element_type=jnp.float32,
    )
    delta_sum = jnp.sum(exact_probs * grad_weights, axis=-1, keepdims=True)
    grad_scores = (exact_probs * (grad_weights - delta_sum)).astype(jnp.bfloat16)
    grad_query = (
        jnp.einsum(
            "hqk,khd->qhd",
            grad_scores,
            key_one.reshape(-1, HEADS, HD),
            preferred_element_type=jnp.float32,
        )
        * score_scale
    )
    grad_keys = (
        jnp.einsum(
            "hqk,qhd->khd",
            grad_scores,
            query_rows.reshape(BLK, HEADS, HD),
            preferred_element_type=jnp.float32,
        )
        * score_scale
    )
    grad_values = jnp.einsum(
        "hqk,qhd->khd",
        exact_probs.astype(jnp.bfloat16),
        grad_heads,
        preferred_element_type=jnp.float32,
    )
    return (
        grad_query.reshape(BLK, -1),
        grad_keys.reshape(key_one.shape[0], -1),
        grad_values.reshape(key_one.shape[0], -1),
    )


def global_back_skip(query_rows, grad_rows, key_one, value_one, length, row_totals):
    key_zeros = jnp.zeros(key_one.shape, jnp.float32)
    return (jnp.zeros((BLK, key_one.shape[1]), jnp.float32), key_zeros, key_zeros)


def attend_forward(query_one, key_one, value_one, length, rand_rows, device):
    local_blocks = rand_rows.shape[0]
    slot_blocks, slot_valid = slot_table(device * local_blocks, rand_rows, length)
    allowed = slot_mask(slot_blocks, slot_valid, length)
    query_blocks = query_one.reshape(local_blocks, BLK, HEADS, HD)
    scores = jnp.einsum(
        "nqhd,nkhd->nhqk",
        query_blocks,
        gather_slots(key_one, slot_blocks),
        preferred_element_type=jnp.float32,
    ) * HD ** (-0.5)
    totals = log_total(scores, allowed)
    weighting = exp_probs(scores, allowed, totals).astype(jnp.bfloat16)
    attended = jnp.einsum(
        "nhqk,nkhd->nqhd",
        weighting,
        gather_slots(value_one, slot_blocks),
        preferred_element_type=jnp.float32,
    ).reshape(query_one.shape[0], -1)
    global_totals = []
    for is_owner, local_block in global_targets(length, device, local_blocks):
        query_rows = lax.dynamic_slice_in_dim(query_one, local_block * BLK, BLK, 0)
        out_rows, row_totals = lax.cond(
            is_owner, global_forward, global_skip, query_rows, key_one, value_one, length
        )
        updated = lax.dynamic_update_slice_in_dim(attended, out_rows, local_block * BLK, 0)
        attended = jnp.where(is_owner, updated, attended)
        global_totals.append(row_totals)
    return (attended, totals, global_totals[0], global_totals[1])


def attend_backward(
    query_one,
    key_one,
    value_one,
    length,
    rand_rows,
    totals,
    first_totals,
    last_totals,
    grad_one,
    device,
):
    score_scale = HD ** (-0.5)
    local_blocks = rand_rows.shape[0]
    first_block = device * local_blocks
    slot_blocks, slot_valid = slot_table(first_block, rand_rows, length)
    allowed = slot_mask(slot_blocks, slot_valid, length)
    query_blocks = query_one.reshape(local_blocks, BLK, HEADS, HD)
    key_slots = gather_slots(key_one, slot_blocks)
    value_slots = gather_slots(value_one, slot_blocks)
    scores = (
        jnp.einsum("nqhd,nkhd->nhqk", query_blocks, key_slots, preferred_element_type=jnp.float32)
        * score_scale
    )
    exact_probs = exp_probs(scores, allowed, totals)
    last_block = (length + BLK - 1) // BLK - 1
    row_blocks = first_block + jnp.arange(query_one.shape[0], dtype=jnp.int32) // BLK
    is_global = (row_blocks == 0) | (row_blocks == last_block)
    grad_sparse = jnp.where(is_global[:, None], jnp.zeros_like(grad_one), grad_one)
    grad_heads = grad_sparse.reshape(local_blocks, BLK, HEADS, HD)
    grad_weights = jnp.einsum(
        "nqhd,nkhd->nhqk", grad_heads, value_slots, preferred_element_type=jnp.float32
    )
    delta_sum = jnp.sum(exact_probs * grad_weights, axis=-1, keepdims=True)
    grad_scores = (exact_probs * (grad_weights - delta_sum)).astype(jnp.bfloat16)
    grad_query = (
        jnp.einsum(
            "nhqk,nkhd->nqhd", grad_scores, key_slots, preferred_element_type=jnp.float32
        ).reshape(query_one.shape[0], -1)
        * score_scale
    )
    grad_key_slots = (
        jnp.einsum("nhqk,nqhd->nkhd", grad_scores, query_blocks, preferred_element_type=jnp.float32)
        * score_scale
    )
    grad_value_slots = jnp.einsum(
        "nhqk,nqhd->nkhd",
        exact_probs.astype(jnp.bfloat16),
        grad_heads,
        preferred_element_type=jnp.float32,
    )
    flat_ids = slot_blocks.reshape(-1)
    slot_width = BLK * query_one.shape[1]
    grad_keys = jax.ops.segment_sum(
        grad_key_slots.reshape(-1, slot_width), flat_ids, num_segments=NB
    ).reshape(-1, query_one.shape[1])
    grad_values = jax.ops.segment_sum(
        grad_value_slots.reshape(-1, slot_width), flat_ids, num_segments=NB
    ).reshape(-1, query_one.shape[1])
    for (is_owner, local_block), row_totals in zip(
        global_targets(length, device, local_blocks), (first_totals, last_totals)
    ):
        query_rows = lax.dynamic_slice_in_dim(query_one, local_block * BLK, BLK, 0)
        grad_rows = lax.dynamic_slice_in_dim(grad_one, local_block * BLK, BLK, 0)
        query_add, key_add, value_add = lax.cond(
            is_owner,
            global_backward,
            global_back_skip,
            query_rows,
            grad_rows,
            key_one,
            value_one,
            length,
            row_totals,
        )
        current = lax.dynamic_slice_in_dim(grad_query, local_block * BLK, BLK, 0)
        grad_query = lax.dynamic_update_slice_in_dim(
            grad_query, current + query_add, local_block * BLK, 0
        )
        grad_keys = grad_keys + key_add
        grad_values = grad_values + value_add
    return (grad_query, grad_keys, grad_values)


def local(
    inputs,
    grad_out,
    lengths,
    rand_blocks,
    w_query,
    b_query,
    w_key,
    w_value,
    b_value,
    w_output,
    b_output,
    gain_one,
    shift_one,
    w_in,
    b_in,
    w_out,
    b_out,
    gain_two,
    shift_two,
):
    device = lax.axis_index("mp")
    seq_count, local_rows, width = inputs.shape
    flat_in = inputs.reshape(-1, width)
    query = (jnp.dot(flat_in, w_query, preferred_element_type=jnp.float32) + b_query).astype(
        jnp.bfloat16
    )
    keys = jnp.dot(flat_in, w_key, preferred_element_type=jnp.float32).astype(jnp.bfloat16)
    values = (jnp.dot(flat_in, w_value, preferred_element_type=jnp.float32) + b_value).astype(
        jnp.bfloat16
    )
    key_all, value_all = (
        lax.all_gather(keys.reshape(seq_count, local_rows, width), "mp", axis=1, tiled=True),
        lax.all_gather(values.reshape(seq_count, local_rows, width), "mp", axis=1, tiled=True),
    )
    query_seq = query.reshape(seq_count, local_rows, width)

    def forward_item(seq_items):
        query_one, key_one, value_one, length, rand_rows = seq_items
        return attend_forward(query_one, key_one, value_one, length, rand_rows, device)

    attended, totals, first_totals, last_totals = lax.map(
        forward_item, (query_seq, key_all, value_all, lengths, rand_blocks)
    )
    attended_low = attended.reshape(-1, width).astype(jnp.bfloat16)
    summed_one = (
        flat_in.astype(jnp.float32)
        + jnp.dot(attended_low, w_output, preferred_element_type=jnp.float32)
        + b_output
    )
    first, norm_one_back = jax.vjp(
        layer_norm, summed_one, gain_one.astype(jnp.float32), shift_one.astype(jnp.float32)
    )
    first_low = first.astype(jnp.bfloat16)
    rows_all = lax.all_gather(first_low, "mp", axis=0, tiled=True)
    hidden = jnp.dot(rows_all, w_in, preferred_element_type=jnp.float32) + b_in
    active_full, gelu_back = jax.vjp(gelu_tanh, hidden)
    active = active_full.astype(jnp.bfloat16)
    feed = lax.psum_scatter(
        jnp.einsum(
            "rf,df->rd",
            lax.slice_in_dim(active, 0, first_low.shape[0] * lax.axis_size("mp"), axis=0),
            w_out,
            preferred_element_type=jnp.float32,
        ),
        "mp",
        scatter_dimension=0,
        tiled=True,
    )
    summed_two = first + feed + b_out
    output, norm_two_back = jax.vjp(
        layer_norm, summed_two, gain_two.astype(jnp.float32), shift_two.astype(jnp.float32)
    )
    grad_two, gain_two_grad, shift_two_grad = norm_two_back(
        grad_out.reshape(-1, width).astype(jnp.float32)
    )
    grad_feed = grad_two.astype(jnp.bfloat16)
    b_out_grad = jnp.sum(grad_feed, axis=0, dtype=jnp.float32)
    grads_all = lax.all_gather(grad_feed, "mp", axis=0, tiled=True)
    w_out_grad = jnp.einsum("rd,rf->df", grads_all, active, preferred_element_type=jnp.float32)
    grad_hidden = gelu_back(jnp.dot(grads_all, w_out, preferred_element_type=jnp.float32))[
        0
    ].astype(jnp.bfloat16)
    w_in_grad = jnp.einsum("rd,rf->df", rows_all, grad_hidden, preferred_element_type=jnp.float32)
    grad_first = grad_two + lax.psum_scatter(
        jnp.einsum(
            "rf,df->rd",
            lax.slice_in_dim(grad_hidden, 0, grad_feed.shape[0] * lax.axis_size("mp"), axis=0),
            w_in,
            preferred_element_type=jnp.float32,
        ),
        "mp",
        scatter_dimension=0,
        tiled=True,
    )
    b_in_grad = lax.dynamic_update_slice_in_dim(
        jnp.zeros((FF,), jnp.float32),
        jnp.sum(grad_hidden, axis=0, dtype=jnp.float32),
        device * w_in.shape[1],
        0,
    )
    grad_sum_one, gain_one_grad, shift_one_grad = norm_one_back(grad_first)
    grad_branch = grad_sum_one.astype(jnp.bfloat16)
    b_output_grad = jnp.sum(grad_branch, axis=0, dtype=jnp.float32)
    w_output_grad = jnp.einsum(
        "rd,re->de", attended_low, grad_branch, preferred_element_type=jnp.float32
    )
    grad_attended = (
        jnp.einsum("re,de->rd", grad_branch, w_output, preferred_element_type=jnp.float32)
        .astype(jnp.bfloat16)
        .reshape(seq_count, local_rows, width)
    )

    def backward_item(seq_items):
        (
            query_one,
            key_one,
            value_one,
            length,
            rand_rows,
            sparse_totals,
            first_one,
            last_one,
            grad_one,
        ) = seq_items
        return attend_backward(
            query_one,
            key_one,
            value_one,
            length,
            rand_rows,
            sparse_totals,
            first_one,
            last_one,
            grad_one,
            device,
        )

    grad_query, grad_keys, grad_values = lax.map(
        backward_item,
        (
            query_seq,
            key_all,
            value_all,
            lengths,
            rand_blocks,
            totals,
            first_totals,
            last_totals,
            grad_attended,
        ),
    )
    key_sums, value_sums = (
        lax.psum_scatter(
            grad_keys.astype(jnp.bfloat16), "mp", scatter_dimension=1, tiled=True
        ).astype(jnp.float32),
        lax.psum_scatter(
            grad_values.astype(jnp.bfloat16), "mp", scatter_dimension=1, tiled=True
        ).astype(jnp.float32),
    )
    grad_q_low = grad_query.reshape(-1, width).astype(jnp.bfloat16)
    grad_k_low = key_sums.reshape(-1, width).astype(jnp.bfloat16)
    grad_v_low = value_sums.reshape(-1, width).astype(jnp.bfloat16)
    input_grad = grad_sum_one + jnp.einsum(
        "re,de->rd", grad_q_low, w_query, preferred_element_type=jnp.float32
    )
    input_grad = input_grad + jnp.einsum(
        "re,de->rd", grad_k_low, w_key, preferred_element_type=jnp.float32
    )
    input_grad = input_grad + jnp.einsum(
        "re,de->rd", grad_v_low, w_value, preferred_element_type=jnp.float32
    )
    w_query_grad = jnp.einsum("rd,re->de", flat_in, grad_q_low, preferred_element_type=jnp.float32)
    w_key_grad = jnp.einsum("rd,re->de", flat_in, grad_k_low, preferred_element_type=jnp.float32)
    w_value_grad = jnp.einsum("rd,re->de", flat_in, grad_v_low, preferred_element_type=jnp.float32)
    b_query_grad = jnp.sum(grad_q_low, axis=0, dtype=jnp.float32)
    b_value_grad = jnp.sum(grad_v_low, axis=0, dtype=jnp.float32)
    reduced = (
        lax.psum_scatter(
            w_query_grad.astype(jnp.bfloat16), "dp", scatter_dimension=0, tiled=True
        ).astype(jnp.float32),
        lax.psum_scatter(
            w_key_grad.astype(jnp.bfloat16), "dp", scatter_dimension=0, tiled=True
        ).astype(jnp.float32),
        lax.psum_scatter(
            w_value_grad.astype(jnp.bfloat16), "dp", scatter_dimension=0, tiled=True
        ).astype(jnp.float32),
        lax.psum_scatter(
            w_output_grad.astype(jnp.bfloat16), "dp", scatter_dimension=0, tiled=True
        ).astype(jnp.float32),
        lax.psum_scatter(
            w_in_grad.astype(jnp.bfloat16), "dp", scatter_dimension=0, tiled=True
        ).astype(jnp.float32),
        lax.psum_scatter(
            w_out_grad.astype(jnp.bfloat16), "dp", scatter_dimension=0, tiled=True
        ).astype(jnp.float32),
        lax.psum_scatter(
            b_query_grad.astype(jnp.bfloat16), "dp", scatter_dimension=0, tiled=True
        ).astype(jnp.float32),
        lax.psum_scatter(
            b_value_grad.astype(jnp.bfloat16), "dp", scatter_dimension=0, tiled=True
        ).astype(jnp.float32),
        lax.psum_scatter(
            b_output_grad.astype(jnp.bfloat16), "dp", scatter_dimension=0, tiled=True
        ).astype(jnp.float32),
        lax.psum_scatter(
            gain_one_grad.astype(jnp.bfloat16), "dp", scatter_dimension=0, tiled=True
        ).astype(jnp.float32),
        lax.psum_scatter(
            shift_one_grad.astype(jnp.bfloat16), "dp", scatter_dimension=0, tiled=True
        ).astype(jnp.float32),
        lax.psum_scatter(
            b_in_grad.astype(jnp.bfloat16), "dp", scatter_dimension=0, tiled=True
        ).astype(jnp.float32),
        lax.psum_scatter(
            b_out_grad.astype(jnp.bfloat16), "dp", scatter_dimension=0, tiled=True
        ).astype(jnp.float32),
        lax.psum_scatter(
            gain_two_grad.astype(jnp.bfloat16), "dp", scatter_dimension=0, tiled=True
        ).astype(jnp.float32),
        lax.psum_scatter(
            shift_two_grad.astype(jnp.bfloat16), "dp", scatter_dimension=0, tiled=True
        ).astype(jnp.float32),
    )
    query_part, key_part_out, value_part, output_part = (
        lax.psum_scatter(
            reduced[0].astype(jnp.bfloat16), "mp", scatter_dimension=1, tiled=True
        ).astype(jnp.float32),
        lax.psum_scatter(
            reduced[1].astype(jnp.bfloat16), "mp", scatter_dimension=1, tiled=True
        ).astype(jnp.float32),
        lax.psum_scatter(
            reduced[2].astype(jnp.bfloat16), "mp", scatter_dimension=1, tiled=True
        ).astype(jnp.float32),
        lax.psum_scatter(
            reduced[3].astype(jnp.bfloat16), "mp", scatter_dimension=1, tiled=True
        ).astype(jnp.float32),
    )
    in_part = reduced[4]
    out_part = reduced[5]
    vectors = lax.psum(
        (
            reduced[6],
            reduced[7],
            reduced[8],
            reduced[9],
            reduced[10],
            reduced[11],
            reduced[12],
            reduced[13],
            reduced[14],
        ),
        "mp",
    )
    return (
        output.astype(jnp.bfloat16).reshape(seq_count, local_rows, width),
        input_grad.reshape(seq_count, local_rows, width),
        query_part,
        vectors[0],
        key_part_out,
        value_part,
        vectors[1],
        output_part,
        vectors[2],
        vectors[3],
        vectors[4],
        in_part,
        vectors[5],
        out_part,
        vectors[6],
        vectors[7],
        vectors[8],
    )


def solution(mesh):
    in_specs = (
        P("dp", "mp", None),
        P("dp", "mp", None),
        P("dp"),
        P("dp", "mp", None),
        P(),
        P(),
        P(),
        P(),
        P(),
        P(),
        P(),
        P(),
        P(),
        P(None, "mp"),
        P("mp"),
        P(None, "mp"),
        P(),
        P(),
        P(),
    )
    out_specs = (
        P("dp", "mp", None),
        P("dp", "mp", None),
        P("dp", "mp"),
        P("dp"),
        P("dp", "mp"),
        P("dp", "mp"),
        P("dp"),
        P("dp", "mp"),
        P("dp"),
        P("dp"),
        P("dp"),
        P("dp", "mp"),
        P("dp"),
        P("dp", "mp"),
        P("dp"),
        P("dp"),
        P("dp"),
    )
    sizes = dict(mesh.shape)
    if sizes["mp"] == 2 and sizes["dp"] % 4 == 0:
        local_fn = functools.partial(local_pair, sizes["dp"])
    else:
        local_fn = local
    return jax.shard_map(local_fn, mesh=mesh, in_specs=in_specs, out_specs=out_specs, check_vma=False)
```

```python
import functools

import jax
import jax.numpy as jnp
from jax import lax
from jax.experimental import pallas as pl
from jax.experimental.pallas import tpu as pltpu
from jax.sharding import PartitionSpec as P

HEADS = 12
HD = 64
FF = 3072
BLK = 64
NB = 16


negative_fill = -1000000000.0
norm_epsilon = 1e-12


F32 = jnp.float32
BF16 = jnp.bfloat16
NN = (((1,), (0,)), ((), ()))
NT = (((1,), (1,)), ((), ()))
TN = (((0,), (0,)), ((), ()))


def mm(a, b, dims=NN):
    return lax.dot_general(a, b, dims, preferred_element_type=F32)


def params(mib=56):
    return pltpu.CompilerParams(vmem_limit_bytes=mib << 20)


def cost(flops, nbytes, trans=0):
    return pl.CostEstimate(flops=int(flops), bytes_accessed=int(nbytes), transcendentals=int(trans))


def shape(dims, dtype):
    return jax.ShapeDtypeStruct(dims, dtype)


def row_stats(u):
    mean = jnp.mean(u, axis=-1, keepdims=True)
    cen = u - mean
    var = jnp.mean(cen * cen, axis=-1, keepdims=True)
    rs = lax.rsqrt(var + norm_epsilon)
    return cen * rs, rs


def attn_fwd_body(sc, xo, xt, wq, wk, wv, bq, bv, rand, q_o, k_o, v_o, p_o, ao, at, bias):
    half = xo.shape[0]
    rows = 2 * half
    nb = rows // BLK
    tile = 256

    @pl.when(pl.program_id(0) == 0)
    def _():
        c = sc[0]
        ln = sc[1]
        last = (ln + BLK - 1) // BLK - 1
        lb = lax.broadcasted_iota(jnp.int32, (nb, rows), 0)
        kp = lax.broadcasted_iota(jnp.int32, (nb, rows), 1)
        qb = jnp.where(lb < nb // 2, lb + (nb // 2) * c, lb - (nb // 2) * c)
        kpos = jnp.where(kp < half, kp + half * c, kp - half * c)
        kb = kpos // BLK
        ok = (jnp.abs(kb - qb) <= 1) | (kb == 0) | (kb == last)
        for j in range(rand.shape[1]):
            ok = ok | (kb == rand[:, j : j + 1])
        ok = ok | (qb == 0) | (qb == last)
        ok = ok & (kpos < ln)
        table = jnp.where(ok, 0.0, -1e30).astype(F32)
        for b in range(nb):
            bias[b] = jnp.broadcast_to(table[b : b + 1, :], (8, rows))

    for i, xr in enumerate((xo, xt)):
        rs = slice(i * half, (i + 1) * half)
        q_o[rs, :] = (mm(xr[...], wq[...]) + bq[...].astype(F32)).astype(BF16)
        k_o[rs, :] = mm(xr[...], wk[...]).astype(BF16)
        v_o[rs, :] = (mm(xr[...], wv[...]) + bv[...].astype(F32)).astype(BF16)

    lane = lax.broadcasted_iota(jnp.int32, (tile, 2 * HD), 1)
    low = lane < HD
    for i, a_ref in enumerate((ao, at)):

        def step(t, carry, i=i, a_ref=a_ref):
            r0 = pl.multiple_of(i * half + t * tile, tile)
            q = q_o[pl.ds(r0, tile), :] * BF16(HD**-0.5)
            outs = []
            for h in range(2):
                qh = jnp.where(low if h == 0 else ~low, q, BF16(0))
                s = mm(qh, k_o[...], NT)
                s = s.reshape(tile // BLK, BLK // 8, 8, rows)
                s = s + bias[pl.ds(r0 // BLK, tile // BLK)][:, None]
                s = s.reshape(tile, rows)
                e = jnp.exp(s - jnp.max(s, axis=-1, keepdims=True))
                p = (e * (1.0 / jnp.sum(e, axis=-1, keepdims=True))).astype(BF16)
                p_o[h, pl.ds(r0, tile), :] = p
                outs.append(mm(p, v_o[...]))
            a = jnp.where(low, outs[0], outs[1]).astype(BF16)
            a_ref[pl.ds(pl.multiple_of(t * tile, tile), tile), :] = a
            return carry

        lax.fori_loop(0, half // tile, step, 0)


def attn_fwd(sc, xo, xt, wq, wk, wv, bq, bv, rand):
    half, width = xo.shape
    rows = 2 * half
    pairs = HEADS // 4
    pw = 2 * HD
    whole = lambda a: pl.BlockSpec(a.shape, lambda p, s: (0,) * a.ndim)
    wspec = pl.BlockSpec((width, pw), lambda p, s: (0, s[0] * pairs + p))
    bspec = pl.BlockSpec((1, pw), lambda p, s: (0, s[0] * pairs + p))
    ospec = lambda r: pl.BlockSpec((r, pw), lambda p, s: (0, p))
    return pl.pallas_call(
        attn_fwd_body,
        grid_spec=pltpu.PrefetchScalarGridSpec(
            num_scalar_prefetch=1,
            grid=(pairs,),
            in_specs=[whole(xo), whole(xt), wspec, wspec, wspec, bspec, bspec, whole(rand)],
            out_specs=[ospec(rows)] * 3
            + [pl.BlockSpec((2, rows, rows), lambda p, s: (p, 0, 0))]
            + [ospec(half)] * 2,
            scratch_shapes=[pltpu.VMEM((rows // BLK, 8, rows), F32)],
        ),
        out_shape=[shape((rows, pairs * pw), BF16)] * 3
        + [shape((2 * pairs, rows, rows), BF16)]
        + [shape((half, pairs * pw), BF16)] * 2,
        compiler_params=params(),
        cost_estimate=cost(20e9, 20e6, 6 * rows * rows),
        name="attn_fwd",
    )(sc, xo, xt, wq, wk, wv, bq, bv, rand)


def partner_copy(src, dst, send, recv, me):
    return pltpu.make_async_remote_copy(
        src_ref=src, dst_ref=dst, send_sem=send, recv_sem=recv,
        device_id={"mp": 1 - me}, device_id_type=pl.DeviceIdType.MESH,
    )


class Piece:
    def __init__(self, x_first, sems, base, refs, dp_size):
        self.x_first = x_first
        self.send, self.recv = sems
        self.base = base
        self.half, self.got1, self.mine, self.got2, self.got3 = refs
        me = lax.axis_index("dp")
        bits = (me % 2, (me // 2) % 2)
        steps = (1, 2)
        self.groups = dp_size // 4
        self.high = me // 4
        first, second = (0, 1) if x_first else (1, 0)
        self.bit1, self.bit2 = bits[first], bits[second]
        self.peer1 = me + steps[first] * (1 - 2 * bits[first])
        self.peer2 = me + steps[second] * (1 - 2 * bits[second])
        self.peers3 = [
            ((self.high + s) % self.groups, ((self.high + s) % self.groups) * 4 + me % 4)
            for s in range(1, self.groups)
        ]

    def copy(self, src, dst, i, peer):
        return pltpu.make_async_remote_copy(
            src_ref=src, dst_ref=dst, send_sem=self.send.at[self.base + i],
            recv_sem=self.recv.at[self.base + i], device_id={"dp": peer},
            device_id_type=pl.DeviceIdType.MESH,
        )

    def side(self, src, bit):
        return src.at[:, :, bit] if self.x_first else src.at[:, bit]

    def stage1(self, src):
        return self.copy(self.side(src, 1 - self.bit1), self.got1, 0, self.peer1)

    def stage2(self, src=None):
        src = self.half if src is None else src
        return self.copy(src.at[:, 1 - self.bit2], self.got2, 1, self.peer2)

    def stage3(self):
        return [
            self.copy(self.mine.at[z], self.got3.at[s], 2 + s, peer)
            for s, (z, peer) in enumerate(self.peers3)
        ]

    def add1(self, own):
        def step(z, carry):
            total = own(z).astype(F32) + self.got1[z].astype(F32)
            self.half[z] = total.astype(BF16)
            return carry

        lax.fori_loop(0, self.groups, step, 0)

    def add2(self, own=None):
        def step(z, carry):
            kept = self.half[z, self.bit2] if own is None else own(z)
            self.mine[z] = (kept.astype(F32) + self.got2[z].astype(F32)).astype(BF16)
            return carry

        lax.fori_loop(0, self.groups, step, 0)

    def result(self):
        total = self.mine[self.high].astype(F32)
        for s in range(self.groups - 1):
            total = total + self.got3[s].astype(F32)
        return total


def gelu_and_slope(v):
    k0 = 0.7978845608028654
    k1 = 0.044715
    v2 = v * v
    t = jnp.tanh(v * (k0 + (k0 * k1) * v2))
    hp = 0.5 * t + 0.5
    return v * hp, hp + (0.5 * v) * (1.0 - t * t) * (k0 + (3 * k0 * k1) * v2)


def norm_back(e, n, rs, gain):
    eg = e * gain
    return (eg - jnp.mean(eg, -1, keepdims=True) - n * jnp.mean(eg * n, -1, keepdims=True)) * rs


def middle_body(
    dp_size, a_own, a_send, x, gout, b_output, gain1, shift1, b_in, b_out, gain2, shift2,
    w_o_h, w_in_h, w_out_h,
    out_o, gsum_o, ga_o, gat_o, sa1, sa2, win_g, wo_g, vec_o, bi_o,
    a_got, fl, feed_s, feed_g, gf, part_s, part_g, gat_s, gb, wo_s, wo_r, vec_s, vec_r, bi_s, bi_s2, bi_r, wout_g, got_a1, got_a2,
    w_o, w_in, w_out, act, slope, gh, u_s, first_s, own_s, gtwo_s,
    load_sem, send_sem, recv_sem, a_send_sem, a_recv_sem,
):
    me = lax.axis_index("mp")
    half, width = x.shape
    hw = width // 2
    tile = 256
    tiles = half // tile
    cut = sa1.shape[-1]
    sems = (a_send_sem, a_recv_sem)
    A1 = Piece(True, sems, 0, (sa1, got_a1, None, None, None), dp_size)
    A2 = Piece(False, sems, 1, (sa2, got_a2, None, None, None), dp_size)
    A1_copy = A1.stage1(wout_g.at[:, :, :, :, :cut])
    A2_copy = A2.stage1(wout_g.at[:, :, :, :, cut:])
    barrier = pltpu.get_barrier_semaphore()
    for device in ({"mp": 1 - me}, {"dp": A1.peer1}, {"dp": A2.peer1}):
        pl.semaphore_signal(barrier, inc=1, device_id=device, device_id_type=pl.DeviceIdType.MESH)
    loads = []
    for i, (src, dst) in enumerate(((w_o_h, w_o), (w_in_h, w_in), (w_out_h, w_out))):
        loads.append(pltpu.make_async_copy(src, dst, load_sem.at[i]))
        loads[-1].start()
    pl.semaphore_wait(barrier, 3)

    def copy(src, dst, i):
        return partner_copy(src, dst, send_sem.at[i], recv_sem.at[i], me)

    a_copy = copy(a_send, a_got, 0)
    a_copy.start()
    loads[0].wait()
    a_copy.wait_recv()

    def rows(t):
        return pl.ds(pl.multiple_of(t * tile, tile), tile)

    def fl_copy(t):
        return copy(fl.at[0, rows(t)], fl.at[1, rows(t)], 1 + t)

    def feed_copy(t):
        return copy(feed_s.at[rows(t)], feed_g.at[rows(t)], 3 + t)

    def gf_copy(t):
        return copy(gf.at[0, rows(t)], gf.at[1, rows(t)], 5 + t)

    def part_copy(t):
        return copy(part_s.at[rows(t)], part_g.at[rows(t)], 7 + t)

    def ga_copy(t):
        return copy(gat_s.at[rows(t)], gat_o.at[rows(t)], 9 + t)

    own_o = pl.ds(pl.multiple_of(me * hw, hw), hw)
    got_o = pl.ds(pl.multiple_of((1 - me) * hw, hw), hw)

    def project(t, carry):
        r = rows(t)
        u = x[r, :].astype(F32) + (
            mm(a_own[r, :], w_o[own_o, :]) + mm(a_got[r, :], w_o[got_o, :])
        ) + b_output[...].astype(F32)[None, :]
        n, _ = row_stats(u)
        first = n * gain1[...].astype(F32)[None, :] + shift1[...].astype(F32)[None, :]
        u_s[r, :] = u
        first_s[r, :] = first
        fl[0, r, :] = first.astype(BF16)
        fl_copy(t).start()
        return carry

    lax.fori_loop(0, tiles, project, 0)
    loads[1].wait()
    loads[2].wait()

    def feed_forward(i, t):
        r = rows(t)
        v = mm(fl[i, r, :], w_in[...]) + b_in[...].astype(F32)[None, :]
        a, s = gelu_and_slope(v)
        a = a.astype(BF16)
        act[i, r, :] = a
        slope[i, r, :] = s.astype(BF16)
        return mm(a, w_out[...], NT)

    def forward_own(t, carry):
        own_s[rows(t), :] = feed_forward(0, t)
        return carry

    def forward_got(t, carry):
        fl_copy(t).wait_recv()
        feed_s[rows(t), :] = feed_forward(1, t).astype(BF16)
        feed_copy(t).start()
        return carry

    lax.fori_loop(0, tiles, forward_own, 0)
    lax.fori_loop(0, tiles, forward_got, 0)

    vec_s[...] = jnp.zeros_like(vec_s)

    def add_vec(i, value):
        vec_s[i : i + 1, :] += jnp.sum(value, 0, keepdims=True)

    def second_norm(t, carry):
        r = rows(t)
        feed_copy(t).wait_recv()
        u = first_s[r, :] + (own_s[r, :] + feed_g[r, :].astype(F32)) + b_out[...].astype(F32)[None, :]
        n, rs = row_stats(u)
        gain = gain2[...].astype(F32)[None, :]
        out_o[r, :] = (n * gain + shift2[...].astype(F32)[None, :]).astype(BF16)
        e = gout[r, :].astype(F32)
        d = norm_back(e, n, rs, gain)
        low = d.astype(BF16)
        gtwo_s[r, :] = d
        gf[0, r, :] = low
        gf_copy(t).start()
        add_vec(6, e * n)
        add_vec(7, e)
        add_vec(5, low.astype(F32))
        return carry

    lax.fori_loop(0, tiles, second_norm, 0)
    bi_s[...] = jnp.zeros_like(bi_s)

    def feed_back(i, t):
        r = rows(t)
        g = (mm(gf[i, r, :], w_out[...]) * slope[i, r, :].astype(F32)).astype(BF16)
        gh[i, r, :] = g
        bi_s[0:1, :] += jnp.sum(g.astype(F32), 0, keepdims=True)
        return mm(g, w_in[...], NT)

    def back_own(t, carry):
        own_s[rows(t), :] = feed_back(0, t)
        return carry

    def wait_gf(t, carry):
        gf_copy(t).wait_recv()
        return carry

    def back_got(t, carry):
        part_s[rows(t), :] = feed_back(1, t).astype(BF16)
        part_copy(t).start()
        return carry

    lax.fori_loop(0, tiles, back_own, 0)
    lax.fori_loop(0, tiles, wait_gf, 0)

    def out_weights(j, carry):
        c = pl.ds(pl.multiple_of(j * hw, hw), hw)
        total = mm(gf[0, :, c], act[0], TN) + mm(gf[1, :, c], act[1], TN)
        zs = wout_g.shape[0] // 2
        wout_g[pl.ds(j * zs, zs)] = total.astype(BF16).reshape((zs,) + wout_g.shape[1:])
        return carry

    lax.fori_loop(0, 2, out_weights, 0)
    A1_copy.start()
    A2_copy.start()
    lax.fori_loop(0, tiles, back_got, 0)

    def weights(out, lhs, rhs):
        def step(j, carry):
            c = pl.ds(pl.multiple_of(j * tile, tile), tile)
            out[c, :] = (
                mm(lhs[0, :, c], rhs[0], TN) + mm(lhs[1, :, c], rhs[1], TN)
            ).astype(BF16)
            return carry

        lax.fori_loop(0, width // tile, step, 0)

    weights(win_g, fl, gh)

    def first_norm(t, carry):
        r = rows(t)
        part_copy(t).wait_recv()
        e = gtwo_s[r, :] + own_s[r, :] + part_g[r, :].astype(F32)
        n, rs = row_stats(u_s[r, :])
        d = norm_back(e, n, rs, gain1[...].astype(F32)[None, :])
        low = d.astype(BF16)
        gsum_o[r, :] = d
        gb[r, :] = low
        gat_s[r, :] = mm(low, w_o[got_o, :], NT).astype(BF16)
        ga_copy(t).start()
        ga_o[r, :] = mm(low, w_o[own_o, :], NT).astype(BF16)
        add_vec(3, e * n)
        add_vec(4, e)
        add_vec(2, low.astype(F32))
        return carry

    lax.fori_loop(0, tiles, first_norm, 0)
    vec_copy = copy(vec_s, vec_r, 11)
    vec_copy.start()
    bi_s2[0:1, :] = bi_s[0:1, :width]
    bi_s2[1:2, :] = bi_s[0:1, width:]
    bi_copy = copy(bi_s2, bi_r, 12)
    bi_copy.start()
    cols_own = own_o
    cols_got = got_o
    wo_s[own_o, :] = mm(a_own[...], gb[:, cols_got], TN).astype(BF16)
    wo_s[got_o, :] = mm(a_got[...], gb[:, cols_got], TN).astype(BF16)
    wo_copy = copy(wo_s, wo_r, 13)
    wo_copy.start()
    own_part = mm(a_own[...], gb[:, cols_own], TN)
    got_part = mm(a_got[...], gb[:, cols_own], TN)
    wo_copy.wait_recv()
    wo_g[own_o, :] = (own_part + wo_r[own_o, :].astype(F32)).astype(BF16)
    wo_g[got_o, :] = (got_part + wo_r[got_o, :].astype(F32)).astype(BF16)
    vec_copy.wait_recv()
    vec_o[...] = vec_s[...] + vec_r[...]
    bi_copy.wait_recv()
    bi_o[...] = jnp.zeros_like(bi_o)
    first_core = me == 0
    bi_o[0:2, :] = jnp.where(first_core, bi_s2[0:2, :], bi_r[0:2, :])
    bi_o[2:4, :] = jnp.where(first_core, bi_r[0:2, :], bi_s2[0:2, :])
    A1_copy.wait_recv()
    A1.add1(lambda z: wout_g[z, :, A1.bit1, :, :cut])
    A2_copy.wait_recv()
    A2.add1(lambda z: wout_g[z, A2.bit1, :, :, cut:])

    def finish(t, carry):
        ga_copy(t).wait_recv()
        fl_copy(t).wait_send()
        feed_copy(t).wait_send()
        gf_copy(t).wait_send()
        part_copy(t).wait_send()
        ga_copy(t).wait_send()
        return carry

    lax.fori_loop(0, tiles, finish, 0)
    a_copy.wait_send()
    A1_copy.wait_send()
    A2_copy.wait_send()
    vec_copy.wait_send()
    bi_copy.wait_send()
    wo_copy.wait_send()


def middle(dp_size, a_own, a_send, x, gout, b_output, gain1, shift1, b_in, b_out, gain2, shift2, w_o, w_in, w_out):
    half, width = x.shape
    hw = width // 2
    ff = w_in.shape[1]
    groups = dp_size // 4
    n = width // dp_size
    vm = pl.BlockSpec(memory_space=pltpu.VMEM)
    hbm = pl.BlockSpec(memory_space=pl.ANY)
    V = pltpu.VMEM
    return pl.pallas_call(
        functools.partial(middle_body, dp_size),
        in_specs=[vm] * 11 + [hbm] * 3,
        out_specs=[vm] * 10,
        out_shape=[
            shape((half, width), BF16),
            shape((half, width), F32),
            shape((half, hw), BF16),
            shape((half, hw), BF16),
            shape((groups, 2, n, ff // 2), BF16),
            shape((groups, 2, n, ff // 2), BF16),
            shape((width, ff), BF16),
            shape((width, hw), BF16),
            shape((8, width), F32),
            shape((8, width), F32),
        ],
        scratch_shapes=[
            V((half, hw), BF16),
            V((2, half, width), BF16),
            V((half, width), BF16),
            V((half, width), BF16),
            V((2, half, width), BF16),
            V((half, width), BF16),
            V((half, width), BF16),
            V((half, hw), BF16),
            V((half, width), BF16),
            V((width, hw), BF16),
            V((width, hw), BF16),
            V((8, width), F32),
            V((8, width), F32),
            V((8, ff), F32),
            V((8, width), F32),
            V((8, width), F32),
            V((groups, 2, 2, n, ff), BF16),
            V((groups, 2, n, ff // 2), BF16),
            V((groups, 2, n, ff // 2), BF16),
            V((width, width), BF16),
            V((width, ff), BF16),
            V((width, ff), BF16),
            V((2, half, ff), BF16),
            V((2, half, ff), BF16),
            V((2, half, ff), BF16),
            V((half, width), F32),
            V((half, width), F32),
            V((half, width), F32),
            V((half, width), F32),
            pltpu.SemaphoreType.DMA((3,)),
            pltpu.SemaphoreType.DMA((14,)),
            pltpu.SemaphoreType.DMA((14,)),
            pltpu.SemaphoreType.DMA((2,)),
            pltpu.SemaphoreType.DMA((2,)),
        ],
        compiler_params=pltpu.CompilerParams(
            vmem_limit_bytes=62 << 20, collective_id=1, has_side_effects=True
        ),
        cost_estimate=cost(17e9, 20e6),
        name="middle",
    )(a_own, a_send, x, gout, b_output, gain1, shift1, b_in, b_out, gain2, shift2, w_o, w_in, w_out)


def back_body(
    dp_size, xo, xt, q_i, k_i, v_i, p_i, ao, at, go, gt, gsum, vec, bi,
    wq, wk, wv, sa1, sa2, win, wo,
    ig_o, wq_o, wk_o, wv_o, wo_o, win_o, wout_o, o0, o1, o2, o3, o4, o5, o6, o7, bi_o,
    g_s, gT, qT, dkT, dvT, dqkv, wcat, xT, acc, ig_s, ig_r, wsrc,
    a1, a2, b1, b2, w1, c0, c1, c2, c3,
    tb, tb_m, t0, t1, t2, r0_, r1_, r2_,
    send, recv, lsem, vsend, vrecv, wsem,
):
    half, width = xo.shape
    rows = 2 * half
    pw = 2 * HD
    tile = 256
    p = pl.program_id(0)
    me = lax.axis_index("mp")
    dev = lax.axis_index("dp")
    groups = dp_size // 4
    per = 2 + groups - 1
    sems = (send, recv)
    cut = win.shape[-1] // 2
    piece = lambda i, xf, refs: Piece(xf, sems, i * per, refs, dp_size)
    A1, A2 = piece(0, True, (None, None) + a1), piece(1, False, (None, None) + a2)
    B1, B2 = piece(2, True, b1), piece(3, False, b2)
    WO = piece(4, False, w1)
    C0, C1 = piece(5, True, c0), piece(6, False, c1)
    C2, C3 = piece(7, True, c2), piece(8, False, c3)
    win1, win2 = win.at[:, :, :, :, :cut], win.at[:, :, :, :, cut:]
    src2 = wsrc.at[2, :, :, :, :, : 2 * pw]
    src3 = wsrc.at[2, :, :, :, :, 2 * pw :]
    locals_ = [
        (sa1.at[:, A1.bit2], A1.mine),
        (sa2.at[:, A2.bit2], A2.mine),
        (B1.side(win1, B1.bit1), B1.half),
        (B2.side(win2, B2.bit1), B2.half),
        (WO.side(wo, WO.bit1), WO.half),
    ]
    local = [pltpu.make_async_copy(s, d, lsem.at[i]) for i, (s, d) in enumerate(locals_)]
    ig_copy = partner_copy(ig_s, ig_r, vsend.at[0], vrecv.at[0], me)
    tb_copy = partner_copy(tb, tb_m, vsend.at[1], vrecv.at[1], me)

    def vec_copy(src, dst, i, peer):
        return pltpu.make_async_remote_copy(
            src_ref=src, dst_ref=dst, send_sem=vsend.at[i], recv_sem=vrecv.at[i],
            device_id={"dp": peer}, device_id_type=pl.DeviceIdType.MESH,
        )

    t0_copy = vec_copy(t0, r0_, 2, C2.peer1)
    t1_copy = vec_copy(t1, r1_, 3, C2.peer2)
    t2_copies = [vec_copy(t2, r2_.at[s], 4 + s, peer) for s, (_, peer) in enumerate(C2.peers3)]

    @pl.when(p == 0)
    def _():
        barrier = pltpu.get_barrier_semaphore()
        everyone = [{"mp": 1 - me}, {"dp": C0.peer1}, {"dp": C0.peer2}]
        everyone += [{"dp": peer} for _, peer in C0.peers3]
        for device in everyone:
            pl.semaphore_signal(
                barrier, inc=1, device_id=device, device_id_type=pl.DeviceIdType.MESH
            )
        for c in local:
            c.start()
        pl.semaphore_wait(barrier, len(everyone))
        A1.stage2(sa1).start()
        A2.stage2(sa2).start()
        B1.stage1(win1).start()
        B2.stage1(win2).start()
        WO.stage1(wo).start()
        xT[:, :half] = xo[...].T
        xT[:, half:] = xt[...].T
        tb[...] = jnp.zeros_like(tb)

    c_off = pl.multiple_of(me * (width // 2) + p * pw, pw)
    w_copies = [
        pltpu.make_async_copy(
            w.at[:, pl.ds(c_off, pw)], wcat.at[:, i * pw : (i + 1) * pw], wsem.at[i]
        )
        for i, w in enumerate((wq, wk, wv))
    ]
    for c in w_copies:
        c.start()
    g_s[:half, :] = go[...]
    g_s[half:, :] = gt[...]
    gT[...] = g_s[...].T
    qT[...] = q_i[...].T
    dkT[...] = jnp.zeros_like(dkT)
    dvT[...] = jnp.zeros_like(dvT)
    lane = lax.broadcasted_iota(jnp.int32, (tile, pw), 1)
    low = lane < HD

    for t in range(rows // tile):
        rs = slice(t * tile, (t + 1) * tile)
        a_ref = ao if t * tile < half else at
        as_ = slice(t * tile % half, t * tile % half + tile)
        g = g_s[rs, :]
        ga = g.astype(F32) * a_ref[as_, :].astype(F32)
        outs = []
        for h in range(2):
            mine = low if h == 0 else ~low
            hs = slice(h * HD, (h + 1) * HD)
            dp = mm(jnp.where(mine, g, BF16(0)), v_i[...], NT)
            delta = jnp.sum(jnp.where(mine, ga, 0.0), axis=-1, keepdims=True)
            pr = p_i[h, rs, :]
            ds = (pr.astype(F32) * (dp - delta)).astype(BF16)
            outs.append(mm(ds, k_i[...]))
            dvT[hs, :] += mm(gT[hs, rs], pr)
            dkT[hs, :] += mm(qT[hs, rs], ds)
        dq = jnp.where(low, outs[0], outs[1]) * HD**-0.5
        dqkv[rs, 0:pw] = dq.astype(BF16)

        if t == 3:

            @pl.when(p == 1)
            def _():
                local[0].wait()
                local[1].wait()
                for x in (A1, A2):
                    x.stage2(sa1 if x is A1 else sa2).wait_recv()
                    x.add2(lambda z, x=x: x.mine[z])
                    for c in x.stage3():
                        c.start()

        if t == 1:

            @pl.when(p == 2)
            def _():
                for j, (x, s) in enumerate(((B1, win1), (B2, win2), (WO, wo))):
                    local[2 + j].wait()
                    x.stage1(s).wait_recv()
                    x.add1(lambda z, x=x: x.half[z])
                    x.stage2().start()

    dqkv[:, pw : 2 * pw] = (dkT[...].T * HD**-0.5).astype(BF16)
    dqkv[:, 2 * pw : 3 * pw] = dvT[...].T.astype(BF16)
    d = dqkv[...]
    wg = mm(xT[...], d).astype(BF16).reshape(wsrc.shape[1:])
    wsrc[p] = wg
    tb[0:1, pl.ds(c_off, pw)] = jnp.sum(d[:, 0:pw].astype(F32), axis=0, keepdims=True)
    tb[1:2, pl.ds(c_off, pw)] = jnp.sum(d[:, 2 * pw :].astype(F32), axis=0, keepdims=True)

    @pl.when(p == 0)
    def _():
        C0.stage1(wsrc.at[0]).start()

    @pl.when(p == 1)
    def _():
        C1.stage1(wsrc.at[1]).start()

    @pl.when(p == 2)
    def _():
        C2.stage1(src2).start()
        C3.stage1(src3).start()
        tb_copy.start()

    for c in w_copies:
        c.wait()
    part = mm(d, wcat[...], NT)

    @pl.when(p == 0)
    def _():
        acc[...] = part

    @pl.when(p == 1)
    def _():
        acc[...] += part

    @pl.when(p == 2)
    def _():
        ig_s[...] = (acc[half:, :] + part[half:]).astype(BF16)
        ig_copy.start()
        acc[:half, :] += part[:half]

        def own(j, piece):
            def get(z):
                return wsrc[j, z, :, piece.bit1] if piece.x_first else wsrc[j, z, piece.bit1]

            return get

        def forward2(x):
            x.stage2().wait_recv()
            x.add2()
            for c in x.stage3():
                c.start()

        C0.stage1(wsrc.at[0]).wait_recv()
        C0.add1(own(0, C0))
        C0.stage2().start()
        tb_copy.wait_recv()
        t0[0:8, :] = tb[...] + tb_m[...] + vec[...]
        t0[8:16, :] = bi[...]
        t0_copy.start()
        forward2(B1)
        forward2(B2)
        C1.stage1(wsrc.at[1]).wait_recv()
        C1.add1(own(1, C1))
        C1.stage2().start()
        forward2(WO)
        t0_copy.wait_recv()
        t1[...] = t0[...] + r0_[...]
        t1_copy.start()
        forward2(C0)
        C2.stage1(src2).wait_recv()
        C2.add1(lambda z: wsrc[2, z, :, C2.bit1, :, : 2 * pw])
        C2.stage2().start()
        C3.stage1(src3).wait_recv()
        C3.add1(lambda z: wsrc[2, z, C3.bit1, :, :, 2 * pw :])
        C3.stage2().start()
        forward2(C1)
        t1_copy.wait_recv()
        t2[...] = t1[...] + r1_[...]
        for c in t2_copies:
            c.start()
        ig_copy.wait_recv()
        ig_o[...] = gsum[...] + (acc[:half, :] + ig_r[...].astype(F32))
        forward2(C2)
        forward2(C3)

        def arrived(x):
            for c in x.stage3():
                c.wait_recv()
            return x.result()

        wout_o[:, :cut] = arrived(A1)
        wout_o[:, cut:] = arrived(A2)
        win_o[:, :cut] = arrived(B1)
        win_o[:, cut:] = arrived(B2)
        wo_o[...] = arrived(WO)
        for c in t2_copies:
            c.wait_recv()
        table = t2[...]
        for s in range(groups - 1):
            table = table + r2_[s]
        n = width // dp_size
        m = bi_o.shape[0]
        vals = table[0:8, 0:n]
        biv = table[8:9, 0:m]
        for j in range(1, dp_size):
            vals = jnp.where(dev == j, table[0:8, j * n : (j + 1) * n], vals)
            r = 8 + (j * m) // width
            k = (j * m) % width
            biv = jnp.where(dev == j, table[r : r + 1, k : k + m], biv)
        for j, o in enumerate((o0, o1, o2, o3, o4, o5, o6, o7)):
            o[...] = vals[j]
        bi_o[...] = biv[0]
        for j, x in enumerate((C0, C1)):
            v = arrived(x)
            cs = slice(j * pw, (j + 1) * pw)
            for i, o in enumerate((wq_o, wk_o, wv_o)):
                o[:, cs] = v[:, i * pw : (i + 1) * pw]
        v = arrived(C2)
        cs = slice(2 * pw, 3 * pw)
        wq_o[:, cs] = v[:, :pw]
        wk_o[:, cs] = v[:, pw:]
        wv_o[:, cs] = arrived(C3)

        A1.stage2(sa1).wait_send()
        A2.stage2(sa2).wait_send()
        for x, s in ((B1, win1), (B2, win2), (WO, wo), (C0, wsrc.at[0]), (C1, wsrc.at[1]), (C2, src2), (C3, src3)):
            x.stage1(s).wait_send()
            x.stage2().wait_send()
        for x in (A1, A2, B1, B2, WO, C0, C1, C2, C3):
            for c in x.stage3():
                c.wait_send()
        ig_copy.wait_send()
        tb_copy.wait_send()
        t0_copy.wait_send()
        t1_copy.wait_send()
        for c in t2_copies:
            c.wait_send()


def back(dp_size, xo, xt, wq, wk, wv, q, k, v, probs, ao, at, go, gt, gsum, vec, bi, sa1, sa2, win, wo):
    half, width = xo.shape
    rows = 2 * half
    pairs = HEADS // 4
    pw = 2 * HD
    ff = win.shape[1]
    groups = dp_size // 4
    n = width // dp_size
    five = lambda a: a.reshape(groups, 2, 2, n, a.shape[-1])
    whole = lambda a: pl.BlockSpec(
        a.shape, lambda p: (0,) * a.ndim, pipeline_mode=pl.Buffered(1)
    )
    col = lambda r, w: pl.BlockSpec((r, w), lambda p: (0, p))
    hbm = pl.BlockSpec(memory_space=pl.ANY)
    vm = pl.BlockSpec(memory_space=pltpu.VMEM)
    V = pltpu.VMEM

    def late(w):
        return (V((groups, n, w), BF16), V((groups, n, w), BF16), V((groups - 1, n, w), BF16))

    def bufs(w):
        return (V((groups, 2, n, w), BF16), V((groups, 2, n, w), BF16)) + late(w)

    fw = ff // 2
    pieces = 9
    per = 2 + groups - 1
    table = lambda: V((16, width), F32)
    return pl.pallas_call(
        functools.partial(back_body, dp_size),
        grid_spec=pltpu.PrefetchScalarGridSpec(
            num_scalar_prefetch=0,
            grid=(pairs,),
            in_specs=[whole(xo), whole(xt)]
            + [col(rows, pw)] * 3
            + [pl.BlockSpec((2, rows, rows), lambda p: (p, 0, 0))]
            + [col(half, pw)] * 4
            + [whole(gsum), whole(vec), whole(bi)]
            + [hbm] * 7,
            out_specs=[vm] * 16,
            scratch_shapes=[
                V((rows, pw), BF16),
                V((pw, rows), BF16),
                V((pw, rows), BF16),
                V((pw, rows), F32),
                V((pw, rows), F32),
                V((rows, 3 * pw), BF16),
                V((width, 3 * pw), BF16),
                V((width, rows), BF16),
                V((rows, width), F32),
                V((half, width), BF16),
                V((half, width), BF16),
                V((pairs, groups, 2, 2, n, 3 * pw), BF16),
                late(fw), late(fw), bufs(fw), bufs(fw), bufs(width // 2),
                bufs(3 * pw), bufs(3 * pw), bufs(2 * pw), bufs(pw),
                V((8, width), F32), V((8, width), F32),
                table(), table(), table(), table(), table(), V((groups - 1, 16, width), F32),
                pltpu.SemaphoreType.DMA((pieces * per,)),
                pltpu.SemaphoreType.DMA((pieces * per,)),
                pltpu.SemaphoreType.DMA((5,)),
                pltpu.SemaphoreType.DMA((4 + groups - 1,)),
                pltpu.SemaphoreType.DMA((4 + groups - 1,)),
                pltpu.SemaphoreType.DMA((3,)),
            ],
        ),
        out_shape=[shape((half, width), F32)]
        + [shape((n, width // 2), F32)] * 4
        + [shape((n, ff), F32)] * 2
        + [shape((n,), F32)] * 8
        + [shape((2 * ff // dp_size,), F32)],
        compiler_params=pltpu.CompilerParams(
            vmem_limit_bytes=60 << 20, collective_id=2, has_side_effects=True
        ),
        cost_estimate=cost(40e9, 20e6),
        name="back",
    )(xo, xt, q, k, v, probs, ao, at, go, gt, gsum, vec, bi, wq, wk, wv, sa1, sa2, five(win), five(wo))


def local_pair(
    dp_size, inputs, grad_out, lengths, rand_blocks, w_query, b_query, w_key, w_value, b_value,
    w_output, b_output, gain_one, shift_one, w_in, b_in, w_out, b_out, gain_two, shift_two,
):
    core = lax.axis_index("mp").astype(jnp.int32)
    swap = lambda a: lax.ppermute(a, "mp", [(0, 1), (1, 0)])
    vec = lambda a: a.reshape(1, -1)
    x = inputs[0]
    half, width = x.shape
    x_got = swap(x)
    rand = jnp.concatenate([rand_blocks[0], swap(rand_blocks[0])], axis=0)
    sc = jnp.stack([core, lengths[0]])
    q, k, v, probs, a_own, a_send = attn_fwd(
        sc, x, x_got, w_query, w_key, w_value, vec(b_query), vec(b_value), rand
    )
    out, gsum, ga0, ga_got, sa1, sa2, w_in_g, w_output_g, vec_g, bi_g = middle(
        dp_size, a_own, a_send, x, grad_out[0], b_output, gain_one, shift_one, b_in, b_out,
        gain_two, shift_two, w_output, w_in, w_out,
    )
    (
        input_grad, wq_p, wk_p, wv_p, wo_p, in_part, out_part, bq_p, bv_p, bo_p, g1_p, s1_p, b2_p,
        g2_p, s2_p, bi_p,
    ) = back(
        dp_size, x, x_got, w_query, w_key, w_value, q, k, v, probs, a_own, a_send, ga0, ga_got,
        gsum, vec_g, bi_g, sa1, sa2, w_in_g, w_output_g,
    )
    return (
        out[None], input_grad[None], wq_p, bq_p, wk_p, wv_p, bv_p, wo_p, bo_p, g1_p, s1_p,
        in_part, bi_p, out_part, b2_p, g2_p, s2_p,
    )


def layer_norm(features, norm_gain, norm_shift):
    row_mean = jnp.mean(features, axis=-1, keepdims=True)
    centered = features - row_mean
    variance = jnp.mean(centered * centered, axis=-1, keepdims=True)
    return centered * lax.rsqrt(variance + norm_epsilon) * norm_gain + norm_shift


def gelu_tanh(features):
    return jax.nn.gelu(features, approximate=True)


def slot_table_ids(block_ids, rand_rows, length):
    valid_blocks = (length + BLK - 1) // BLK
    column = block_ids[:, None]
    columns = jnp.concatenate(
        [
            column - 1,
            column,
            column + 1,
            rand_rows,
            jnp.zeros_like(column),
            jnp.zeros_like(column) + valid_blocks - 1,
        ],
        axis=1,
    )
    in_range = (columns >= 0) & (columns < valid_blocks)
    slot_ids = jnp.arange(columns.shape[1], dtype=jnp.int32)
    earlier = slot_ids[None, :] < slot_ids[:, None]
    repeated = jnp.any(
        (columns[:, :, None] == columns[:, None, :]) & earlier[None, :, :] & in_range[:, None, :],
        axis=2,
    )
    return (jnp.clip(columns, 0, NB - 1), in_range & jnp.logical_not(repeated))


def slot_table(first_block, rand_rows, length):
    block_ids = first_block + jnp.arange(rand_rows.shape[0], dtype=jnp.int32)
    return slot_table_ids(block_ids, rand_rows, length)


def slot_mask(slot_blocks, slot_valid, length):
    positions = slot_blocks[:, :, None] * BLK + jnp.arange(BLK, dtype=jnp.int32)
    allowed = slot_valid[:, :, None] & (positions < length)
    return allowed.reshape(slot_blocks.shape[0], 1, 1, -1)


def gather_slots(whole_rows, slot_blocks):
    picked = whole_rows.reshape(NB, BLK, whole_rows.shape[1])[slot_blocks]
    return picked.reshape(slot_blocks.shape[0], slot_blocks.shape[1] * BLK, HEADS, HD)


def log_total(scores, allowed):
    masked = jnp.where(allowed, scores, negative_fill)
    top_score = jnp.max(masked, axis=-1, keepdims=True)
    return top_score + jnp.log(jnp.sum(jnp.exp(masked - top_score), axis=-1, keepdims=True))


def exp_probs(scores, allowed, totals):
    return jnp.exp(jnp.where(allowed, scores, negative_fill) - totals)


def global_targets(length, device, local_blocks):
    last_block = (length + BLK - 1) // BLK - 1
    targets = []
    for target_block in (jnp.zeros_like(last_block), last_block):
        is_owner = target_block // local_blocks == device
        local_block = jnp.clip(target_block - device * local_blocks, 0, local_blocks - 1)
        targets.append((is_owner, local_block))
    return targets


def global_scores(query_rows, key_one, length):
    scores = jnp.einsum(
        "qhd,khd->hqk",
        query_rows.reshape(BLK, HEADS, HD),
        key_one.reshape(-1, HEADS, HD),
        preferred_element_type=jnp.float32,
    ) * HD ** (-0.5)
    allowed = (jnp.arange(key_one.shape[0], dtype=jnp.int32) < length)[None, None, :]
    return (scores, allowed)


def global_forward(query_rows, key_one, value_one, length):
    scores, allowed = global_scores(query_rows, key_one, length)
    totals = log_total(scores, allowed)
    weighting = exp_probs(scores, allowed, totals).astype(jnp.bfloat16)
    out_rows = jnp.einsum(
        "hqk,khd->qhd",
        weighting,
        value_one.reshape(-1, HEADS, HD),
        preferred_element_type=jnp.float32,
    )
    return (out_rows.reshape(BLK, -1), totals)


def global_skip(query_rows, key_one, value_one, length):
    return (jnp.zeros((BLK, HEADS * HD), jnp.float32), jnp.zeros((HEADS, BLK, 1), jnp.float32))


def global_backward(query_rows, grad_rows, key_one, value_one, length, row_totals):
    score_scale = HD ** (-0.5)
    scores, allowed = global_scores(query_rows, key_one, length)
    exact_probs = exp_probs(scores, allowed, row_totals)
    grad_heads = grad_rows.reshape(BLK, HEADS, HD)
    grad_weights = jnp.einsum(
        "qhd,khd->hqk",
        grad_heads,
        value_one.reshape(-1, HEADS, HD),
        preferred_element_type=jnp.float32,
    )
    delta_sum = jnp.sum(exact_probs * grad_weights, axis=-1, keepdims=True)
    grad_scores = (exact_probs * (grad_weights - delta_sum)).astype(jnp.bfloat16)
    grad_query = (
        jnp.einsum(
            "hqk,khd->qhd",
            grad_scores,
            key_one.reshape(-1, HEADS, HD),
            preferred_element_type=jnp.float32,
        )
        * score_scale
    )
    grad_keys = (
        jnp.einsum(
            "hqk,qhd->khd",
            grad_scores,
            query_rows.reshape(BLK, HEADS, HD),
            preferred_element_type=jnp.float32,
        )
        * score_scale
    )
    grad_values = jnp.einsum(
        "hqk,qhd->khd",
        exact_probs.astype(jnp.bfloat16),
        grad_heads,
        preferred_element_type=jnp.float32,
    )
    return (
        grad_query.reshape(BLK, -1),
        grad_keys.reshape(key_one.shape[0], -1),
        grad_values.reshape(key_one.shape[0], -1),
    )


def global_back_skip(query_rows, grad_rows, key_one, value_one, length, row_totals):
    key_zeros = jnp.zeros(key_one.shape, jnp.float32)
    return (jnp.zeros((BLK, key_one.shape[1]), jnp.float32), key_zeros, key_zeros)


def attend_forward(query_one, key_one, value_one, length, rand_rows, device):
    local_blocks = rand_rows.shape[0]
    slot_blocks, slot_valid = slot_table(device * local_blocks, rand_rows, length)
    allowed = slot_mask(slot_blocks, slot_valid, length)
    query_blocks = query_one.reshape(local_blocks, BLK, HEADS, HD)
    scores = jnp.einsum(
        "nqhd,nkhd->nhqk",
        query_blocks,
        gather_slots(key_one, slot_blocks),
        preferred_element_type=jnp.float32,
    ) * HD ** (-0.5)
    totals = log_total(scores, allowed)
    weighting = exp_probs(scores, allowed, totals).astype(jnp.bfloat16)
    attended = jnp.einsum(
        "nhqk,nkhd->nqhd",
        weighting,
        gather_slots(value_one, slot_blocks),
        preferred_element_type=jnp.float32,
    ).reshape(query_one.shape[0], -1)
    global_totals = []
    for is_owner, local_block in global_targets(length, device, local_blocks):
        query_rows = lax.dynamic_slice_in_dim(query_one, local_block * BLK, BLK, 0)
        out_rows, row_totals = lax.cond(
            is_owner, global_forward, global_skip, query_rows, key_one, value_one, length
        )
        updated = lax.dynamic_update_slice_in_dim(attended, out_rows, local_block * BLK, 0)
        attended = jnp.where(is_owner, updated, attended)
        global_totals.append(row_totals)
    return (attended, totals, global_totals[0], global_totals[1])


def attend_backward(
    query_one,
    key_one,
    value_one,
    length,
    rand_rows,
    totals,
    first_totals,
    last_totals,
    grad_one,
    device,
):
    score_scale = HD ** (-0.5)
    local_blocks = rand_rows.shape[0]
    first_block = device * local_blocks
    slot_blocks, slot_valid = slot_table(first_block, rand_rows, length)
    allowed = slot_mask(slot_blocks, slot_valid, length)
    query_blocks = query_one.reshape(local_blocks, BLK, HEADS, HD)
    key_slots = gather_slots(key_one, slot_blocks)
    value_slots = gather_slots(value_one, slot_blocks)
    scores = (
        jnp.einsum("nqhd,nkhd->nhqk", query_blocks, key_slots, preferred_element_type=jnp.float32)
        * score_scale
    )
    exact_probs = exp_probs(scores, allowed, totals)
    last_block = (length + BLK - 1) // BLK - 1
    row_blocks = first_block + jnp.arange(query_one.shape[0], dtype=jnp.int32) // BLK
    is_global = (row_blocks == 0) | (row_blocks == last_block)
    grad_sparse = jnp.where(is_global[:, None], jnp.zeros_like(grad_one), grad_one)
    grad_heads = grad_sparse.reshape(local_blocks, BLK, HEADS, HD)
    grad_weights = jnp.einsum(
        "nqhd,nkhd->nhqk", grad_heads, value_slots, preferred_element_type=jnp.float32
    )
    delta_sum = jnp.sum(exact_probs * grad_weights, axis=-1, keepdims=True)
    grad_scores = (exact_probs * (grad_weights - delta_sum)).astype(jnp.bfloat16)
    grad_query = (
        jnp.einsum(
            "nhqk,nkhd->nqhd", grad_scores, key_slots, preferred_element_type=jnp.float32
        ).reshape(query_one.shape[0], -1)
        * score_scale
    )
    grad_key_slots = (
        jnp.einsum("nhqk,nqhd->nkhd", grad_scores, query_blocks, preferred_element_type=jnp.float32)
        * score_scale
    )
    grad_value_slots = jnp.einsum(
        "nhqk,nqhd->nkhd",
        exact_probs.astype(jnp.bfloat16),
        grad_heads,
        preferred_element_type=jnp.float32,
    )
    flat_ids = slot_blocks.reshape(-1)
    slot_width = BLK * query_one.shape[1]
    grad_keys = jax.ops.segment_sum(
        grad_key_slots.reshape(-1, slot_width), flat_ids, num_segments=NB
    ).reshape(-1, query_one.shape[1])
    grad_values = jax.ops.segment_sum(
        grad_value_slots.reshape(-1, slot_width), flat_ids, num_segments=NB
    ).reshape(-1, query_one.shape[1])
    for (is_owner, local_block), row_totals in zip(
        global_targets(length, device, local_blocks), (first_totals, last_totals)
    ):
        query_rows = lax.dynamic_slice_in_dim(query_one, local_block * BLK, BLK, 0)
        grad_rows = lax.dynamic_slice_in_dim(grad_one, local_block * BLK, BLK, 0)
        query_add, key_add, value_add = lax.cond(
            is_owner,
            global_backward,
            global_back_skip,
            query_rows,
            grad_rows,
            key_one,
            value_one,
            length,
            row_totals,
        )
        current = lax.dynamic_slice_in_dim(grad_query, local_block * BLK, BLK, 0)
        grad_query = lax.dynamic_update_slice_in_dim(
            grad_query, current + query_add, local_block * BLK, 0
        )
        grad_keys = grad_keys + key_add
        grad_values = grad_values + value_add
    return (grad_query, grad_keys, grad_values)


def local(
    inputs,
    grad_out,
    lengths,
    rand_blocks,
    w_query,
    b_query,
    w_key,
    w_value,
    b_value,
    w_output,
    b_output,
    gain_one,
    shift_one,
    w_in,
    b_in,
    w_out,
    b_out,
    gain_two,
    shift_two,
):
    device = lax.axis_index("mp")
    seq_count, local_rows, width = inputs.shape
    flat_in = inputs.reshape(-1, width)
    query = (jnp.dot(flat_in, w_query, preferred_element_type=jnp.float32) + b_query).astype(
        jnp.bfloat16
    )
    keys = jnp.dot(flat_in, w_key, preferred_element_type=jnp.float32).astype(jnp.bfloat16)
    values = (jnp.dot(flat_in, w_value, preferred_element_type=jnp.float32) + b_value).astype(
        jnp.bfloat16
    )
    key_all, value_all = (
        lax.all_gather(keys.reshape(seq_count, local_rows, width), "mp", axis=1, tiled=True),
        lax.all_gather(values.reshape(seq_count, local_rows, width), "mp", axis=1, tiled=True),
    )
    query_seq = query.reshape(seq_count, local_rows, width)

    def forward_item(seq_items):
        query_one, key_one, value_one, length, rand_rows = seq_items
        return attend_forward(query_one, key_one, value_one, length, rand_rows, device)

    attended, totals, first_totals, last_totals = lax.map(
        forward_item, (query_seq, key_all, value_all, lengths, rand_blocks)
    )
    attended_low = attended.reshape(-1, width).astype(jnp.bfloat16)
    summed_one = (
        flat_in.astype(jnp.float32)
        + jnp.dot(attended_low, w_output, preferred_element_type=jnp.float32)
        + b_output
    )
    first, norm_one_back = jax.vjp(
        layer_norm, summed_one, gain_one.astype(jnp.float32), shift_one.astype(jnp.float32)
    )
    first_low = first.astype(jnp.bfloat16)
    rows_all = lax.all_gather(first_low, "mp", axis=0, tiled=True)
    hidden = jnp.dot(rows_all, w_in, preferred_element_type=jnp.float32) + b_in
    active_full, gelu_back = jax.vjp(gelu_tanh, hidden)
    active = active_full.astype(jnp.bfloat16)
    feed = lax.psum_scatter(
        jnp.einsum(
            "rf,df->rd",
            lax.slice_in_dim(active, 0, first_low.shape[0] * lax.axis_size("mp"), axis=0),
            w_out,
            preferred_element_type=jnp.float32,
        ),
        "mp",
        scatter_dimension=0,
        tiled=True,
    )
    summed_two = first + feed + b_out
    output, norm_two_back = jax.vjp(
        layer_norm, summed_two, gain_two.astype(jnp.float32), shift_two.astype(jnp.float32)
    )
    grad_two, gain_two_grad, shift_two_grad = norm_two_back(
        grad_out.reshape(-1, width).astype(jnp.float32)
    )
    grad_feed = grad_two.astype(jnp.bfloat16)
    b_out_grad = jnp.sum(grad_feed, axis=0, dtype=jnp.float32)
    grads_all = lax.all_gather(grad_feed, "mp", axis=0, tiled=True)
    w_out_grad = jnp.einsum("rd,rf->df", grads_all, active, preferred_element_type=jnp.float32)
    grad_hidden = gelu_back(jnp.dot(grads_all, w_out, preferred_element_type=jnp.float32))[
        0
    ].astype(jnp.bfloat16)
    w_in_grad = jnp.einsum("rd,rf->df", rows_all, grad_hidden, preferred_element_type=jnp.float32)
    grad_first = grad_two + lax.psum_scatter(
        jnp.einsum(
            "rf,df->rd",
            lax.slice_in_dim(grad_hidden, 0, grad_feed.shape[0] * lax.axis_size("mp"), axis=0),
            w_in,
            preferred_element_type=jnp.float32,
        ),
        "mp",
        scatter_dimension=0,
        tiled=True,
    )
    b_in_grad = lax.dynamic_update_slice_in_dim(
        jnp.zeros((FF,), jnp.float32),
        jnp.sum(grad_hidden, axis=0, dtype=jnp.float32),
        device * w_in.shape[1],
        0,
    )
    grad_sum_one, gain_one_grad, shift_one_grad = norm_one_back(grad_first)
    grad_branch = grad_sum_one.astype(jnp.bfloat16)
    b_output_grad = jnp.sum(grad_branch, axis=0, dtype=jnp.float32)
    w_output_grad = jnp.einsum(
        "rd,re->de", attended_low, grad_branch, preferred_element_type=jnp.float32
    )
    grad_attended = (
        jnp.einsum("re,de->rd", grad_branch, w_output, preferred_element_type=jnp.float32)
        .astype(jnp.bfloat16)
        .reshape(seq_count, local_rows, width)
    )

    def backward_item(seq_items):
        (
            query_one,
            key_one,
            value_one,
            length,
            rand_rows,
            sparse_totals,
            first_one,
            last_one,
            grad_one,
        ) = seq_items
        return attend_backward(
            query_one,
            key_one,
            value_one,
            length,
            rand_rows,
            sparse_totals,
            first_one,
            last_one,
            grad_one,
            device,
        )

    grad_query, grad_keys, grad_values = lax.map(
        backward_item,
        (
            query_seq,
            key_all,
            value_all,
            lengths,
            rand_blocks,
            totals,
            first_totals,
            last_totals,
            grad_attended,
        ),
    )
    key_sums, value_sums = (
        lax.psum_scatter(
            grad_keys.astype(jnp.bfloat16), "mp", scatter_dimension=1, tiled=True
        ).astype(jnp.float32),
        lax.psum_scatter(
            grad_values.astype(jnp.bfloat16), "mp", scatter_dimension=1, tiled=True
        ).astype(jnp.float32),
    )
    grad_q_low = grad_query.reshape(-1, width).astype(jnp.bfloat16)
    grad_k_low = key_sums.reshape(-1, width).astype(jnp.bfloat16)
    grad_v_low = value_sums.reshape(-1, width).astype(jnp.bfloat16)
    input_grad = grad_sum_one + jnp.einsum(
        "re,de->rd", grad_q_low, w_query, preferred_element_type=jnp.float32
    )
    input_grad = input_grad + jnp.einsum(
        "re,de->rd", grad_k_low, w_key, preferred_element_type=jnp.float32
    )
    input_grad = input_grad + jnp.einsum(
        "re,de->rd", grad_v_low, w_value, preferred_element_type=jnp.float32
    )
    w_query_grad = jnp.einsum("rd,re->de", flat_in, grad_q_low, preferred_element_type=jnp.float32)
    w_key_grad = jnp.einsum("rd,re->de", flat_in, grad_k_low, preferred_element_type=jnp.float32)
    w_value_grad = jnp.einsum("rd,re->de", flat_in, grad_v_low, preferred_element_type=jnp.float32)
    b_query_grad = jnp.sum(grad_q_low, axis=0, dtype=jnp.float32)
    b_value_grad = jnp.sum(grad_v_low, axis=0, dtype=jnp.float32)
    reduced = (
        lax.psum_scatter(
            w_query_grad.astype(jnp.bfloat16), "dp", scatter_dimension=0, tiled=True
        ).astype(jnp.float32),
        lax.psum_scatter(
            w_key_grad.astype(jnp.bfloat16), "dp", scatter_dimension=0, tiled=True
        ).astype(jnp.float32),
        lax.psum_scatter(
            w_value_grad.astype(jnp.bfloat16), "dp", scatter_dimension=0, tiled=True
        ).astype(jnp.float32),
        lax.psum_scatter(
            w_output_grad.astype(jnp.bfloat16), "dp", scatter_dimension=0, tiled=True
        ).astype(jnp.float32),
        lax.psum_scatter(
            w_in_grad.astype(jnp.bfloat16), "dp", scatter_dimension=0, tiled=True
        ).astype(jnp.float32),
        lax.psum_scatter(
            w_out_grad.astype(jnp.bfloat16), "dp", scatter_dimension=0, tiled=True
        ).astype(jnp.float32),
        lax.psum_scatter(
            b_query_grad.astype(jnp.bfloat16), "dp", scatter_dimension=0, tiled=True
        ).astype(jnp.float32),
        lax.psum_scatter(
            b_value_grad.astype(jnp.bfloat16), "dp", scatter_dimension=0, tiled=True
        ).astype(jnp.float32),
        lax.psum_scatter(
            b_output_grad.astype(jnp.bfloat16), "dp", scatter_dimension=0, tiled=True
        ).astype(jnp.float32),
        lax.psum_scatter(
            gain_one_grad.astype(jnp.bfloat16), "dp", scatter_dimension=0, tiled=True
        ).astype(jnp.float32),
        lax.psum_scatter(
            shift_one_grad.astype(jnp.bfloat16), "dp", scatter_dimension=0, tiled=True
        ).astype(jnp.float32),
        lax.psum_scatter(
            b_in_grad.astype(jnp.bfloat16), "dp", scatter_dimension=0, tiled=True
        ).astype(jnp.float32),
        lax.psum_scatter(
            b_out_grad.astype(jnp.bfloat16), "dp", scatter_dimension=0, tiled=True
        ).astype(jnp.float32),
        lax.psum_scatter(
            gain_two_grad.astype(jnp.bfloat16), "dp", scatter_dimension=0, tiled=True
        ).astype(jnp.float32),
        lax.psum_scatter(
            shift_two_grad.astype(jnp.bfloat16), "dp", scatter_dimension=0, tiled=True
        ).astype(jnp.float32),
    )
    query_part, key_part_out, value_part, output_part = (
        lax.psum_scatter(
            reduced[0].astype(jnp.bfloat16), "mp", scatter_dimension=1, tiled=True
        ).astype(jnp.float32),
        lax.psum_scatter(
            reduced[1].astype(jnp.bfloat16), "mp", scatter_dimension=1, tiled=True
        ).astype(jnp.float32),
        lax.psum_scatter(
            reduced[2].astype(jnp.bfloat16), "mp", scatter_dimension=1, tiled=True
        ).astype(jnp.float32),
        lax.psum_scatter(
            reduced[3].astype(jnp.bfloat16), "mp", scatter_dimension=1, tiled=True
        ).astype(jnp.float32),
    )
    in_part = reduced[4]
    out_part = reduced[5]
    vectors = lax.psum(
        (
            reduced[6],
            reduced[7],
            reduced[8],
            reduced[9],
            reduced[10],
            reduced[11],
            reduced[12],
            reduced[13],
            reduced[14],
        ),
        "mp",
    )
    return (
        output.astype(jnp.bfloat16).reshape(seq_count, local_rows, width),
        input_grad.reshape(seq_count, local_rows, width),
        query_part,
        vectors[0],
        key_part_out,
        value_part,
        vectors[1],
        output_part,
        vectors[2],
        vectors[3],
        vectors[4],
        in_part,
        vectors[5],
        out_part,
        vectors[6],
        vectors[7],
        vectors[8],
    )


def solution(mesh):
    in_specs = (
        P("dp", "mp", None),
        P("dp", "mp", None),
        P("dp"),
        P("dp", "mp", None),
        P(),
        P(),
        P(),
        P(),
        P(),
        P(),
        P(),
        P(),
        P(),
        P(None, "mp"),
        P("mp"),
        P(None, "mp"),
        P(),
        P(),
        P(),
    )
    out_specs = (
        P("dp", "mp", None),
        P("dp", "mp", None),
        P("dp", "mp"),
        P("dp"),
        P("dp", "mp"),
        P("dp", "mp"),
        P("dp"),
        P("dp", "mp"),
        P("dp"),
        P("dp"),
        P("dp"),
        P("dp", "mp"),
        P("dp"),
        P("dp", "mp"),
        P("dp"),
        P("dp"),
        P("dp"),
    )
    sizes = dict(mesh.shape)
    if sizes["mp"] == 2 and sizes["dp"] % 4 == 0:
        local_fn = functools.partial(local_pair, sizes["dp"])
    else:
        local_fn = local
    return jax.shard_map(local_fn, mesh=mesh, in_specs=in_specs, out_specs=out_specs, check_vma=False)
```

```python
import functools

import jax
import jax.numpy as jnp
from jax import lax
from jax.experimental import pallas as pl
from jax.experimental.pallas import tpu as pltpu
from jax.sharding import PartitionSpec as P

HEADS = 12
HD = 64
FF = 3072
BLK = 64
NB = 16


negative_fill = -1000000000.0
norm_epsilon = 1e-12


F32 = jnp.float32
BF16 = jnp.bfloat16
NN = (((1,), (0,)), ((), ()))
NT = (((1,), (1,)), ((), ()))
TN = (((0,), (0,)), ((), ()))


def mm(a, b, dims=NN):
    return lax.dot_general(a, b, dims, preferred_element_type=F32)


def params(mib=56):
    return pltpu.CompilerParams(vmem_limit_bytes=mib << 20)


def cost(flops, nbytes, trans=0):
    return pl.CostEstimate(flops=int(flops), bytes_accessed=int(nbytes), transcendentals=int(trans))


def shape(dims, dtype):
    return jax.ShapeDtypeStruct(dims, dtype)


def row_stats(u):
    mean = jnp.mean(u, axis=-1, keepdims=True)
    cen = u - mean
    var = jnp.mean(cen * cen, axis=-1, keepdims=True)
    rs = lax.rsqrt(var + norm_epsilon)
    return cen * rs, rs


def attn_fwd_body(sc, xo, xt, wq, wk, wv, bq, bv, rand, q_o, k_o, v_o, p_o, ao, at, bias):
    half = xo.shape[0]
    rows = 2 * half
    nb = rows // BLK
    tile = 256

    @pl.when(pl.program_id(0) == 0)
    def _():
        c = sc[0]
        ln = sc[1]
        last = (ln + BLK - 1) // BLK - 1
        lb = lax.broadcasted_iota(jnp.int32, (nb, rows), 0)
        kp = lax.broadcasted_iota(jnp.int32, (nb, rows), 1)
        qb = jnp.where(lb < nb // 2, lb + (nb // 2) * c, lb - (nb // 2) * c)
        kpos = jnp.where(kp < half, kp + half * c, kp - half * c)
        kb = kpos // BLK
        ok = (jnp.abs(kb - qb) <= 1) | (kb == 0) | (kb == last)
        for j in range(rand.shape[1]):
            ok = ok | (kb == rand[:, j : j + 1])
        ok = ok | (qb == 0) | (qb == last)
        ok = ok & (kpos < ln)
        table = jnp.where(ok, 0.0, -1e30).astype(F32)
        for b in range(nb):
            bias[b] = jnp.broadcast_to(table[b : b + 1, :], (8, rows))

    for i, xr in enumerate((xo, xt)):
        rs = slice(i * half, (i + 1) * half)
        q_o[rs, :] = (mm(xr[...], wq[...]) + bq[...].astype(F32)).astype(BF16)
        k_o[rs, :] = mm(xr[...], wk[...]).astype(BF16)
        v_o[rs, :] = (mm(xr[...], wv[...]) + bv[...].astype(F32)).astype(BF16)

    lane = lax.broadcasted_iota(jnp.int32, (tile, 2 * HD), 1)
    low = lane < HD
    for i, a_ref in enumerate((ao, at)):

        def step(t, carry, i=i, a_ref=a_ref):
            r0 = pl.multiple_of(i * half + t * tile, tile)
            q = q_o[pl.ds(r0, tile), :] * BF16(HD**-0.5)
            outs = []
            for h in range(2):
                qh = jnp.where(low if h == 0 else ~low, q, BF16(0))
                s = mm(qh, k_o[...], NT)
                s = s.reshape(tile // BLK, BLK // 8, 8, rows)
                s = s + bias[pl.ds(r0 // BLK, tile // BLK)][:, None]
                s = s.reshape(tile, rows)
                e = jnp.exp(s - jnp.max(s, axis=-1, keepdims=True))
                p = (e * (1.0 / jnp.sum(e, axis=-1, keepdims=True))).astype(BF16)
                p_o[h, pl.ds(r0, tile), :] = p
                outs.append(mm(p, v_o[...]))
            a = jnp.where(low, outs[0], outs[1]).astype(BF16)
            a_ref[pl.ds(pl.multiple_of(t * tile, tile), tile), :] = a
            return carry

        lax.fori_loop(0, half // tile, step, 0)


def attn_fwd(sc, xo, xt, wq, wk, wv, bq, bv, rand):
    half, width = xo.shape
    rows = 2 * half
    pairs = HEADS // 4
    pw = 2 * HD
    whole = lambda a: pl.BlockSpec(a.shape, lambda p, s: (0,) * a.ndim)
    wspec = pl.BlockSpec((width, pw), lambda p, s: (0, s[0] * pairs + p))
    bspec = pl.BlockSpec((1, pw), lambda p, s: (0, s[0] * pairs + p))
    ospec = lambda r: pl.BlockSpec((r, pw), lambda p, s: (0, p))
    return pl.pallas_call(
        attn_fwd_body,
        grid_spec=pltpu.PrefetchScalarGridSpec(
            num_scalar_prefetch=1,
            grid=(pairs,),
            in_specs=[whole(xo), whole(xt), wspec, wspec, wspec, bspec, bspec, whole(rand)],
            out_specs=[ospec(rows)] * 3
            + [pl.BlockSpec((2, rows, rows), lambda p, s: (p, 0, 0))]
            + [ospec(half)] * 2,
            scratch_shapes=[pltpu.VMEM((rows // BLK, 8, rows), F32)],
        ),
        out_shape=[shape((rows, pairs * pw), BF16)] * 3
        + [shape((2 * pairs, rows, rows), BF16)]
        + [shape((half, pairs * pw), BF16)] * 2,
        compiler_params=params(),
        cost_estimate=cost(20e9, 20e6, 6 * rows * rows),
        name="attn_fwd",
    )(sc, xo, xt, wq, wk, wv, bq, bv, rand)


def partner_copy(src, dst, send, recv, me):
    return pltpu.make_async_remote_copy(
        src_ref=src, dst_ref=dst, send_sem=send, recv_sem=recv,
        device_id={"mp": 1 - me}, device_id_type=pl.DeviceIdType.MESH,
    )


class Piece:
    def __init__(self, bits, sems, base, src, got, kept, stage0=0):
        self.bits = bits
        self.send, self.recv, self.load = sems
        self.base = base
        self.src, self.got, self.kept = src, got, kept
        self.stage0 = stage0
        self.dev = lax.axis_index("dp")

    def mine(self, k):
        return (self.dev // 2 ** self.bits[k]) % 2

    def peer(self, k):
        return self.dev + 2 ** self.bits[k] * (1 - 2 * self.mine(k))

    def side(self, k, bit, lead=None):
        left = sorted(self.bits[k:], reverse=True)
        where = left.index(self.bits[k])
        idx = [slice(None)] * len(left) if lead is None else list(lead[:where]) + [None] + list(lead[where:])
        idx[where] = bit
        return tuple(idx)

    def source(self, k):
        return self.src if k == self.stage0 else self.kept[k - 1]

    def copy(self, k):
        i = self.base + k
        return pltpu.make_async_remote_copy(
            src_ref=self.source(k).at[self.side(k, 1 - self.mine(k))], dst_ref=self.got[k],
            send_sem=self.send.at[i], recv_sem=self.recv.at[i],
            device_id={"dp": self.peer(k)}, device_id_type=pl.DeviceIdType.MESH,
        )

    def load_own(self):
        k = self.stage0
        return pltpu.make_async_copy(
            self.src.at[self.side(k, self.mine(k))], self.kept[k], self.load.at[self.base // len(self.bits)]
        )

    def total(self, k, lead, loaded):
        if loaded:
            own = self.kept[k][lead]
        else:
            own = self.source(k)[self.side(k, self.mine(k), lead)]
        return own.astype(F32) + self.got[k][lead].astype(F32)

    def add(self, k, loaded=False):
        free = len(self.bits) - 1 - k

        def step(i, carry):
            lead = tuple((i // 2 ** (free - 1 - j)) % 2 for j in range(free))
            self.kept[k][lead] = self.total(k, lead, loaded).astype(BF16)
            return carry

        lax.fori_loop(0, 2**free, step, 0)

    def forward(self, k, loaded=False):
        self.copy(k).wait_recv()
        self.add(k, loaded)
        self.copy(k + 1).start()

    def result(self):
        k = len(self.bits) - 1
        self.copy(k).wait_recv()
        return self.total(k, (), False)

    def drain(self):
        for k in range(self.stage0, len(self.bits)):
            self.copy(k).wait_send()


def bit_orders(dp_size):
    nb = dp_size.bit_length() - 1
    rest = list(range(2, nb))
    return [0, 1] + rest, [1, 0] + rest, rest + [0, 1]


def gelu_and_slope(v):
    k0 = 0.7978845608028654
    k1 = 0.044715
    v2 = v * v
    t = jnp.tanh(v * (k0 + (k0 * k1) * v2))
    hp = 0.5 * t + 0.5
    return v * hp, hp + (0.5 * v) * (1.0 - t * t) * (k0 + (3 * k0 * k1) * v2)


def norm_back(e, n, rs, gain):
    eg = e * gain
    return (eg - jnp.mean(eg, -1, keepdims=True) - n * jnp.mean(eg * n, -1, keepdims=True)) * rs


def middle_body(
    dp_size, a_own, a_send, x, gout, b_output, gain1, shift1, b_in, b_out, gain2, shift2,
    w_o_h, w_in_h, w_out_h,
    out_o, gsum_o, ga_o, gat_o, sa1, sa2, sa3, win_g, wo_g, vec_o, bi_o,
    a_got, fl, feed_s, feed_g, gf, part_s, part_g, gat_s, gb, wo_s, wo_r, vec_s, vec_r, bi_s, bi_s2, bi_r, wout_g, got_a1, got_a2, got_a3,
    w_o, w_in, w_out, act, slope, gh, u_s, first_s, own_s, gtwo_s,
    load_sem, send_sem, recv_sem, a_send_sem, a_recv_sem,
):
    me = lax.axis_index("mp")
    half, width = x.shape
    hw = width // 2
    tile = 256
    tiles = half // tile
    cut = sa1.shape[-1]
    nb = dp_size.bit_length() - 1
    sems = (a_send_sem, a_recv_sem, None)
    chunks = [slice(None)] * (nb + 1)
    outs_a = [
        Piece(
            bits, sems, i * nb, wout_g.at[tuple(chunks + [slice(i * cut, (i + 1) * cut)])],
            (g,), (s,),
        )
        for i, (bits, g, s) in enumerate(
            zip(bit_orders(dp_size), (got_a1, got_a2, got_a3), (sa1, sa2, sa3))
        )
    ]
    barrier = pltpu.get_barrier_semaphore()
    for device in [{"mp": 1 - me}] + [{"dp": a.peer(0)} for a in outs_a]:
        pl.semaphore_signal(barrier, inc=1, device_id=device, device_id_type=pl.DeviceIdType.MESH)
    loads = []
    for i, (src, dst) in enumerate(((w_o_h, w_o), (w_in_h, w_in), (w_out_h, w_out))):
        loads.append(pltpu.make_async_copy(src, dst, load_sem.at[i]))
        loads[-1].start()
    pl.semaphore_wait(barrier, 4)

    def copy(src, dst, i):
        return partner_copy(src, dst, send_sem.at[i], recv_sem.at[i], me)

    a_copy = copy(a_send, a_got, 0)
    a_copy.start()
    loads[0].wait()
    a_copy.wait_recv()

    def rows(t):
        return pl.ds(pl.multiple_of(t * tile, tile), tile)

    def fl_copy(t):
        return copy(fl.at[0, rows(t)], fl.at[1, rows(t)], 1 + t)

    def feed_copy(t):
        return copy(feed_s.at[rows(t)], feed_g.at[rows(t)], 3 + t)

    def gf_copy(t):
        return copy(gf.at[0, rows(t)], gf.at[1, rows(t)], 5 + t)

    def part_copy(t):
        return copy(part_s.at[rows(t)], part_g.at[rows(t)], 7 + t)

    def ga_copy(t):
        return copy(gat_s.at[rows(t)], gat_o.at[rows(t)], 9 + t)

    own_o = pl.ds(pl.multiple_of(me * hw, hw), hw)
    got_o = pl.ds(pl.multiple_of((1 - me) * hw, hw), hw)

    def project(t, carry):
        r = rows(t)
        u = x[r, :].astype(F32) + (
            mm(a_own[r, :], w_o[own_o, :]) + mm(a_got[r, :], w_o[got_o, :])
        ) + b_output[...].astype(F32)[None, :]
        n, _ = row_stats(u)
        first = n * gain1[...].astype(F32)[None, :] + shift1[...].astype(F32)[None, :]
        u_s[r, :] = u
        first_s[r, :] = first
        fl[0, r, :] = first.astype(BF16)
        fl_copy(t).start()
        return carry

    lax.fori_loop(0, tiles, project, 0)
    loads[1].wait()
    loads[2].wait()

    def feed_forward(i, t):
        r = rows(t)
        v = mm(fl[i, r, :], w_in[...]) + b_in[...].astype(F32)[None, :]
        a, s = gelu_and_slope(v)
        a = a.astype(BF16)
        act[i, r, :] = a
        slope[i, r, :] = s.astype(BF16)
        return mm(a, w_out[...], NT)

    def forward_own(t, carry):
        own_s[rows(t), :] = feed_forward(0, t)
        return carry

    def forward_got(t, carry):
        fl_copy(t).wait_recv()
        feed_s[rows(t), :] = feed_forward(1, t).astype(BF16)
        feed_copy(t).start()
        return carry

    lax.fori_loop(0, tiles, forward_own, 0)
    lax.fori_loop(0, tiles, forward_got, 0)

    vec_s[...] = jnp.zeros_like(vec_s)

    def add_vec(i, value):
        vec_s[i : i + 1, :] += jnp.sum(value, 0, keepdims=True)

    def second_norm(t, carry):
        r = rows(t)
        feed_copy(t).wait_recv()
        u = first_s[r, :] + (own_s[r, :] + feed_g[r, :].astype(F32)) + b_out[...].astype(F32)[None, :]
        n, rs = row_stats(u)
        gain = gain2[...].astype(F32)[None, :]
        out_o[r, :] = (n * gain + shift2[...].astype(F32)[None, :]).astype(BF16)
        e = gout[r, :].astype(F32)
        d = norm_back(e, n, rs, gain)
        low = d.astype(BF16)
        gtwo_s[r, :] = d
        gf[0, r, :] = low
        gf_copy(t).start()
        add_vec(6, e * n)
        add_vec(7, e)
        add_vec(5, low.astype(F32))
        return carry

    lax.fori_loop(0, tiles, second_norm, 0)
    bi_s[...] = jnp.zeros_like(bi_s)

    def feed_back(i, t):
        r = rows(t)
        g = (mm(gf[i, r, :], w_out[...]) * slope[i, r, :].astype(F32)).astype(BF16)
        gh[i, r, :] = g
        bi_s[0:1, :] += jnp.sum(g.astype(F32), 0, keepdims=True)
        return mm(g, w_in[...], NT)

    def back_own(t, carry):
        own_s[rows(t), :] = feed_back(0, t)
        return carry

    def wait_gf(t, carry):
        gf_copy(t).wait_recv()
        return carry

    def back_got(t, carry):
        part_s[rows(t), :] = feed_back(1, t).astype(BF16)
        part_copy(t).start()
        return carry

    lax.fori_loop(0, tiles, back_own, 0)
    lax.fori_loop(0, tiles, wait_gf, 0)

    def out_weights(j, carry):
        c = pl.ds(pl.multiple_of(j * hw, hw), hw)
        total = mm(gf[0, :, c], act[0], TN) + mm(gf[1, :, c], act[1], TN)
        wout_g[j] = total.astype(BF16).reshape(wout_g.shape[1:])
        return carry

    lax.fori_loop(0, 2, out_weights, 0)
    for a in outs_a:
        a.copy(0).start()
    lax.fori_loop(0, tiles, back_got, 0)

    def weights(out, lhs, rhs):
        def step(j, carry):
            c = pl.ds(pl.multiple_of(j * tile, tile), tile)
            out[c, :] = (
                mm(lhs[0, :, c], rhs[0], TN) + mm(lhs[1, :, c], rhs[1], TN)
            ).astype(BF16)
            return carry

        lax.fori_loop(0, width // tile, step, 0)

    weights(win_g, fl, gh)

    def first_norm(t, carry):
        r = rows(t)
        part_copy(t).wait_recv()
        e = gtwo_s[r, :] + own_s[r, :] + part_g[r, :].astype(F32)
        n, rs = row_stats(u_s[r, :])
        d = norm_back(e, n, rs, gain1[...].astype(F32)[None, :])
        low = d.astype(BF16)
        gsum_o[r, :] = d
        gb[r, :] = low
        gat_s[r, :] = mm(low, w_o[got_o, :], NT).astype(BF16)
        ga_copy(t).start()
        ga_o[r, :] = mm(low, w_o[own_o, :], NT).astype(BF16)
        add_vec(3, e * n)
        add_vec(4, e)
        add_vec(2, low.astype(F32))
        return carry

    lax.fori_loop(0, tiles, first_norm, 0)
    vec_copy = copy(vec_s, vec_r, 11)
    vec_copy.start()
    bi_s2[0:1, :] = bi_s[0:1, :width]
    bi_s2[1:2, :] = bi_s[0:1, width:]
    bi_copy = copy(bi_s2, bi_r, 12)
    bi_copy.start()
    cols_own = own_o
    cols_got = got_o
    wo_s[own_o, :] = mm(a_own[...], gb[:, cols_got], TN).astype(BF16)
    wo_s[got_o, :] = mm(a_got[...], gb[:, cols_got], TN).astype(BF16)
    wo_copy = copy(wo_s, wo_r, 13)
    wo_copy.start()
    own_part = mm(a_own[...], gb[:, cols_own], TN)
    got_part = mm(a_got[...], gb[:, cols_own], TN)
    wo_copy.wait_recv()
    wo_g[own_o, :] = (own_part + wo_r[own_o, :].astype(F32)).astype(BF16)
    wo_g[got_o, :] = (got_part + wo_r[got_o, :].astype(F32)).astype(BF16)
    vec_copy.wait_recv()
    vec_o[...] = vec_s[...] + vec_r[...]
    bi_copy.wait_recv()
    bi_o[...] = jnp.zeros_like(bi_o)
    first_core = me == 0
    bi_o[0:2, :] = jnp.where(first_core, bi_s2[0:2, :], bi_r[0:2, :])
    bi_o[2:4, :] = jnp.where(first_core, bi_r[0:2, :], bi_s2[0:2, :])
    for a in outs_a:
        a.copy(0).wait_recv()
        a.add(0)

    def finish(t, carry):
        ga_copy(t).wait_recv()
        fl_copy(t).wait_send()
        feed_copy(t).wait_send()
        gf_copy(t).wait_send()
        part_copy(t).wait_send()
        ga_copy(t).wait_send()
        return carry

    lax.fori_loop(0, tiles, finish, 0)
    a_copy.wait_send()
    for a in outs_a:
        a.copy(0).wait_send()
    vec_copy.wait_send()
    bi_copy.wait_send()
    wo_copy.wait_send()


def middle(dp_size, a_own, a_send, x, gout, b_output, gain1, shift1, b_in, b_out, gain2, shift2, w_o, w_in, w_out):
    half, width = x.shape
    hw = width // 2
    ff = w_in.shape[1]
    nb = dp_size.bit_length() - 1
    n = width // dp_size
    part = (2,) * (nb - 1) + (n, ff // 3)
    vm = pl.BlockSpec(memory_space=pltpu.VMEM)
    hbm = pl.BlockSpec(memory_space=pl.ANY)
    V = pltpu.VMEM
    return pl.pallas_call(
        functools.partial(middle_body, dp_size),
        in_specs=[vm] * 11 + [hbm] * 3,
        out_specs=[vm] * 11,
        out_shape=[
            shape((half, width), BF16),
            shape((half, width), F32),
            shape((half, hw), BF16),
            shape((half, hw), BF16),
            shape(part, BF16),
            shape(part, BF16),
            shape(part, BF16),
            shape((width, ff), BF16),
            shape((width, hw), BF16),
            shape((8, width), F32),
            shape((8, width), F32),
        ],
        scratch_shapes=[
            V((half, hw), BF16),
            V((2, half, width), BF16),
            V((half, width), BF16),
            V((half, width), BF16),
            V((2, half, width), BF16),
            V((half, width), BF16),
            V((half, width), BF16),
            V((half, hw), BF16),
            V((half, width), BF16),
            V((width, hw), BF16),
            V((width, hw), BF16),
            V((8, width), F32),
            V((8, width), F32),
            V((8, ff), F32),
            V((8, width), F32),
            V((8, width), F32),
            V((2,) * nb + (n, ff), BF16),
            V(part, BF16),
            V(part, BF16),
            V(part, BF16),
            V((width, width), BF16),
            V((width, ff), BF16),
            V((width, ff), BF16),
            V((2, half, ff), BF16),
            V((2, half, ff), BF16),
            V((2, half, ff), BF16),
            V((half, width), F32),
            V((half, width), F32),
            V((half, width), F32),
            V((half, width), F32),
            pltpu.SemaphoreType.DMA((3,)),
            pltpu.SemaphoreType.DMA((14,)),
            pltpu.SemaphoreType.DMA((14,)),
            pltpu.SemaphoreType.DMA((3 * nb,)),
            pltpu.SemaphoreType.DMA((3 * nb,)),
        ],
        compiler_params=pltpu.CompilerParams(
            vmem_limit_bytes=62 << 20, collective_id=1, has_side_effects=True
        ),
        cost_estimate=cost(17e9, 20e6),
        name="middle",
    )(a_own, a_send, x, gout, b_output, gain1, shift1, b_in, b_out, gain2, shift2, w_o, w_in, w_out)


PIECES = ("A1", "A2", "A3", "B1", "B2", "B3", "WO", "C0", "C1", "C2", "C3")


def piece_plan(dp_size, width, ff):
    x, y, z = bit_orders(dp_size)
    third, pw = ff // 3, 2 * HD
    return (
        (x, third), (y, third), (z, third), (x, third), (y, third), (z, third), (y, width // 2),
        (x, 3 * pw), (y, 3 * pw), (x, 2 * pw), (y, pw),
    )


def back_body(
    dp_size, xo, xt, q_i, k_i, v_i, p_i, ao, at, go, gt, gsum, vec, bi,
    wq, wk, wv, sa1, sa2, sa3, win, wo,
    ig_o, wq_o, wk_o, wv_o, wo_o, win_o, wout_o, vals_o, bi_o,
    g_s, gT, qT, dkT, dvT, dqkv, wcat, xT, acc, ig_s, ig_r, wsrc, gots, kepts,
    tb, tb_m, ts, trs, send, recv, lsem, vsend, vrecv, wsem,
):
    half, width = xo.shape
    rows = 2 * half
    pw = 2 * HD
    tile = 256
    p = pl.program_id(0)
    me = lax.axis_index("mp")
    dev = lax.axis_index("dp")
    nb = dp_size.bit_length() - 1
    sems = (send, recv, lsem)
    chunks = [slice(None)] * (nb + 1)
    third = sa1.shape[-1]

    def columns(ref, a, b):
        return ref.at[tuple(chunks + [slice(a, b)])]

    srcs = [sa1, sa2, sa3] + [columns(win, i * third, (i + 1) * third) for i in range(3)] + [wo]
    srcs += [wsrc.at[0], wsrc.at[1], columns(wsrc.at[2], 0, 2 * pw), columns(wsrc.at[2], 2 * pw, 3 * pw)]
    P = {}
    for i, (name, src) in enumerate(zip(PIECES, srcs)):
        bits = piece_plan(dp_size, width, win.shape[-1])[i][0]
        s0 = 1 if name[0] == "A" else 0
        P[name] = Piece(bits, sems, i * nb, src, gots[i], kepts[i], s0)
    from_hbm = PIECES[:7]
    ig_copy = partner_copy(ig_s, ig_r, vsend.at[0], vrecv.at[0], me)
    tb_copy = partner_copy(tb, tb_m, vsend.at[1], vrecv.at[1], me)
    t_copies = [
        pltpu.make_async_remote_copy(
            src_ref=ts[k], dst_ref=trs[k], send_sem=vsend.at[2 + k], recv_sem=vrecv.at[2 + k],
            device_id={"dp": P["C0"].peer(k)}, device_id_type=pl.DeviceIdType.MESH,
        )
        for k in range(nb)
    ]

    @pl.when(p == 0)
    def _():
        barrier = pltpu.get_barrier_semaphore()
        everyone = [{"mp": 1 - me}] + [{"dp": P["C0"].peer(k)} for k in range(nb)]
        for device in everyone:
            pl.semaphore_signal(
                barrier, inc=1, device_id=device, device_id_type=pl.DeviceIdType.MESH
            )
        for name in from_hbm:
            P[name].load_own().start()
        pl.semaphore_wait(barrier, len(everyone))
        for name in from_hbm:
            P[name].copy(P[name].stage0).start()
        xT[:, :half] = xo[...].T
        xT[:, half:] = xt[...].T
        tb[...] = jnp.zeros_like(tb)

    c_off = pl.multiple_of(me * (width // 2) + p * pw, pw)
    w_copies = [
        pltpu.make_async_copy(
            w.at[:, pl.ds(c_off, pw)], wcat.at[:, i * pw : (i + 1) * pw], wsem.at[i]
        )
        for i, w in enumerate((wq, wk, wv))
    ]
    for c in w_copies:
        c.start()
    g_s[:half, :] = go[...]
    g_s[half:, :] = gt[...]
    gT[...] = g_s[...].T
    qT[...] = q_i[...].T
    dkT[...] = jnp.zeros_like(dkT)
    dvT[...] = jnp.zeros_like(dvT)
    lane = lax.broadcasted_iota(jnp.int32, (tile, pw), 1)
    low = lane < HD

    def forward(k, *names):
        for name in names:
            x = P[name]
            loaded = name in from_hbm and k == x.stage0
            if loaded:
                x.load_own().wait()
            x.forward(k, loaded)

    def at_tile(t):
        if t == 3:

            @pl.when(p == 0)
            def _():
                forward(1, "A1", "A2")

            @pl.when(p == 1)
            def _():
                forward(1, "A3")
                forward(0, "B3")
                forward(2, "A1", "A2")

        if t == 1:

            @pl.when(p == 1)
            def _():
                forward(0, "B1", "B2")

            @pl.when(p == 2)
            def _():
                forward(1, "B1", "B2")
                forward(2, "A3")
                forward(0, "WO")

    for t in range(rows // tile):
        rs = slice(t * tile, (t + 1) * tile)
        a_ref = ao if t * tile < half else at
        as_ = slice(t * tile % half, t * tile % half + tile)
        g = g_s[rs, :]
        ga = g.astype(F32) * a_ref[as_, :].astype(F32)
        outs = []
        for h in range(2):
            mine = low if h == 0 else ~low
            hs = slice(h * HD, (h + 1) * HD)
            dp = mm(jnp.where(mine, g, BF16(0)), v_i[...], NT)
            delta = jnp.sum(jnp.where(mine, ga, 0.0), axis=-1, keepdims=True)
            pr = p_i[h, rs, :]
            ds = (pr.astype(F32) * (dp - delta)).astype(BF16)
            outs.append(mm(ds, k_i[...]))
            dvT[hs, :] += mm(gT[hs, rs], pr)
            dkT[hs, :] += mm(qT[hs, rs], ds)
        dq = jnp.where(low, outs[0], outs[1]) * HD**-0.5
        dqkv[rs, 0:pw] = dq.astype(BF16)

        at_tile(t)

    dqkv[:, pw : 2 * pw] = (dkT[...].T * HD**-0.5).astype(BF16)
    dqkv[:, 2 * pw : 3 * pw] = dvT[...].T.astype(BF16)
    d = dqkv[...]
    wg = mm(xT[...], d).astype(BF16).reshape(wsrc.shape[1:])
    wsrc[p] = wg
    tb[0:1, pl.ds(c_off, pw)] = jnp.sum(d[:, 0:pw].astype(F32), axis=0, keepdims=True)
    tb[1:2, pl.ds(c_off, pw)] = jnp.sum(d[:, 2 * pw :].astype(F32), axis=0, keepdims=True)

    @pl.when(p == 0)
    def _():
        P["C0"].copy(0).start()

    @pl.when(p == 1)
    def _():
        P["C1"].copy(0).start()

    @pl.when(p == 2)
    def _():
        P["C2"].copy(0).start()
        P["C3"].copy(0).start()
        tb_copy.start()

    for c in w_copies:
        c.wait()
    part = mm(d, wcat[...], NT)

    @pl.when(p == 0)
    def _():
        acc[...] = part

    @pl.when(p == 1)
    def _():
        acc[...] += part

    @pl.when(p == 2)
    def _():
        ig_s[...] = (acc[half:, :] + part[half:]).astype(BF16)
        ig_copy.start()
        acc[:half, :] += part[:half]

        def next_table(k):
            t_copies[k].wait_recv()
            ts[k + 1][...] = ts[k][...] + trs[k][...]
            if k + 1 < nb:
                t_copies[k + 1].start()

        forward(0, "C0")
        tb_copy.wait_recv()
        ts[0][0:8, :] = tb[...] + tb_m[...] + vec[...]
        ts[0][8:16, :] = bi[...]
        t_copies[0].start()
        forward(1, "B3")
        forward(2, "B1", "B2")
        forward(0, "C1")
        forward(1, "WO")
        next_table(0)
        forward(1, "C0")
        forward(0, "C2", "C3")
        ig_copy.wait_recv()
        ig_o[...] = gsum[...] + (acc[:half, :] + ig_r[...].astype(F32))
        next_table(1)
        forward(2, "B3")
        forward(1, "C1")
        forward(2, "WO", "C0")
        for k in range(2, nb - 1):
            next_table(k)
        forward(1, "C2", "C3")
        forward(2, "C1")
        for i in range(3):
            wout_o[:, i * third : (i + 1) * third] = P["A%d" % (i + 1)].result()
            win_o[:, i * third : (i + 1) * third] = P["B%d" % (i + 1)].result()
        forward(2, "C2", "C3")
        wo_o[...] = P["WO"].result()
        next_table(nb - 1)
        table = ts[nb][...]
        n = width // dp_size
        m = bi_o.shape[1]
        vals = table[0:8, 0:n]
        biv = table[8:9, 0:m]
        for j in range(1, dp_size):
            vals = jnp.where(dev == j, table[0:8, j * n : (j + 1) * n], vals)
            r = 8 + (j * m) // width
            k = (j * m) % width
            biv = jnp.where(dev == j, table[r : r + 1, k : k + m], biv)
        vals_o[...] = vals
        bi_o[...] = biv
        for j in range(3):
            cs = slice(j * pw, (j + 1) * pw)
            v = P["C%d" % j].result()
            wq_o[:, cs] = v[:, :pw]
            wk_o[:, cs] = v[:, pw : 2 * pw]
            wv_o[:, cs] = v[:, 2 * pw :] if j < 2 else P["C3"].result()

        for name in PIECES:
            P[name].drain()
        ig_copy.wait_send()
        tb_copy.wait_send()
        for c in t_copies:
            c.wait_send()


def back(dp_size, xo, xt, wq, wk, wv, q, k, v, probs, ao, at, go, gt, gsum, vec, bi, sa, win, wo):
    half, width = xo.shape
    rows = 2 * half
    pairs = HEADS // 4
    pw = 2 * HD
    ff = win.shape[1]
    nb = dp_size.bit_length() - 1
    n = width // dp_size
    split = lambda a: a.reshape((2,) * nb + (n, a.shape[-1]))
    whole = lambda a: pl.BlockSpec(
        a.shape, lambda p: (0,) * a.ndim, pipeline_mode=pl.Buffered(1)
    )
    col = lambda r, w: pl.BlockSpec((r, w), lambda p: (0, p))
    hbm = pl.BlockSpec(memory_space=pl.ANY)
    vm = pl.BlockSpec(memory_space=pltpu.VMEM)
    V = pltpu.VMEM
    plan = piece_plan(dp_size, width, ff)

    def stages(last):
        return tuple(
            tuple(
                V((2,) * (nb - 1 - k) + (n, w), BF16) if k < nb - last else V((16, 128), BF16)
                for k in range(nb)
            )
            for _, w in plan
        )

    table = lambda: V((16, width), F32)
    sem = pltpu.SemaphoreType.DMA
    return pl.pallas_call(
        functools.partial(back_body, dp_size),
        grid_spec=pltpu.PrefetchScalarGridSpec(
            num_scalar_prefetch=0,
            grid=(pairs,),
            in_specs=[whole(xo), whole(xt)]
            + [col(rows, pw)] * 3
            + [pl.BlockSpec((2, rows, rows), lambda p: (p, 0, 0))]
            + [col(half, pw)] * 4
            + [whole(gsum), whole(vec), whole(bi)]
            + [hbm] * 8,
            out_specs=[vm] * 9,
            scratch_shapes=[
                V((rows, pw), BF16),
                V((pw, rows), BF16),
                V((pw, rows), BF16),
                V((pw, rows), F32),
                V((pw, rows), F32),
                V((rows, 3 * pw), BF16),
                V((width, 3 * pw), BF16),
                V((width, rows), BF16),
                V((rows, width), F32),
                V((half, width), BF16),
                V((half, width), BF16),
                V((pairs,) + (2,) * nb + (n, 3 * pw), BF16),
                stages(0),
                stages(1),
                V((8, width), F32),
                V((8, width), F32),
                tuple(table() for _ in range(nb + 1)),
                tuple(table() for _ in range(nb)),
                sem((len(plan) * nb,)),
                sem((len(plan) * nb,)),
                sem((len(plan),)),
                sem((2 + nb,)),
                sem((2 + nb,)),
                sem((3,)),
            ],
        ),
        out_shape=[shape((half, width), F32)]
        + [shape((n, width // 2), F32)] * 4
        + [shape((n, ff), F32)] * 2
        + [shape((8, n), F32), shape((1, 2 * ff // dp_size), F32)],
        compiler_params=pltpu.CompilerParams(
            vmem_limit_bytes=60 << 20, collective_id=2, has_side_effects=True
        ),
        cost_estimate=cost(40e9, 20e6),
        name="back",
    )(xo, xt, q, k, v, probs, ao, at, go, gt, gsum, vec, bi, wq, wk, wv, *sa, split(win), split(wo))


def emit_body(big, *refs):
    ins, outs = refs[: big + 2], refs[big + 2 :]
    for i in range(big):
        outs[i][...] = ins[i][...]
    vals = ins[big][...]
    for j in range(8):
        outs[big + j][...] = vals[j]
    outs[big + 8][...] = ins[big + 1][0]


def emit(arrays, vals, bi):
    vm = pl.BlockSpec(memory_space=pltpu.VMEM)
    return pl.pallas_call(
        functools.partial(emit_body, len(arrays)),
        in_specs=[vm] * (len(arrays) + 2),
        out_specs=[vm] * (len(arrays) + 9),
        out_shape=[shape(a.shape, a.dtype) for a in arrays]
        + [shape((vals.shape[1],), F32)] * 8
        + [shape((bi.shape[1],), F32)],
        compiler_params=params(60),
        name="emit",
    )(*arrays, vals, bi)


def local_pair(
    dp_size, inputs, grad_out, lengths, rand_blocks, w_query, b_query, w_key, w_value, b_value,
    w_output, b_output, gain_one, shift_one, w_in, b_in, w_out, b_out, gain_two, shift_two,
):
    core = lax.axis_index("mp").astype(jnp.int32)
    swap = lambda a: lax.ppermute(a, "mp", [(0, 1), (1, 0)])
    vec = lambda a: a.reshape(1, -1)
    x = inputs[0]
    half, width = x.shape
    x_got = swap(x)
    rand = jnp.concatenate([rand_blocks[0], swap(rand_blocks[0])], axis=0)
    sc = jnp.stack([core, lengths[0]])
    q, k, v, probs, a_own, a_send = attn_fwd(
        sc, x, x_got, w_query, w_key, w_value, vec(b_query), vec(b_value), rand
    )
    out, gsum, ga0, ga_got, sa1, sa2, sa3, w_in_g, w_output_g, vec_g, bi_g = middle(
        dp_size, a_own, a_send, x, grad_out[0], b_output, gain_one, shift_one, b_in, b_out,
        gain_two, shift_two, w_output, w_in, w_out,
    )
    *mats, vals, bi = back(
        dp_size, x, x_got, w_query, w_key, w_value, q, k, v, probs, a_own, a_send, ga0, ga_got,
        gsum, vec_g, bi_g, (sa1, sa2, sa3), w_in_g, w_output_g,
    )
    (
        out, input_grad, wq_p, wk_p, wv_p, wo_p, in_part, out_part, bq_p, bv_p, bo_p, g1_p, s1_p,
        b2_p, g2_p, s2_p, bi_p,
    ) = emit([out] + mats, vals, bi)
    return (
        out[None], input_grad[None], wq_p, bq_p, wk_p, wv_p, bv_p, wo_p, bo_p, g1_p, s1_p,
        in_part, bi_p, out_part, b2_p, g2_p, s2_p,
    )


def layer_norm(features, norm_gain, norm_shift):
    row_mean = jnp.mean(features, axis=-1, keepdims=True)
    centered = features - row_mean
    variance = jnp.mean(centered * centered, axis=-1, keepdims=True)
    return centered * lax.rsqrt(variance + norm_epsilon) * norm_gain + norm_shift


def gelu_tanh(features):
    return jax.nn.gelu(features, approximate=True)


def slot_table_ids(block_ids, rand_rows, length):
    valid_blocks = (length + BLK - 1) // BLK
    column = block_ids[:, None]
    columns = jnp.concatenate(
        [
            column - 1,
            column,
            column + 1,
            rand_rows,
            jnp.zeros_like(column),
            jnp.zeros_like(column) + valid_blocks - 1,
        ],
        axis=1,
    )
    in_range = (columns >= 0) & (columns < valid_blocks)
    slot_ids = jnp.arange(columns.shape[1], dtype=jnp.int32)
    earlier = slot_ids[None, :] < slot_ids[:, None]
    repeated = jnp.any(
        (columns[:, :, None] == columns[:, None, :]) & earlier[None, :, :] & in_range[:, None, :],
        axis=2,
    )
    return (jnp.clip(columns, 0, NB - 1), in_range & jnp.logical_not(repeated))


def slot_table(first_block, rand_rows, length):
    block_ids = first_block + jnp.arange(rand_rows.shape[0], dtype=jnp.int32)
    return slot_table_ids(block_ids, rand_rows, length)


def slot_mask(slot_blocks, slot_valid, length):
    positions = slot_blocks[:, :, None] * BLK + jnp.arange(BLK, dtype=jnp.int32)
    allowed = slot_valid[:, :, None] & (positions < length)
    return allowed.reshape(slot_blocks.shape[0], 1, 1, -1)


def gather_slots(whole_rows, slot_blocks):
    picked = whole_rows.reshape(NB, BLK, whole_rows.shape[1])[slot_blocks]
    return picked.reshape(slot_blocks.shape[0], slot_blocks.shape[1] * BLK, HEADS, HD)


def log_total(scores, allowed):
    masked = jnp.where(allowed, scores, negative_fill)
    top_score = jnp.max(masked, axis=-1, keepdims=True)
    return top_score + jnp.log(jnp.sum(jnp.exp(masked - top_score), axis=-1, keepdims=True))


def exp_probs(scores, allowed, totals):
    return jnp.exp(jnp.where(allowed, scores, negative_fill) - totals)


def global_targets(length, device, local_blocks):
    last_block = (length + BLK - 1) // BLK - 1
    targets = []
    for target_block in (jnp.zeros_like(last_block), last_block):
        is_owner = target_block // local_blocks == device
        local_block = jnp.clip(target_block - device * local_blocks, 0, local_blocks - 1)
        targets.append((is_owner, local_block))
    return targets


def global_scores(query_rows, key_one, length):
    scores = jnp.einsum(
        "qhd,khd->hqk",
        query_rows.reshape(BLK, HEADS, HD),
        key_one.reshape(-1, HEADS, HD),
        preferred_element_type=jnp.float32,
    ) * HD ** (-0.5)
    allowed = (jnp.arange(key_one.shape[0], dtype=jnp.int32) < length)[None, None, :]
    return (scores, allowed)


def global_forward(query_rows, key_one, value_one, length):
    scores, allowed = global_scores(query_rows, key_one, length)
    totals = log_total(scores, allowed)
    weighting = exp_probs(scores, allowed, totals).astype(jnp.bfloat16)
    out_rows = jnp.einsum(
        "hqk,khd->qhd",
        weighting,
        value_one.reshape(-1, HEADS, HD),
        preferred_element_type=jnp.float32,
    )
    return (out_rows.reshape(BLK, -1), totals)


def global_skip(query_rows, key_one, value_one, length):
    return (jnp.zeros((BLK, HEADS * HD), jnp.float32), jnp.zeros((HEADS, BLK, 1), jnp.float32))


def global_backward(query_rows, grad_rows, key_one, value_one, length, row_totals):
    score_scale = HD ** (-0.5)
    scores, allowed = global_scores(query_rows, key_one, length)
    exact_probs = exp_probs(scores, allowed, row_totals)
    grad_heads = grad_rows.reshape(BLK, HEADS, HD)
    grad_weights = jnp.einsum(
        "qhd,khd->hqk",
        grad_heads,
        value_one.reshape(-1, HEADS, HD),
        preferred_element_type=jnp.float32,
    )
    delta_sum = jnp.sum(exact_probs * grad_weights, axis=-1, keepdims=True)
    grad_scores = (exact_probs * (grad_weights - delta_sum)).astype(jnp.bfloat16)
    grad_query = (
        jnp.einsum(
            "hqk,khd->qhd",
            grad_scores,
            key_one.reshape(-1, HEADS, HD),
            preferred_element_type=jnp.float32,
        )
        * score_scale
    )
    grad_keys = (
        jnp.einsum(
            "hqk,qhd->khd",
            grad_scores,
            query_rows.reshape(BLK, HEADS, HD),
            preferred_element_type=jnp.float32,
        )
        * score_scale
    )
    grad_values = jnp.einsum(
        "hqk,qhd->khd",
        exact_probs.astype(jnp.bfloat16),
        grad_heads,
        preferred_element_type=jnp.float32,
    )
    return (
        grad_query.reshape(BLK, -1),
        grad_keys.reshape(key_one.shape[0], -1),
        grad_values.reshape(key_one.shape[0], -1),
    )


def global_back_skip(query_rows, grad_rows, key_one, value_one, length, row_totals):
    key_zeros = jnp.zeros(key_one.shape, jnp.float32)
    return (jnp.zeros((BLK, key_one.shape[1]), jnp.float32), key_zeros, key_zeros)


def attend_forward(query_one, key_one, value_one, length, rand_rows, device):
    local_blocks = rand_rows.shape[0]
    slot_blocks, slot_valid = slot_table(device * local_blocks, rand_rows, length)
    allowed = slot_mask(slot_blocks, slot_valid, length)
    query_blocks = query_one.reshape(local_blocks, BLK, HEADS, HD)
    scores = jnp.einsum(
        "nqhd,nkhd->nhqk",
        query_blocks,
        gather_slots(key_one, slot_blocks),
        preferred_element_type=jnp.float32,
    ) * HD ** (-0.5)
    totals = log_total(scores, allowed)
    weighting = exp_probs(scores, allowed, totals).astype(jnp.bfloat16)
    attended = jnp.einsum(
        "nhqk,nkhd->nqhd",
        weighting,
        gather_slots(value_one, slot_blocks),
        preferred_element_type=jnp.float32,
    ).reshape(query_one.shape[0], -1)
    global_totals = []
    for is_owner, local_block in global_targets(length, device, local_blocks):
        query_rows = lax.dynamic_slice_in_dim(query_one, local_block * BLK, BLK, 0)
        out_rows, row_totals = lax.cond(
            is_owner, global_forward, global_skip, query_rows, key_one, value_one, length
        )
        updated = lax.dynamic_update_slice_in_dim(attended, out_rows, local_block * BLK, 0)
        attended = jnp.where(is_owner, updated, attended)
        global_totals.append(row_totals)
    return (attended, totals, global_totals[0], global_totals[1])


def attend_backward(
    query_one,
    key_one,
    value_one,
    length,
    rand_rows,
    totals,
    first_totals,
    last_totals,
    grad_one,
    device,
):
    score_scale = HD ** (-0.5)
    local_blocks = rand_rows.shape[0]
    first_block = device * local_blocks
    slot_blocks, slot_valid = slot_table(first_block, rand_rows, length)
    allowed = slot_mask(slot_blocks, slot_valid, length)
    query_blocks = query_one.reshape(local_blocks, BLK, HEADS, HD)
    key_slots = gather_slots(key_one, slot_blocks)
    value_slots = gather_slots(value_one, slot_blocks)
    scores = (
        jnp.einsum("nqhd,nkhd->nhqk", query_blocks, key_slots, preferred_element_type=jnp.float32)
        * score_scale
    )
    exact_probs = exp_probs(scores, allowed, totals)
    last_block = (length + BLK - 1) // BLK - 1
    row_blocks = first_block + jnp.arange(query_one.shape[0], dtype=jnp.int32) // BLK
    is_global = (row_blocks == 0) | (row_blocks == last_block)
    grad_sparse = jnp.where(is_global[:, None], jnp.zeros_like(grad_one), grad_one)
    grad_heads = grad_sparse.reshape(local_blocks, BLK, HEADS, HD)
    grad_weights = jnp.einsum(
        "nqhd,nkhd->nhqk", grad_heads, value_slots, preferred_element_type=jnp.float32
    )
    delta_sum = jnp.sum(exact_probs * grad_weights, axis=-1, keepdims=True)
    grad_scores = (exact_probs * (grad_weights - delta_sum)).astype(jnp.bfloat16)
    grad_query = (
        jnp.einsum(
            "nhqk,nkhd->nqhd", grad_scores, key_slots, preferred_element_type=jnp.float32
        ).reshape(query_one.shape[0], -1)
        * score_scale
    )
    grad_key_slots = (
        jnp.einsum("nhqk,nqhd->nkhd", grad_scores, query_blocks, preferred_element_type=jnp.float32)
        * score_scale
    )
    grad_value_slots = jnp.einsum(
        "nhqk,nqhd->nkhd",
        exact_probs.astype(jnp.bfloat16),
        grad_heads,
        preferred_element_type=jnp.float32,
    )
    flat_ids = slot_blocks.reshape(-1)
    slot_width = BLK * query_one.shape[1]
    grad_keys = jax.ops.segment_sum(
        grad_key_slots.reshape(-1, slot_width), flat_ids, num_segments=NB
    ).reshape(-1, query_one.shape[1])
    grad_values = jax.ops.segment_sum(
        grad_value_slots.reshape(-1, slot_width), flat_ids, num_segments=NB
    ).reshape(-1, query_one.shape[1])
    for (is_owner, local_block), row_totals in zip(
        global_targets(length, device, local_blocks), (first_totals, last_totals)
    ):
        query_rows = lax.dynamic_slice_in_dim(query_one, local_block * BLK, BLK, 0)
        grad_rows = lax.dynamic_slice_in_dim(grad_one, local_block * BLK, BLK, 0)
        query_add, key_add, value_add = lax.cond(
            is_owner,
            global_backward,
            global_back_skip,
            query_rows,
            grad_rows,
            key_one,
            value_one,
            length,
            row_totals,
        )
        current = lax.dynamic_slice_in_dim(grad_query, local_block * BLK, BLK, 0)
        grad_query = lax.dynamic_update_slice_in_dim(
            grad_query, current + query_add, local_block * BLK, 0
        )
        grad_keys = grad_keys + key_add
        grad_values = grad_values + value_add
    return (grad_query, grad_keys, grad_values)


def local(
    inputs,
    grad_out,
    lengths,
    rand_blocks,
    w_query,
    b_query,
    w_key,
    w_value,
    b_value,
    w_output,
    b_output,
    gain_one,
    shift_one,
    w_in,
    b_in,
    w_out,
    b_out,
    gain_two,
    shift_two,
):
    device = lax.axis_index("mp")
    seq_count, local_rows, width = inputs.shape
    flat_in = inputs.reshape(-1, width)
    query = (jnp.dot(flat_in, w_query, preferred_element_type=jnp.float32) + b_query).astype(
        jnp.bfloat16
    )
    keys = jnp.dot(flat_in, w_key, preferred_element_type=jnp.float32).astype(jnp.bfloat16)
    values = (jnp.dot(flat_in, w_value, preferred_element_type=jnp.float32) + b_value).astype(
        jnp.bfloat16
    )
    key_all, value_all = (
        lax.all_gather(keys.reshape(seq_count, local_rows, width), "mp", axis=1, tiled=True),
        lax.all_gather(values.reshape(seq_count, local_rows, width), "mp", axis=1, tiled=True),
    )
    query_seq = query.reshape(seq_count, local_rows, width)

    def forward_item(seq_items):
        query_one, key_one, value_one, length, rand_rows = seq_items
        return attend_forward(query_one, key_one, value_one, length, rand_rows, device)

    attended, totals, first_totals, last_totals = lax.map(
        forward_item, (query_seq, key_all, value_all, lengths, rand_blocks)
    )
    attended_low = attended.reshape(-1, width).astype(jnp.bfloat16)
    summed_one = (
        flat_in.astype(jnp.float32)
        + jnp.dot(attended_low, w_output, preferred_element_type=jnp.float32)
        + b_output
    )
    first, norm_one_back = jax.vjp(
        layer_norm, summed_one, gain_one.astype(jnp.float32), shift_one.astype(jnp.float32)
    )
    first_low = first.astype(jnp.bfloat16)
    rows_all = lax.all_gather(first_low, "mp", axis=0, tiled=True)
    hidden = jnp.dot(rows_all, w_in, preferred_element_type=jnp.float32) + b_in
    active_full, gelu_back = jax.vjp(gelu_tanh, hidden)
    active = active_full.astype(jnp.bfloat16)
    feed = lax.psum_scatter(
        jnp.einsum(
            "rf,df->rd",
            lax.slice_in_dim(active, 0, first_low.shape[0] * lax.axis_size("mp"), axis=0),
            w_out,
            preferred_element_type=jnp.float32,
        ),
        "mp",
        scatter_dimension=0,
        tiled=True,
    )
    summed_two = first + feed + b_out
    output, norm_two_back = jax.vjp(
        layer_norm, summed_two, gain_two.astype(jnp.float32), shift_two.astype(jnp.float32)
    )
    grad_two, gain_two_grad, shift_two_grad = norm_two_back(
        grad_out.reshape(-1, width).astype(jnp.float32)
    )
    grad_feed = grad_two.astype(jnp.bfloat16)
    b_out_grad = jnp.sum(grad_feed, axis=0, dtype=jnp.float32)
    grads_all = lax.all_gather(grad_feed, "mp", axis=0, tiled=True)
    w_out_grad = jnp.einsum("rd,rf->df", grads_all, active, preferred_element_type=jnp.float32)
    grad_hidden = gelu_back(jnp.dot(grads_all, w_out, preferred_element_type=jnp.float32))[
        0
    ].astype(jnp.bfloat16)
    w_in_grad = jnp.einsum("rd,rf->df", rows_all, grad_hidden, preferred_element_type=jnp.float32)
    grad_first = grad_two + lax.psum_scatter(
        jnp.einsum(
            "rf,df->rd",
            lax.slice_in_dim(grad_hidden, 0, grad_feed.shape[0] * lax.axis_size("mp"), axis=0),
            w_in,
            preferred_element_type=jnp.float32,
        ),
        "mp",
        scatter_dimension=0,
        tiled=True,
    )
    b_in_grad = lax.dynamic_update_slice_in_dim(
        jnp.zeros((FF,), jnp.float32),
        jnp.sum(grad_hidden, axis=0, dtype=jnp.float32),
        device * w_in.shape[1],
        0,
    )
    grad_sum_one, gain_one_grad, shift_one_grad = norm_one_back(grad_first)
    grad_branch = grad_sum_one.astype(jnp.bfloat16)
    b_output_grad = jnp.sum(grad_branch, axis=0, dtype=jnp.float32)
    w_output_grad = jnp.einsum(
        "rd,re->de", attended_low, grad_branch, preferred_element_type=jnp.float32
    )
    grad_attended = (
        jnp.einsum("re,de->rd", grad_branch, w_output, preferred_element_type=jnp.float32)
        .astype(jnp.bfloat16)
        .reshape(seq_count, local_rows, width)
    )

    def backward_item(seq_items):
        (
            query_one,
            key_one,
            value_one,
            length,
            rand_rows,
            sparse_totals,
            first_one,
            last_one,
            grad_one,
        ) = seq_items
        return attend_backward(
            query_one,
            key_one,
            value_one,
            length,
            rand_rows,
            sparse_totals,
            first_one,
            last_one,
            grad_one,
            device,
        )

    grad_query, grad_keys, grad_values = lax.map(
        backward_item,
        (
            query_seq,
            key_all,
            value_all,
            lengths,
            rand_blocks,
            totals,
            first_totals,
            last_totals,
            grad_attended,
        ),
    )
    key_sums, value_sums = (
        lax.psum_scatter(
            grad_keys.astype(jnp.bfloat16), "mp", scatter_dimension=1, tiled=True
        ).astype(jnp.float32),
        lax.psum_scatter(
            grad_values.astype(jnp.bfloat16), "mp", scatter_dimension=1, tiled=True
        ).astype(jnp.float32),
    )
    grad_q_low = grad_query.reshape(-1, width).astype(jnp.bfloat16)
    grad_k_low = key_sums.reshape(-1, width).astype(jnp.bfloat16)
    grad_v_low = value_sums.reshape(-1, width).astype(jnp.bfloat16)
    input_grad = grad_sum_one + jnp.einsum(
        "re,de->rd", grad_q_low, w_query, preferred_element_type=jnp.float32
    )
    input_grad = input_grad + jnp.einsum(
        "re,de->rd", grad_k_low, w_key, preferred_element_type=jnp.float32
    )
    input_grad = input_grad + jnp.einsum(
        "re,de->rd", grad_v_low, w_value, preferred_element_type=jnp.float32
    )
    w_query_grad = jnp.einsum("rd,re->de", flat_in, grad_q_low, preferred_element_type=jnp.float32)
    w_key_grad = jnp.einsum("rd,re->de", flat_in, grad_k_low, preferred_element_type=jnp.float32)
    w_value_grad = jnp.einsum("rd,re->de", flat_in, grad_v_low, preferred_element_type=jnp.float32)
    b_query_grad = jnp.sum(grad_q_low, axis=0, dtype=jnp.float32)
    b_value_grad = jnp.sum(grad_v_low, axis=0, dtype=jnp.float32)
    reduced = (
        lax.psum_scatter(
            w_query_grad.astype(jnp.bfloat16), "dp", scatter_dimension=0, tiled=True
        ).astype(jnp.float32),
        lax.psum_scatter(
            w_key_grad.astype(jnp.bfloat16), "dp", scatter_dimension=0, tiled=True
        ).astype(jnp.float32),
        lax.psum_scatter(
            w_value_grad.astype(jnp.bfloat16), "dp", scatter_dimension=0, tiled=True
        ).astype(jnp.float32),
        lax.psum_scatter(
            w_output_grad.astype(jnp.bfloat16), "dp", scatter_dimension=0, tiled=True
        ).astype(jnp.float32),
        lax.psum_scatter(
            w_in_grad.astype(jnp.bfloat16), "dp", scatter_dimension=0, tiled=True
        ).astype(jnp.float32),
        lax.psum_scatter(
            w_out_grad.astype(jnp.bfloat16), "dp", scatter_dimension=0, tiled=True
        ).astype(jnp.float32),
        lax.psum_scatter(
            b_query_grad.astype(jnp.bfloat16), "dp", scatter_dimension=0, tiled=True
        ).astype(jnp.float32),
        lax.psum_scatter(
            b_value_grad.astype(jnp.bfloat16), "dp", scatter_dimension=0, tiled=True
        ).astype(jnp.float32),
        lax.psum_scatter(
            b_output_grad.astype(jnp.bfloat16), "dp", scatter_dimension=0, tiled=True
        ).astype(jnp.float32),
        lax.psum_scatter(
            gain_one_grad.astype(jnp.bfloat16), "dp", scatter_dimension=0, tiled=True
        ).astype(jnp.float32),
        lax.psum_scatter(
            shift_one_grad.astype(jnp.bfloat16), "dp", scatter_dimension=0, tiled=True
        ).astype(jnp.float32),
        lax.psum_scatter(
            b_in_grad.astype(jnp.bfloat16), "dp", scatter_dimension=0, tiled=True
        ).astype(jnp.float32),
        lax.psum_scatter(
            b_out_grad.astype(jnp.bfloat16), "dp", scatter_dimension=0, tiled=True
        ).astype(jnp.float32),
        lax.psum_scatter(
            gain_two_grad.astype(jnp.bfloat16), "dp", scatter_dimension=0, tiled=True
        ).astype(jnp.float32),
        lax.psum_scatter(
            shift_two_grad.astype(jnp.bfloat16), "dp", scatter_dimension=0, tiled=True
        ).astype(jnp.float32),
    )
    query_part, key_part_out, value_part, output_part = (
        lax.psum_scatter(
            reduced[0].astype(jnp.bfloat16), "mp", scatter_dimension=1, tiled=True
        ).astype(jnp.float32),
        lax.psum_scatter(
            reduced[1].astype(jnp.bfloat16), "mp", scatter_dimension=1, tiled=True
        ).astype(jnp.float32),
        lax.psum_scatter(
            reduced[2].astype(jnp.bfloat16), "mp", scatter_dimension=1, tiled=True
        ).astype(jnp.float32),
        lax.psum_scatter(
            reduced[3].astype(jnp.bfloat16), "mp", scatter_dimension=1, tiled=True
        ).astype(jnp.float32),
    )
    in_part = reduced[4]
    out_part = reduced[5]
    vectors = lax.psum(
        (
            reduced[6],
            reduced[7],
            reduced[8],
            reduced[9],
            reduced[10],
            reduced[11],
            reduced[12],
            reduced[13],
            reduced[14],
        ),
        "mp",
    )
    return (
        output.astype(jnp.bfloat16).reshape(seq_count, local_rows, width),
        input_grad.reshape(seq_count, local_rows, width),
        query_part,
        vectors[0],
        key_part_out,
        value_part,
        vectors[1],
        output_part,
        vectors[2],
        vectors[3],
        vectors[4],
        in_part,
        vectors[5],
        out_part,
        vectors[6],
        vectors[7],
        vectors[8],
    )


def solution(mesh):
    in_specs = (
        P("dp", "mp", None),
        P("dp", "mp", None),
        P("dp"),
        P("dp", "mp", None),
        P(),
        P(),
        P(),
        P(),
        P(),
        P(),
        P(),
        P(),
        P(),
        P(None, "mp"),
        P("mp"),
        P(None, "mp"),
        P(),
        P(),
        P(),
    )
    out_specs = (
        P("dp", "mp", None),
        P("dp", "mp", None),
        P("dp", "mp"),
        P("dp"),
        P("dp", "mp"),
        P("dp", "mp"),
        P("dp"),
        P("dp", "mp"),
        P("dp"),
        P("dp"),
        P("dp"),
        P("dp", "mp"),
        P("dp"),
        P("dp", "mp"),
        P("dp"),
        P("dp"),
        P("dp"),
    )
    sizes = dict(mesh.shape)
    if sizes["mp"] == 2 and sizes["dp"] in (4, 8, 16, 32):
        local_fn = functools.partial(local_pair, sizes["dp"])
    else:
        local_fn = local
    return jax.shard_map(local_fn, mesh=mesh, in_specs=in_specs, out_specs=out_specs, check_vma=False)
```

```python
import functools

import jax
import jax.numpy as jnp
from jax import lax
from jax.experimental import pallas as pl
from jax.experimental.pallas import tpu as pltpu
from jax.sharding import PartitionSpec as P

HEADS = 12
HD = 64
FF = 3072
BLK = 64
NB = 16


negative_fill = -1000000000.0
norm_epsilon = 1e-12


F32 = jnp.float32
BF16 = jnp.bfloat16
NN = (((1,), (0,)), ((), ()))
NT = (((1,), (1,)), ((), ()))
TN = (((0,), (0,)), ((), ()))


def mm(a, b, dims=NN):
    return lax.dot_general(a, b, dims, preferred_element_type=F32)


def params(mib=56):
    return pltpu.CompilerParams(vmem_limit_bytes=mib << 20)


def cost(flops, nbytes, trans=0):
    return pl.CostEstimate(flops=int(flops), bytes_accessed=int(nbytes), transcendentals=int(trans))


def shape(dims, dtype):
    return jax.ShapeDtypeStruct(dims, dtype)


def row_stats(u):
    mean = jnp.mean(u, axis=-1, keepdims=True)
    cen = u - mean
    var = jnp.mean(cen * cen, axis=-1, keepdims=True)
    rs = lax.rsqrt(var + norm_epsilon)
    return cen * rs, rs


def partner_copy(src, dst, send, recv, me):
    return pltpu.make_async_remote_copy(
        src_ref=src, dst_ref=dst, send_sem=send, recv_sem=recv,
        device_id={"mp": 1 - me}, device_id_type=pl.DeviceIdType.MESH,
    )


def front_body(
    lengths, x, rand, bq, bv, wq, wk, wv,
    x_got, a_own, a_oth, a_got, q_o, k_o, v_o, p_o,
    xg_s, ag_s, w_s, b_s, rand_s, rand_r, bias, wsem, send, recv,
):
    me = lax.axis_index("mp")
    p = pl.program_id(0)
    half, width = x.shape
    rows = 2 * half
    hw = width // 2
    pw = 2 * HD
    nb = rows // BLK
    tile = 256
    x_copy = partner_copy(x, xg_s, send.at[0], recv.at[0], me)
    rand_copy = partner_copy(rand_s, rand_r, send.at[1], recv.at[1], me)
    own_cols = pl.ds(pl.multiple_of(me * hw, hw), hw)

    @pl.when(p == 0)
    def _():
        barrier = pltpu.get_barrier_semaphore()
        pl.semaphore_signal(
            barrier, inc=1, device_id={"mp": 1 - me}, device_id_type=pl.DeviceIdType.MESH
        )
        loads = [
            pltpu.make_async_copy(w.at[:, own_cols], w_s.at[i], wsem.at[i])
            for i, w in enumerate((wq, wk, wv))
        ]
        for c in loads:
            c.start()
        rand_s[...] = jnp.zeros_like(rand_s)
        rand_s[:, : rand.shape[2]] = rand[0]
        b_s[0:1, :] = bq[...].astype(F32)[None, :]
        b_s[1:2, :] = bv[...].astype(F32)[None, :]
        pl.semaphore_wait(barrier, 1)
        x_copy.start()
        rand_copy.start()
        for c in loads:
            c.wait()

    cols = pl.ds(pl.multiple_of(p * pw, pw), pw)
    bias_cols = pl.ds(pl.multiple_of(me * hw + p * pw, pw), pw)

    def project(i, xr):
        rs = slice(i * half, (i + 1) * half)
        q_o[rs, :] = (mm(xr[...], w_s[0, :, cols]) + b_s[0:1, bias_cols]).astype(BF16)
        k_o[rs, :] = mm(xr[...], w_s[1, :, cols]).astype(BF16)
        v_o[rs, :] = (mm(xr[...], w_s[2, :, cols]) + b_s[1:2, bias_cols]).astype(BF16)

    project(0, x)

    @pl.when(p == 0)
    def _():
        rand_copy.wait_recv()
        ln = lengths[0]
        last = (ln + BLK - 1) // BLK - 1
        lb = lax.broadcasted_iota(jnp.int32, (nb, rows), 0)
        kp = lax.broadcasted_iota(jnp.int32, (nb, rows), 1)
        qb = jnp.where(lb < nb // 2, lb + (nb // 2) * me, lb - (nb // 2) * me)
        kpos = jnp.where(kp < half, kp + half * me, kp - half * me)
        kb = kpos // BLK
        ok = (jnp.abs(kb - qb) <= 1) | (kb == 0) | (kb == last)
        both = jnp.concatenate([rand_s[...], rand_r[...]], axis=0)
        for j in range(rand.shape[2]):
            ok = ok | (kb == both[:, j : j + 1])
        ok = ok | (qb == 0) | (qb == last)
        ok = ok & (kpos < ln)
        table = jnp.where(ok, 0.0, -1e30).astype(F32)
        for b in range(nb):
            bias[b] = jnp.broadcast_to(table[b : b + 1, :], (8, rows))
        x_copy.wait_recv()
        x_got[...] = xg_s[...]

    project(1, xg_s)

    low = lax.broadcasted_iota(jnp.int32, (tile, pw), 1) < HD
    order = [half + t * tile for t in range(half // tile)] + [t * tile for t in range(half // tile)]
    units = [(r0, h) for r0 in order for h in range(2)]
    scores, probs, outs = {}, {}, {}

    def score(i):
        r0, h = units[i]
        q = q_o[r0 : r0 + tile, :] * BF16(HD**-0.5)
        s = mm(jnp.where(low if h == 0 else ~low, q, BF16(0)), k_o[...], NT)
        b0 = r0 // BLK
        s = s.reshape(tile // BLK, BLK // 8, 8, rows) + bias[b0 : b0 + tile // BLK][:, None]
        scores[i] = s.reshape(tile, rows)

    def attend(i):
        r0, h = units[i]
        outs[i] = mm(probs.pop(i), v_o[...])
        if h == 1:
            a = jnp.where(low, outs.pop(i - 1), outs.pop(i)).astype(BF16)
            if r0 < half:
                a_own[r0 : r0 + tile, cols] = a
            else:
                a_oth[r0 - half : r0 - half + tile, cols] = a
                if r0 + tile == rows:
                    partner_copy(
                        a_oth.at[:, cols], ag_s.at[:, cols], send.at[2 + p], recv.at[2 + p], me
                    ).start()

    score(0)
    for i, (r0, h) in enumerate(units):
        if i + 1 < len(units):
            score(i + 1)
        s = scores.pop(i)
        e = jnp.exp(s - jnp.max(s, axis=-1, keepdims=True))
        pr = (e * (1.0 / jnp.sum(e, axis=-1, keepdims=True))).astype(BF16)
        p_o[h, r0 : r0 + tile, :] = pr
        probs[i] = pr
        if i >= 1:
            attend(i - 1)
    attend(len(units) - 1)

    @pl.when(p == pl.num_programs(0) - 1)
    def _():
        x_copy.wait_send()
        rand_copy.wait_send()
        for j in range(hw // pw):
            cs = slice(j * pw, (j + 1) * pw)
            c = partner_copy(a_oth.at[:, cs], ag_s.at[:, cs], send.at[2 + j], recv.at[2 + j], me)
            c.wait_send()
            c.wait_recv()
        a_got[...] = ag_s[...]


def front(lengths, x, rand, bq, bv, wq, wk, wv):
    half, width = x.shape
    rows = 2 * half
    pairs = HEADS // 4
    pw = 2 * HD
    hw = width // 2
    vm = pl.BlockSpec(memory_space=pltpu.VMEM)
    hbm = pl.BlockSpec(memory_space=pl.ANY)
    col = pl.BlockSpec((rows, pw), lambda p: (0, p))
    V = pltpu.VMEM
    sem = pltpu.SemaphoreType.DMA
    return pl.pallas_call(
        front_body,
        grid_spec=pltpu.PrefetchScalarGridSpec(
            num_scalar_prefetch=0,
            grid=(pairs,),
            in_specs=[pl.BlockSpec(memory_space=pltpu.SMEM)] + [vm] * 4 + [hbm] * 3,
            out_specs=[vm] * 4 + [col] * 3 + [pl.BlockSpec((2, rows, rows), lambda p: (p, 0, 0))],
            scratch_shapes=[
                V((half, width), BF16),
                V((half, hw), BF16),
                V((3, width, hw), BF16),
                V((8, width), F32),
                V((rand.shape[1], 128), jnp.int32),
                V((rand.shape[1], 128), jnp.int32),
                V((rows // BLK, 8, rows), F32),
                sem((3,)),
                sem((2 + pairs,)),
                sem((2 + pairs,)),
            ],
        ),
        out_shape=[shape((half, width), BF16)]
        + [shape((half, hw), BF16)] * 3
        + [shape((rows, hw), BF16)] * 3
        + [shape((2 * pairs, rows, rows), BF16)],
        compiler_params=pltpu.CompilerParams(
            vmem_limit_bytes=60 << 20, collective_id=3, has_side_effects=True
        ),
        cost_estimate=cost(20e9, 20e6, 6 * rows * rows),
        name="front",
    )(lengths, x, rand, bq, bv, wq, wk, wv)


class Piece:
    def __init__(self, bits, sems, base, src, got, kept, stage0=0):
        self.bits = bits
        self.send, self.recv, self.load = sems
        self.base = base
        self.src, self.got, self.kept = src, got, kept
        self.stage0 = stage0
        self.dev = lax.axis_index("dp")

    def mine(self, k):
        return (self.dev // 2 ** self.bits[k]) % 2

    def peer(self, k):
        return self.dev + 2 ** self.bits[k] * (1 - 2 * self.mine(k))

    def side(self, k, bit, lead=None):
        left = sorted(self.bits[k:], reverse=True)
        where = left.index(self.bits[k])
        idx = [slice(None)] * len(left) if lead is None else list(lead[:where]) + [None] + list(lead[where:])
        idx[where] = bit
        return tuple(idx)

    def source(self, k):
        return self.src if k == self.stage0 else self.kept[k - 1]

    def copy(self, k):
        i = self.base + k
        return pltpu.make_async_remote_copy(
            src_ref=self.source(k).at[self.side(k, 1 - self.mine(k))], dst_ref=self.got[k],
            send_sem=self.send.at[i], recv_sem=self.recv.at[i],
            device_id={"dp": self.peer(k)}, device_id_type=pl.DeviceIdType.MESH,
        )

    def load_own(self):
        k = self.stage0
        return pltpu.make_async_copy(
            self.src.at[self.side(k, self.mine(k))], self.kept[k], self.load.at[self.base // len(self.bits)]
        )

    def total(self, k, lead, loaded):
        if loaded:
            own = self.kept[k][lead]
        else:
            own = self.source(k)[self.side(k, self.mine(k), lead)]
        return own.astype(F32) + self.got[k][lead].astype(F32)

    def add(self, k, loaded=False):
        free = len(self.bits) - 1 - k

        def step(i, carry):
            lead = tuple((i // 2 ** (free - 1 - j)) % 2 for j in range(free))
            self.kept[k][lead] = self.total(k, lead, loaded).astype(BF16)
            return carry

        lax.fori_loop(0, 2**free, step, 0)

    def forward(self, k, loaded=False):
        self.copy(k).wait_recv()
        self.add(k, loaded)
        self.copy(k + 1).start()

    def result(self):
        k = len(self.bits) - 1
        self.copy(k).wait_recv()
        return self.total(k, (), False)

    def drain(self):
        for k in range(self.stage0, len(self.bits)):
            self.copy(k).wait_send()


def bit_orders(dp_size):
    nb = dp_size.bit_length() - 1
    rest = list(range(2, nb))
    return [0, 1] + rest, [1, 0] + rest, rest + [0, 1]


def gelu_and_slope(v):
    k0 = 0.7978845608028654
    k1 = 0.044715
    v2 = v * v
    t = jnp.tanh(v * (k0 + (k0 * k1) * v2))
    hp = 0.5 * t + 0.5
    return v * hp, hp + (0.5 * v) * (1.0 - t * t) * (k0 + (3 * k0 * k1) * v2)


def norm_back(e, n, rs, gain):
    eg = e * gain
    return (eg - jnp.mean(eg, -1, keepdims=True) - n * jnp.mean(eg * n, -1, keepdims=True)) * rs


def middle_body(
    dp_size, a_own, a_got, x, gout, b_output, gain1, shift1, b_in, b_out, gain2, shift2,
    w_o_h, w_in_h, w_out_h,
    out_o, gsum_o, ga_o, gat_o, sa1, sa2, sa3, win_g, wo_g, vec_o, bi_o,
    fl, feed_s, feed_g, gf, part_s, part_g, gat_s, gb, wo_s, wo_r, vec_s, vec_r, bi_s, bi_s2, bi_r, wout_g, got_a1, got_a2, got_a3,
    w_o, w_in, w_out, act, slope, gh, u_s, first_s, own_s, gtwo_s,
    load_sem, send_sem, recv_sem, a_send_sem, a_recv_sem,
):
    me = lax.axis_index("mp")
    half, width = x.shape
    hw = width // 2
    tile = 256
    tiles = half // tile
    cut = sa1.shape[-1]
    nb = dp_size.bit_length() - 1
    sems = (a_send_sem, a_recv_sem, None)
    chunks = [slice(None)] * (nb + 1)
    outs_a = [
        Piece(
            bits, sems, i * nb, wout_g.at[tuple(chunks + [slice(i * cut, (i + 1) * cut)])],
            (g,), (s,),
        )
        for i, (bits, g, s) in enumerate(
            zip(bit_orders(dp_size), (got_a1, got_a2, got_a3), (sa1, sa2, sa3))
        )
    ]
    barrier = pltpu.get_barrier_semaphore()
    for device in [{"mp": 1 - me}] + [{"dp": a.peer(0)} for a in outs_a]:
        pl.semaphore_signal(barrier, inc=1, device_id=device, device_id_type=pl.DeviceIdType.MESH)
    loads = []
    for i, (src, dst) in enumerate(((w_o_h, w_o), (w_in_h, w_in), (w_out_h, w_out))):
        loads.append(pltpu.make_async_copy(src, dst, load_sem.at[i]))
        loads[-1].start()
    pl.semaphore_wait(barrier, 4)

    def copy(src, dst, i):
        return partner_copy(src, dst, send_sem.at[i], recv_sem.at[i], me)

    loads[0].wait()

    def rows(t):
        return pl.ds(pl.multiple_of(t * tile, tile), tile)

    def fl_copy(t):
        return copy(fl.at[0, rows(t)], fl.at[1, rows(t)], 1 + t)

    def feed_copy(t):
        return copy(feed_s.at[rows(t)], feed_g.at[rows(t)], 3 + t)

    def gf_copy(t):
        return copy(gf.at[0, rows(t)], gf.at[1, rows(t)], 5 + t)

    def part_copy(t):
        return copy(part_s.at[rows(t)], part_g.at[rows(t)], 7 + t)

    def ga_copy(t):
        return copy(gat_s.at[rows(t)], gat_o.at[rows(t)], 9 + t)

    own_o = pl.ds(pl.multiple_of(me * hw, hw), hw)
    got_o = pl.ds(pl.multiple_of((1 - me) * hw, hw), hw)

    def project(t, carry):
        r = rows(t)
        u = x[r, :].astype(F32) + (
            mm(a_own[r, :], w_o[own_o, :]) + mm(a_got[r, :], w_o[got_o, :])
        ) + b_output[...].astype(F32)[None, :]
        n, _ = row_stats(u)
        first = n * gain1[...].astype(F32)[None, :] + shift1[...].astype(F32)[None, :]
        u_s[r, :] = u
        first_s[r, :] = first
        fl[0, r, :] = first.astype(BF16)
        fl_copy(t).start()
        return carry

    lax.fori_loop(0, tiles, project, 0)
    loads[1].wait()
    loads[2].wait()

    def feed_forward(i, t):
        r = rows(t)
        v = mm(fl[i, r, :], w_in[...]) + b_in[...].astype(F32)[None, :]
        a, s = gelu_and_slope(v)
        a = a.astype(BF16)
        act[i, r, :] = a
        slope[i, r, :] = s.astype(BF16)
        return mm(a, w_out[...], NT)

    def forward_own(t, carry):
        own_s[rows(t), :] = feed_forward(0, t)
        return carry

    def forward_got(t, carry):
        fl_copy(t).wait_recv()
        feed_s[rows(t), :] = feed_forward(1, t).astype(BF16)
        feed_copy(t).start()
        return carry

    lax.fori_loop(0, tiles, forward_own, 0)
    lax.fori_loop(0, tiles, forward_got, 0)

    vec_s[...] = jnp.zeros_like(vec_s)

    def add_vec(i, value):
        vec_s[i : i + 1, :] += jnp.sum(value, 0, keepdims=True)

    def second_norm(t, carry):
        r = rows(t)
        feed_copy(t).wait_recv()
        u = first_s[r, :] + (own_s[r, :] + feed_g[r, :].astype(F32)) + b_out[...].astype(F32)[None, :]
        n, rs = row_stats(u)
        gain = gain2[...].astype(F32)[None, :]
        out_o[r, :] = (n * gain + shift2[...].astype(F32)[None, :]).astype(BF16)
        e = gout[r, :].astype(F32)
        d = norm_back(e, n, rs, gain)
        low = d.astype(BF16)
        gtwo_s[r, :] = d
        gf[0, r, :] = low
        gf_copy(t).start()
        add_vec(6, e * n)
        add_vec(7, e)
        add_vec(5, low.astype(F32))
        return carry

    lax.fori_loop(0, tiles, second_norm, 0)
    bi_s[...] = jnp.zeros_like(bi_s)

    def feed_back(i, t):
        r = rows(t)
        g = (mm(gf[i, r, :], w_out[...]) * slope[i, r, :].astype(F32)).astype(BF16)
        gh[i, r, :] = g
        bi_s[0:1, :] += jnp.sum(g.astype(F32), 0, keepdims=True)
        return mm(g, w_in[...], NT)

    def back_own(t, carry):
        own_s[rows(t), :] = feed_back(0, t)
        return carry

    def wait_gf(t, carry):
        gf_copy(t).wait_recv()
        return carry

    def back_got(t, carry):
        part_s[rows(t), :] = feed_back(1, t).astype(BF16)
        part_copy(t).start()
        return carry

    lax.fori_loop(0, tiles, back_own, 0)
    lax.fori_loop(0, tiles, wait_gf, 0)

    def out_weights(j, carry):
        c = pl.ds(pl.multiple_of(j * hw, hw), hw)
        total = mm(gf[0, :, c], act[0], TN) + mm(gf[1, :, c], act[1], TN)
        wout_g[j] = total.astype(BF16).reshape(wout_g.shape[1:])
        return carry

    lax.fori_loop(0, 2, out_weights, 0)
    for a in outs_a:
        a.copy(0).start()
    lax.fori_loop(0, tiles, back_got, 0)

    def weights(out, lhs, rhs):
        def step(j, carry):
            c = pl.ds(pl.multiple_of(j * tile, tile), tile)
            out[c, :] = (
                mm(lhs[0, :, c], rhs[0], TN) + mm(lhs[1, :, c], rhs[1], TN)
            ).astype(BF16)
            return carry

        lax.fori_loop(0, width // tile, step, 0)

    weights(win_g, fl, gh)

    def first_norm(t, carry):
        r = rows(t)
        part_copy(t).wait_recv()
        e = gtwo_s[r, :] + own_s[r, :] + part_g[r, :].astype(F32)
        n, rs = row_stats(u_s[r, :])
        d = norm_back(e, n, rs, gain1[...].astype(F32)[None, :])
        low = d.astype(BF16)
        gsum_o[r, :] = d
        gb[r, :] = low
        gat_s[r, :] = mm(low, w_o[got_o, :], NT).astype(BF16)
        ga_copy(t).start()
        ga_o[r, :] = mm(low, w_o[own_o, :], NT).astype(BF16)
        add_vec(3, e * n)
        add_vec(4, e)
        add_vec(2, low.astype(F32))
        return carry

    lax.fori_loop(0, tiles, first_norm, 0)
    vec_copy = copy(vec_s, vec_r, 11)
    vec_copy.start()
    bi_s2[0:1, :] = bi_s[0:1, :width]
    bi_s2[1:2, :] = bi_s[0:1, width:]
    bi_copy = copy(bi_s2, bi_r, 12)
    bi_copy.start()
    cols_own = own_o
    cols_got = got_o
    wo_s[own_o, :] = mm(a_own[...], gb[:, cols_got], TN).astype(BF16)
    wo_s[got_o, :] = mm(a_got[...], gb[:, cols_got], TN).astype(BF16)
    wo_copy = copy(wo_s, wo_r, 13)
    wo_copy.start()
    own_part = mm(a_own[...], gb[:, cols_own], TN)
    got_part = mm(a_got[...], gb[:, cols_own], TN)
    wo_copy.wait_recv()
    wo_g[own_o, :] = (own_part + wo_r[own_o, :].astype(F32)).astype(BF16)
    wo_g[got_o, :] = (got_part + wo_r[got_o, :].astype(F32)).astype(BF16)
    vec_copy.wait_recv()
    vec_o[...] = vec_s[...] + vec_r[...]
    bi_copy.wait_recv()
    bi_o[...] = jnp.zeros_like(bi_o)
    first_core = me == 0
    bi_o[0:2, :] = jnp.where(first_core, bi_s2[0:2, :], bi_r[0:2, :])
    bi_o[2:4, :] = jnp.where(first_core, bi_r[0:2, :], bi_s2[0:2, :])
    for a in outs_a:
        a.copy(0).wait_recv()
        a.add(0)

    def finish(t, carry):
        ga_copy(t).wait_recv()
        fl_copy(t).wait_send()
        feed_copy(t).wait_send()
        gf_copy(t).wait_send()
        part_copy(t).wait_send()
        ga_copy(t).wait_send()
        return carry

    lax.fori_loop(0, tiles, finish, 0)
    for a in outs_a:
        a.copy(0).wait_send()
    vec_copy.wait_send()
    bi_copy.wait_send()
    wo_copy.wait_send()


def middle(dp_size, a_own, a_got, x, gout, b_output, gain1, shift1, b_in, b_out, gain2, shift2, w_o, w_in, w_out):
    half, width = x.shape
    hw = width // 2
    ff = w_in.shape[1]
    nb = dp_size.bit_length() - 1
    n = width // dp_size
    part = (2,) * (nb - 1) + (n, ff // 3)
    vm = pl.BlockSpec(memory_space=pltpu.VMEM)
    hbm = pl.BlockSpec(memory_space=pl.ANY)
    V = pltpu.VMEM
    return pl.pallas_call(
        functools.partial(middle_body, dp_size),
        in_specs=[vm] * 11 + [hbm] * 3,
        out_specs=[vm] * 11,
        out_shape=[
            shape((half, width), BF16),
            shape((half, width), F32),
            shape((half, hw), BF16),
            shape((half, hw), BF16),
            shape(part, BF16),
            shape(part, BF16),
            shape(part, BF16),
            shape((width, ff), BF16),
            shape((width, hw), BF16),
            shape((8, width), F32),
            shape((8, width), F32),
        ],
        scratch_shapes=[
            V((2, half, width), BF16),
            V((half, width), BF16),
            V((half, width), BF16),
            V((2, half, width), BF16),
            V((half, width), BF16),
            V((half, width), BF16),
            V((half, hw), BF16),
            V((half, width), BF16),
            V((width, hw), BF16),
            V((width, hw), BF16),
            V((8, width), F32),
            V((8, width), F32),
            V((8, ff), F32),
            V((8, width), F32),
            V((8, width), F32),
            V((2,) * nb + (n, ff), BF16),
            V(part, BF16),
            V(part, BF16),
            V(part, BF16),
            V((width, width), BF16),
            V((width, ff), BF16),
            V((width, ff), BF16),
            V((2, half, ff), BF16),
            V((2, half, ff), BF16),
            V((2, half, ff), BF16),
            V((half, width), F32),
            V((half, width), F32),
            V((half, width), F32),
            V((half, width), F32),
            pltpu.SemaphoreType.DMA((3,)),
            pltpu.SemaphoreType.DMA((14,)),
            pltpu.SemaphoreType.DMA((14,)),
            pltpu.SemaphoreType.DMA((3 * nb,)),
            pltpu.SemaphoreType.DMA((3 * nb,)),
        ],
        compiler_params=pltpu.CompilerParams(
            vmem_limit_bytes=62 << 20, collective_id=1, has_side_effects=True
        ),
        cost_estimate=cost(17e9, 20e6),
        name="middle",
    )(a_own, a_got, x, gout, b_output, gain1, shift1, b_in, b_out, gain2, shift2, w_o, w_in, w_out)


PIECES = ("A1", "A2", "A3", "B1", "B2", "B3", "WO", "C0", "C1", "C2", "C3")


def piece_plan(dp_size, width, ff):
    x, y, z = bit_orders(dp_size)
    third, pw = ff // 3, 2 * HD
    return (
        (x, third), (y, third), (z, third), (x, third), (y, third), (z, third), (y, width // 2),
        (x, 3 * pw), (y, 3 * pw), (x, 2 * pw), (y, pw),
    )


def back_body(
    dp_size, xo, xt, q_i, k_i, v_i, p_i, ao, at, go, gt, gsum, vec, bi,
    wq, wk, wv, sa1, sa2, sa3, win, wo,
    ig_o, wq_o, wk_o, wv_o, wo_o, win_o, wout_o, vals_o, bi_o,
    g_s, gT, qT, dkT, dvT, dqkv, wcat, xT, acc, ig_s, ig_r, wsrc, gots, kepts,
    tb, tb_m, ts, trs, send, recv, lsem, vsend, vrecv, wsem,
):
    half, width = xo.shape
    rows = 2 * half
    pw = 2 * HD
    tile = 256
    p = pl.program_id(0)
    me = lax.axis_index("mp")
    dev = lax.axis_index("dp")
    nb = dp_size.bit_length() - 1
    sems = (send, recv, lsem)
    chunks = [slice(None)] * (nb + 1)
    third = sa1.shape[-1]

    def columns(ref, a, b):
        return ref.at[tuple(chunks + [slice(a, b)])]

    srcs = [sa1, sa2, sa3] + [columns(win, i * third, (i + 1) * third) for i in range(3)] + [wo]
    srcs += [wsrc.at[0], wsrc.at[1], columns(wsrc.at[2], 0, 2 * pw), columns(wsrc.at[2], 2 * pw, 3 * pw)]
    P = {}
    for i, (name, src) in enumerate(zip(PIECES, srcs)):
        bits = piece_plan(dp_size, width, win.shape[-1])[i][0]
        s0 = 1 if name[0] == "A" else 0
        P[name] = Piece(bits, sems, i * nb, src, gots[i], kepts[i], s0)
    from_hbm = PIECES[:7]
    ig_copy = partner_copy(ig_s, ig_r, vsend.at[0], vrecv.at[0], me)
    tb_copy = partner_copy(tb, tb_m, vsend.at[1], vrecv.at[1], me)
    t_copies = [
        pltpu.make_async_remote_copy(
            src_ref=ts[k], dst_ref=trs[k], send_sem=vsend.at[2 + k], recv_sem=vrecv.at[2 + k],
            device_id={"dp": P["C0"].peer(k)}, device_id_type=pl.DeviceIdType.MESH,
        )
        for k in range(nb)
    ]

    @pl.when(p == 0)
    def _():
        barrier = pltpu.get_barrier_semaphore()
        everyone = [{"mp": 1 - me}] + [{"dp": P["C0"].peer(k)} for k in range(nb)]
        for device in everyone:
            pl.semaphore_signal(
                barrier, inc=1, device_id=device, device_id_type=pl.DeviceIdType.MESH
            )
        for name in from_hbm:
            P[name].load_own().start()
        pl.semaphore_wait(barrier, len(everyone))
        for name in from_hbm:
            P[name].copy(P[name].stage0).start()
        xT[:, :half] = xo[...].T
        xT[:, half:] = xt[...].T
        tb[...] = jnp.zeros_like(tb)

    c_off = pl.multiple_of(me * (width // 2) + p * pw, pw)
    w_copies = [
        pltpu.make_async_copy(
            w.at[:, pl.ds(c_off, pw)], wcat.at[:, i * pw : (i + 1) * pw], wsem.at[i]
        )
        for i, w in enumerate((wq, wk, wv))
    ]
    for c in w_copies:
        c.start()
    g_s[:half, :] = go[...]
    g_s[half:, :] = gt[...]
    gT[...] = g_s[...].T
    qT[...] = q_i[...].T
    dkT[...] = jnp.zeros_like(dkT)
    dvT[...] = jnp.zeros_like(dvT)
    lane = lax.broadcasted_iota(jnp.int32, (tile, pw), 1)
    low = lane < HD

    def forward(k, *names):
        for name in names:
            x = P[name]
            loaded = name in from_hbm and k == x.stage0
            if loaded:
                x.load_own().wait()
            x.forward(k, loaded)

    def at_tile(t):
        if t == 3:

            @pl.when(p == 0)
            def _():
                forward(1, "A1", "A2")

            @pl.when(p == 1)
            def _():
                forward(1, "A3")
                forward(0, "B3")
                forward(2, "A1", "A2")

        if t == 1:

            @pl.when(p == 1)
            def _():
                forward(0, "B1", "B2")

            @pl.when(p == 2)
            def _():
                forward(1, "B1", "B2")
                forward(2, "A3")
                forward(0, "WO")

    for t in range(rows // tile):
        rs = slice(t * tile, (t + 1) * tile)
        a_ref = ao if t * tile < half else at
        as_ = slice(t * tile % half, t * tile % half + tile)
        g = g_s[rs, :]
        ga = g.astype(F32) * a_ref[as_, :].astype(F32)
        outs = []
        for h in range(2):
            mine = low if h == 0 else ~low
            hs = slice(h * HD, (h + 1) * HD)
            dp = mm(jnp.where(mine, g, BF16(0)), v_i[...], NT)
            delta = jnp.sum(jnp.where(mine, ga, 0.0), axis=-1, keepdims=True)
            pr = p_i[h, rs, :]
            ds = (pr.astype(F32) * (dp - delta)).astype(BF16)
            outs.append(mm(ds, k_i[...]))
            dvT[hs, :] += mm(gT[hs, rs], pr)
            dkT[hs, :] += mm(qT[hs, rs], ds)
        dq = jnp.where(low, outs[0], outs[1]) * HD**-0.5
        dqkv[rs, 0:pw] = dq.astype(BF16)

        at_tile(t)

    dqkv[:, pw : 2 * pw] = (dkT[...].T * HD**-0.5).astype(BF16)
    dqkv[:, 2 * pw : 3 * pw] = dvT[...].T.astype(BF16)
    d = dqkv[...]
    wg = mm(xT[...], d).astype(BF16).reshape(wsrc.shape[1:])
    wsrc[p] = wg
    tb[0:1, pl.ds(c_off, pw)] = jnp.sum(d[:, 0:pw].astype(F32), axis=0, keepdims=True)
    tb[1:2, pl.ds(c_off, pw)] = jnp.sum(d[:, 2 * pw :].astype(F32), axis=0, keepdims=True)

    @pl.when(p == 0)
    def _():
        P["C0"].copy(0).start()

    @pl.when(p == 1)
    def _():
        P["C1"].copy(0).start()

    @pl.when(p == 2)
    def _():
        P["C2"].copy(0).start()
        P["C3"].copy(0).start()
        tb_copy.start()

    for c in w_copies:
        c.wait()
    part = mm(d, wcat[...], NT)

    @pl.when(p == 0)
    def _():
        acc[...] = part

    @pl.when(p == 1)
    def _():
        acc[...] += part

    @pl.when(p == 2)
    def _():
        ig_s[...] = (acc[half:, :] + part[half:]).astype(BF16)
        ig_copy.start()
        acc[:half, :] += part[:half]

        def next_table(k):
            t_copies[k].wait_recv()
            ts[k + 1][...] = ts[k][...] + trs[k][...]
            if k + 1 < nb:
                t_copies[k + 1].start()

        forward(0, "C0")
        tb_copy.wait_recv()
        ts[0][0:8, :] = tb[...] + tb_m[...] + vec[...]
        ts[0][8:16, :] = bi[...]
        t_copies[0].start()
        forward(1, "B3")
        forward(2, "B1", "B2")
        forward(0, "C1")
        forward(1, "WO")
        next_table(0)
        forward(1, "C0")
        forward(0, "C2", "C3")
        ig_copy.wait_recv()
        ig_o[...] = gsum[...] + (acc[:half, :] + ig_r[...].astype(F32))
        next_table(1)
        forward(2, "B3")
        forward(1, "C1")
        forward(2, "WO", "C0")
        for k in range(2, nb - 1):
            next_table(k)
        forward(1, "C2", "C3")
        forward(2, "C1")
        for i in range(3):
            wout_o[:, i * third : (i + 1) * third] = P["A%d" % (i + 1)].result()
            win_o[:, i * third : (i + 1) * third] = P["B%d" % (i + 1)].result()
        forward(2, "C2", "C3")
        wo_o[...] = P["WO"].result()
        next_table(nb - 1)
        table = ts[nb][...]
        n = width // dp_size
        m = bi_o.shape[1]
        vals = table[0:8, 0:n]
        biv = table[8:9, 0:m]
        for j in range(1, dp_size):
            vals = jnp.where(dev == j, table[0:8, j * n : (j + 1) * n], vals)
            r = 8 + (j * m) // width
            k = (j * m) % width
            biv = jnp.where(dev == j, table[r : r + 1, k : k + m], biv)
        vals_o[...] = vals
        bi_o[...] = biv
        for j in range(3):
            cs = slice(j * pw, (j + 1) * pw)
            v = P["C%d" % j].result()
            wq_o[:, cs] = v[:, :pw]
            wk_o[:, cs] = v[:, pw : 2 * pw]
            wv_o[:, cs] = v[:, 2 * pw :] if j < 2 else P["C3"].result()

        for name in PIECES:
            P[name].drain()
        ig_copy.wait_send()
        tb_copy.wait_send()
        for c in t_copies:
            c.wait_send()


def back(dp_size, xo, xt, wq, wk, wv, q, k, v, probs, ao, at, go, gt, gsum, vec, bi, sa, win, wo):
    half, width = xo.shape
    rows = 2 * half
    pairs = HEADS // 4
    pw = 2 * HD
    ff = win.shape[1]
    nb = dp_size.bit_length() - 1
    n = width // dp_size
    split = lambda a: a.reshape((2,) * nb + (n, a.shape[-1]))
    whole = lambda a: pl.BlockSpec(
        a.shape, lambda p: (0,) * a.ndim, pipeline_mode=pl.Buffered(1)
    )
    col = lambda r, w: pl.BlockSpec((r, w), lambda p: (0, p))
    hbm = pl.BlockSpec(memory_space=pl.ANY)
    vm = pl.BlockSpec(memory_space=pltpu.VMEM)
    V = pltpu.VMEM
    plan = piece_plan(dp_size, width, ff)

    def stages(last):
        return tuple(
            tuple(
                V((2,) * (nb - 1 - k) + (n, w), BF16) if k < nb - last else V((16, 128), BF16)
                for k in range(nb)
            )
            for _, w in plan
        )

    table = lambda: V((16, width), F32)
    sem = pltpu.SemaphoreType.DMA
    return pl.pallas_call(
        functools.partial(back_body, dp_size),
        grid_spec=pltpu.PrefetchScalarGridSpec(
            num_scalar_prefetch=0,
            grid=(pairs,),
            in_specs=[whole(xo), whole(xt)]
            + [col(rows, pw)] * 3
            + [pl.BlockSpec((2, rows, rows), lambda p: (p, 0, 0))]
            + [col(half, pw)] * 4
            + [whole(gsum), whole(vec), whole(bi)]
            + [hbm] * 8,
            out_specs=[vm] * 9,
            scratch_shapes=[
                V((rows, pw), BF16),
                V((pw, rows), BF16),
                V((pw, rows), BF16),
                V((pw, rows), F32),
                V((pw, rows), F32),
                V((rows, 3 * pw), BF16),
                V((width, 3 * pw), BF16),
                V((width, rows), BF16),
                V((rows, width), F32),
                V((half, width), BF16),
                V((half, width), BF16),
                V((pairs,) + (2,) * nb + (n, 3 * pw), BF16),
                stages(0),
                stages(1),
                V((8, width), F32),
                V((8, width), F32),
                tuple(table() for _ in range(nb + 1)),
                tuple(table() for _ in range(nb)),
                sem((len(plan) * nb,)),
                sem((len(plan) * nb,)),
                sem((len(plan),)),
                sem((2 + nb,)),
                sem((2 + nb,)),
                sem((3,)),
            ],
        ),
        out_shape=[shape((half, width), F32)]
        + [shape((n, width // 2), F32)] * 4
        + [shape((n, ff), F32)] * 2
        + [shape((8, n), F32), shape((1, 2 * ff // dp_size), F32)],
        compiler_params=pltpu.CompilerParams(
            vmem_limit_bytes=60 << 20, collective_id=2, has_side_effects=True
        ),
        cost_estimate=cost(40e9, 20e6),
        name="back",
    )(xo, xt, q, k, v, probs, ao, at, go, gt, gsum, vec, bi, wq, wk, wv, *sa, split(win), split(wo))


def emit_body(big, *refs):
    ins, outs = refs[: big + 2], refs[big + 2 :]
    for i in range(big):
        outs[i][...] = ins[i][...]
    vals = ins[big][...]
    for j in range(8):
        outs[big + j][...] = vals[j]
    outs[big + 8][...] = ins[big + 1][0]


def emit(arrays, vals, bi):
    vm = pl.BlockSpec(memory_space=pltpu.VMEM)
    return pl.pallas_call(
        functools.partial(emit_body, len(arrays)),
        in_specs=[vm] * (len(arrays) + 2),
        out_specs=[vm] * (len(arrays) + 9),
        out_shape=[shape(a.shape, a.dtype) for a in arrays]
        + [shape((vals.shape[1],), F32)] * 8
        + [shape((bi.shape[1],), F32)],
        compiler_params=params(60),
        name="emit",
    )(*arrays, vals, bi)


def local_pair(
    dp_size, inputs, grad_out, lengths, rand_blocks, w_query, b_query, w_key, w_value, b_value,
    w_output, b_output, gain_one, shift_one, w_in, b_in, w_out, b_out, gain_two, shift_two,
):
    x = inputs[0]
    x_got, a_own, a_oth, a_got, q, k, v, probs = front(
        lengths, x, rand_blocks, b_query, b_value, w_query, w_key, w_value
    )
    out, gsum, ga0, ga_got, sa1, sa2, sa3, w_in_g, w_output_g, vec_g, bi_g = middle(
        dp_size, a_own, a_got, x, grad_out[0], b_output, gain_one, shift_one, b_in, b_out,
        gain_two, shift_two, w_output, w_in, w_out,
    )
    *mats, vals, bi = back(
        dp_size, x, x_got, w_query, w_key, w_value, q, k, v, probs, a_own, a_oth, ga0, ga_got,
        gsum, vec_g, bi_g, (sa1, sa2, sa3), w_in_g, w_output_g,
    )
    (
        out, input_grad, wq_p, wk_p, wv_p, wo_p, in_part, out_part, bq_p, bv_p, bo_p, g1_p, s1_p,
        b2_p, g2_p, s2_p, bi_p,
    ) = emit([out] + mats, vals, bi)
    return (
        out[None], input_grad[None], wq_p, bq_p, wk_p, wv_p, bv_p, wo_p, bo_p, g1_p, s1_p,
        in_part, bi_p, out_part, b2_p, g2_p, s2_p,
    )


def layer_norm(features, norm_gain, norm_shift):
    row_mean = jnp.mean(features, axis=-1, keepdims=True)
    centered = features - row_mean
    variance = jnp.mean(centered * centered, axis=-1, keepdims=True)
    return centered * lax.rsqrt(variance + norm_epsilon) * norm_gain + norm_shift


def gelu_tanh(features):
    return jax.nn.gelu(features, approximate=True)


def slot_table_ids(block_ids, rand_rows, length):
    valid_blocks = (length + BLK - 1) // BLK
    column = block_ids[:, None]
    columns = jnp.concatenate(
        [
            column - 1,
            column,
            column + 1,
            rand_rows,
            jnp.zeros_like(column),
            jnp.zeros_like(column) + valid_blocks - 1,
        ],
        axis=1,
    )
    in_range = (columns >= 0) & (columns < valid_blocks)
    slot_ids = jnp.arange(columns.shape[1], dtype=jnp.int32)
    earlier = slot_ids[None, :] < slot_ids[:, None]
    repeated = jnp.any(
        (columns[:, :, None] == columns[:, None, :]) & earlier[None, :, :] & in_range[:, None, :],
        axis=2,
    )
    return (jnp.clip(columns, 0, NB - 1), in_range & jnp.logical_not(repeated))


def slot_table(first_block, rand_rows, length):
    block_ids = first_block + jnp.arange(rand_rows.shape[0], dtype=jnp.int32)
    return slot_table_ids(block_ids, rand_rows, length)


def slot_mask(slot_blocks, slot_valid, length):
    positions = slot_blocks[:, :, None] * BLK + jnp.arange(BLK, dtype=jnp.int32)
    allowed = slot_valid[:, :, None] & (positions < length)
    return allowed.reshape(slot_blocks.shape[0], 1, 1, -1)


def gather_slots(whole_rows, slot_blocks):
    picked = whole_rows.reshape(NB, BLK, whole_rows.shape[1])[slot_blocks]
    return picked.reshape(slot_blocks.shape[0], slot_blocks.shape[1] * BLK, HEADS, HD)


def log_total(scores, allowed):
    masked = jnp.where(allowed, scores, negative_fill)
    top_score = jnp.max(masked, axis=-1, keepdims=True)
    return top_score + jnp.log(jnp.sum(jnp.exp(masked - top_score), axis=-1, keepdims=True))


def exp_probs(scores, allowed, totals):
    return jnp.exp(jnp.where(allowed, scores, negative_fill) - totals)


def global_targets(length, device, local_blocks):
    last_block = (length + BLK - 1) // BLK - 1
    targets = []
    for target_block in (jnp.zeros_like(last_block), last_block):
        is_owner = target_block // local_blocks == device
        local_block = jnp.clip(target_block - device * local_blocks, 0, local_blocks - 1)
        targets.append((is_owner, local_block))
    return targets


def global_scores(query_rows, key_one, length):
    scores = jnp.einsum(
        "qhd,khd->hqk",
        query_rows.reshape(BLK, HEADS, HD),
        key_one.reshape(-1, HEADS, HD),
        preferred_element_type=jnp.float32,
    ) * HD ** (-0.5)
    allowed = (jnp.arange(key_one.shape[0], dtype=jnp.int32) < length)[None, None, :]
    return (scores, allowed)


def global_forward(query_rows, key_one, value_one, length):
    scores, allowed = global_scores(query_rows, key_one, length)
    totals = log_total(scores, allowed)
    weighting = exp_probs(scores, allowed, totals).astype(jnp.bfloat16)
    out_rows = jnp.einsum(
        "hqk,khd->qhd",
        weighting,
        value_one.reshape(-1, HEADS, HD),
        preferred_element_type=jnp.float32,
    )
    return (out_rows.reshape(BLK, -1), totals)


def global_skip(query_rows, key_one, value_one, length):
    return (jnp.zeros((BLK, HEADS * HD), jnp.float32), jnp.zeros((HEADS, BLK, 1), jnp.float32))


def global_backward(query_rows, grad_rows, key_one, value_one, length, row_totals):
    score_scale = HD ** (-0.5)
    scores, allowed = global_scores(query_rows, key_one, length)
    exact_probs = exp_probs(scores, allowed, row_totals)
    grad_heads = grad_rows.reshape(BLK, HEADS, HD)
    grad_weights = jnp.einsum(
        "qhd,khd->hqk",
        grad_heads,
        value_one.reshape(-1, HEADS, HD),
        preferred_element_type=jnp.float32,
    )
    delta_sum = jnp.sum(exact_probs * grad_weights, axis=-1, keepdims=True)
    grad_scores = (exact_probs * (grad_weights - delta_sum)).astype(jnp.bfloat16)
    grad_query = (
        jnp.einsum(
            "hqk,khd->qhd",
            grad_scores,
            key_one.reshape(-1, HEADS, HD),
            preferred_element_type=jnp.float32,
        )
        * score_scale
    )
    grad_keys = (
        jnp.einsum(
            "hqk,qhd->khd",
            grad_scores,
            query_rows.reshape(BLK, HEADS, HD),
            preferred_element_type=jnp.float32,
        )
        * score_scale
    )
    grad_values = jnp.einsum(
        "hqk,qhd->khd",
        exact_probs.astype(jnp.bfloat16),
        grad_heads,
        preferred_element_type=jnp.float32,
    )
    return (
        grad_query.reshape(BLK, -1),
        grad_keys.reshape(key_one.shape[0], -1),
        grad_values.reshape(key_one.shape[0], -1),
    )


def global_back_skip(query_rows, grad_rows, key_one, value_one, length, row_totals):
    key_zeros = jnp.zeros(key_one.shape, jnp.float32)
    return (jnp.zeros((BLK, key_one.shape[1]), jnp.float32), key_zeros, key_zeros)


def attend_forward(query_one, key_one, value_one, length, rand_rows, device):
    local_blocks = rand_rows.shape[0]
    slot_blocks, slot_valid = slot_table(device * local_blocks, rand_rows, length)
    allowed = slot_mask(slot_blocks, slot_valid, length)
    query_blocks = query_one.reshape(local_blocks, BLK, HEADS, HD)
    scores = jnp.einsum(
        "nqhd,nkhd->nhqk",
        query_blocks,
        gather_slots(key_one, slot_blocks),
        preferred_element_type=jnp.float32,
    ) * HD ** (-0.5)
    totals = log_total(scores, allowed)
    weighting = exp_probs(scores, allowed, totals).astype(jnp.bfloat16)
    attended = jnp.einsum(
        "nhqk,nkhd->nqhd",
        weighting,
        gather_slots(value_one, slot_blocks),
        preferred_element_type=jnp.float32,
    ).reshape(query_one.shape[0], -1)
    global_totals = []
    for is_owner, local_block in global_targets(length, device, local_blocks):
        query_rows = lax.dynamic_slice_in_dim(query_one, local_block * BLK, BLK, 0)
        out_rows, row_totals = lax.cond(
            is_owner, global_forward, global_skip, query_rows, key_one, value_one, length
        )
        updated = lax.dynamic_update_slice_in_dim(attended, out_rows, local_block * BLK, 0)
        attended = jnp.where(is_owner, updated, attended)
        global_totals.append(row_totals)
    return (attended, totals, global_totals[0], global_totals[1])


def attend_backward(
    query_one,
    key_one,
    value_one,
    length,
    rand_rows,
    totals,
    first_totals,
    last_totals,
    grad_one,
    device,
):
    score_scale = HD ** (-0.5)
    local_blocks = rand_rows.shape[0]
    first_block = device * local_blocks
    slot_blocks, slot_valid = slot_table(first_block, rand_rows, length)
    allowed = slot_mask(slot_blocks, slot_valid, length)
    query_blocks = query_one.reshape(local_blocks, BLK, HEADS, HD)
    key_slots = gather_slots(key_one, slot_blocks)
    value_slots = gather_slots(value_one, slot_blocks)
    scores = (
        jnp.einsum("nqhd,nkhd->nhqk", query_blocks, key_slots, preferred_element_type=jnp.float32)
        * score_scale
    )
    exact_probs = exp_probs(scores, allowed, totals)
    last_block = (length + BLK - 1) // BLK - 1
    row_blocks = first_block + jnp.arange(query_one.shape[0], dtype=jnp.int32) // BLK
    is_global = (row_blocks == 0) | (row_blocks == last_block)
    grad_sparse = jnp.where(is_global[:, None], jnp.zeros_like(grad_one), grad_one)
    grad_heads = grad_sparse.reshape(local_blocks, BLK, HEADS, HD)
    grad_weights = jnp.einsum(
        "nqhd,nkhd->nhqk", grad_heads, value_slots, preferred_element_type=jnp.float32
    )
    delta_sum = jnp.sum(exact_probs * grad_weights, axis=-1, keepdims=True)
    grad_scores = (exact_probs * (grad_weights - delta_sum)).astype(jnp.bfloat16)
    grad_query = (
        jnp.einsum(
            "nhqk,nkhd->nqhd", grad_scores, key_slots, preferred_element_type=jnp.float32
        ).reshape(query_one.shape[0], -1)
        * score_scale
    )
    grad_key_slots = (
        jnp.einsum("nhqk,nqhd->nkhd", grad_scores, query_blocks, preferred_element_type=jnp.float32)
        * score_scale
    )
    grad_value_slots = jnp.einsum(
        "nhqk,nqhd->nkhd",
        exact_probs.astype(jnp.bfloat16),
        grad_heads,
        preferred_element_type=jnp.float32,
    )
    flat_ids = slot_blocks.reshape(-1)
    slot_width = BLK * query_one.shape[1]
    grad_keys = jax.ops.segment_sum(
        grad_key_slots.reshape(-1, slot_width), flat_ids, num_segments=NB
    ).reshape(-1, query_one.shape[1])
    grad_values = jax.ops.segment_sum(
        grad_value_slots.reshape(-1, slot_width), flat_ids, num_segments=NB
    ).reshape(-1, query_one.shape[1])
    for (is_owner, local_block), row_totals in zip(
        global_targets(length, device, local_blocks), (first_totals, last_totals)
    ):
        query_rows = lax.dynamic_slice_in_dim(query_one, local_block * BLK, BLK, 0)
        grad_rows = lax.dynamic_slice_in_dim(grad_one, local_block * BLK, BLK, 0)
        query_add, key_add, value_add = lax.cond(
            is_owner,
            global_backward,
            global_back_skip,
            query_rows,
            grad_rows,
            key_one,
            value_one,
            length,
            row_totals,
        )
        current = lax.dynamic_slice_in_dim(grad_query, local_block * BLK, BLK, 0)
        grad_query = lax.dynamic_update_slice_in_dim(
            grad_query, current + query_add, local_block * BLK, 0
        )
        grad_keys = grad_keys + key_add
        grad_values = grad_values + value_add
    return (grad_query, grad_keys, grad_values)


def local(
    inputs,
    grad_out,
    lengths,
    rand_blocks,
    w_query,
    b_query,
    w_key,
    w_value,
    b_value,
    w_output,
    b_output,
    gain_one,
    shift_one,
    w_in,
    b_in,
    w_out,
    b_out,
    gain_two,
    shift_two,
):
    device = lax.axis_index("mp")
    seq_count, local_rows, width = inputs.shape
    flat_in = inputs.reshape(-1, width)
    query = (jnp.dot(flat_in, w_query, preferred_element_type=jnp.float32) + b_query).astype(
        jnp.bfloat16
    )
    keys = jnp.dot(flat_in, w_key, preferred_element_type=jnp.float32).astype(jnp.bfloat16)
    values = (jnp.dot(flat_in, w_value, preferred_element_type=jnp.float32) + b_value).astype(
        jnp.bfloat16
    )
    key_all, value_all = (
        lax.all_gather(keys.reshape(seq_count, local_rows, width), "mp", axis=1, tiled=True),
        lax.all_gather(values.reshape(seq_count, local_rows, width), "mp", axis=1, tiled=True),
    )
    query_seq = query.reshape(seq_count, local_rows, width)

    def forward_item(seq_items):
        query_one, key_one, value_one, length, rand_rows = seq_items
        return attend_forward(query_one, key_one, value_one, length, rand_rows, device)

    attended, totals, first_totals, last_totals = lax.map(
        forward_item, (query_seq, key_all, value_all, lengths, rand_blocks)
    )
    attended_low = attended.reshape(-1, width).astype(jnp.bfloat16)
    summed_one = (
        flat_in.astype(jnp.float32)
        + jnp.dot(attended_low, w_output, preferred_element_type=jnp.float32)
        + b_output
    )
    first, norm_one_back = jax.vjp(
        layer_norm, summed_one, gain_one.astype(jnp.float32), shift_one.astype(jnp.float32)
    )
    first_low = first.astype(jnp.bfloat16)
    rows_all = lax.all_gather(first_low, "mp", axis=0, tiled=True)
    hidden = jnp.dot(rows_all, w_in, preferred_element_type=jnp.float32) + b_in
    active_full, gelu_back = jax.vjp(gelu_tanh, hidden)
    active = active_full.astype(jnp.bfloat16)
    feed = lax.psum_scatter(
        jnp.einsum(
            "rf,df->rd",
            lax.slice_in_dim(active, 0, first_low.shape[0] * lax.axis_size("mp"), axis=0),
            w_out,
            preferred_element_type=jnp.float32,
        ),
        "mp",
        scatter_dimension=0,
        tiled=True,
    )
    summed_two = first + feed + b_out
    output, norm_two_back = jax.vjp(
        layer_norm, summed_two, gain_two.astype(jnp.float32), shift_two.astype(jnp.float32)
    )
    grad_two, gain_two_grad, shift_two_grad = norm_two_back(
        grad_out.reshape(-1, width).astype(jnp.float32)
    )
    grad_feed = grad_two.astype(jnp.bfloat16)
    b_out_grad = jnp.sum(grad_feed, axis=0, dtype=jnp.float32)
    grads_all = lax.all_gather(grad_feed, "mp", axis=0, tiled=True)
    w_out_grad = jnp.einsum("rd,rf->df", grads_all, active, preferred_element_type=jnp.float32)
    grad_hidden = gelu_back(jnp.dot(grads_all, w_out, preferred_element_type=jnp.float32))[
        0
    ].astype(jnp.bfloat16)
    w_in_grad = jnp.einsum("rd,rf->df", rows_all, grad_hidden, preferred_element_type=jnp.float32)
    grad_first = grad_two + lax.psum_scatter(
        jnp.einsum(
            "rf,df->rd",
            lax.slice_in_dim(grad_hidden, 0, grad_feed.shape[0] * lax.axis_size("mp"), axis=0),
            w_in,
            preferred_element_type=jnp.float32,
        ),
        "mp",
        scatter_dimension=0,
        tiled=True,
    )
    b_in_grad = lax.dynamic_update_slice_in_dim(
        jnp.zeros((FF,), jnp.float32),
        jnp.sum(grad_hidden, axis=0, dtype=jnp.float32),
        device * w_in.shape[1],
        0,
    )
    grad_sum_one, gain_one_grad, shift_one_grad = norm_one_back(grad_first)
    grad_branch = grad_sum_one.astype(jnp.bfloat16)
    b_output_grad = jnp.sum(grad_branch, axis=0, dtype=jnp.float32)
    w_output_grad = jnp.einsum(
        "rd,re->de", attended_low, grad_branch, preferred_element_type=jnp.float32
    )
    grad_attended = (
        jnp.einsum("re,de->rd", grad_branch, w_output, preferred_element_type=jnp.float32)
        .astype(jnp.bfloat16)
        .reshape(seq_count, local_rows, width)
    )

    def backward_item(seq_items):
        (
            query_one,
            key_one,
            value_one,
            length,
            rand_rows,
            sparse_totals,
            first_one,
            last_one,
            grad_one,
        ) = seq_items
        return attend_backward(
            query_one,
            key_one,
            value_one,
            length,
            rand_rows,
            sparse_totals,
            first_one,
            last_one,
            grad_one,
            device,
        )

    grad_query, grad_keys, grad_values = lax.map(
        backward_item,
        (
            query_seq,
            key_all,
            value_all,
            lengths,
            rand_blocks,
            totals,
            first_totals,
            last_totals,
            grad_attended,
        ),
    )
    key_sums, value_sums = (
        lax.psum_scatter(
            grad_keys.astype(jnp.bfloat16), "mp", scatter_dimension=1, tiled=True
        ).astype(jnp.float32),
        lax.psum_scatter(
            grad_values.astype(jnp.bfloat16), "mp", scatter_dimension=1, tiled=True
        ).astype(jnp.float32),
    )
    grad_q_low = grad_query.reshape(-1, width).astype(jnp.bfloat16)
    grad_k_low = key_sums.reshape(-1, width).astype(jnp.bfloat16)
    grad_v_low = value_sums.reshape(-1, width).astype(jnp.bfloat16)
    input_grad = grad_sum_one + jnp.einsum(
        "re,de->rd", grad_q_low, w_query, preferred_element_type=jnp.float32
    )
    input_grad = input_grad + jnp.einsum(
        "re,de->rd", grad_k_low, w_key, preferred_element_type=jnp.float32
    )
    input_grad = input_grad + jnp.einsum(
        "re,de->rd", grad_v_low, w_value, preferred_element_type=jnp.float32
    )
    w_query_grad = jnp.einsum("rd,re->de", flat_in, grad_q_low, preferred_element_type=jnp.float32)
    w_key_grad = jnp.einsum("rd,re->de", flat_in, grad_k_low, preferred_element_type=jnp.float32)
    w_value_grad = jnp.einsum("rd,re->de", flat_in, grad_v_low, preferred_element_type=jnp.float32)
    b_query_grad = jnp.sum(grad_q_low, axis=0, dtype=jnp.float32)
    b_value_grad = jnp.sum(grad_v_low, axis=0, dtype=jnp.float32)
    reduced = (
        lax.psum_scatter(
            w_query_grad.astype(jnp.bfloat16), "dp", scatter_dimension=0, tiled=True
        ).astype(jnp.float32),
        lax.psum_scatter(
            w_key_grad.astype(jnp.bfloat16), "dp", scatter_dimension=0, tiled=True
        ).astype(jnp.float32),
        lax.psum_scatter(
            w_value_grad.astype(jnp.bfloat16), "dp", scatter_dimension=0, tiled=True
        ).astype(jnp.float32),
        lax.psum_scatter(
            w_output_grad.astype(jnp.bfloat16), "dp", scatter_dimension=0, tiled=True
        ).astype(jnp.float32),
        lax.psum_scatter(
            w_in_grad.astype(jnp.bfloat16), "dp", scatter_dimension=0, tiled=True
        ).astype(jnp.float32),
        lax.psum_scatter(
            w_out_grad.astype(jnp.bfloat16), "dp", scatter_dimension=0, tiled=True
        ).astype(jnp.float32),
        lax.psum_scatter(
            b_query_grad.astype(jnp.bfloat16), "dp", scatter_dimension=0, tiled=True
        ).astype(jnp.float32),
        lax.psum_scatter(
            b_value_grad.astype(jnp.bfloat16), "dp", scatter_dimension=0, tiled=True
        ).astype(jnp.float32),
        lax.psum_scatter(
            b_output_grad.astype(jnp.bfloat16), "dp", scatter_dimension=0, tiled=True
        ).astype(jnp.float32),
        lax.psum_scatter(
            gain_one_grad.astype(jnp.bfloat16), "dp", scatter_dimension=0, tiled=True
        ).astype(jnp.float32),
        lax.psum_scatter(
            shift_one_grad.astype(jnp.bfloat16), "dp", scatter_dimension=0, tiled=True
        ).astype(jnp.float32),
        lax.psum_scatter(
            b_in_grad.astype(jnp.bfloat16), "dp", scatter_dimension=0, tiled=True
        ).astype(jnp.float32),
        lax.psum_scatter(
            b_out_grad.astype(jnp.bfloat16), "dp", scatter_dimension=0, tiled=True
        ).astype(jnp.float32),
        lax.psum_scatter(
            gain_two_grad.astype(jnp.bfloat16), "dp", scatter_dimension=0, tiled=True
        ).astype(jnp.float32),
        lax.psum_scatter(
            shift_two_grad.astype(jnp.bfloat16), "dp", scatter_dimension=0, tiled=True
        ).astype(jnp.float32),
    )
    query_part, key_part_out, value_part, output_part = (
        lax.psum_scatter(
            reduced[0].astype(jnp.bfloat16), "mp", scatter_dimension=1, tiled=True
        ).astype(jnp.float32),
        lax.psum_scatter(
            reduced[1].astype(jnp.bfloat16), "mp", scatter_dimension=1, tiled=True
        ).astype(jnp.float32),
        lax.psum_scatter(
            reduced[2].astype(jnp.bfloat16), "mp", scatter_dimension=1, tiled=True
        ).astype(jnp.float32),
        lax.psum_scatter(
            reduced[3].astype(jnp.bfloat16), "mp", scatter_dimension=1, tiled=True
        ).astype(jnp.float32),
    )
    in_part = reduced[4]
    out_part = reduced[5]
    vectors = lax.psum(
        (
            reduced[6],
            reduced[7],
            reduced[8],
            reduced[9],
            reduced[10],
            reduced[11],
            reduced[12],
            reduced[13],
            reduced[14],
        ),
        "mp",
    )
    return (
        output.astype(jnp.bfloat16).reshape(seq_count, local_rows, width),
        input_grad.reshape(seq_count, local_rows, width),
        query_part,
        vectors[0],
        key_part_out,
        value_part,
        vectors[1],
        output_part,
        vectors[2],
        vectors[3],
        vectors[4],
        in_part,
        vectors[5],
        out_part,
        vectors[6],
        vectors[7],
        vectors[8],
    )


def solution(mesh):
    in_specs = (
        P("dp", "mp", None),
        P("dp", "mp", None),
        P("dp"),
        P("dp", "mp", None),
        P(),
        P(),
        P(),
        P(),
        P(),
        P(),
        P(),
        P(),
        P(),
        P(None, "mp"),
        P("mp"),
        P(None, "mp"),
        P(),
        P(),
        P(),
    )
    out_specs = (
        P("dp", "mp", None),
        P("dp", "mp", None),
        P("dp", "mp"),
        P("dp"),
        P("dp", "mp"),
        P("dp", "mp"),
        P("dp"),
        P("dp", "mp"),
        P("dp"),
        P("dp"),
        P("dp"),
        P("dp", "mp"),
        P("dp"),
        P("dp", "mp"),
        P("dp"),
        P("dp"),
        P("dp"),
    )
    sizes = dict(mesh.shape)
    if sizes["mp"] == 2 and sizes["dp"] == 16:
        local_fn = functools.partial(local_pair, sizes["dp"])
    else:
        local_fn = local
    return jax.shard_map(local_fn, mesh=mesh, in_specs=in_specs, out_specs=out_specs, check_vma=False)
```

```python
import functools

import jax
import jax.numpy as jnp
from jax import lax
from jax.experimental import pallas as pl
from jax.experimental.pallas import tpu as pltpu
from jax.sharding import PartitionSpec as P

HEADS = 12
HD = 64
FF = 3072
BLK = 64
NB = 16


negative_fill = -1000000000.0
norm_epsilon = 1e-12


F32 = jnp.float32
BF16 = jnp.bfloat16
NN = (((1,), (0,)), ((), ()))
NT = (((1,), (1,)), ((), ()))
TN = (((0,), (0,)), ((), ()))


def mm(a, b, dims=NN):
    return lax.dot_general(a, b, dims, preferred_element_type=F32)


def params(mib=56):
    return pltpu.CompilerParams(vmem_limit_bytes=mib << 20)


def cost(flops, nbytes, trans=0):
    return pl.CostEstimate(flops=int(flops), bytes_accessed=int(nbytes), transcendentals=int(trans))


def shape(dims, dtype):
    return jax.ShapeDtypeStruct(dims, dtype)


def row_stats(u):
    mean = jnp.mean(u, axis=-1, keepdims=True)
    cen = u - mean
    var = jnp.mean(cen * cen, axis=-1, keepdims=True)
    rs = lax.rsqrt(var + norm_epsilon)
    return cen * rs, rs


def partner_copy(src, dst, send, recv, me):
    return pltpu.make_async_remote_copy(
        src_ref=src, dst_ref=dst, send_sem=send, recv_sem=recv,
        device_id={"mp": 1 - me}, device_id_type=pl.DeviceIdType.MESH,
    )


def front_body(
    lengths, x, rand, bq, bv, wq, wk, wv,
    x_got, a_own, a_oth, a_got, q_o, k_o, v_o, p_h,
    xg_s, ag_s, p_s, w_s, b_s, rand_s, rand_r, bias, wsem, psem, send, recv,
):
    me = lax.axis_index("mp")
    p = pl.program_id(0)
    half, width = x.shape
    rows = 2 * half
    hw = width // 2
    pw = 2 * HD
    nb = rows // BLK
    tile = 256
    x_copy = partner_copy(x, xg_s, send.at[0], recv.at[0], me)
    rand_copy = partner_copy(rand_s, rand_r, send.at[1], recv.at[1], me)

    def w_loads(j):
        own = pl.ds(pl.multiple_of(me * hw + j * pw, pw), pw)
        return [
            pltpu.make_async_copy(
                w.at[:, own], w_s.at[j, :, i * pw : (i + 1) * pw], wsem.at[3 * j + i]
            )
            for i, w in enumerate((wq, wk, wv))
        ]

    slot = p % 2

    def p_store(slot_j, j, i):
        r0, h = units[i]
        return pltpu.make_async_copy(
            p_s.at[slot_j, h, r0 : r0 + tile], p_h.at[2 * j + h, r0 : r0 + tile],
            psem.at[slot_j, i],
        )

    order = [half + t * tile for t in range(half // tile)] + [t * tile for t in range(half // tile)]
    units = [(r0, h) for r0 in order for h in range(2)]

    @pl.when(p == 0)
    def _():
        barrier = pltpu.get_barrier_semaphore()
        pl.semaphore_signal(
            barrier, inc=1, device_id={"mp": 1 - me}, device_id_type=pl.DeviceIdType.MESH
        )
        for j in range(hw // pw):
            for c in w_loads(j):
                c.start()
        rand_s[...] = jnp.zeros_like(rand_s)
        for j in range(rand.shape[0]):
            rand_s[j : j + 1, : nb // 2] = rand[j]
        b_s[0:1, :] = bq[...].astype(F32)[None, :]
        b_s[1:2, :] = bv[...].astype(F32)[None, :]
        pl.semaphore_wait(barrier, 1)
        x_copy.start()
        rand_copy.start()

    cols = pl.ds(pl.multiple_of(p * pw, pw), pw)
    bias_cols = pl.ds(pl.multiple_of(me * hw + p * pw, pw), pw)

    for j in range(hw // pw):

        @pl.when(p == j)
        def _(j=j):
            for c in w_loads(j):
                c.wait()
            if j == 2:
                for i in range(len(units)):
                    p_store(0, 0, i).wait()

    def project(i, xr):
        rs = slice(i * half, (i + 1) * half)
        qkv = mm(xr[...], w_s[p])
        q_o[rs, :] = (qkv[:, :pw] + b_s[0:1, bias_cols]).astype(BF16)
        k_o[rs, :] = qkv[:, pw : 2 * pw].astype(BF16)
        v_o[rs, :] = (qkv[:, 2 * pw :] + b_s[1:2, bias_cols]).astype(BF16)

    project(0, x)

    @pl.when(p == 0)
    def _():
        rand_copy.wait_recv()
        ln = lengths[0]
        last = (ln + BLK - 1) // BLK - 1
        lb = lax.broadcasted_iota(jnp.int32, (nb, rows), 0)
        kp = lax.broadcasted_iota(jnp.int32, (nb, rows), 1)
        qb = jnp.where(lb < nb // 2, lb + (nb // 2) * me, lb - (nb // 2) * me)
        kpos = jnp.where(kp < half, kp + half * me, kp - half * me)
        kb = kpos // BLK
        ok = (jnp.abs(kb - qb) <= 1) | (kb == 0) | (kb == last)
        listed = [r[...].astype(F32).T[: nb // 2] for r in (rand_s, rand_r)]
        both = jnp.concatenate(listed, axis=0).astype(jnp.int32)
        for j in range(rand.shape[0]):
            ok = ok | (kb == both[:, j : j + 1])
        ok = ok | (qb == 0) | (qb == last)
        ok = ok & (kpos < ln)
        table = jnp.where(ok, 0.0, -1e30).astype(F32)
        for b in range(nb):
            bias[b] = jnp.broadcast_to(table[b : b + 1, :], (8, rows))
        x_copy.wait_recv()
        x_got[...] = xg_s[...]

    project(1, xg_s)

    low = lax.broadcasted_iota(jnp.int32, (tile, pw), 1) < HD
    scores, probs, outs = {}, {}, {}

    def score(i):
        r0, h = units[i]
        q = q_o[r0 : r0 + tile, :] * BF16(HD**-0.5)
        s = mm(jnp.where(low if h == 0 else ~low, q, BF16(0)), k_o[...], NT)
        b0 = r0 // BLK
        s = s.reshape(tile // BLK, BLK // 8, 8, rows) + bias[b0 : b0 + tile // BLK][:, None]
        scores[i] = s.reshape(tile, rows)

    def attend(i):
        r0, h = units[i]
        outs[i] = mm(probs.pop(i), v_o[...])
        if h == 1:
            a = jnp.where(low, outs.pop(i - 1), outs.pop(i)).astype(BF16)
            if r0 < half:
                a_own[r0 : r0 + tile, cols] = a
            else:
                a_oth[r0 - half : r0 - half + tile, cols] = a
                if r0 + tile == rows:
                    partner_copy(
                        a_oth.at[:, cols], ag_s.at[:, cols], send.at[2 + p], recv.at[2 + p], me
                    ).start()

    score(0)
    for i, (r0, h) in enumerate(units):
        if i + 1 < len(units):
            score(i + 1)
        s = scores.pop(i)
        e = jnp.exp(s - jnp.max(s, axis=-1, keepdims=True))
        pr = (e * (1.0 / jnp.sum(e, axis=-1, keepdims=True))).astype(BF16)
        p_s[slot, h, r0 : r0 + tile, :] = pr
        p_store(slot, p, i).start()
        probs[i] = pr
        if i >= 1:
            attend(i - 1)
    attend(len(units) - 1)

    @pl.when(p == pl.num_programs(0) - 1)
    def _():
        x_copy.wait_send()
        rand_copy.wait_send()
        for j in range(hw // pw):
            cs = slice(j * pw, (j + 1) * pw)
            c = partner_copy(a_oth.at[:, cs], ag_s.at[:, cs], send.at[2 + j], recv.at[2 + j], me)
            c.wait_send()
            c.wait_recv()
        a_got[...] = ag_s[...]
        for j in range(1, hw // pw):
            for i in range(len(units)):
                p_store(j % 2, j, i).wait()


def front(lengths, x, rand, bq, bv, wq, wk, wv):
    half, width = x.shape
    rows = 2 * half
    pairs = HEADS // 4
    pw = 2 * HD
    hw = width // 2
    vm = pl.BlockSpec(memory_space=pltpu.VMEM)
    hbm = pl.BlockSpec(memory_space=pl.ANY)
    col = pl.BlockSpec((rows, pw), lambda p: (0, p))
    V = pltpu.VMEM
    sem = pltpu.SemaphoreType.DMA
    return pl.pallas_call(
        front_body,
        grid_spec=pltpu.PrefetchScalarGridSpec(
            num_scalar_prefetch=0,
            grid=(pairs,),
            in_specs=[pl.BlockSpec(memory_space=pltpu.SMEM)] + [vm] * 4 + [hbm] * 3,
            out_specs=[vm] * 4 + [col] * 3 + [hbm],
            scratch_shapes=[
                V((half, width), BF16),
                V((half, hw), BF16),
                V((2, 2, rows, rows), BF16),
                V((pairs, width, 3 * pw), BF16),
                V((8, width), F32),
                V((8, 128), jnp.int32),
                V((8, 128), jnp.int32),
                V((rows // BLK, 8, rows), F32),
                sem((3 * pairs,)),
                sem((2, 8)),
                sem((2 + pairs,)),
                sem((2 + pairs,)),
            ],
        ),
        out_shape=[shape((half, width), BF16)]
        + [shape((half, hw), BF16)] * 3
        + [shape((rows, hw), BF16)] * 3
        + [shape((2 * pairs, rows, rows), BF16)],
        compiler_params=pltpu.CompilerParams(
            vmem_limit_bytes=60 << 20, collective_id=3, has_side_effects=True
        ),
        cost_estimate=cost(20e9, 20e6, 6 * rows * rows),
        name="front",
    )(lengths, x, rand, bq, bv, wq, wk, wv)


class Piece:
    def __init__(self, bits, sems, base, src, got, kept, stage0=0):
        self.bits = bits
        self.send, self.recv, self.load = sems
        self.base = base
        self.src, self.got, self.kept = src, got, kept
        self.stage0 = stage0
        self.dev = lax.axis_index("dp")

    def mine(self, k):
        return (self.dev // 2 ** self.bits[k]) % 2

    def peer(self, k):
        return self.dev + 2 ** self.bits[k] * (1 - 2 * self.mine(k))

    def side(self, k, bit, lead=None):
        left = sorted(self.bits[k:], reverse=True)
        where = left.index(self.bits[k])
        idx = [slice(None)] * len(left) if lead is None else list(lead[:where]) + [None] + list(lead[where:])
        idx[where] = bit
        return tuple(idx)

    def source(self, k):
        return self.src if k == self.stage0 else self.kept[k - 1]

    def copy(self, k):
        i = self.base + k
        return pltpu.make_async_remote_copy(
            src_ref=self.source(k).at[self.side(k, 1 - self.mine(k))], dst_ref=self.got[k],
            send_sem=self.send.at[i], recv_sem=self.recv.at[i],
            device_id={"dp": self.peer(k)}, device_id_type=pl.DeviceIdType.MESH,
        )

    def load_own(self):
        k = self.stage0
        return pltpu.make_async_copy(
            self.src.at[self.side(k, self.mine(k))], self.kept[k], self.load.at[self.base // len(self.bits)]
        )

    def total(self, k, lead, loaded):
        if loaded:
            own = self.kept[k][lead]
        else:
            own = self.source(k)[self.side(k, self.mine(k), lead)]
        return own.astype(F32) + self.got[k][lead].astype(F32)

    def add(self, k, loaded=False):
        free = len(self.bits) - 1 - k

        def step(i, carry):
            lead = tuple((i // 2 ** (free - 1 - j)) % 2 for j in range(free))
            self.kept[k][lead] = self.total(k, lead, loaded).astype(BF16)
            return carry

        lax.fori_loop(0, 2**free, step, 0)

    def forward(self, k, loaded=False):
        self.copy(k).wait_recv()
        self.add(k, loaded)
        self.copy(k + 1).start()

    def result(self):
        k = len(self.bits) - 1
        self.copy(k).wait_recv()
        return self.total(k, (), False)

    def drain(self):
        for k in range(self.stage0, len(self.bits)):
            self.copy(k).wait_send()


def bit_orders(dp_size):
    nb = dp_size.bit_length() - 1
    rest = list(range(2, nb))
    return [0, 1] + rest, [1, 0] + rest, rest + [0, 1]


def gelu_and_slope(v):
    k0 = 0.7978845608028654
    k1 = 0.044715
    v2 = v * v
    t = jnp.tanh(v * (k0 + (k0 * k1) * v2))
    hp = 0.5 * t + 0.5
    return v * hp, hp + (0.5 * v) * (1.0 - t * t) * (k0 + (3 * k0 * k1) * v2)


def norm_back(e, n, rs, gain):
    eg = e * gain
    return (eg - jnp.mean(eg, -1, keepdims=True) - n * jnp.mean(eg * n, -1, keepdims=True)) * rs


def middle_body(
    dp_size, a_own, a_got, x, gout, b_output, gain1, shift1, b_in, b_out, gain2, shift2,
    w_o_h, w_in_h, w_out_h,
    out_h, gsum_h, ga_o, gat_o, sa1, sa2, sa3, win_h, wo_g, vec_o, bi_o,
    out_o, gsum_o, win_g,
    fl, feed_s, feed_g, gf, part_s, part_g, gat_s, gb, wo_s, wo_r, vec_s, vec_r, bi_s, bi_s2, bi_r, wout_g, got_a1, got_a2, got_a3,
    w_o, w_in, w_out, act, slope, gh, u_s, first_s, own_s, gtwo_s,
    load_sem, store_sem, send_sem, recv_sem, a_send_sem, a_recv_sem,
):
    me = lax.axis_index("mp")
    half, width = x.shape
    hw = width // 2
    tile = 256
    tiles = half // tile
    cut = sa1.shape[-1]
    nb = dp_size.bit_length() - 1
    sems = (a_send_sem, a_recv_sem, None)
    chunks = [slice(None)] * (nb + 1)
    outs_a = [
        Piece(
            bits, sems, i * nb, wout_g.at[tuple(chunks + [slice(i * cut, (i + 1) * cut)])],
            (g,), (s,),
        )
        for i, (bits, g, s) in enumerate(
            zip(bit_orders(dp_size), (got_a1, got_a2, got_a3), (sa1, sa2, sa3))
        )
    ]
    barrier = pltpu.get_barrier_semaphore()
    for device in [{"mp": 1 - me}] + [{"dp": a.peer(0)} for a in outs_a]:
        pl.semaphore_signal(barrier, inc=1, device_id=device, device_id_type=pl.DeviceIdType.MESH)
    stores = [
        pltpu.make_async_copy(src, dst, store_sem.at[i])
        for i, (src, dst) in enumerate(((out_o, out_h), (win_g, win_h), (gsum_o, gsum_h)))
    ]
    loads = []
    for i, (src, dst) in enumerate(((w_o_h, w_o), (w_in_h, w_in), (w_out_h, w_out))):
        loads.append(pltpu.make_async_copy(src, dst, load_sem.at[i]))
        loads[-1].start()
    pl.semaphore_wait(barrier, 4)

    def copy(src, dst, i):
        return partner_copy(src, dst, send_sem.at[i], recv_sem.at[i], me)

    loads[0].wait()

    def rows(t):
        return pl.ds(pl.multiple_of(t * tile, tile), tile)

    def fl_copy(t):
        return copy(fl.at[0, rows(t)], fl.at[1, rows(t)], 1 + t)

    def feed_copy(t):
        return copy(feed_s.at[rows(t)], feed_g.at[rows(t)], 3 + t)

    def gf_copy(t):
        return copy(gf.at[0, rows(t)], gf.at[1, rows(t)], 5 + t)

    def part_copy(t):
        return copy(part_s.at[rows(t)], part_g.at[rows(t)], 7 + t)

    def ga_copy(t):
        return copy(gat_s.at[rows(t)], gat_o.at[rows(t)], 9 + t)

    own_o = pl.ds(pl.multiple_of(me * hw, hw), hw)
    got_o = pl.ds(pl.multiple_of((1 - me) * hw, hw), hw)

    def project(t, carry):
        r = rows(t)
        u = x[r, :].astype(F32) + (
            mm(a_own[r, :], w_o[own_o, :]) + mm(a_got[r, :], w_o[got_o, :])
        ) + b_output[...].astype(F32)[None, :]
        n, _ = row_stats(u)
        first = n * gain1[...].astype(F32)[None, :] + shift1[...].astype(F32)[None, :]
        u_s[r, :] = u
        first_s[r, :] = first
        fl[0, r, :] = first.astype(BF16)
        fl_copy(t).start()
        return carry

    lax.fori_loop(0, tiles, project, 0)
    loads[1].wait()
    loads[2].wait()

    def feed_forward(i, t):
        r = rows(t)
        v = mm(fl[i, r, :], w_in[...]) + b_in[...].astype(F32)[None, :]
        a, s = gelu_and_slope(v)
        a = a.astype(BF16)
        act[i, r, :] = a
        slope[i, r, :] = s.astype(BF16)
        return mm(a, w_out[...], NT)

    def forward_own(t, carry):
        own_s[rows(t), :] = feed_forward(0, t)
        return carry

    def forward_got(t, carry):
        fl_copy(t).wait_recv()
        feed_s[rows(t), :] = feed_forward(1, t).astype(BF16)
        feed_copy(t).start()
        return carry

    lax.fori_loop(0, tiles, forward_own, 0)
    lax.fori_loop(0, tiles, forward_got, 0)

    vec_s[...] = jnp.zeros_like(vec_s)

    def add_vec(i, value):
        vec_s[i : i + 1, :] += jnp.sum(value, 0, keepdims=True)

    def second_norm(t, carry):
        r = rows(t)
        feed_copy(t).wait_recv()
        u = first_s[r, :] + (own_s[r, :] + feed_g[r, :].astype(F32)) + b_out[...].astype(F32)[None, :]
        n, rs = row_stats(u)
        gain = gain2[...].astype(F32)[None, :]
        out_o[r, :] = (n * gain + shift2[...].astype(F32)[None, :]).astype(BF16)
        e = gout[r, :].astype(F32)
        d = norm_back(e, n, rs, gain)
        low = d.astype(BF16)
        gtwo_s[r, :] = d
        gf[0, r, :] = low
        gf_copy(t).start()
        add_vec(6, e * n)
        add_vec(7, e)
        add_vec(5, low.astype(F32))
        return carry

    lax.fori_loop(0, tiles, second_norm, 0)
    stores[0].start()
    bi_s[...] = jnp.zeros_like(bi_s)

    def feed_back(i, t):
        r = rows(t)
        g = (mm(gf[i, r, :], w_out[...]) * slope[i, r, :].astype(F32)).astype(BF16)
        gh[i, r, :] = g
        bi_s[0:1, :] += jnp.sum(g.astype(F32), 0, keepdims=True)
        return mm(g, w_in[...], NT)

    def back_own(t, carry):
        own_s[rows(t), :] = feed_back(0, t)
        return carry

    def wait_gf(t, carry):
        gf_copy(t).wait_recv()
        return carry

    def back_got(t, carry):
        part_s[rows(t), :] = feed_back(1, t).astype(BF16)
        part_copy(t).start()
        return carry

    lax.fori_loop(0, tiles, back_own, 0)
    lax.fori_loop(0, tiles, wait_gf, 0)

    def out_weights(j, carry):
        c = pl.ds(pl.multiple_of(j * hw, hw), hw)
        total = mm(gf[0, :, c], act[0], TN) + mm(gf[1, :, c], act[1], TN)
        wout_g[j] = total.astype(BF16).reshape(wout_g.shape[1:])
        return carry

    lax.fori_loop(0, 2, out_weights, 0)
    for a in outs_a:
        a.copy(0).start()
    lax.fori_loop(0, tiles, back_got, 0)

    def weights(out, lhs, rhs):
        def step(j, carry):
            c = pl.ds(pl.multiple_of(j * tile, tile), tile)
            out[c, :] = (
                mm(lhs[0, :, c], rhs[0], TN) + mm(lhs[1, :, c], rhs[1], TN)
            ).astype(BF16)
            return carry

        lax.fori_loop(0, width // tile, step, 0)

    weights(win_g, fl, gh)
    stores[1].start()

    def first_norm(t, carry):
        r = rows(t)
        part_copy(t).wait_recv()
        e = gtwo_s[r, :] + own_s[r, :] + part_g[r, :].astype(F32)
        n, rs = row_stats(u_s[r, :])
        d = norm_back(e, n, rs, gain1[...].astype(F32)[None, :])
        low = d.astype(BF16)
        gsum_o[r, :] = d
        gb[r, :] = low
        gat_s[r, :] = mm(low, w_o[got_o, :], NT).astype(BF16)
        ga_copy(t).start()
        ga_o[r, :] = mm(low, w_o[own_o, :], NT).astype(BF16)
        add_vec(3, e * n)
        add_vec(4, e)
        add_vec(2, low.astype(F32))
        return carry

    lax.fori_loop(0, tiles, first_norm, 0)
    stores[2].start()
    vec_copy = copy(vec_s, vec_r, 11)
    vec_copy.start()
    bi_s2[0:1, :] = bi_s[0:1, :width]
    bi_s2[1:2, :] = bi_s[0:1, width:]
    bi_copy = copy(bi_s2, bi_r, 12)
    bi_copy.start()
    cols_own = own_o
    cols_got = got_o
    wo_s[own_o, :] = mm(a_own[...], gb[:, cols_got], TN).astype(BF16)
    wo_s[got_o, :] = mm(a_got[...], gb[:, cols_got], TN).astype(BF16)
    wo_copy = copy(wo_s, wo_r, 13)
    wo_copy.start()
    own_part = mm(a_own[...], gb[:, cols_own], TN)
    got_part = mm(a_got[...], gb[:, cols_own], TN)
    wo_copy.wait_recv()
    wo_g[own_o, :] = (own_part + wo_r[own_o, :].astype(F32)).astype(BF16)
    wo_g[got_o, :] = (got_part + wo_r[got_o, :].astype(F32)).astype(BF16)
    vec_copy.wait_recv()
    vec_o[...] = vec_s[...] + vec_r[...]
    bi_copy.wait_recv()
    bi_o[...] = jnp.zeros_like(bi_o)
    first_core = me == 0
    bi_o[0:2, :] = jnp.where(first_core, bi_s2[0:2, :], bi_r[0:2, :])
    bi_o[2:4, :] = jnp.where(first_core, bi_r[0:2, :], bi_s2[0:2, :])
    for a in outs_a:
        a.copy(0).wait_recv()
        a.add(0)

    def finish(t, carry):
        ga_copy(t).wait_recv()
        fl_copy(t).wait_send()
        feed_copy(t).wait_send()
        gf_copy(t).wait_send()
        part_copy(t).wait_send()
        ga_copy(t).wait_send()
        return carry

    lax.fori_loop(0, tiles, finish, 0)
    for c in stores:
        c.wait()
    for a in outs_a:
        a.copy(0).wait_send()
    vec_copy.wait_send()
    bi_copy.wait_send()
    wo_copy.wait_send()


def middle(dp_size, a_own, a_got, x, gout, b_output, gain1, shift1, b_in, b_out, gain2, shift2, w_o, w_in, w_out):
    half, width = x.shape
    hw = width // 2
    ff = w_in.shape[1]
    nb = dp_size.bit_length() - 1
    n = width // dp_size
    part = (2,) * (nb - 1) + (n, ff // 3)
    vm = pl.BlockSpec(memory_space=pltpu.VMEM)
    hbm = pl.BlockSpec(memory_space=pl.ANY)
    V = pltpu.VMEM
    return pl.pallas_call(
        functools.partial(middle_body, dp_size),
        in_specs=[vm] * 11 + [hbm] * 3,
        out_specs=[hbm] * 2 + [vm] * 5 + [hbm] + [vm] * 3,
        out_shape=[
            shape((half, width), BF16),
            shape((half, width), F32),
            shape((half, hw), BF16),
            shape((half, hw), BF16),
            shape(part, BF16),
            shape(part, BF16),
            shape(part, BF16),
            shape((width, ff), BF16),
            shape((width, hw), BF16),
            shape((8, width), F32),
            shape((8, width), F32),
        ],
        scratch_shapes=[
            V((half, width), BF16),
            V((half, width), F32),
            V((width, ff), BF16),
            V((2, half, width), BF16),
            V((half, width), BF16),
            V((half, width), BF16),
            V((2, half, width), BF16),
            V((half, width), BF16),
            V((half, width), BF16),
            V((half, hw), BF16),
            V((half, width), BF16),
            V((width, hw), BF16),
            V((width, hw), BF16),
            V((8, width), F32),
            V((8, width), F32),
            V((8, ff), F32),
            V((8, width), F32),
            V((8, width), F32),
            V((2,) * nb + (n, ff), BF16),
            V(part, BF16),
            V(part, BF16),
            V(part, BF16),
            V((width, width), BF16),
            V((width, ff), BF16),
            V((width, ff), BF16),
            V((2, half, ff), BF16),
            V((2, half, ff), BF16),
            V((2, half, ff), BF16),
            V((half, width), F32),
            V((half, width), F32),
            V((half, width), F32),
            V((half, width), F32),
            pltpu.SemaphoreType.DMA((3,)),
            pltpu.SemaphoreType.DMA((3,)),
            pltpu.SemaphoreType.DMA((14,)),
            pltpu.SemaphoreType.DMA((14,)),
            pltpu.SemaphoreType.DMA((3 * nb,)),
            pltpu.SemaphoreType.DMA((3 * nb,)),
        ],
        compiler_params=pltpu.CompilerParams(
            vmem_limit_bytes=62 << 20, collective_id=1, has_side_effects=True
        ),
        cost_estimate=cost(17e9, 20e6),
        name="middle",
    )(a_own, a_got, x, gout, b_output, gain1, shift1, b_in, b_out, gain2, shift2, w_o, w_in, w_out)


PIECES = ("A1", "A2", "A3", "B1", "B2", "B3", "WO", "C0", "C1", "C2", "C3")


def piece_plan(dp_size, width, ff):
    x, y, z = bit_orders(dp_size)
    third, pw = ff // 3, 2 * HD
    return (
        (x, third), (y, third), (z, third), (x, third), (y, third), (z, third), (y, width // 2),
        (x, 3 * pw), (y, 3 * pw), (x, 2 * pw), (y, pw),
    )


def back_body(
    dp_size, q_i, k_i, v_i, ao, at, go, gt, vec, bi,
    xo_h, xt_h, p_h, gsum_h, wq, wk, wv, sa1, sa2, sa3, win, wo,
    ig_o, wq_o, wk_o, wv_o, wo_o, win_o, wout_o, vals_o, bi_o,
    xo, xt, p_s, gsum, g_s, gT, qT, dkT, dvT, dqkv, wcat, xT, acc, ig_s, ig_r, wsrc, gots, kepts,
    tb, tb_m, ts, trs, send, recv, lsem, vsend, vrecv, wsem,
):
    half, width = ig_o.shape
    rows = 2 * half
    pw = 2 * HD
    tile = 256
    p = pl.program_id(0)
    me = lax.axis_index("mp")
    dev = lax.axis_index("dp")
    nb = dp_size.bit_length() - 1
    sems = (send, recv, lsem)
    chunks = [slice(None)] * (nb + 1)
    third = sa1.shape[-1]

    def columns(ref, a, b):
        return ref.at[tuple(chunks + [slice(a, b)])]

    srcs = [sa1, sa2, sa3] + [columns(win, i * third, (i + 1) * third) for i in range(3)] + [wo]
    srcs += [wsrc.at[0], wsrc.at[1], columns(wsrc.at[2], 0, 2 * pw), columns(wsrc.at[2], 2 * pw, 3 * pw)]
    P = {}
    for i, (name, src) in enumerate(zip(PIECES, srcs)):
        bits = piece_plan(dp_size, width, win.shape[-1])[i][0]
        s0 = 1 if name[0] == "A" else 0
        P[name] = Piece(bits, sems, i * nb, src, gots[i], kepts[i], s0)
    from_hbm = PIECES[:7]
    x_loads = [
        pltpu.make_async_copy(s, d, wsem.at[5 + i])
        for i, (s, d) in enumerate(((xo_h, xo), (xt_h, xt), (gsum_h, gsum)))
    ]

    def p_load(j):
        return pltpu.make_async_copy(p_h.at[2 * j : 2 * j + 2], p_s.at[j % 2], wsem.at[3 + j % 2])

    ig_copy = partner_copy(ig_s, ig_r, vsend.at[0], vrecv.at[0], me)
    tb_copy = partner_copy(tb, tb_m, vsend.at[1], vrecv.at[1], me)
    t_copies = [
        pltpu.make_async_remote_copy(
            src_ref=ts[k], dst_ref=trs[k], send_sem=vsend.at[2 + k], recv_sem=vrecv.at[2 + k],
            device_id={"dp": P["C0"].peer(k)}, device_id_type=pl.DeviceIdType.MESH,
        )
        for k in range(nb)
    ]

    @pl.when(p == 0)
    def _():
        barrier = pltpu.get_barrier_semaphore()
        everyone = [{"mp": 1 - me}] + [{"dp": P["C0"].peer(k)} for k in range(nb)]
        for device in everyone:
            pl.semaphore_signal(
                barrier, inc=1, device_id=device, device_id_type=pl.DeviceIdType.MESH
            )
        for name in from_hbm:
            P[name].load_own().start()
        pl.semaphore_wait(barrier, len(everyone))
        for name in from_hbm:
            P[name].copy(P[name].stage0).start()
        for c in x_loads[:2]:
            c.start()
        p_load(0).start()
        p_load(1).start()
        x_loads[2].start()
        for c in x_loads[:2]:
            c.wait()
        xT[:, :half] = xo[...].T
        xT[:, half:] = xt[...].T
        tb[...] = jnp.zeros_like(tb)

    for j in range(HEADS // 4):

        @pl.when(p == j)
        def _(j=j):
            if j == 1:
                p_load(2).start()
            p_load(j).wait()

    slot = p % 2
    c_off = pl.multiple_of(me * (width // 2) + p * pw, pw)
    w_copies = [
        pltpu.make_async_copy(
            w.at[:, pl.ds(c_off, pw)], wcat.at[:, i * pw : (i + 1) * pw], wsem.at[i]
        )
        for i, w in enumerate((wq, wk, wv))
    ]
    for c in w_copies:
        c.start()
    g_s[:half, :] = go[...]
    g_s[half:, :] = gt[...]
    gT[...] = g_s[...].T
    qT[...] = q_i[...].T
    dkT[...] = jnp.zeros_like(dkT)
    dvT[...] = jnp.zeros_like(dvT)
    lane = lax.broadcasted_iota(jnp.int32, (tile, pw), 1)
    low = lane < HD

    def forward(k, *names):
        for name in names:
            x = P[name]
            loaded = name in from_hbm and k == x.stage0
            if loaded:
                x.load_own().wait()
            x.forward(k, loaded)

    def at_tile(t):
        if t == 3:

            @pl.when(p == 0)
            def _():
                forward(1, "A1", "A2")

            @pl.when(p == 1)
            def _():
                forward(1, "A3")
                forward(0, "B3")
                forward(2, "A1", "A2")

        if t == 1:

            @pl.when(p == 1)
            def _():
                forward(0, "B1", "B2")

            @pl.when(p == 2)
            def _():
                forward(1, "B1", "B2")
                forward(2, "A3")
                forward(0, "WO")

    for t in range(rows // tile):
        rs = slice(t * tile, (t + 1) * tile)
        a_ref = ao if t * tile < half else at
        as_ = slice(t * tile % half, t * tile % half + tile)
        g = g_s[rs, :]
        ga = g.astype(F32) * a_ref[as_, :].astype(F32)
        outs = []
        for h in range(2):
            mine = low if h == 0 else ~low
            hs = slice(h * HD, (h + 1) * HD)
            dp = mm(jnp.where(mine, g, BF16(0)), v_i[...], NT)
            delta = jnp.sum(jnp.where(mine, ga, 0.0), axis=-1, keepdims=True)
            pr = p_s[slot, h, rs, :]
            ds = (pr.astype(F32) * (dp - delta)).astype(BF16)
            outs.append(mm(ds, k_i[...]))
            dvT[hs, :] += mm(gT[hs, rs], pr)
            dkT[hs, :] += mm(qT[hs, rs], ds)
        dq = jnp.where(low, outs[0], outs[1]) * HD**-0.5
        dqkv[rs, 0:pw] = dq.astype(BF16)

        at_tile(t)

    dqkv[:, pw : 2 * pw] = (dkT[...].T * HD**-0.5).astype(BF16)
    dqkv[:, 2 * pw : 3 * pw] = dvT[...].T.astype(BF16)
    d = dqkv[...]
    wg = mm(xT[...], d).astype(BF16).reshape(wsrc.shape[1:])
    wsrc[p] = wg
    tb[0:1, pl.ds(c_off, pw)] = jnp.sum(d[:, 0:pw].astype(F32), axis=0, keepdims=True)
    tb[1:2, pl.ds(c_off, pw)] = jnp.sum(d[:, 2 * pw :].astype(F32), axis=0, keepdims=True)

    @pl.when(p == 0)
    def _():
        P["C0"].copy(0).start()

    @pl.when(p == 1)
    def _():
        P["C1"].copy(0).start()

    @pl.when(p == 2)
    def _():
        P["C2"].copy(0).start()
        P["C3"].copy(0).start()
        tb_copy.start()

    for c in w_copies:
        c.wait()
    part = mm(d, wcat[...], NT)

    @pl.when(p == 0)
    def _():
        acc[...] = part

    @pl.when(p == 1)
    def _():
        acc[...] += part

    @pl.when(p == 2)
    def _():
        ig_s[...] = (acc[half:, :] + part[half:]).astype(BF16)
        ig_copy.start()
        acc[:half, :] += part[:half]

        def next_table(k):
            t_copies[k].wait_recv()
            ts[k + 1][...] = ts[k][...] + trs[k][...]
            if k + 1 < nb:
                t_copies[k + 1].start()

        forward(0, "C0")
        tb_copy.wait_recv()
        ts[0][0:8, :] = tb[...] + tb_m[...] + vec[...]
        ts[0][8:16, :] = bi[...]
        t_copies[0].start()
        forward(1, "B3")
        forward(2, "B1", "B2")
        forward(0, "C1")
        forward(1, "WO")
        next_table(0)
        forward(1, "C0")
        forward(0, "C2", "C3")
        ig_copy.wait_recv()
        x_loads[2].wait()
        ig_o[...] = gsum[...] + (acc[:half, :] + ig_r[...].astype(F32))
        next_table(1)
        forward(2, "B3")
        forward(1, "C1")
        forward(2, "WO", "C0")
        for k in range(2, nb - 1):
            next_table(k)
        forward(1, "C2", "C3")
        forward(2, "C1")
        for i in range(3):
            wout_o[:, i * third : (i + 1) * third] = P["A%d" % (i + 1)].result()
            win_o[:, i * third : (i + 1) * third] = P["B%d" % (i + 1)].result()
        forward(2, "C2", "C3")
        wo_o[...] = P["WO"].result()
        next_table(nb - 1)
        table = ts[nb][...]
        n = width // dp_size
        m = bi_o.shape[1]
        vals = table[0:8, 0:n]
        biv = table[8:9, 0:m]
        for j in range(1, dp_size):
            vals = jnp.where(dev == j, table[0:8, j * n : (j + 1) * n], vals)
            r = 8 + (j * m) // width
            k = (j * m) % width
            biv = jnp.where(dev == j, table[r : r + 1, k : k + m], biv)
        vals_o[...] = vals
        bi_o[...] = biv
        for j in range(3):
            cs = slice(j * pw, (j + 1) * pw)
            v = P["C%d" % j].result()
            wq_o[:, cs] = v[:, :pw]
            wk_o[:, cs] = v[:, pw : 2 * pw]
            wv_o[:, cs] = v[:, 2 * pw :] if j < 2 else P["C3"].result()

        for name in PIECES:
            P[name].drain()
        ig_copy.wait_send()
        tb_copy.wait_send()
        for c in t_copies:
            c.wait_send()


def back(dp_size, xo, xt, wq, wk, wv, q, k, v, probs, ao, at, go, gt, gsum, vec, bi, sa, win, wo):
    half, width = xo.shape
    rows = 2 * half
    pairs = HEADS // 4
    pw = 2 * HD
    ff = win.shape[1]
    nb = dp_size.bit_length() - 1
    n = width // dp_size
    split = lambda a: a.reshape((2,) * nb + (n, a.shape[-1]))
    whole = lambda a: pl.BlockSpec(
        a.shape, lambda p: (0,) * a.ndim, pipeline_mode=pl.Buffered(1)
    )
    col = lambda r, w: pl.BlockSpec((r, w), lambda p: (0, p))
    hbm = pl.BlockSpec(memory_space=pl.ANY)
    vm = pl.BlockSpec(memory_space=pltpu.VMEM)
    V = pltpu.VMEM
    plan = piece_plan(dp_size, width, ff)

    def stages(last):
        return tuple(
            tuple(
                V((2,) * (nb - 1 - k) + (n, w), BF16) if k < nb - last else V((16, 128), BF16)
                for k in range(nb)
            )
            for _, w in plan
        )

    table = lambda: V((16, width), F32)
    sem = pltpu.SemaphoreType.DMA
    return pl.pallas_call(
        functools.partial(back_body, dp_size),
        grid_spec=pltpu.PrefetchScalarGridSpec(
            num_scalar_prefetch=0,
            grid=(pairs,),
            in_specs=[col(rows, pw)] * 3 + [col(half, pw)] * 4 + [whole(vec), whole(bi)] + [hbm] * 12,
            out_specs=[vm] * 9,
            scratch_shapes=[
                V((half, width), BF16),
                V((half, width), BF16),
                V((2, 2, rows, rows), BF16),
                V((half, width), F32),
                V((rows, pw), BF16),
                V((pw, rows), BF16),
                V((pw, rows), BF16),
                V((pw, rows), F32),
                V((pw, rows), F32),
                V((rows, 3 * pw), BF16),
                V((width, 3 * pw), BF16),
                V((width, rows), BF16),
                V((rows, width), F32),
                V((half, width), BF16),
                V((half, width), BF16),
                V((pairs,) + (2,) * nb + (n, 3 * pw), BF16),
                stages(0),
                stages(1),
                V((8, width), F32),
                V((8, width), F32),
                tuple(table() for _ in range(nb + 1)),
                tuple(table() for _ in range(nb)),
                sem((len(plan) * nb,)),
                sem((len(plan) * nb,)),
                sem((len(plan),)),
                sem((2 + nb,)),
                sem((2 + nb,)),
                sem((8,)),
            ],
        ),
        out_shape=[shape((half, width), F32)]
        + [shape((n, width // 2), F32)] * 4
        + [shape((n, ff), F32)] * 2
        + [shape((8, n), F32), shape((1, 2 * ff // dp_size), F32)],
        compiler_params=pltpu.CompilerParams(
            vmem_limit_bytes=60 << 20, collective_id=2, has_side_effects=True
        ),
        cost_estimate=cost(40e9, 20e6),
        name="back",
    )(q, k, v, ao, at, go, gt, vec, bi, xo, xt, probs, gsum, wq, wk, wv, *sa, split(win), split(wo))


def emit_body(big, *refs):
    ins, outs = refs[: big + 2], refs[big + 2 :]
    for i in range(big):
        outs[i][...] = ins[i][...]
    vals = ins[big][...]
    for j in range(8):
        outs[big + j][...] = vals[j]
    outs[big + 8][...] = ins[big + 1][0]


def emit(arrays, vals, bi):
    vm = pl.BlockSpec(memory_space=pltpu.VMEM)
    return pl.pallas_call(
        functools.partial(emit_body, len(arrays)),
        in_specs=[vm] * (len(arrays) + 2),
        out_specs=[vm] * (len(arrays) + 9),
        out_shape=[shape(a.shape, a.dtype) for a in arrays]
        + [shape((vals.shape[1],), F32)] * 8
        + [shape((bi.shape[1],), F32)],
        compiler_params=params(60),
        name="emit",
    )(*arrays, vals, bi)


def local_pair(
    dp_size, inputs, grad_out, lengths, rand_blocks, w_query, b_query, w_key, w_value, b_value,
    w_output, b_output, gain_one, shift_one, w_in, b_in, w_out, b_out, gain_two, shift_two,
):
    x = inputs[0]
    x_got, a_own, a_oth, a_got, q, k, v, probs = front(
        lengths, x, rand_blocks.transpose(2, 0, 1), b_query, b_value, w_query, w_key, w_value
    )
    out, gsum, ga0, ga_got, sa1, sa2, sa3, w_in_g, w_output_g, vec_g, bi_g = middle(
        dp_size, a_own, a_got, x, grad_out[0], b_output, gain_one, shift_one, b_in, b_out,
        gain_two, shift_two, w_output, w_in, w_out,
    )
    *mats, vals, bi = back(
        dp_size, x, x_got, w_query, w_key, w_value, q, k, v, probs, a_own, a_oth, ga0, ga_got,
        gsum, vec_g, bi_g, (sa1, sa2, sa3), w_in_g, w_output_g,
    )
    (
        out, input_grad, wq_p, wk_p, wv_p, wo_p, in_part, out_part, bq_p, bv_p, bo_p, g1_p, s1_p,
        b2_p, g2_p, s2_p, bi_p,
    ) = emit([out] + mats, vals, bi)
    return (
        out[None], input_grad[None], wq_p, bq_p, wk_p, wv_p, bv_p, wo_p, bo_p, g1_p, s1_p,
        in_part, bi_p, out_part, b2_p, g2_p, s2_p,
    )


def layer_norm(features, norm_gain, norm_shift):
    row_mean = jnp.mean(features, axis=-1, keepdims=True)
    centered = features - row_mean
    variance = jnp.mean(centered * centered, axis=-1, keepdims=True)
    return centered * lax.rsqrt(variance + norm_epsilon) * norm_gain + norm_shift


def gelu_tanh(features):
    return jax.nn.gelu(features, approximate=True)


def slot_table_ids(block_ids, rand_rows, length):
    valid_blocks = (length + BLK - 1) // BLK
    column = block_ids[:, None]
    columns = jnp.concatenate(
        [
            column - 1,
            column,
            column + 1,
            rand_rows,
            jnp.zeros_like(column),
            jnp.zeros_like(column) + valid_blocks - 1,
        ],
        axis=1,
    )
    in_range = (columns >= 0) & (columns < valid_blocks)
    slot_ids = jnp.arange(columns.shape[1], dtype=jnp.int32)
    earlier = slot_ids[None, :] < slot_ids[:, None]
    repeated = jnp.any(
        (columns[:, :, None] == columns[:, None, :]) & earlier[None, :, :] & in_range[:, None, :],
        axis=2,
    )
    return (jnp.clip(columns, 0, NB - 1), in_range & jnp.logical_not(repeated))


def slot_table(first_block, rand_rows, length):
    block_ids = first_block + jnp.arange(rand_rows.shape[0], dtype=jnp.int32)
    return slot_table_ids(block_ids, rand_rows, length)


def slot_mask(slot_blocks, slot_valid, length):
    positions = slot_blocks[:, :, None] * BLK + jnp.arange(BLK, dtype=jnp.int32)
    allowed = slot_valid[:, :, None] & (positions < length)
    return allowed.reshape(slot_blocks.shape[0], 1, 1, -1)


def gather_slots(whole_rows, slot_blocks):
    picked = whole_rows.reshape(NB, BLK, whole_rows.shape[1])[slot_blocks]
    return picked.reshape(slot_blocks.shape[0], slot_blocks.shape[1] * BLK, HEADS, HD)


def log_total(scores, allowed):
    masked = jnp.where(allowed, scores, negative_fill)
    top_score = jnp.max(masked, axis=-1, keepdims=True)
    return top_score + jnp.log(jnp.sum(jnp.exp(masked - top_score), axis=-1, keepdims=True))


def exp_probs(scores, allowed, totals):
    return jnp.exp(jnp.where(allowed, scores, negative_fill) - totals)


def global_targets(length, device, local_blocks):
    last_block = (length + BLK - 1) // BLK - 1
    targets = []
    for target_block in (jnp.zeros_like(last_block), last_block):
        is_owner = target_block // local_blocks == device
        local_block = jnp.clip(target_block - device * local_blocks, 0, local_blocks - 1)
        targets.append((is_owner, local_block))
    return targets


def global_scores(query_rows, key_one, length):
    scores = jnp.einsum(
        "qhd,khd->hqk",
        query_rows.reshape(BLK, HEADS, HD),
        key_one.reshape(-1, HEADS, HD),
        preferred_element_type=jnp.float32,
    ) * HD ** (-0.5)
    allowed = (jnp.arange(key_one.shape[0], dtype=jnp.int32) < length)[None, None, :]
    return (scores, allowed)


def global_forward(query_rows, key_one, value_one, length):
    scores, allowed = global_scores(query_rows, key_one, length)
    totals = log_total(scores, allowed)
    weighting = exp_probs(scores, allowed, totals).astype(jnp.bfloat16)
    out_rows = jnp.einsum(
        "hqk,khd->qhd",
        weighting,
        value_one.reshape(-1, HEADS, HD),
        preferred_element_type=jnp.float32,
    )
    return (out_rows.reshape(BLK, -1), totals)


def global_skip(query_rows, key_one, value_one, length):
    return (jnp.zeros((BLK, HEADS * HD), jnp.float32), jnp.zeros((HEADS, BLK, 1), jnp.float32))


def global_backward(query_rows, grad_rows, key_one, value_one, length, row_totals):
    score_scale = HD ** (-0.5)
    scores, allowed = global_scores(query_rows, key_one, length)
    exact_probs = exp_probs(scores, allowed, row_totals)
    grad_heads = grad_rows.reshape(BLK, HEADS, HD)
    grad_weights = jnp.einsum(
        "qhd,khd->hqk",
        grad_heads,
        value_one.reshape(-1, HEADS, HD),
        preferred_element_type=jnp.float32,
    )
    delta_sum = jnp.sum(exact_probs * grad_weights, axis=-1, keepdims=True)
    grad_scores = (exact_probs * (grad_weights - delta_sum)).astype(jnp.bfloat16)
    grad_query = (
        jnp.einsum(
            "hqk,khd->qhd",
            grad_scores,
            key_one.reshape(-1, HEADS, HD),
            preferred_element_type=jnp.float32,
        )
        * score_scale
    )
    grad_keys = (
        jnp.einsum(
            "hqk,qhd->khd",
            grad_scores,
            query_rows.reshape(BLK, HEADS, HD),
            preferred_element_type=jnp.float32,
        )
        * score_scale
    )
    grad_values = jnp.einsum(
        "hqk,qhd->khd",
        exact_probs.astype(jnp.bfloat16),
        grad_heads,
        preferred_element_type=jnp.float32,
    )
    return (
        grad_query.reshape(BLK, -1),
        grad_keys.reshape(key_one.shape[0], -1),
        grad_values.reshape(key_one.shape[0], -1),
    )


def global_back_skip(query_rows, grad_rows, key_one, value_one, length, row_totals):
    key_zeros = jnp.zeros(key_one.shape, jnp.float32)
    return (jnp.zeros((BLK, key_one.shape[1]), jnp.float32), key_zeros, key_zeros)


def attend_forward(query_one, key_one, value_one, length, rand_rows, device):
    local_blocks = rand_rows.shape[0]
    slot_blocks, slot_valid = slot_table(device * local_blocks, rand_rows, length)
    allowed = slot_mask(slot_blocks, slot_valid, length)
    query_blocks = query_one.reshape(local_blocks, BLK, HEADS, HD)
    scores = jnp.einsum(
        "nqhd,nkhd->nhqk",
        query_blocks,
        gather_slots(key_one, slot_blocks),
        preferred_element_type=jnp.float32,
    ) * HD ** (-0.5)
    totals = log_total(scores, allowed)
    weighting = exp_probs(scores, allowed, totals).astype(jnp.bfloat16)
    attended = jnp.einsum(
        "nhqk,nkhd->nqhd",
        weighting,
        gather_slots(value_one, slot_blocks),
        preferred_element_type=jnp.float32,
    ).reshape(query_one.shape[0], -1)
    global_totals = []
    for is_owner, local_block in global_targets(length, device, local_blocks):
        query_rows = lax.dynamic_slice_in_dim(query_one, local_block * BLK, BLK, 0)
        out_rows, row_totals = lax.cond(
            is_owner, global_forward, global_skip, query_rows, key_one, value_one, length
        )
        updated = lax.dynamic_update_slice_in_dim(attended, out_rows, local_block * BLK, 0)
        attended = jnp.where(is_owner, updated, attended)
        global_totals.append(row_totals)
    return (attended, totals, global_totals[0], global_totals[1])


def attend_backward(
    query_one,
    key_one,
    value_one,
    length,
    rand_rows,
    totals,
    first_totals,
    last_totals,
    grad_one,
    device,
):
    score_scale = HD ** (-0.5)
    local_blocks = rand_rows.shape[0]
    first_block = device * local_blocks
    slot_blocks, slot_valid = slot_table(first_block, rand_rows, length)
    allowed = slot_mask(slot_blocks, slot_valid, length)
    query_blocks = query_one.reshape(local_blocks, BLK, HEADS, HD)
    key_slots = gather_slots(key_one, slot_blocks)
    value_slots = gather_slots(value_one, slot_blocks)
    scores = (
        jnp.einsum("nqhd,nkhd->nhqk", query_blocks, key_slots, preferred_element_type=jnp.float32)
        * score_scale
    )
    exact_probs = exp_probs(scores, allowed, totals)
    last_block = (length + BLK - 1) // BLK - 1
    row_blocks = first_block + jnp.arange(query_one.shape[0], dtype=jnp.int32) // BLK
    is_global = (row_blocks == 0) | (row_blocks == last_block)
    grad_sparse = jnp.where(is_global[:, None], jnp.zeros_like(grad_one), grad_one)
    grad_heads = grad_sparse.reshape(local_blocks, BLK, HEADS, HD)
    grad_weights = jnp.einsum(
        "nqhd,nkhd->nhqk", grad_heads, value_slots, preferred_element_type=jnp.float32
    )
    delta_sum = jnp.sum(exact_probs * grad_weights, axis=-1, keepdims=True)
    grad_scores = (exact_probs * (grad_weights - delta_sum)).astype(jnp.bfloat16)
    grad_query = (
        jnp.einsum(
            "nhqk,nkhd->nqhd", grad_scores, key_slots, preferred_element_type=jnp.float32
        ).reshape(query_one.shape[0], -1)
        * score_scale
    )
    grad_key_slots = (
        jnp.einsum("nhqk,nqhd->nkhd", grad_scores, query_blocks, preferred_element_type=jnp.float32)
        * score_scale
    )
    grad_value_slots = jnp.einsum(
        "nhqk,nqhd->nkhd",
        exact_probs.astype(jnp.bfloat16),
        grad_heads,
        preferred_element_type=jnp.float32,
    )
    flat_ids = slot_blocks.reshape(-1)
    slot_width = BLK * query_one.shape[1]
    grad_keys = jax.ops.segment_sum(
        grad_key_slots.reshape(-1, slot_width), flat_ids, num_segments=NB
    ).reshape(-1, query_one.shape[1])
    grad_values = jax.ops.segment_sum(
        grad_value_slots.reshape(-1, slot_width), flat_ids, num_segments=NB
    ).reshape(-1, query_one.shape[1])
    for (is_owner, local_block), row_totals in zip(
        global_targets(length, device, local_blocks), (first_totals, last_totals)
    ):
        query_rows = lax.dynamic_slice_in_dim(query_one, local_block * BLK, BLK, 0)
        grad_rows = lax.dynamic_slice_in_dim(grad_one, local_block * BLK, BLK, 0)
        query_add, key_add, value_add = lax.cond(
            is_owner,
            global_backward,
            global_back_skip,
            query_rows,
            grad_rows,
            key_one,
            value_one,
            length,
            row_totals,
        )
        current = lax.dynamic_slice_in_dim(grad_query, local_block * BLK, BLK, 0)
        grad_query = lax.dynamic_update_slice_in_dim(
            grad_query, current + query_add, local_block * BLK, 0
        )
        grad_keys = grad_keys + key_add
        grad_values = grad_values + value_add
    return (grad_query, grad_keys, grad_values)


def local(
    inputs,
    grad_out,
    lengths,
    rand_blocks,
    w_query,
    b_query,
    w_key,
    w_value,
    b_value,
    w_output,
    b_output,
    gain_one,
    shift_one,
    w_in,
    b_in,
    w_out,
    b_out,
    gain_two,
    shift_two,
):
    device = lax.axis_index("mp")
    seq_count, local_rows, width = inputs.shape
    flat_in = inputs.reshape(-1, width)
    query = (jnp.dot(flat_in, w_query, preferred_element_type=jnp.float32) + b_query).astype(
        jnp.bfloat16
    )
    keys = jnp.dot(flat_in, w_key, preferred_element_type=jnp.float32).astype(jnp.bfloat16)
    values = (jnp.dot(flat_in, w_value, preferred_element_type=jnp.float32) + b_value).astype(
        jnp.bfloat16
    )
    key_all, value_all = (
        lax.all_gather(keys.reshape(seq_count, local_rows, width), "mp", axis=1, tiled=True),
        lax.all_gather(values.reshape(seq_count, local_rows, width), "mp", axis=1, tiled=True),
    )
    query_seq = query.reshape(seq_count, local_rows, width)

    def forward_item(seq_items):
        query_one, key_one, value_one, length, rand_rows = seq_items
        return attend_forward(query_one, key_one, value_one, length, rand_rows, device)

    attended, totals, first_totals, last_totals = lax.map(
        forward_item, (query_seq, key_all, value_all, lengths, rand_blocks)
    )
    attended_low = attended.reshape(-1, width).astype(jnp.bfloat16)
    summed_one = (
        flat_in.astype(jnp.float32)
        + jnp.dot(attended_low, w_output, preferred_element_type=jnp.float32)
        + b_output
    )
    first, norm_one_back = jax.vjp(
        layer_norm, summed_one, gain_one.astype(jnp.float32), shift_one.astype(jnp.float32)
    )
    first_low = first.astype(jnp.bfloat16)
    rows_all = lax.all_gather(first_low, "mp", axis=0, tiled=True)
    hidden = jnp.dot(rows_all, w_in, preferred_element_type=jnp.float32) + b_in
    active_full, gelu_back = jax.vjp(gelu_tanh, hidden)
    active = active_full.astype(jnp.bfloat16)
    feed = lax.psum_scatter(
        jnp.einsum(
            "rf,df->rd",
            lax.slice_in_dim(active, 0, first_low.shape[0] * lax.axis_size("mp"), axis=0),
            w_out,
            preferred_element_type=jnp.float32,
        ),
        "mp",
        scatter_dimension=0,
        tiled=True,
    )
    summed_two = first + feed + b_out
    output, norm_two_back = jax.vjp(
        layer_norm, summed_two, gain_two.astype(jnp.float32), shift_two.astype(jnp.float32)
    )
    grad_two, gain_two_grad, shift_two_grad = norm_two_back(
        grad_out.reshape(-1, width).astype(jnp.float32)
    )
    grad_feed = grad_two.astype(jnp.bfloat16)
    b_out_grad = jnp.sum(grad_feed, axis=0, dtype=jnp.float32)
    grads_all = lax.all_gather(grad_feed, "mp", axis=0, tiled=True)
    w_out_grad = jnp.einsum("rd,rf->df", grads_all, active, preferred_element_type=jnp.float32)
    grad_hidden = gelu_back(jnp.dot(grads_all, w_out, preferred_element_type=jnp.float32))[
        0
    ].astype(jnp.bfloat16)
    w_in_grad = jnp.einsum("rd,rf->df", rows_all, grad_hidden, preferred_element_type=jnp.float32)
    grad_first = grad_two + lax.psum_scatter(
        jnp.einsum(
            "rf,df->rd",
            lax.slice_in_dim(grad_hidden, 0, grad_feed.shape[0] * lax.axis_size("mp"), axis=0),
            w_in,
            preferred_element_type=jnp.float32,
        ),
        "mp",
        scatter_dimension=0,
        tiled=True,
    )
    b_in_grad = lax.dynamic_update_slice_in_dim(
        jnp.zeros((FF,), jnp.float32),
        jnp.sum(grad_hidden, axis=0, dtype=jnp.float32),
        device * w_in.shape[1],
        0,
    )
    grad_sum_one, gain_one_grad, shift_one_grad = norm_one_back(grad_first)
    grad_branch = grad_sum_one.astype(jnp.bfloat16)
    b_output_grad = jnp.sum(grad_branch, axis=0, dtype=jnp.float32)
    w_output_grad = jnp.einsum(
        "rd,re->de", attended_low, grad_branch, preferred_element_type=jnp.float32
    )
    grad_attended = (
        jnp.einsum("re,de->rd", grad_branch, w_output, preferred_element_type=jnp.float32)
        .astype(jnp.bfloat16)
        .reshape(seq_count, local_rows, width)
    )

    def backward_item(seq_items):
        (
            query_one,
            key_one,
            value_one,
            length,
            rand_rows,
            sparse_totals,
            first_one,
            last_one,
            grad_one,
        ) = seq_items
        return attend_backward(
            query_one,
            key_one,
            value_one,
            length,
            rand_rows,
            sparse_totals,
            first_one,
            last_one,
            grad_one,
            device,
        )

    grad_query, grad_keys, grad_values = lax.map(
        backward_item,
        (
            query_seq,
            key_all,
            value_all,
            lengths,
            rand_blocks,
            totals,
            first_totals,
            last_totals,
            grad_attended,
        ),
    )
    key_sums, value_sums = (
        lax.psum_scatter(
            grad_keys.astype(jnp.bfloat16), "mp", scatter_dimension=1, tiled=True
        ).astype(jnp.float32),
        lax.psum_scatter(
            grad_values.astype(jnp.bfloat16), "mp", scatter_dimension=1, tiled=True
        ).astype(jnp.float32),
    )
    grad_q_low = grad_query.reshape(-1, width).astype(jnp.bfloat16)
    grad_k_low = key_sums.reshape(-1, width).astype(jnp.bfloat16)
    grad_v_low = value_sums.reshape(-1, width).astype(jnp.bfloat16)
    input_grad = grad_sum_one + jnp.einsum(
        "re,de->rd", grad_q_low, w_query, preferred_element_type=jnp.float32
    )
    input_grad = input_grad + jnp.einsum(
        "re,de->rd", grad_k_low, w_key, preferred_element_type=jnp.float32
    )
    input_grad = input_grad + jnp.einsum(
        "re,de->rd", grad_v_low, w_value, preferred_element_type=jnp.float32
    )
    w_query_grad = jnp.einsum("rd,re->de", flat_in, grad_q_low, preferred_element_type=jnp.float32)
    w_key_grad = jnp.einsum("rd,re->de", flat_in, grad_k_low, preferred_element_type=jnp.float32)
    w_value_grad = jnp.einsum("rd,re->de", flat_in, grad_v_low, preferred_element_type=jnp.float32)
    b_query_grad = jnp.sum(grad_q_low, axis=0, dtype=jnp.float32)
    b_value_grad = jnp.sum(grad_v_low, axis=0, dtype=jnp.float32)
    reduced = (
        lax.psum_scatter(
            w_query_grad.astype(jnp.bfloat16), "dp", scatter_dimension=0, tiled=True
        ).astype(jnp.float32),
        lax.psum_scatter(
            w_key_grad.astype(jnp.bfloat16), "dp", scatter_dimension=0, tiled=True
        ).astype(jnp.float32),
        lax.psum_scatter(
            w_value_grad.astype(jnp.bfloat16), "dp", scatter_dimension=0, tiled=True
        ).astype(jnp.float32),
        lax.psum_scatter(
            w_output_grad.astype(jnp.bfloat16), "dp", scatter_dimension=0, tiled=True
        ).astype(jnp.float32),
        lax.psum_scatter(
            w_in_grad.astype(jnp.bfloat16), "dp", scatter_dimension=0, tiled=True
        ).astype(jnp.float32),
        lax.psum_scatter(
            w_out_grad.astype(jnp.bfloat16), "dp", scatter_dimension=0, tiled=True
        ).astype(jnp.float32),
        lax.psum_scatter(
            b_query_grad.astype(jnp.bfloat16), "dp", scatter_dimension=0, tiled=True
        ).astype(jnp.float32),
        lax.psum_scatter(
            b_value_grad.astype(jnp.bfloat16), "dp", scatter_dimension=0, tiled=True
        ).astype(jnp.float32),
        lax.psum_scatter(
            b_output_grad.astype(jnp.bfloat16), "dp", scatter_dimension=0, tiled=True
        ).astype(jnp.float32),
        lax.psum_scatter(
            gain_one_grad.astype(jnp.bfloat16), "dp", scatter_dimension=0, tiled=True
        ).astype(jnp.float32),
        lax.psum_scatter(
            shift_one_grad.astype(jnp.bfloat16), "dp", scatter_dimension=0, tiled=True
        ).astype(jnp.float32),
        lax.psum_scatter(
            b_in_grad.astype(jnp.bfloat16), "dp", scatter_dimension=0, tiled=True
        ).astype(jnp.float32),
        lax.psum_scatter(
            b_out_grad.astype(jnp.bfloat16), "dp", scatter_dimension=0, tiled=True
        ).astype(jnp.float32),
        lax.psum_scatter(
            gain_two_grad.astype(jnp.bfloat16), "dp", scatter_dimension=0, tiled=True
        ).astype(jnp.float32),
        lax.psum_scatter(
            shift_two_grad.astype(jnp.bfloat16), "dp", scatter_dimension=0, tiled=True
        ).astype(jnp.float32),
    )
    query_part, key_part_out, value_part, output_part = (
        lax.psum_scatter(
            reduced[0].astype(jnp.bfloat16), "mp", scatter_dimension=1, tiled=True
        ).astype(jnp.float32),
        lax.psum_scatter(
            reduced[1].astype(jnp.bfloat16), "mp", scatter_dimension=1, tiled=True
        ).astype(jnp.float32),
        lax.psum_scatter(
            reduced[2].astype(jnp.bfloat16), "mp", scatter_dimension=1, tiled=True
        ).astype(jnp.float32),
        lax.psum_scatter(
            reduced[3].astype(jnp.bfloat16), "mp", scatter_dimension=1, tiled=True
        ).astype(jnp.float32),
    )
    in_part = reduced[4]
    out_part = reduced[5]
    vectors = lax.psum(
        (
            reduced[6],
            reduced[7],
            reduced[8],
            reduced[9],
            reduced[10],
            reduced[11],
            reduced[12],
            reduced[13],
            reduced[14],
        ),
        "mp",
    )
    return (
        output.astype(jnp.bfloat16).reshape(seq_count, local_rows, width),
        input_grad.reshape(seq_count, local_rows, width),
        query_part,
        vectors[0],
        key_part_out,
        value_part,
        vectors[1],
        output_part,
        vectors[2],
        vectors[3],
        vectors[4],
        in_part,
        vectors[5],
        out_part,
        vectors[6],
        vectors[7],
        vectors[8],
    )


def solution(mesh):
    in_specs = (
        P("dp", "mp", None),
        P("dp", "mp", None),
        P("dp"),
        P("dp", "mp", None),
        P(),
        P(),
        P(),
        P(),
        P(),
        P(),
        P(),
        P(),
        P(),
        P(None, "mp"),
        P("mp"),
        P(None, "mp"),
        P(),
        P(),
        P(),
    )
    out_specs = (
        P("dp", "mp", None),
        P("dp", "mp", None),
        P("dp", "mp"),
        P("dp"),
        P("dp", "mp"),
        P("dp", "mp"),
        P("dp"),
        P("dp", "mp"),
        P("dp"),
        P("dp"),
        P("dp"),
        P("dp", "mp"),
        P("dp"),
        P("dp", "mp"),
        P("dp"),
        P("dp"),
        P("dp"),
    )
    sizes = dict(mesh.shape)
    if sizes["mp"] == 2 and sizes["dp"] == 16:
        local_fn = functools.partial(local_pair, sizes["dp"])
    else:
        local_fn = local
    return jax.shard_map(local_fn, mesh=mesh, in_specs=in_specs, out_specs=out_specs, check_vma=False)
```

```python
import functools

import jax
import jax.numpy as jnp
from jax import lax
from jax.experimental import pallas as pl
from jax.experimental.pallas import tpu as pltpu
from jax.sharding import PartitionSpec as P

HEADS = 12
HD = 64
FF = 3072
BLK = 64
NB = 16


negative_fill = -1000000000.0
norm_epsilon = 1e-12


F32 = jnp.float32
BF16 = jnp.bfloat16
NN = (((1,), (0,)), ((), ()))
NT = (((1,), (1,)), ((), ()))
TN = (((0,), (0,)), ((), ()))


def mm(a, b, dims=NN):
    return lax.dot_general(a, b, dims, preferred_element_type=F32)


def params(mib=56):
    return pltpu.CompilerParams(vmem_limit_bytes=mib << 20)


def cost(flops, nbytes, trans=0):
    return pl.CostEstimate(flops=int(flops), bytes_accessed=int(nbytes), transcendentals=int(trans))


def shape(dims, dtype):
    return jax.ShapeDtypeStruct(dims, dtype)


def row_stats(u):
    mean = jnp.mean(u, axis=-1, keepdims=True)
    cen = u - mean
    var = jnp.mean(cen * cen, axis=-1, keepdims=True)
    rs = lax.rsqrt(var + norm_epsilon)
    return cen * rs, rs


def partner_copy(src, dst, send, recv, me):
    return pltpu.make_async_remote_copy(
        src_ref=src, dst_ref=dst, send_sem=send, recv_sem=recv,
        device_id={"mp": 1 - me}, device_id_type=pl.DeviceIdType.MESH,
    )


def front_body(
    lengths, x, rand, bq, bv, wq, wk, wv,
    x_got, a_own, a_oth, a_got, q_o, k_o, v_o, p_h,
    xg_s, ag_s, p_s, w_s, b_s, rand_s, rand_r, bias, wsem, psem, send, recv,
):
    me = lax.axis_index("mp")
    p = pl.program_id(0)
    half, width = x.shape
    rows = 2 * half
    hw = width // 2
    pw = 2 * HD
    nb = rows // BLK
    tile = 256
    x_copy = partner_copy(x, xg_s, send.at[0], recv.at[0], me)
    rand_copy = partner_copy(rand_s, rand_r, send.at[1], recv.at[1], me)

    def w_loads(j):
        own = pl.ds(pl.multiple_of(me * hw + j * pw, pw), pw)
        return [
            pltpu.make_async_copy(
                w.at[:, own], w_s.at[j, :, i * pw : (i + 1) * pw], wsem.at[3 * j + i]
            )
            for i, w in enumerate((wq, wk, wv))
        ]

    slot = p % 2

    def p_store(slot_j, j, i):
        r0, h = units[i]
        return pltpu.make_async_copy(
            p_s.at[slot_j, h, r0 : r0 + tile], p_h.at[2 * j + h, r0 : r0 + tile],
            psem.at[slot_j, i],
        )

    order = [half + t * tile for t in range(half // tile)] + [t * tile for t in range(half // tile)]
    units = [(r0, h) for r0 in order for h in range(2)]

    @pl.when(p == 0)
    def _():
        barrier = pltpu.get_barrier_semaphore()
        pl.semaphore_signal(
            barrier, inc=1, device_id={"mp": 1 - me}, device_id_type=pl.DeviceIdType.MESH
        )
        for j in range(hw // pw):
            for c in w_loads(j):
                c.start()
        rand_s[...] = jnp.zeros_like(rand_s)
        for j in range(rand.shape[0]):
            rand_s[j : j + 1, : nb // 2] = rand[j]
        b_s[0:1, :] = bq[...].astype(F32)[None, :]
        b_s[1:2, :] = bv[...].astype(F32)[None, :]
        pl.semaphore_wait(barrier, 1)
        x_copy.start()
        rand_copy.start()

    cols = pl.ds(pl.multiple_of(p * pw, pw), pw)
    bias_cols = pl.ds(pl.multiple_of(me * hw + p * pw, pw), pw)

    for j in range(hw // pw):

        @pl.when(p == j)
        def _(j=j):
            for c in w_loads(j):
                c.wait()
            if j == 2:
                for i in range(len(units)):
                    p_store(0, 0, i).wait()

    def project(i, xr):
        rs = slice(i * half, (i + 1) * half)
        qkv = mm(xr[...], w_s[p])
        q_o[rs, :] = (qkv[:, :pw] + b_s[0:1, bias_cols]).astype(BF16)
        k_o[rs, :] = qkv[:, pw : 2 * pw].astype(BF16)
        v_o[rs, :] = (qkv[:, 2 * pw :] + b_s[1:2, bias_cols]).astype(BF16)

    project(0, x)

    @pl.when(p == 0)
    def _():
        rand_copy.wait_recv()
        ln = lengths[0]
        last = (ln + BLK - 1) // BLK - 1
        lb = lax.broadcasted_iota(jnp.int32, (nb, rows), 0)
        kp = lax.broadcasted_iota(jnp.int32, (nb, rows), 1)
        qb = jnp.where(lb < nb // 2, lb + (nb // 2) * me, lb - (nb // 2) * me)
        kpos = jnp.where(kp < half, kp + half * me, kp - half * me)
        kb = kpos // BLK
        ok = (jnp.abs(kb - qb) <= 1) | (kb == 0) | (kb == last)
        listed = [r[...].astype(F32).T[: nb // 2] for r in (rand_s, rand_r)]
        both = jnp.concatenate(listed, axis=0).astype(jnp.int32)
        for j in range(rand.shape[0]):
            ok = ok | (kb == both[:, j : j + 1])
        ok = ok | (qb == 0) | (qb == last)
        ok = ok & (kpos < ln)
        table = jnp.where(ok, 0.0, -1e30).astype(F32)
        for b in range(nb):
            bias[b] = jnp.broadcast_to(table[b : b + 1, :], (8, rows))
        x_copy.wait_recv()
        x_got[...] = xg_s[...]

    project(1, xg_s)

    low = lax.broadcasted_iota(jnp.int32, (tile, pw), 1) < HD
    scores, probs, outs = {}, {}, {}

    def score(i):
        r0, h = units[i]
        q = q_o[r0 : r0 + tile, :] * BF16(HD**-0.5)
        s = mm(jnp.where(low if h == 0 else ~low, q, BF16(0)), k_o[...], NT)
        b0 = r0 // BLK
        s = s.reshape(tile // BLK, BLK // 8, 8, rows) + bias[b0 : b0 + tile // BLK][:, None]
        scores[i] = s.reshape(tile, rows)

    def attend(i):
        r0, h = units[i]
        outs[i] = mm(probs.pop(i), v_o[...])
        if h == 1:
            a = jnp.where(low, outs.pop(i - 1), outs.pop(i)).astype(BF16)
            if r0 < half:
                a_own[r0 : r0 + tile, cols] = a
            else:
                a_oth[r0 - half : r0 - half + tile, cols] = a
                if r0 + tile == rows:
                    partner_copy(
                        a_oth.at[:, cols], ag_s.at[:, cols], send.at[2 + p], recv.at[2 + p], me
                    ).start()

    score(0)
    for i, (r0, h) in enumerate(units):
        if i + 1 < len(units):
            score(i + 1)
        s = scores.pop(i)
        e = jnp.exp(s - jnp.max(s, axis=-1, keepdims=True))
        pr = (e * (1.0 / jnp.sum(e, axis=-1, keepdims=True))).astype(BF16)
        p_s[slot, h, r0 : r0 + tile, :] = pr
        p_store(slot, p, i).start()
        probs[i] = pr
        if i >= 1:
            attend(i - 1)
    attend(len(units) - 1)

    @pl.when(p == pl.num_programs(0) - 1)
    def _():
        x_copy.wait_send()
        rand_copy.wait_send()
        for j in range(hw // pw):
            cs = slice(j * pw, (j + 1) * pw)
            c = partner_copy(a_oth.at[:, cs], ag_s.at[:, cs], send.at[2 + j], recv.at[2 + j], me)
            c.wait_send()
            c.wait_recv()
        a_got[...] = ag_s[...]
        for j in range(1, hw // pw):
            for i in range(len(units)):
                p_store(j % 2, j, i).wait()


def front(lengths, x, rand, bq, bv, wq, wk, wv):
    half, width = x.shape
    rows = 2 * half
    pairs = HEADS // 4
    pw = 2 * HD
    hw = width // 2
    vm = pl.BlockSpec(memory_space=pltpu.VMEM)
    hbm = pl.BlockSpec(memory_space=pl.ANY)
    col = pl.BlockSpec((rows, pw), lambda p: (0, p))
    V = pltpu.VMEM
    sem = pltpu.SemaphoreType.DMA
    return pl.pallas_call(
        front_body,
        grid_spec=pltpu.PrefetchScalarGridSpec(
            num_scalar_prefetch=0,
            grid=(pairs,),
            in_specs=[pl.BlockSpec(memory_space=pltpu.SMEM)] + [vm] * 4 + [hbm] * 3,
            out_specs=[vm] * 4 + [col] * 3 + [hbm],
            scratch_shapes=[
                V((half, width), BF16),
                V((half, hw), BF16),
                V((2, 2, rows, rows), BF16),
                V((pairs, width, 3 * pw), BF16),
                V((8, width), F32),
                V((8, 128), jnp.int32),
                V((8, 128), jnp.int32),
                V((rows // BLK, 8, rows), F32),
                sem((3 * pairs,)),
                sem((2, 8)),
                sem((2 + pairs,)),
                sem((2 + pairs,)),
            ],
        ),
        out_shape=[shape((half, width), BF16)]
        + [shape((half, hw), BF16)] * 3
        + [shape((rows, hw), BF16)] * 3
        + [shape((2 * pairs, rows, rows), BF16)],
        compiler_params=pltpu.CompilerParams(
            vmem_limit_bytes=60 << 20, collective_id=3, has_side_effects=True
        ),
        cost_estimate=cost(20e9, 20e6, 6 * rows * rows),
        name="front",
    )(lengths, x, rand, bq, bv, wq, wk, wv)


class Piece:
    def __init__(self, bits, sems, base, src, got, kept, stage0=0):
        self.bits = bits
        self.send, self.recv, self.load = sems
        self.base = base
        self.src, self.got, self.kept = src, got, kept
        self.stage0 = stage0
        self.dev = lax.axis_index("dp")

    def mine(self, k):
        return (self.dev // 2 ** self.bits[k]) % 2

    def peer(self, k):
        return self.dev + 2 ** self.bits[k] * (1 - 2 * self.mine(k))

    def side(self, k, bit, lead=None):
        left = sorted(self.bits[k:], reverse=True)
        where = left.index(self.bits[k])
        idx = [slice(None)] * len(left) if lead is None else list(lead[:where]) + [None] + list(lead[where:])
        idx[where] = bit
        return tuple(idx)

    def source(self, k):
        return self.src if k == self.stage0 else self.kept[k - 1]

    def copy(self, k):
        i = self.base + k
        return pltpu.make_async_remote_copy(
            src_ref=self.source(k).at[self.side(k, 1 - self.mine(k))], dst_ref=self.got[k],
            send_sem=self.send.at[i], recv_sem=self.recv.at[i],
            device_id={"dp": self.peer(k)}, device_id_type=pl.DeviceIdType.MESH,
        )

    def load_own(self):
        k = self.stage0
        return pltpu.make_async_copy(
            self.src.at[self.side(k, self.mine(k))], self.kept[k], self.load.at[self.base // len(self.bits)]
        )

    def total(self, k, lead, loaded):
        if loaded:
            own = self.kept[k][lead]
        else:
            own = self.source(k)[self.side(k, self.mine(k), lead)]
        return own.astype(F32) + self.got[k][lead].astype(F32)

    def add(self, k, loaded=False):
        free = len(self.bits) - 1 - k

        def step(i, carry):
            lead = tuple((i // 2 ** (free - 1 - j)) % 2 for j in range(free))
            self.kept[k][lead] = self.total(k, lead, loaded).astype(BF16)
            return carry

        lax.fori_loop(0, 2**free, step, 0)

    def forward(self, k, loaded=False):
        self.copy(k).wait_recv()
        self.add(k, loaded)
        self.copy(k + 1).start()

    def result(self):
        k = len(self.bits) - 1
        self.copy(k).wait_recv()
        return self.total(k, (), False)

    def drain(self):
        for k in range(self.stage0, len(self.bits)):
            self.copy(k).wait_send()


def bit_orders(dp_size):
    nb = dp_size.bit_length() - 1
    rest = list(range(2, nb))
    return [0, 1] + rest, [1, 0] + rest, rest + [0, 1]


def gelu_and_slope(v):
    k0 = 0.7978845608028654
    k1 = 0.044715
    v2 = v * v
    t = jnp.tanh(v * (k0 + (k0 * k1) * v2))
    hp = 0.5 * t + 0.5
    return v * hp, hp + (0.5 * v) * (1.0 - t * t) * (k0 + (3 * k0 * k1) * v2)


def norm_back(e, n, rs, gain):
    eg = e * gain
    return (eg - jnp.mean(eg, -1, keepdims=True) - n * jnp.mean(eg * n, -1, keepdims=True)) * rs


def middle_body(
    dp_size, a_own, a_got, x, gout, b_output, gain1, shift1, b_in, b_out, gain2, shift2,
    w_o_h, w_in_h, w_out_h,
    out_h, gsum_h, ga_o, gat_o, sa1, sa2, sa3, win_h, wo_g, vec_o, bi_o,
    out_o, gsum_o, win_g,
    fl, feed_s, feed_g, gf, part_s, part_g, gat_s, gb, wo_s, wo_r, vec_s, vec_r, bi_s, bi_s2, bi_r, wout_g, got_a1, got_a2, got_a3,
    w_o, w_in, w_out, act, slope, gh, u_s, first_s, own_s, gtwo_s,
    load_sem, store_sem, send_sem, recv_sem, a_send_sem, a_recv_sem,
):
    me = lax.axis_index("mp")
    half, width = x.shape
    hw = width // 2
    tile = 256
    tiles = half // tile
    cut = sa1.shape[-1]
    nb = dp_size.bit_length() - 1
    sems = (a_send_sem, a_recv_sem, None)
    chunks = [slice(None)] * (nb + 1)
    outs_a = [
        Piece(
            bits, sems, i * nb, wout_g.at[tuple(chunks + [slice(i * cut, (i + 1) * cut)])],
            (g,), (s,),
        )
        for i, (bits, g, s) in enumerate(
            zip(bit_orders(dp_size), (got_a1, got_a2, got_a3), (sa1, sa2, sa3))
        )
    ]
    barrier = pltpu.get_barrier_semaphore()
    for device in [{"mp": 1 - me}] + [{"dp": a.peer(0)} for a in outs_a]:
        pl.semaphore_signal(barrier, inc=1, device_id=device, device_id_type=pl.DeviceIdType.MESH)
    stores = [
        pltpu.make_async_copy(src, dst, store_sem.at[i])
        for i, (src, dst) in enumerate(((out_o, out_h), (win_g, win_h), (gsum_o, gsum_h)))
    ]
    loads = []
    for i, (src, dst) in enumerate(((w_o_h, w_o), (w_in_h, w_in), (w_out_h, w_out))):
        loads.append(pltpu.make_async_copy(src, dst, load_sem.at[i]))
        loads[-1].start()
    pl.semaphore_wait(barrier, 4)

    def copy(src, dst, i):
        return partner_copy(src, dst, send_sem.at[i], recv_sem.at[i], me)

    loads[0].wait()

    def rows(t):
        return pl.ds(pl.multiple_of(t * tile, tile), tile)

    def fl_copy(t):
        return copy(fl.at[0, rows(t)], fl.at[1, rows(t)], 1 + t)

    def feed_copy(t):
        return copy(feed_s.at[rows(t)], feed_g.at[rows(t)], 3 + t)

    def gf_copy(t):
        return copy(gf.at[0, rows(t)], gf.at[1, rows(t)], 5 + t)

    def part_copy(t):
        return copy(part_s.at[rows(t)], part_g.at[rows(t)], 7 + t)

    def ga_copy(t):
        return copy(gat_s.at[rows(t)], gat_o.at[rows(t)], 9 + t)

    own_o = pl.ds(pl.multiple_of(me * hw, hw), hw)
    got_o = pl.ds(pl.multiple_of((1 - me) * hw, hw), hw)

    def project(t, carry):
        r = rows(t)
        u = x[r, :].astype(F32) + (
            mm(a_own[r, :], w_o[own_o, :]) + mm(a_got[r, :], w_o[got_o, :])
        ) + b_output[...].astype(F32)[None, :]
        n, _ = row_stats(u)
        first = n * gain1[...].astype(F32)[None, :] + shift1[...].astype(F32)[None, :]
        u_s[r, :] = u
        first_s[r, :] = first
        fl[0, r, :] = first.astype(BF16)
        fl_copy(t).start()
        return carry

    lax.fori_loop(0, tiles, project, 0)
    loads[1].wait()
    loads[2].wait()

    def feed_forward(i, t):
        r = rows(t)
        v = mm(fl[i, r, :], w_in[...]) + b_in[...].astype(F32)[None, :]
        a, s = gelu_and_slope(v)
        a = a.astype(BF16)
        act[i, r, :] = a
        slope[i, r, :] = s.astype(BF16)
        return mm(a, w_out[...], NT)

    def forward_own(t, carry):
        own_s[rows(t), :] = feed_forward(0, t)
        return carry

    def forward_got(t, carry):
        fl_copy(t).wait_recv()
        feed_s[rows(t), :] = feed_forward(1, t).astype(BF16)
        feed_copy(t).start()
        return carry

    lax.fori_loop(0, tiles, forward_own, 0)
    lax.fori_loop(0, tiles, forward_got, 0)

    vec_s[...] = jnp.zeros_like(vec_s)

    def add_vec(i, value):
        vec_s[i : i + 1, :] += jnp.sum(value, 0, keepdims=True)

    def second_norm(t, carry):
        r = rows(t)
        feed_copy(t).wait_recv()
        u = first_s[r, :] + (own_s[r, :] + feed_g[r, :].astype(F32)) + b_out[...].astype(F32)[None, :]
        n, rs = row_stats(u)
        gain = gain2[...].astype(F32)[None, :]
        out_o[r, :] = (n * gain + shift2[...].astype(F32)[None, :]).astype(BF16)
        e = gout[r, :].astype(F32)
        d = norm_back(e, n, rs, gain)
        low = d.astype(BF16)
        gtwo_s[r, :] = d
        gf[0, r, :] = low
        gf_copy(t).start()
        add_vec(6, e * n)
        add_vec(7, e)
        add_vec(5, low.astype(F32))
        return carry

    lax.fori_loop(0, tiles, second_norm, 0)
    stores[0].start()
    bi_s[...] = jnp.zeros_like(bi_s)

    def feed_back(i, t):
        r = rows(t)
        g = (mm(gf[i, r, :], w_out[...]) * slope[i, r, :].astype(F32)).astype(BF16)
        gh[i, r, :] = g
        bi_s[0:1, :] += jnp.sum(g.astype(F32), 0, keepdims=True)
        return mm(g, w_in[...], NT)

    def back_own(t, carry):
        own_s[rows(t), :] = feed_back(0, t)
        return carry

    def wait_gf(t, carry):
        gf_copy(t).wait_recv()
        return carry

    def back_got(t, carry):
        part_s[rows(t), :] = feed_back(1, t).astype(BF16)
        part_copy(t).start()
        return carry

    lax.fori_loop(0, tiles, back_own, 0)
    lax.fori_loop(0, tiles, wait_gf, 0)

    def out_weights(j, carry):
        c = pl.ds(pl.multiple_of(j * hw, hw), hw)
        total = mm(gf[0, :, c], act[0], TN) + mm(gf[1, :, c], act[1], TN)
        wout_g[j] = total.astype(BF16).reshape(wout_g.shape[1:])
        return carry

    lax.fori_loop(0, 2, out_weights, 0)
    for a in outs_a:
        a.copy(0).start()
    lax.fori_loop(0, tiles, back_got, 0)

    def weights(out, lhs, rhs):
        def step(j, carry):
            c = pl.ds(pl.multiple_of(j * tile, tile), tile)
            out[c, :] = (
                mm(lhs[0, :, c], rhs[0], TN) + mm(lhs[1, :, c], rhs[1], TN)
            ).astype(BF16)
            return carry

        lax.fori_loop(0, width // tile, step, 0)

    weights(win_g, fl, gh)
    stores[1].start()

    def first_norm(t, carry):
        r = rows(t)
        part_copy(t).wait_recv()
        e = gtwo_s[r, :] + own_s[r, :] + part_g[r, :].astype(F32)
        n, rs = row_stats(u_s[r, :])
        d = norm_back(e, n, rs, gain1[...].astype(F32)[None, :])
        low = d.astype(BF16)
        gsum_o[r, :] = d
        gb[r, :] = low
        gat_s[r, :] = mm(low, w_o[got_o, :], NT).astype(BF16)
        ga_copy(t).start()
        ga_o[r, :] = mm(low, w_o[own_o, :], NT).astype(BF16)
        add_vec(3, e * n)
        add_vec(4, e)
        add_vec(2, low.astype(F32))
        return carry

    lax.fori_loop(0, tiles, first_norm, 0)
    stores[2].start()
    vec_copy = copy(vec_s, vec_r, 11)
    vec_copy.start()
    bi_s2[0:1, :] = bi_s[0:1, :width]
    bi_s2[1:2, :] = bi_s[0:1, width:]
    bi_copy = copy(bi_s2, bi_r, 12)
    bi_copy.start()
    cols_own = own_o
    cols_got = got_o
    wo_s[own_o, :] = mm(a_own[...], gb[:, cols_got], TN).astype(BF16)
    wo_s[got_o, :] = mm(a_got[...], gb[:, cols_got], TN).astype(BF16)
    wo_copy = copy(wo_s, wo_r, 13)
    wo_copy.start()
    own_part = mm(a_own[...], gb[:, cols_own], TN)
    got_part = mm(a_got[...], gb[:, cols_own], TN)
    wo_copy.wait_recv()
    wo_g[own_o, :] = (own_part + wo_r[own_o, :].astype(F32)).astype(BF16)
    wo_g[got_o, :] = (got_part + wo_r[got_o, :].astype(F32)).astype(BF16)
    vec_copy.wait_recv()
    vec_o[...] = vec_s[...] + vec_r[...]
    bi_copy.wait_recv()
    bi_o[...] = jnp.zeros_like(bi_o)
    first_core = me == 0
    bi_o[0:2, :] = jnp.where(first_core, bi_s2[0:2, :], bi_r[0:2, :])
    bi_o[2:4, :] = jnp.where(first_core, bi_r[0:2, :], bi_s2[0:2, :])
    for a in outs_a:
        a.copy(0).wait_recv()
        a.add(0)

    def finish(t, carry):
        ga_copy(t).wait_recv()
        fl_copy(t).wait_send()
        feed_copy(t).wait_send()
        gf_copy(t).wait_send()
        part_copy(t).wait_send()
        ga_copy(t).wait_send()
        return carry

    lax.fori_loop(0, tiles, finish, 0)
    for c in stores:
        c.wait()
    for a in outs_a:
        a.copy(0).wait_send()
    vec_copy.wait_send()
    bi_copy.wait_send()
    wo_copy.wait_send()


def middle(dp_size, a_own, a_got, x, gout, b_output, gain1, shift1, b_in, b_out, gain2, shift2, w_o, w_in, w_out):
    half, width = x.shape
    hw = width // 2
    ff = w_in.shape[1]
    nb = dp_size.bit_length() - 1
    n = width // dp_size
    part = (2,) * (nb - 1) + (n, ff // 3)
    vm = pl.BlockSpec(memory_space=pltpu.VMEM)
    hbm = pl.BlockSpec(memory_space=pl.ANY)
    V = pltpu.VMEM
    return pl.pallas_call(
        functools.partial(middle_body, dp_size),
        in_specs=[vm] * 11 + [hbm] * 3,
        out_specs=[hbm] * 2 + [vm] * 5 + [hbm] + [vm] * 3,
        out_shape=[
            shape((half, width), BF16),
            shape((half, width), F32),
            shape((half, hw), BF16),
            shape((half, hw), BF16),
            shape(part, BF16),
            shape(part, BF16),
            shape(part, BF16),
            shape((width, ff), BF16),
            shape((width, hw), BF16),
            shape((8, width), F32),
            shape((8, width), F32),
        ],
        scratch_shapes=[
            V((half, width), BF16),
            V((half, width), F32),
            V((width, ff), BF16),
            V((2, half, width), BF16),
            V((half, width), BF16),
            V((half, width), BF16),
            V((2, half, width), BF16),
            V((half, width), BF16),
            V((half, width), BF16),
            V((half, hw), BF16),
            V((half, width), BF16),
            V((width, hw), BF16),
            V((width, hw), BF16),
            V((8, width), F32),
            V((8, width), F32),
            V((8, ff), F32),
            V((8, width), F32),
            V((8, width), F32),
            V((2,) * nb + (n, ff), BF16),
            V(part, BF16),
            V(part, BF16),
            V(part, BF16),
            V((width, width), BF16),
            V((width, ff), BF16),
            V((width, ff), BF16),
            V((2, half, ff), BF16),
            V((2, half, ff), BF16),
            V((2, half, ff), BF16),
            V((half, width), F32),
            V((half, width), F32),
            V((half, width), F32),
            V((half, width), F32),
            pltpu.SemaphoreType.DMA((3,)),
            pltpu.SemaphoreType.DMA((3,)),
            pltpu.SemaphoreType.DMA((14,)),
            pltpu.SemaphoreType.DMA((14,)),
            pltpu.SemaphoreType.DMA((3 * nb,)),
            pltpu.SemaphoreType.DMA((3 * nb,)),
        ],
        compiler_params=pltpu.CompilerParams(
            vmem_limit_bytes=62 << 20, collective_id=1, has_side_effects=True
        ),
        cost_estimate=cost(17e9, 20e6),
        name="middle",
    )(a_own, a_got, x, gout, b_output, gain1, shift1, b_in, b_out, gain2, shift2, w_o, w_in, w_out)


PIECES = ("A1", "A2", "A3", "B1", "B2", "B3", "WO", "C0", "C1", "C2", "C3")


def piece_plan(dp_size, width, ff):
    x, y, z = bit_orders(dp_size)
    third, pw = ff // 3, 2 * HD
    return (
        (x, third), (y, third), (z, third), (x, third), (y, third), (z, third), (y, width // 2),
        (x, 3 * pw), (y, 3 * pw), (x, 2 * pw), (y, pw),
    )


def back_body(
    dp_size, q_i, k_i, v_i, ao, at, go, gt, vec, bi,
    xo_h, xt_h, p_h, gsum_h, wq, wk, wv, sa1, sa2, sa3, win, wo,
    ig_o, wq_o, wk_o, wv_o, wo_o, win_o, wout_o, vals_o, bi_o,
    xo, xt, p_s, gsum, g_s, gT, qT, dkT, dvT, dqkv, wcat, xT, acc, ig_s, ig_r, wsrc, gots, kepts,
    tb, tb_m, ts, trs, send, recv, lsem, vsend, vrecv, wsem,
):
    half, width = ig_o.shape
    rows = 2 * half
    pw = 2 * HD
    tile = 256
    p = pl.program_id(0)
    me = lax.axis_index("mp")
    dev = lax.axis_index("dp")
    nb = dp_size.bit_length() - 1
    sems = (send, recv, lsem)
    chunks = [slice(None)] * (nb + 1)
    third = sa1.shape[-1]

    def columns(ref, a, b):
        return ref.at[tuple(chunks + [slice(a, b)])]

    srcs = [sa1, sa2, sa3] + [columns(win, i * third, (i + 1) * third) for i in range(3)] + [wo]
    srcs += [wsrc.at[0], wsrc.at[1], columns(wsrc.at[2], 0, 2 * pw), columns(wsrc.at[2], 2 * pw, 3 * pw)]
    P = {}
    for i, (name, src) in enumerate(zip(PIECES, srcs)):
        bits = piece_plan(dp_size, width, win.shape[-1])[i][0]
        s0 = 1 if name[0] == "A" else 0
        P[name] = Piece(bits, sems, i * nb, src, gots[i], kepts[i], s0)
    from_hbm = PIECES[:7]
    x_loads = [
        pltpu.make_async_copy(s, d, wsem.at[5 + i])
        for i, (s, d) in enumerate(((xo_h, xo), (xt_h, xt), (gsum_h, gsum)))
    ]

    def p_load(j):
        return pltpu.make_async_copy(p_h.at[2 * j : 2 * j + 2], p_s.at[j % 2], wsem.at[3 + j % 2])

    ig_copy = partner_copy(ig_s, ig_r, vsend.at[0], vrecv.at[0], me)
    tb_copy = partner_copy(tb, tb_m, vsend.at[1], vrecv.at[1], me)
    t_copies = [
        pltpu.make_async_remote_copy(
            src_ref=ts[k], dst_ref=trs[k], send_sem=vsend.at[2 + k], recv_sem=vrecv.at[2 + k],
            device_id={"dp": P["C0"].peer(k)}, device_id_type=pl.DeviceIdType.MESH,
        )
        for k in range(nb)
    ]

    @pl.when(p == 0)
    def _():
        barrier = pltpu.get_barrier_semaphore()
        everyone = [{"mp": 1 - me}] + [{"dp": P["C0"].peer(k)} for k in range(nb)]
        for device in everyone:
            pl.semaphore_signal(
                barrier, inc=1, device_id=device, device_id_type=pl.DeviceIdType.MESH
            )
        for name in from_hbm:
            P[name].load_own().start()
        pl.semaphore_wait(barrier, len(everyone))
        for name in from_hbm:
            P[name].copy(P[name].stage0).start()
        for c in x_loads[:2]:
            c.start()
        p_load(0).start()
        p_load(1).start()
        x_loads[2].start()
        for c in x_loads[:2]:
            c.wait()
        xT[:, :half] = xo[...].T
        xT[:, half:] = xt[...].T
        tb[...] = jnp.zeros_like(tb)

    for j in range(HEADS // 4):

        @pl.when(p == j)
        def _(j=j):
            if j == 1:
                p_load(2).start()
            p_load(j).wait()

    slot = p % 2
    c_off = pl.multiple_of(me * (width // 2) + p * pw, pw)
    w_copies = [
        pltpu.make_async_copy(
            w.at[:, pl.ds(c_off, pw)], wcat.at[:, i * pw : (i + 1) * pw], wsem.at[i]
        )
        for i, w in enumerate((wq, wk, wv))
    ]
    for c in w_copies:
        c.start()
    g_s[:half, :] = go[...]
    g_s[half:, :] = gt[...]
    gT[...] = g_s[...].T
    qT[...] = q_i[...].T
    dkT[...] = jnp.zeros_like(dkT)
    dvT[...] = jnp.zeros_like(dvT)
    lane = lax.broadcasted_iota(jnp.int32, (tile, pw), 1)
    low = lane < HD

    def forward(k, *names):
        for name in names:
            x = P[name]
            loaded = name in from_hbm and k == x.stage0
            if loaded:
                x.load_own().wait()
            x.forward(k, loaded)

    def at_tile(t):
        if t == 3:

            @pl.when(p == 0)
            def _():
                forward(1, "A1", "A2")

            @pl.when(p == 1)
            def _():
                forward(0, "B1", "B2", "B3")
                forward(1, "A3")
                forward(2, "A1", "A2")

            @pl.when(p == 2)
            def _():
                forward(1, "B1", "B2")
                forward(2, "A3")
                forward(0, "WO")

    for t in range(rows // tile):
        rs = slice(t * tile, (t + 1) * tile)
        a_ref = ao if t * tile < half else at
        as_ = slice(t * tile % half, t * tile % half + tile)
        g = g_s[rs, :]
        ga = g.astype(F32) * a_ref[as_, :].astype(F32)
        outs = []
        for h in range(2):
            mine = low if h == 0 else ~low
            hs = slice(h * HD, (h + 1) * HD)
            dp = mm(jnp.where(mine, g, BF16(0)), v_i[...], NT)
            delta = jnp.sum(jnp.where(mine, ga, 0.0), axis=-1, keepdims=True)
            pr = p_s[slot, h, rs, :]
            ds = (pr.astype(F32) * (dp - delta)).astype(BF16)
            outs.append(mm(ds, k_i[...]))
            dvT[hs, :] += mm(gT[hs, rs], pr)
            dkT[hs, :] += mm(qT[hs, rs], ds)
        dq = jnp.where(low, outs[0], outs[1]) * HD**-0.5
        dqkv[rs, 0:pw] = dq.astype(BF16)

        at_tile(t)

    dqkv[:, pw : 2 * pw] = (dkT[...].T * HD**-0.5).astype(BF16)
    dqkv[:, 2 * pw : 3 * pw] = dvT[...].T.astype(BF16)
    d = dqkv[...]
    wg = mm(xT[...], d).astype(BF16).reshape(wsrc.shape[1:])
    wsrc[p] = wg
    tb[0:1, pl.ds(c_off, pw)] = jnp.sum(d[:, 0:pw].astype(F32), axis=0, keepdims=True)
    tb[1:2, pl.ds(c_off, pw)] = jnp.sum(d[:, 2 * pw :].astype(F32), axis=0, keepdims=True)

    @pl.when(p == 0)
    def _():
        P["C0"].copy(0).start()

    @pl.when(p == 1)
    def _():
        P["C1"].copy(0).start()

    @pl.when(p == 2)
    def _():
        P["C2"].copy(0).start()
        P["C3"].copy(0).start()
        tb_copy.start()

    for c in w_copies:
        c.wait()
    part = mm(d, wcat[...], NT)

    @pl.when(p == 0)
    def _():
        acc[...] = part

    @pl.when(p == 1)
    def _():
        acc[...] += part

    @pl.when(p == 2)
    def _():
        ig_s[...] = (acc[half:, :] + part[half:]).astype(BF16)
        ig_copy.start()
        acc[:half, :] += part[:half]

        def next_table(k):
            t_copies[k].wait_recv()
            ts[k + 1][...] = ts[k][...] + trs[k][...]
            if k + 1 < nb:
                t_copies[k + 1].start()

        forward(0, "C0")
        tb_copy.wait_recv()
        ts[0][0:8, :] = tb[...] + tb_m[...] + vec[...]
        ts[0][8:16, :] = bi[...]
        t_copies[0].start()
        forward(1, "B3")
        forward(2, "B1", "B2")
        forward(0, "C1")
        forward(1, "WO")
        next_table(0)
        forward(1, "C0")
        forward(0, "C2", "C3")
        ig_copy.wait_recv()
        x_loads[2].wait()
        ig_o[...] = gsum[...] + (acc[:half, :] + ig_r[...].astype(F32))
        next_table(1)
        forward(2, "B3")
        forward(1, "C1")
        forward(2, "WO", "C0")
        for k in range(2, nb - 1):
            next_table(k)
        forward(1, "C2", "C3")
        forward(2, "C1")
        for i in range(3):
            wout_o[:, i * third : (i + 1) * third] = P["A%d" % (i + 1)].result()
            win_o[:, i * third : (i + 1) * third] = P["B%d" % (i + 1)].result()
        forward(2, "C2", "C3")
        wo_o[...] = P["WO"].result()
        next_table(nb - 1)
        table = ts[nb][...]
        n = width // dp_size
        m = bi_o.shape[1]
        vals = table[0:8, 0:n]
        biv = table[8:9, 0:m]
        for j in range(1, dp_size):
            vals = jnp.where(dev == j, table[0:8, j * n : (j + 1) * n], vals)
            r = 8 + (j * m) // width
            k = (j * m) % width
            biv = jnp.where(dev == j, table[r : r + 1, k : k + m], biv)
        vals_o[...] = vals
        bi_o[...] = biv
        for j in range(3):
            cs = slice(j * pw, (j + 1) * pw)
            v = P["C%d" % j].result()
            wq_o[:, cs] = v[:, :pw]
            wk_o[:, cs] = v[:, pw : 2 * pw]
            wv_o[:, cs] = v[:, 2 * pw :] if j < 2 else P["C3"].result()

        for name in PIECES:
            P[name].drain()
        ig_copy.wait_send()
        tb_copy.wait_send()
        for c in t_copies:
            c.wait_send()


def back(dp_size, xo, xt, wq, wk, wv, q, k, v, probs, ao, at, go, gt, gsum, vec, bi, sa, win, wo):
    half, width = xo.shape
    rows = 2 * half
    pairs = HEADS // 4
    pw = 2 * HD
    ff = win.shape[1]
    nb = dp_size.bit_length() - 1
    n = width // dp_size
    split = lambda a: a.reshape((2,) * nb + (n, a.shape[-1]))
    whole = lambda a: pl.BlockSpec(
        a.shape, lambda p: (0,) * a.ndim, pipeline_mode=pl.Buffered(1)
    )
    col = lambda r, w: pl.BlockSpec((r, w), lambda p: (0, p))
    hbm = pl.BlockSpec(memory_space=pl.ANY)
    vm = pl.BlockSpec(memory_space=pltpu.VMEM)
    V = pltpu.VMEM
    plan = piece_plan(dp_size, width, ff)

    def stages(last):
        return tuple(
            tuple(
                V((2,) * (nb - 1 - k) + (n, w), BF16) if k < nb - last else V((16, 128), BF16)
                for k in range(nb)
            )
            for _, w in plan
        )

    table = lambda: V((16, width), F32)
    sem = pltpu.SemaphoreType.DMA
    return pl.pallas_call(
        functools.partial(back_body, dp_size),
        grid_spec=pltpu.PrefetchScalarGridSpec(
            num_scalar_prefetch=0,
            grid=(pairs,),
            in_specs=[col(rows, pw)] * 3 + [col(half, pw)] * 4 + [whole(vec), whole(bi)] + [hbm] * 12,
            out_specs=[vm] * 9,
            scratch_shapes=[
                V((half, width), BF16),
                V((half, width), BF16),
                V((2, 2, rows, rows), BF16),
                V((half, width), F32),
                V((rows, pw), BF16),
                V((pw, rows), BF16),
                V((pw, rows), BF16),
                V((pw, rows), F32),
                V((pw, rows), F32),
                V((rows, 3 * pw), BF16),
                V((width, 3 * pw), BF16),
                V((width, rows), BF16),
                V((rows, width), F32),
                V((half, width), BF16),
                V((half, width), BF16),
                V((pairs,) + (2,) * nb + (n, 3 * pw), BF16),
                stages(0),
                stages(1),
                V((8, width), F32),
                V((8, width), F32),
                tuple(table() for _ in range(nb + 1)),
                tuple(table() for _ in range(nb)),
                sem((len(plan) * nb,)),
                sem((len(plan) * nb,)),
                sem((len(plan),)),
                sem((2 + nb,)),
                sem((2 + nb,)),
                sem((8,)),
            ],
        ),
        out_shape=[shape((half, width), F32)]
        + [shape((n, width // 2), F32)] * 4
        + [shape((n, ff), F32)] * 2
        + [shape((8, n), F32), shape((1, 2 * ff // dp_size), F32)],
        compiler_params=pltpu.CompilerParams(
            vmem_limit_bytes=60 << 20, collective_id=2, has_side_effects=True
        ),
        cost_estimate=cost(40e9, 20e6),
        name="back",
    )(q, k, v, ao, at, go, gt, vec, bi, xo, xt, probs, gsum, wq, wk, wv, *sa, split(win), split(wo))


def emit_body(big, *refs):
    ins, outs = refs[: big + 2], refs[big + 2 :]
    for i in range(big):
        outs[i][...] = ins[i][...]
    vals = ins[big][...]
    for j in range(8):
        outs[big + j][...] = vals[j]
    outs[big + 8][...] = ins[big + 1][0]


def emit(arrays, vals, bi):
    vm = pl.BlockSpec(memory_space=pltpu.VMEM)
    return pl.pallas_call(
        functools.partial(emit_body, len(arrays)),
        in_specs=[vm] * (len(arrays) + 2),
        out_specs=[vm] * (len(arrays) + 9),
        out_shape=[shape(a.shape, a.dtype) for a in arrays]
        + [shape((vals.shape[1],), F32)] * 8
        + [shape((bi.shape[1],), F32)],
        compiler_params=params(60),
        name="emit",
    )(*arrays, vals, bi)


def local_pair(
    dp_size, inputs, grad_out, lengths, rand_blocks, w_query, b_query, w_key, w_value, b_value,
    w_output, b_output, gain_one, shift_one, w_in, b_in, w_out, b_out, gain_two, shift_two,
):
    x = inputs[0]
    x_got, a_own, a_oth, a_got, q, k, v, probs = front(
        lengths, x, rand_blocks.transpose(2, 0, 1), b_query, b_value, w_query, w_key, w_value
    )
    out, gsum, ga0, ga_got, sa1, sa2, sa3, w_in_g, w_output_g, vec_g, bi_g = middle(
        dp_size, a_own, a_got, x, grad_out[0], b_output, gain_one, shift_one, b_in, b_out,
        gain_two, shift_two, w_output, w_in, w_out,
    )
    *mats, vals, bi = back(
        dp_size, x, x_got, w_query, w_key, w_value, q, k, v, probs, a_own, a_oth, ga0, ga_got,
        gsum, vec_g, bi_g, (sa1, sa2, sa3), w_in_g, w_output_g,
    )
    (
        out, input_grad, wq_p, wk_p, wv_p, wo_p, in_part, out_part, bq_p, bv_p, bo_p, g1_p, s1_p,
        b2_p, g2_p, s2_p, bi_p,
    ) = emit([out] + mats, vals, bi)
    return (
        out[None], input_grad[None], wq_p, bq_p, wk_p, wv_p, bv_p, wo_p, bo_p, g1_p, s1_p,
        in_part, bi_p, out_part, b2_p, g2_p, s2_p,
    )


def layer_norm(features, norm_gain, norm_shift):
    row_mean = jnp.mean(features, axis=-1, keepdims=True)
    centered = features - row_mean
    variance = jnp.mean(centered * centered, axis=-1, keepdims=True)
    return centered * lax.rsqrt(variance + norm_epsilon) * norm_gain + norm_shift


def gelu_tanh(features):
    return jax.nn.gelu(features, approximate=True)


def slot_table_ids(block_ids, rand_rows, length):
    valid_blocks = (length + BLK - 1) // BLK
    column = block_ids[:, None]
    columns = jnp.concatenate(
        [
            column - 1,
            column,
            column + 1,
            rand_rows,
            jnp.zeros_like(column),
            jnp.zeros_like(column) + valid_blocks - 1,
        ],
        axis=1,
    )
    in_range = (columns >= 0) & (columns < valid_blocks)
    slot_ids = jnp.arange(columns.shape[1], dtype=jnp.int32)
    earlier = slot_ids[None, :] < slot_ids[:, None]
    repeated = jnp.any(
        (columns[:, :, None] == columns[:, None, :]) & earlier[None, :, :] & in_range[:, None, :],
        axis=2,
    )
    return (jnp.clip(columns, 0, NB - 1), in_range & jnp.logical_not(repeated))


def slot_table(first_block, rand_rows, length):
    block_ids = first_block + jnp.arange(rand_rows.shape[0], dtype=jnp.int32)
    return slot_table_ids(block_ids, rand_rows, length)


def slot_mask(slot_blocks, slot_valid, length):
    positions = slot_blocks[:, :, None] * BLK + jnp.arange(BLK, dtype=jnp.int32)
    allowed = slot_valid[:, :, None] & (positions < length)
    return allowed.reshape(slot_blocks.shape[0], 1, 1, -1)


def gather_slots(whole_rows, slot_blocks):
    picked = whole_rows.reshape(NB, BLK, whole_rows.shape[1])[slot_blocks]
    return picked.reshape(slot_blocks.shape[0], slot_blocks.shape[1] * BLK, HEADS, HD)


def log_total(scores, allowed):
    masked = jnp.where(allowed, scores, negative_fill)
    top_score = jnp.max(masked, axis=-1, keepdims=True)
    return top_score + jnp.log(jnp.sum(jnp.exp(masked - top_score), axis=-1, keepdims=True))


def exp_probs(scores, allowed, totals):
    return jnp.exp(jnp.where(allowed, scores, negative_fill) - totals)


def global_targets(length, device, local_blocks):
    last_block = (length + BLK - 1) // BLK - 1
    targets = []
    for target_block in (jnp.zeros_like(last_block), last_block):
        is_owner = target_block // local_blocks == device
        local_block = jnp.clip(target_block - device * local_blocks, 0, local_blocks - 1)
        targets.append((is_owner, local_block))
    return targets


def global_scores(query_rows, key_one, length):
    scores = jnp.einsum(
        "qhd,khd->hqk",
        query_rows.reshape(BLK, HEADS, HD),
        key_one.reshape(-1, HEADS, HD),
        preferred_element_type=jnp.float32,
    ) * HD ** (-0.5)
    allowed = (jnp.arange(key_one.shape[0], dtype=jnp.int32) < length)[None, None, :]
    return (scores, allowed)


def global_forward(query_rows, key_one, value_one, length):
    scores, allowed = global_scores(query_rows, key_one, length)
    totals = log_total(scores, allowed)
    weighting = exp_probs(scores, allowed, totals).astype(jnp.bfloat16)
    out_rows = jnp.einsum(
        "hqk,khd->qhd",
        weighting,
        value_one.reshape(-1, HEADS, HD),
        preferred_element_type=jnp.float32,
    )
    return (out_rows.reshape(BLK, -1), totals)


def global_skip(query_rows, key_one, value_one, length):
    return (jnp.zeros((BLK, HEADS * HD), jnp.float32), jnp.zeros((HEADS, BLK, 1), jnp.float32))


def global_backward(query_rows, grad_rows, key_one, value_one, length, row_totals):
    score_scale = HD ** (-0.5)
    scores, allowed = global_scores(query_rows, key_one, length)
    exact_probs = exp_probs(scores, allowed, row_totals)
    grad_heads = grad_rows.reshape(BLK, HEADS, HD)
    grad_weights = jnp.einsum(
        "qhd,khd->hqk",
        grad_heads,
        value_one.reshape(-1, HEADS, HD),
        preferred_element_type=jnp.float32,
    )
    delta_sum = jnp.sum(exact_probs * grad_weights, axis=-1, keepdims=True)
    grad_scores = (exact_probs * (grad_weights - delta_sum)).astype(jnp.bfloat16)
    grad_query = (
        jnp.einsum(
            "hqk,khd->qhd",
            grad_scores,
            key_one.reshape(-1, HEADS, HD),
            preferred_element_type=jnp.float32,
        )
        * score_scale
    )
    grad_keys = (
        jnp.einsum(
            "hqk,qhd->khd",
            grad_scores,
            query_rows.reshape(BLK, HEADS, HD),
            preferred_element_type=jnp.float32,
        )
        * score_scale
    )
    grad_values = jnp.einsum(
        "hqk,qhd->khd",
        exact_probs.astype(jnp.bfloat16),
        grad_heads,
        preferred_element_type=jnp.float32,
    )
    return (
        grad_query.reshape(BLK, -1),
        grad_keys.reshape(key_one.shape[0], -1),
        grad_values.reshape(key_one.shape[0], -1),
    )


def global_back_skip(query_rows, grad_rows, key_one, value_one, length, row_totals):
    key_zeros = jnp.zeros(key_one.shape, jnp.float32)
    return (jnp.zeros((BLK, key_one.shape[1]), jnp.float32), key_zeros, key_zeros)


def attend_forward(query_one, key_one, value_one, length, rand_rows, device):
    local_blocks = rand_rows.shape[0]
    slot_blocks, slot_valid = slot_table(device * local_blocks, rand_rows, length)
    allowed = slot_mask(slot_blocks, slot_valid, length)
    query_blocks = query_one.reshape(local_blocks, BLK, HEADS, HD)
    scores = jnp.einsum(
        "nqhd,nkhd->nhqk",
        query_blocks,
        gather_slots(key_one, slot_blocks),
        preferred_element_type=jnp.float32,
    ) * HD ** (-0.5)
    totals = log_total(scores, allowed)
    weighting = exp_probs(scores, allowed, totals).astype(jnp.bfloat16)
    attended = jnp.einsum(
        "nhqk,nkhd->nqhd",
        weighting,
        gather_slots(value_one, slot_blocks),
        preferred_element_type=jnp.float32,
    ).reshape(query_one.shape[0], -1)
    global_totals = []
    for is_owner, local_block in global_targets(length, device, local_blocks):
        query_rows = lax.dynamic_slice_in_dim(query_one, local_block * BLK, BLK, 0)
        out_rows, row_totals = lax.cond(
            is_owner, global_forward, global_skip, query_rows, key_one, value_one, length
        )
        updated = lax.dynamic_update_slice_in_dim(attended, out_rows, local_block * BLK, 0)
        attended = jnp.where(is_owner, updated, attended)
        global_totals.append(row_totals)
    return (attended, totals, global_totals[0], global_totals[1])


def attend_backward(
    query_one,
    key_one,
    value_one,
    length,
    rand_rows,
    totals,
    first_totals,
    last_totals,
    grad_one,
    device,
):
    score_scale = HD ** (-0.5)
    local_blocks = rand_rows.shape[0]
    first_block = device * local_blocks
    slot_blocks, slot_valid = slot_table(first_block, rand_rows, length)
    allowed = slot_mask(slot_blocks, slot_valid, length)
    query_blocks = query_one.reshape(local_blocks, BLK, HEADS, HD)
    key_slots = gather_slots(key_one, slot_blocks)
    value_slots = gather_slots(value_one, slot_blocks)
    scores = (
        jnp.einsum("nqhd,nkhd->nhqk", query_blocks, key_slots, preferred_element_type=jnp.float32)
        * score_scale
    )
    exact_probs = exp_probs(scores, allowed, totals)
    last_block = (length + BLK - 1) // BLK - 1
    row_blocks = first_block + jnp.arange(query_one.shape[0], dtype=jnp.int32) // BLK
    is_global = (row_blocks == 0) | (row_blocks == last_block)
    grad_sparse = jnp.where(is_global[:, None], jnp.zeros_like(grad_one), grad_one)
    grad_heads = grad_sparse.reshape(local_blocks, BLK, HEADS, HD)
    grad_weights = jnp.einsum(
        "nqhd,nkhd->nhqk", grad_heads, value_slots, preferred_element_type=jnp.float32
    )
    delta_sum = jnp.sum(exact_probs * grad_weights, axis=-1, keepdims=True)
    grad_scores = (exact_probs * (grad_weights - delta_sum)).astype(jnp.bfloat16)
    grad_query = (
        jnp.einsum(
            "nhqk,nkhd->nqhd", grad_scores, key_slots, preferred_element_type=jnp.float32
        ).reshape(query_one.shape[0], -1)
        * score_scale
    )
    grad_key_slots = (
        jnp.einsum("nhqk,nqhd->nkhd", grad_scores, query_blocks, preferred_element_type=jnp.float32)
        * score_scale
    )
    grad_value_slots = jnp.einsum(
        "nhqk,nqhd->nkhd",
        exact_probs.astype(jnp.bfloat16),
        grad_heads,
        preferred_element_type=jnp.float32,
    )
    flat_ids = slot_blocks.reshape(-1)
    slot_width = BLK * query_one.shape[1]
    grad_keys = jax.ops.segment_sum(
        grad_key_slots.reshape(-1, slot_width), flat_ids, num_segments=NB
    ).reshape(-1, query_one.shape[1])
    grad_values = jax.ops.segment_sum(
        grad_value_slots.reshape(-1, slot_width), flat_ids, num_segments=NB
    ).reshape(-1, query_one.shape[1])
    for (is_owner, local_block), row_totals in zip(
        global_targets(length, device, local_blocks), (first_totals, last_totals)
    ):
        query_rows = lax.dynamic_slice_in_dim(query_one, local_block * BLK, BLK, 0)
        grad_rows = lax.dynamic_slice_in_dim(grad_one, local_block * BLK, BLK, 0)
        query_add, key_add, value_add = lax.cond(
            is_owner,
            global_backward,
            global_back_skip,
            query_rows,
            grad_rows,
            key_one,
            value_one,
            length,
            row_totals,
        )
        current = lax.dynamic_slice_in_dim(grad_query, local_block * BLK, BLK, 0)
        grad_query = lax.dynamic_update_slice_in_dim(
            grad_query, current + query_add, local_block * BLK, 0
        )
        grad_keys = grad_keys + key_add
        grad_values = grad_values + value_add
    return (grad_query, grad_keys, grad_values)


def local(
    inputs,
    grad_out,
    lengths,
    rand_blocks,
    w_query,
    b_query,
    w_key,
    w_value,
    b_value,
    w_output,
    b_output,
    gain_one,
    shift_one,
    w_in,
    b_in,
    w_out,
    b_out,
    gain_two,
    shift_two,
):
    device = lax.axis_index("mp")
    seq_count, local_rows, width = inputs.shape
    flat_in = inputs.reshape(-1, width)
    query = (jnp.dot(flat_in, w_query, preferred_element_type=jnp.float32) + b_query).astype(
        jnp.bfloat16
    )
    keys = jnp.dot(flat_in, w_key, preferred_element_type=jnp.float32).astype(jnp.bfloat16)
    values = (jnp.dot(flat_in, w_value, preferred_element_type=jnp.float32) + b_value).astype(
        jnp.bfloat16
    )
    key_all, value_all = (
        lax.all_gather(keys.reshape(seq_count, local_rows, width), "mp", axis=1, tiled=True),
        lax.all_gather(values.reshape(seq_count, local_rows, width), "mp", axis=1, tiled=True),
    )
    query_seq = query.reshape(seq_count, local_rows, width)

    def forward_item(seq_items):
        query_one, key_one, value_one, length, rand_rows = seq_items
        return attend_forward(query_one, key_one, value_one, length, rand_rows, device)

    attended, totals, first_totals, last_totals = lax.map(
        forward_item, (query_seq, key_all, value_all, lengths, rand_blocks)
    )
    attended_low = attended.reshape(-1, width).astype(jnp.bfloat16)
    summed_one = (
        flat_in.astype(jnp.float32)
        + jnp.dot(attended_low, w_output, preferred_element_type=jnp.float32)
        + b_output
    )
    first, norm_one_back = jax.vjp(
        layer_norm, summed_one, gain_one.astype(jnp.float32), shift_one.astype(jnp.float32)
    )
    first_low = first.astype(jnp.bfloat16)
    rows_all = lax.all_gather(first_low, "mp", axis=0, tiled=True)
    hidden = jnp.dot(rows_all, w_in, preferred_element_type=jnp.float32) + b_in
    active_full, gelu_back = jax.vjp(gelu_tanh, hidden)
    active = active_full.astype(jnp.bfloat16)
    feed = lax.psum_scatter(
        jnp.einsum(
            "rf,df->rd",
            lax.slice_in_dim(active, 0, first_low.shape[0] * lax.axis_size("mp"), axis=0),
            w_out,
            preferred_element_type=jnp.float32,
        ),
        "mp",
        scatter_dimension=0,
        tiled=True,
    )
    summed_two = first + feed + b_out
    output, norm_two_back = jax.vjp(
        layer_norm, summed_two, gain_two.astype(jnp.float32), shift_two.astype(jnp.float32)
    )
    grad_two, gain_two_grad, shift_two_grad = norm_two_back(
        grad_out.reshape(-1, width).astype(jnp.float32)
    )
    grad_feed = grad_two.astype(jnp.bfloat16)
    b_out_grad = jnp.sum(grad_feed, axis=0, dtype=jnp.float32)
    grads_all = lax.all_gather(grad_feed, "mp", axis=0, tiled=True)
    w_out_grad = jnp.einsum("rd,rf->df", grads_all, active, preferred_element_type=jnp.float32)
    grad_hidden = gelu_back(jnp.dot(grads_all, w_out, preferred_element_type=jnp.float32))[
        0
    ].astype(jnp.bfloat16)
    w_in_grad = jnp.einsum("rd,rf->df", rows_all, grad_hidden, preferred_element_type=jnp.float32)
    grad_first = grad_two + lax.psum_scatter(
        jnp.einsum(
            "rf,df->rd",
            lax.slice_in_dim(grad_hidden, 0, grad_feed.shape[0] * lax.axis_size("mp"), axis=0),
            w_in,
            preferred_element_type=jnp.float32,
        ),
        "mp",
        scatter_dimension=0,
        tiled=True,
    )
    b_in_grad = lax.dynamic_update_slice_in_dim(
        jnp.zeros((FF,), jnp.float32),
        jnp.sum(grad_hidden, axis=0, dtype=jnp.float32),
        device * w_in.shape[1],
        0,
    )
    grad_sum_one, gain_one_grad, shift_one_grad = norm_one_back(grad_first)
    grad_branch = grad_sum_one.astype(jnp.bfloat16)
    b_output_grad = jnp.sum(grad_branch, axis=0, dtype=jnp.float32)
    w_output_grad = jnp.einsum(
        "rd,re->de", attended_low, grad_branch, preferred_element_type=jnp.float32
    )
    grad_attended = (
        jnp.einsum("re,de->rd", grad_branch, w_output, preferred_element_type=jnp.float32)
        .astype(jnp.bfloat16)
        .reshape(seq_count, local_rows, width)
    )

    def backward_item(seq_items):
        (
            query_one,
            key_one,
            value_one,
            length,
            rand_rows,
            sparse_totals,
            first_one,
            last_one,
            grad_one,
        ) = seq_items
        return attend_backward(
            query_one,
            key_one,
            value_one,
            length,
            rand_rows,
            sparse_totals,
            first_one,
            last_one,
            grad_one,
            device,
        )

    grad_query, grad_keys, grad_values = lax.map(
        backward_item,
        (
            query_seq,
            key_all,
            value_all,
            lengths,
            rand_blocks,
            totals,
            first_totals,
            last_totals,
            grad_attended,
        ),
    )
    key_sums, value_sums = (
        lax.psum_scatter(
            grad_keys.astype(jnp.bfloat16), "mp", scatter_dimension=1, tiled=True
        ).astype(jnp.float32),
        lax.psum_scatter(
            grad_values.astype(jnp.bfloat16), "mp", scatter_dimension=1, tiled=True
        ).astype(jnp.float32),
    )
    grad_q_low = grad_query.reshape(-1, width).astype(jnp.bfloat16)
    grad_k_low = key_sums.reshape(-1, width).astype(jnp.bfloat16)
    grad_v_low = value_sums.reshape(-1, width).astype(jnp.bfloat16)
    input_grad = grad_sum_one + jnp.einsum(
        "re,de->rd", grad_q_low, w_query, preferred_element_type=jnp.float32
    )
    input_grad = input_grad + jnp.einsum(
        "re,de->rd", grad_k_low, w_key, preferred_element_type=jnp.float32
    )
    input_grad = input_grad + jnp.einsum(
        "re,de->rd", grad_v_low, w_value, preferred_element_type=jnp.float32
    )
    w_query_grad = jnp.einsum("rd,re->de", flat_in, grad_q_low, preferred_element_type=jnp.float32)
    w_key_grad = jnp.einsum("rd,re->de", flat_in, grad_k_low, preferred_element_type=jnp.float32)
    w_value_grad = jnp.einsum("rd,re->de", flat_in, grad_v_low, preferred_element_type=jnp.float32)
    b_query_grad = jnp.sum(grad_q_low, axis=0, dtype=jnp.float32)
    b_value_grad = jnp.sum(grad_v_low, axis=0, dtype=jnp.float32)
    reduced = (
        lax.psum_scatter(
            w_query_grad.astype(jnp.bfloat16), "dp", scatter_dimension=0, tiled=True
        ).astype(jnp.float32),
        lax.psum_scatter(
            w_key_grad.astype(jnp.bfloat16), "dp", scatter_dimension=0, tiled=True
        ).astype(jnp.float32),
        lax.psum_scatter(
            w_value_grad.astype(jnp.bfloat16), "dp", scatter_dimension=0, tiled=True
        ).astype(jnp.float32),
        lax.psum_scatter(
            w_output_grad.astype(jnp.bfloat16), "dp", scatter_dimension=0, tiled=True
        ).astype(jnp.float32),
        lax.psum_scatter(
            w_in_grad.astype(jnp.bfloat16), "dp", scatter_dimension=0, tiled=True
        ).astype(jnp.float32),
        lax.psum_scatter(
            w_out_grad.astype(jnp.bfloat16), "dp", scatter_dimension=0, tiled=True
        ).astype(jnp.float32),
        lax.psum_scatter(
            b_query_grad.astype(jnp.bfloat16), "dp", scatter_dimension=0, tiled=True
        ).astype(jnp.float32),
        lax.psum_scatter(
            b_value_grad.astype(jnp.bfloat16), "dp", scatter_dimension=0, tiled=True
        ).astype(jnp.float32),
        lax.psum_scatter(
            b_output_grad.astype(jnp.bfloat16), "dp", scatter_dimension=0, tiled=True
        ).astype(jnp.float32),
        lax.psum_scatter(
            gain_one_grad.astype(jnp.bfloat16), "dp", scatter_dimension=0, tiled=True
        ).astype(jnp.float32),
        lax.psum_scatter(
            shift_one_grad.astype(jnp.bfloat16), "dp", scatter_dimension=0, tiled=True
        ).astype(jnp.float32),
        lax.psum_scatter(
            b_in_grad.astype(jnp.bfloat16), "dp", scatter_dimension=0, tiled=True
        ).astype(jnp.float32),
        lax.psum_scatter(
            b_out_grad.astype(jnp.bfloat16), "dp", scatter_dimension=0, tiled=True
        ).astype(jnp.float32),
        lax.psum_scatter(
            gain_two_grad.astype(jnp.bfloat16), "dp", scatter_dimension=0, tiled=True
        ).astype(jnp.float32),
        lax.psum_scatter(
            shift_two_grad.astype(jnp.bfloat16), "dp", scatter_dimension=0, tiled=True
        ).astype(jnp.float32),
    )
    query_part, key_part_out, value_part, output_part = (
        lax.psum_scatter(
            reduced[0].astype(jnp.bfloat16), "mp", scatter_dimension=1, tiled=True
        ).astype(jnp.float32),
        lax.psum_scatter(
            reduced[1].astype(jnp.bfloat16), "mp", scatter_dimension=1, tiled=True
        ).astype(jnp.float32),
        lax.psum_scatter(
            reduced[2].astype(jnp.bfloat16), "mp", scatter_dimension=1, tiled=True
        ).astype(jnp.float32),
        lax.psum_scatter(
            reduced[3].astype(jnp.bfloat16), "mp", scatter_dimension=1, tiled=True
        ).astype(jnp.float32),
    )
    in_part = reduced[4]
    out_part = reduced[5]
    vectors = lax.psum(
        (
            reduced[6],
            reduced[7],
            reduced[8],
            reduced[9],
            reduced[10],
            reduced[11],
            reduced[12],
            reduced[13],
            reduced[14],
        ),
        "mp",
    )
    return (
        output.astype(jnp.bfloat16).reshape(seq_count, local_rows, width),
        input_grad.reshape(seq_count, local_rows, width),
        query_part,
        vectors[0],
        key_part_out,
        value_part,
        vectors[1],
        output_part,
        vectors[2],
        vectors[3],
        vectors[4],
        in_part,
        vectors[5],
        out_part,
        vectors[6],
        vectors[7],
        vectors[8],
    )


def solution(mesh):
    in_specs = (
        P("dp", "mp", None),
        P("dp", "mp", None),
        P("dp"),
        P("dp", "mp", None),
        P(),
        P(),
        P(),
        P(),
        P(),
        P(),
        P(),
        P(),
        P(),
        P(None, "mp"),
        P("mp"),
        P(None, "mp"),
        P(),
        P(),
        P(),
    )
    out_specs = (
        P("dp", "mp", None),
        P("dp", "mp", None),
        P("dp", "mp"),
        P("dp"),
        P("dp", "mp"),
        P("dp", "mp"),
        P("dp"),
        P("dp", "mp"),
        P("dp"),
        P("dp"),
        P("dp"),
        P("dp", "mp"),
        P("dp"),
        P("dp", "mp"),
        P("dp"),
        P("dp"),
        P("dp"),
    )
    sizes = dict(mesh.shape)
    if sizes["mp"] == 2 and sizes["dp"] == 16:
        local_fn = functools.partial(local_pair, sizes["dp"])
    else:
        local_fn = local
    return jax.shard_map(local_fn, mesh=mesh, in_specs=in_specs, out_specs=out_specs, check_vma=False)
```

```python
import functools

import jax
import jax.numpy as jnp
from jax import lax
from jax.experimental import pallas as pl
from jax.experimental.pallas import tpu as pltpu
from jax.sharding import PartitionSpec as P

HEADS = 12
HD = 64
FF = 3072
BLK = 64
NB = 16


negative_fill = -1000000000.0
norm_epsilon = 1e-12


F32 = jnp.float32
BF16 = jnp.bfloat16
NN = (((1,), (0,)), ((), ()))
NT = (((1,), (1,)), ((), ()))
TN = (((0,), (0,)), ((), ()))


def mm(a, b, dims=NN):
    return lax.dot_general(a, b, dims, preferred_element_type=F32)


def params(mib=56):
    return pltpu.CompilerParams(vmem_limit_bytes=mib << 20)


def cost(flops, nbytes, trans=0):
    return pl.CostEstimate(flops=int(flops), bytes_accessed=int(nbytes), transcendentals=int(trans))


def shape(dims, dtype):
    return jax.ShapeDtypeStruct(dims, dtype)


def row_stats(u):
    mean = jnp.mean(u, axis=-1, keepdims=True)
    cen = u - mean
    var = jnp.mean(cen * cen, axis=-1, keepdims=True)
    rs = lax.rsqrt(var + norm_epsilon)
    return cen * rs, rs


def partner_copy(src, dst, send, recv, me):
    return pltpu.make_async_remote_copy(
        src_ref=src, dst_ref=dst, send_sem=send, recv_sem=recv,
        device_id={"mp": 1 - me}, device_id_type=pl.DeviceIdType.MESH,
    )


def front_body(
    lengths, x, rand, bq, bv, wq, wk, wv,
    x_got, a_own, a_oth, q_o, k_o, v_o, p_h,
    later_loads, middle_part, xg_s, ag_s, p_s, w_s, b_s, rand_s, rand_r, bias, wsem, psem, send, recv,
):
    me = lax.axis_index("mp")
    p = pl.program_id(0)
    half, width = x.shape
    rows = 2 * half
    hw = width // 2
    pw = 2 * HD
    nb = rows // BLK
    tile = 256
    x_copy = partner_copy(x, xg_s, send.at[0], recv.at[0], me)
    rand_copy = partner_copy(rand_s, rand_r, send.at[1], recv.at[1], me)

    def w_loads(j):
        own = pl.ds(pl.multiple_of(me * hw + j * pw, pw), pw)
        return [
            pltpu.make_async_copy(
                w.at[:, own], w_s.at[j, :, i * pw : (i + 1) * pw], wsem.at[3 * j + i]
            )
            for i, w in enumerate((wq, wk, wv))
        ]

    slot = p % 2

    def p_store(slot_j, j, i):
        r0, h = units[i]
        return pltpu.make_async_copy(
            p_s.at[slot_j, h, r0 : r0 + tile], p_h.at[2 * j + h, r0 : r0 + tile],
            psem.at[slot_j, i],
        )

    order = [half + t * tile for t in range(half // tile)] + [t * tile for t in range(half // tile)]
    units = [(r0, h) for r0 in order for h in range(2)]

    @pl.when(p == 0)
    def _():
        barrier = pltpu.get_barrier_semaphore()
        dev = lax.axis_index("dp")
        everyone = [{"mp": 1 - me}]
        everyone += [{"dp": dev + 2**b * (1 - 2 * ((dev // 2**b) % 2))} for b in range(3)]
        for device in everyone:
            pl.semaphore_signal(
                barrier, inc=1, device_id=device, device_id_type=pl.DeviceIdType.MESH
            )
        for j in range(hw // pw):
            for c in w_loads(j):
                c.start()
        for c in later_loads:
            c.start()
        rand_s[...] = jnp.zeros_like(rand_s)
        for j in range(rand.shape[0]):
            rand_s[j : j + 1, : nb // 2] = rand[j]
        b_s[0:1, :] = bq[...].astype(F32)[None, :]
        b_s[1:2, :] = bv[...].astype(F32)[None, :]
        pl.semaphore_wait(barrier, len(everyone))
        x_copy.start()
        rand_copy.start()

    cols = pl.ds(pl.multiple_of(p * pw, pw), pw)
    bias_cols = pl.ds(pl.multiple_of(me * hw + p * pw, pw), pw)

    for j in range(hw // pw):

        @pl.when(p == j)
        def _(j=j):
            for c in w_loads(j):
                c.wait()
            if j == 2:
                for i in range(len(units)):
                    p_store(0, 0, i).wait()

    def project(i, xr):
        rs = slice(i * half, (i + 1) * half)
        qkv = mm(xr[...], w_s[p])
        q_o[rs, :] = (qkv[:, :pw] + b_s[0:1, bias_cols]).astype(BF16)
        k_o[rs, :] = qkv[:, pw : 2 * pw].astype(BF16)
        v_o[rs, :] = (qkv[:, 2 * pw :] + b_s[1:2, bias_cols]).astype(BF16)

    project(0, x)

    @pl.when(p == 0)
    def _():
        rand_copy.wait_recv()
        ln = lengths[0]
        last = (ln + BLK - 1) // BLK - 1
        lb = lax.broadcasted_iota(jnp.int32, (nb, rows), 0)
        kp = lax.broadcasted_iota(jnp.int32, (nb, rows), 1)
        qb = jnp.where(lb < nb // 2, lb + (nb // 2) * me, lb - (nb // 2) * me)
        kpos = jnp.where(kp < half, kp + half * me, kp - half * me)
        kb = kpos // BLK
        ok = (jnp.abs(kb - qb) <= 1) | (kb == 0) | (kb == last)
        listed = [r[...].astype(F32).T[: nb // 2] for r in (rand_s, rand_r)]
        both = jnp.concatenate(listed, axis=0).astype(jnp.int32)
        for j in range(rand.shape[0]):
            ok = ok | (kb == both[:, j : j + 1])
        ok = ok | (qb == 0) | (qb == last)
        ok = ok & (kpos < ln)
        table = jnp.where(ok, 0.0, -1e30).astype(F32)
        for b in range(nb):
            bias[b] = jnp.broadcast_to(table[b : b + 1, :], (8, rows))
        x_copy.wait_recv()
        x_got[...] = xg_s[...]

    project(1, xg_s)

    low = lax.broadcasted_iota(jnp.int32, (tile, pw), 1) < HD
    scores, probs, outs = {}, {}, {}

    def score(i):
        r0, h = units[i]
        q = q_o[r0 : r0 + tile, :] * BF16(HD**-0.5)
        s = mm(jnp.where(low if h == 0 else ~low, q, BF16(0)), k_o[...], NT)
        b0 = r0 // BLK
        s = s.reshape(tile // BLK, BLK // 8, 8, rows) + bias[b0 : b0 + tile // BLK][:, None]
        scores[i] = s.reshape(tile, rows)

    def attend(i):
        r0, h = units[i]
        outs[i] = mm(probs.pop(i), v_o[...])
        if h == 1:
            a = jnp.where(low, outs.pop(i - 1), outs.pop(i)).astype(BF16)
            if r0 < half:
                a_own[r0 : r0 + tile, cols] = a
            else:
                a_oth[r0 - half : r0 - half + tile, cols] = a
                if r0 + tile == rows:
                    partner_copy(
                        a_oth.at[:, cols], ag_s.at[:, cols], send.at[2 + p], recv.at[2 + p], me
                    ).start()

    score(0)
    for i, (r0, h) in enumerate(units):
        if i + 1 < len(units):
            score(i + 1)
        s = scores.pop(i)
        e = jnp.exp(s - jnp.max(s, axis=-1, keepdims=True))
        pr = (e * (1.0 / jnp.sum(e, axis=-1, keepdims=True))).astype(BF16)
        p_s[slot, h, r0 : r0 + tile, :] = pr
        p_store(slot, p, i).start()
        probs[i] = pr
        if i >= 1:
            attend(i - 1)
    attend(len(units) - 1)

    @pl.when(p == pl.num_programs(0) - 1)
    def _():
        x_copy.wait_send()
        rand_copy.wait_send()
        for j in range(hw // pw):
            cs = slice(j * pw, (j + 1) * pw)
            c = partner_copy(a_oth.at[:, cs], ag_s.at[:, cs], send.at[2 + j], recv.at[2 + j], me)
            c.wait_send()
            c.wait_recv()
        middle_part(ag_s)
        for j in range(1, hw // pw):
            for i in range(len(units)):
                p_store(j % 2, j, i).wait()


class Piece:
    def __init__(self, bits, sems, base, src, got, kept, stage0=0):
        self.bits = bits
        self.send, self.recv, self.load = sems
        self.base = base
        self.src, self.got, self.kept = src, got, kept
        self.stage0 = stage0
        self.dev = lax.axis_index("dp")

    def mine(self, k):
        return (self.dev // 2 ** self.bits[k]) % 2

    def peer(self, k):
        return self.dev + 2 ** self.bits[k] * (1 - 2 * self.mine(k))

    def side(self, k, bit, lead=None):
        left = sorted(self.bits[k:], reverse=True)
        where = left.index(self.bits[k])
        idx = [slice(None)] * len(left) if lead is None else list(lead[:where]) + [None] + list(lead[where:])
        idx[where] = bit
        return tuple(idx)

    def source(self, k):
        return self.src if k == self.stage0 else self.kept[k - 1]

    def copy(self, k):
        i = self.base + k
        return pltpu.make_async_remote_copy(
            src_ref=self.source(k).at[self.side(k, 1 - self.mine(k))], dst_ref=self.got[k],
            send_sem=self.send.at[i], recv_sem=self.recv.at[i],
            device_id={"dp": self.peer(k)}, device_id_type=pl.DeviceIdType.MESH,
        )

    def load_own(self):
        k = self.stage0
        return pltpu.make_async_copy(
            self.src.at[self.side(k, self.mine(k))], self.kept[k], self.load.at[self.base // len(self.bits)]
        )

    def total(self, k, lead, loaded):
        if loaded:
            own = self.kept[k][lead]
        else:
            own = self.source(k)[self.side(k, self.mine(k), lead)]
        return own.astype(F32) + self.got[k][lead].astype(F32)

    def add(self, k, loaded=False):
        free = len(self.bits) - 1 - k

        def step(i, carry):
            lead = tuple((i // 2 ** (free - 1 - j)) % 2 for j in range(free))
            self.kept[k][lead] = self.total(k, lead, loaded).astype(BF16)
            return carry

        lax.fori_loop(0, 2**free, step, 0)

    def forward(self, k, loaded=False):
        self.copy(k).wait_recv()
        self.add(k, loaded)
        self.copy(k + 1).start()

    def result(self):
        k = len(self.bits) - 1
        self.copy(k).wait_recv()
        return self.total(k, (), False)

    def drain(self):
        for k in range(self.stage0, len(self.bits)):
            self.copy(k).wait_send()


def bit_orders(dp_size):
    nb = dp_size.bit_length() - 1
    rest = list(range(2, nb))
    return [0, 1] + rest, [1, 0] + rest, rest + [0, 1]


def gelu_and_slope(v):
    k0 = 0.7978845608028654
    k1 = 0.044715
    v2 = v * v
    t = jnp.tanh(v * (k0 + (k0 * k1) * v2))
    hp = 0.5 * t + 0.5
    return v * hp, hp + (0.5 * v) * (1.0 - t * t) * (k0 + (3 * k0 * k1) * v2)


def norm_back(e, n, rs, gain):
    eg = e * gain
    return (eg - jnp.mean(eg, -1, keepdims=True) - n * jnp.mean(eg * n, -1, keepdims=True)) * rs


def middle_body(
    dp_size, loads, a_own, a_got, x, gout, b_output, gain1, shift1, b_in, b_out, gain2, shift2,
    out_h, gsum_h, ga_o, gat_o, sa1, sa2, sa3, win_h, wo_g, vec_o, bi_o,
    out_o, gsum_o, win_g, gat_r,
    fl, feed_s, feed_g, gf, part_s, part_g, gat_s, wo_s, wo_r, vec_s, vec_r, bi_s, bi_s2, bi_r, wout_g, got_a1, got_a2, got_a3,
    w_o, w_in, w_out, act, gh, u_s, first_s, own_s, gtwo_s,
    store_sem, send_sem, recv_sem, a_send_sem, a_recv_sem,
):
    me = lax.axis_index("mp")
    half, width = x.shape
    hw = width // 2
    tile = 256
    tiles = half // tile
    cut = sa1.shape[-1]
    nb = dp_size.bit_length() - 1
    sems = (a_send_sem, a_recv_sem, None)
    chunks = [slice(None)] * (nb + 1)
    outs_a = [
        Piece(
            bits, sems, i * nb, wout_g.at[tuple(chunks + [slice(i * cut, (i + 1) * cut)])],
            (g,), (s,),
        )
        for i, (bits, g, s) in enumerate(
            zip(bit_orders(dp_size), (got_a1, got_a2, got_a3), (sa1, sa2, sa3))
        )
    ]
    stores = [
        pltpu.make_async_copy(src, dst, store_sem.at[i])
        for i, (src, dst) in enumerate(((out_o, out_h), (win_g, win_h), (gsum_o, gsum_h)))
    ]
    def copy(src, dst, i):
        return partner_copy(src, dst, send_sem.at[i], recv_sem.at[i], me)

    for c in loads:
        c.wait()

    def rows(t):
        return pl.ds(pl.multiple_of(t * tile, tile), tile)

    def fl_copy(t):
        return copy(fl.at[0, rows(t)], fl.at[1, rows(t)], 1 + t)

    def feed_copy(t):
        return copy(feed_s.at[rows(t)], feed_g.at[rows(t)], 3 + t)

    def gf_copy(t):
        return copy(gf.at[0, rows(t)], gf.at[1, rows(t)], 5 + t)

    def part_copy(t):
        return copy(part_s.at[rows(t)], part_g.at[rows(t)], 7 + t)

    def ga_copy(t):
        return copy(gat_s.at[rows(t)], gat_r.at[rows(t)], 9 + t)

    own_o = pl.ds(pl.multiple_of(me * hw, hw), hw)
    got_o = pl.ds(pl.multiple_of((1 - me) * hw, hw), hw)

    def project(t, carry):
        r = rows(t)
        u = x[r, :].astype(F32) + (
            mm(a_own[r, :], w_o[own_o, :]) + mm(a_got[r, :], w_o[got_o, :])
        ) + b_output[...].astype(F32)[None, :]
        n, _ = row_stats(u)
        first = n * gain1[...].astype(F32)[None, :] + shift1[...].astype(F32)[None, :]
        u_s[r, :] = u
        first_s[r, :] = first
        fl[0, r, :] = first.astype(BF16)
        fl_copy(t).start()
        return carry

    lax.fori_loop(0, tiles, project, 0)

    def feed_forward(i, t):
        r = rows(t)
        v = mm(fl[i, r, :], w_in[...]) + b_in[...].astype(F32)[None, :]
        a, s = gelu_and_slope(v)
        a = a.astype(BF16)
        act[i, r, :] = a
        gh[i, r, :] = s.astype(BF16)
        return mm(a, w_out[...], NT)

    def forward_own(t, carry):
        own_s[rows(t), :] = feed_forward(0, t)
        return carry

    def forward_got(t, carry):
        fl_copy(t).wait_recv()
        feed_s[rows(t), :] = feed_forward(1, t).astype(BF16)
        feed_copy(t).start()
        return carry

    lax.fori_loop(0, tiles, forward_own, 0)
    lax.fori_loop(0, tiles, forward_got, 0)

    vec_s[...] = jnp.zeros_like(vec_s)

    def add_vec(i, value):
        vec_s[i : i + 1, :] += jnp.sum(value, 0, keepdims=True)

    def second_norm(t, carry):
        r = rows(t)
        feed_copy(t).wait_recv()
        u = first_s[r, :] + (own_s[r, :] + feed_g[r, :].astype(F32)) + b_out[...].astype(F32)[None, :]
        n, rs = row_stats(u)
        gain = gain2[...].astype(F32)[None, :]
        out_o[r, :] = (n * gain + shift2[...].astype(F32)[None, :]).astype(BF16)
        e = gout[r, :].astype(F32)
        d = norm_back(e, n, rs, gain)
        low = d.astype(BF16)
        gtwo_s[r, :] = d
        gf[0, r, :] = low
        gf_copy(t).start()
        add_vec(6, e * n)
        add_vec(7, e)
        add_vec(5, low.astype(F32))
        return carry

    lax.fori_loop(0, tiles, second_norm, 0)
    stores[0].start()
    bi_s[...] = jnp.zeros_like(bi_s)

    def feed_back(i, t):
        r = rows(t)
        g = (mm(gf[i, r, :], w_out[...]) * gh[i, r, :].astype(F32)).astype(BF16)
        gh[i, r, :] = g
        bi_s[0:1, :] += jnp.sum(g.astype(F32), 0, keepdims=True)
        return mm(g, w_in[...], NT)

    def back_own(t, carry):
        own_s[rows(t), :] = feed_back(0, t)
        return carry

    def wait_gf(t, carry):
        gf_copy(t).wait_recv()
        return carry

    def back_got(t, carry):
        part_s[rows(t), :] = feed_back(1, t).astype(BF16)
        part_copy(t).start()
        return carry

    lax.fori_loop(0, tiles, back_own, 0)
    lax.fori_loop(0, tiles, wait_gf, 0)

    def out_weights(j, carry):
        c = pl.ds(pl.multiple_of(j * hw, hw), hw)
        total = mm(gf[0, :, c], act[0], TN) + mm(gf[1, :, c], act[1], TN)
        wout_g[j] = total.astype(BF16).reshape(wout_g.shape[1:])
        return carry

    lax.fori_loop(0, 2, out_weights, 0)
    for a in outs_a:
        a.copy(0).start()
    lax.fori_loop(0, tiles, back_got, 0)

    def weights(out, lhs, rhs):
        def step(j, carry):
            c = pl.ds(pl.multiple_of(j * tile, tile), tile)
            out[c, :] = (
                mm(lhs[0, :, c], rhs[0], TN) + mm(lhs[1, :, c], rhs[1], TN)
            ).astype(BF16)
            return carry

        lax.fori_loop(0, width // tile, step, 0)

    weights(win_g, fl, gh)
    stores[1].start()

    def first_norm(t, carry):
        r = rows(t)
        part_copy(t).wait_recv()
        e = gtwo_s[r, :] + own_s[r, :] + part_g[r, :].astype(F32)
        n, rs = row_stats(u_s[r, :])
        d = norm_back(e, n, rs, gain1[...].astype(F32)[None, :])
        low = d.astype(BF16)
        gsum_o[r, :] = d
        gout[r, :] = low
        gat_s[r, :] = mm(low, w_o[got_o, :], NT).astype(BF16)
        ga_copy(t).start()
        ga_o[r, :] = mm(low, w_o[own_o, :], NT).astype(BF16)
        add_vec(3, e * n)
        add_vec(4, e)
        add_vec(2, low.astype(F32))
        return carry

    lax.fori_loop(0, tiles, first_norm, 0)
    stores[2].start()
    vec_copy = copy(vec_s, vec_r, 11)
    vec_copy.start()
    bi_s2[0:1, :] = bi_s[0:1, :width]
    bi_s2[1:2, :] = bi_s[0:1, width:]
    bi_copy = copy(bi_s2, bi_r, 12)
    bi_copy.start()
    cols_own = own_o
    cols_got = got_o
    wo_s[own_o, :] = mm(a_own[...], gout[:, cols_got], TN).astype(BF16)
    wo_s[got_o, :] = mm(a_got[...], gout[:, cols_got], TN).astype(BF16)
    wo_copy = copy(wo_s, wo_r, 13)
    wo_copy.start()
    own_part = mm(a_own[...], gout[:, cols_own], TN)
    got_part = mm(a_got[...], gout[:, cols_own], TN)
    wo_copy.wait_recv()
    wo_g[own_o, :] = (own_part + wo_r[own_o, :].astype(F32)).astype(BF16)
    wo_g[got_o, :] = (got_part + wo_r[got_o, :].astype(F32)).astype(BF16)
    vec_copy.wait_recv()
    vec_o[...] = vec_s[...] + vec_r[...]
    bi_copy.wait_recv()
    bi_o[...] = jnp.zeros_like(bi_o)
    first_core = me == 0
    bi_o[0:2, :] = jnp.where(first_core, bi_s2[0:2, :], bi_r[0:2, :])
    bi_o[2:4, :] = jnp.where(first_core, bi_r[0:2, :], bi_s2[0:2, :])
    for a in outs_a:
        a.copy(0).wait_recv()
        a.add(0)

    def finish(t, carry):
        ga_copy(t).wait_recv()
        fl_copy(t).wait_send()
        feed_copy(t).wait_send()
        gf_copy(t).wait_send()
        part_copy(t).wait_send()
        ga_copy(t).wait_send()
        return carry

    lax.fori_loop(0, tiles, finish, 0)
    gat_o[...] = gat_r[...]
    for c in stores:
        c.wait()
    for a in outs_a:
        a.copy(0).wait_send()
    vec_copy.wait_send()
    bi_copy.wait_send()
    wo_copy.wait_send()


def first_half_body(dp_size, *refs):
    ins, refs = refs[:19], refs[19:]
    outs, refs = refs[:18], refs[18:]
    mine, (gout, load_sem), rest = refs[:12], refs[12:14], refs[14:]
    lengths, x, rand, bq, bv, wq, wk, wv, gout_h = ins[:9]
    vectors, weights_h = ins[9:16], ins[16:]
    weights = [rest[i] for i in (22, 23, 24)]
    loads = [
        pltpu.make_async_copy(a, b, load_sem.at[i])
        for i, (a, b) in enumerate(zip((gout_h,) + tuple(weights_h), [gout] + weights))
    ]

    def middle_part(a_got):
        middle_body(
            dp_size, loads, outs[1], a_got, x, gout, *vectors, *outs[7:], *rest
        )

    front_body(lengths, x, rand, bq, bv, wq, wk, wv, *outs[:7], loads, middle_part, *mine)


def first_half(dp_size, lengths, x, rand, bq, bv, wq, wk, wv, gout, vectors, w_o, w_in, w_out):
    half, width = x.shape
    rows = 2 * half
    pairs = HEADS // 4
    pw = 2 * HD
    hw = width // 2
    ff = w_in.shape[1]
    nb = dp_size.bit_length() - 1
    n = width // dp_size
    part = (2,) * (nb - 1) + (n, ff // 3)
    vm = pl.BlockSpec(memory_space=pltpu.VMEM)
    hbm = pl.BlockSpec(memory_space=pl.ANY)
    col = pl.BlockSpec((rows, pw), lambda p: (0, p))
    V = pltpu.VMEM
    sem = pltpu.SemaphoreType.DMA
    return pl.pallas_call(
        functools.partial(first_half_body, dp_size),
        grid_spec=pltpu.PrefetchScalarGridSpec(
            num_scalar_prefetch=0,
            grid=(pairs,),
            in_specs=[pl.BlockSpec(memory_space=pltpu.SMEM)] + [vm] * 4 + [hbm] * 4 + [vm] * 7 + [hbm] * 3,
            out_specs=[vm] * 3 + [col] * 3 + [hbm] + [hbm] * 2 + [vm] * 5 + [hbm] + [vm] * 3,
            scratch_shapes=[
                V((half, width), BF16),
                V((half, hw), BF16),
                V((2, 2, rows, rows), BF16),
                V((pairs, width, 3 * pw), BF16),
                V((8, width), F32),
                V((8, 128), jnp.int32),
                V((8, 128), jnp.int32),
                V((rows // BLK, 8, rows), F32),
                sem((3 * pairs,)),
                sem((2, 8)),
                sem((2 + pairs,)),
                sem((2 + pairs,)),
                V((half, width), BF16),
                sem((4,)),
                V((half, width), BF16),
                V((half, width), F32),
                V((width, ff), BF16),
                V((half, hw), BF16),
                V((2, half, width), BF16),
                V((half, width), BF16),
                V((half, width), BF16),
                V((2, half, width), BF16),
                V((half, width), BF16),
                V((half, width), BF16),
                V((half, hw), BF16),
                V((width, hw), BF16),
                V((width, hw), BF16),
                V((8, width), F32),
                V((8, width), F32),
                V((8, ff), F32),
                V((8, width), F32),
                V((8, width), F32),
                V((2,) * nb + (n, ff), BF16),
                V(part, BF16),
                V(part, BF16),
                V(part, BF16),
                V((width, width), BF16),
                V((width, ff), BF16),
                V((width, ff), BF16),
                V((2, half, ff), BF16),
                V((2, half, ff), BF16),
                V((half, width), F32),
                V((half, width), F32),
                V((half, width), F32),
                V((half, width), F32),
                pltpu.SemaphoreType.DMA((3,)),
                pltpu.SemaphoreType.DMA((14,)),
                pltpu.SemaphoreType.DMA((14,)),
                pltpu.SemaphoreType.DMA((3 * nb,)),
                pltpu.SemaphoreType.DMA((3 * nb,)),
            ],
        ),
        out_shape=[shape((half, width), BF16)]
        + [shape((half, hw), BF16)] * 2
        + [shape((rows, hw), BF16)] * 3
        + [shape((2 * pairs, rows, rows), BF16)]
        + [
            shape((half, width), BF16),
            shape((half, width), F32),
            shape((half, hw), BF16),
            shape((half, hw), BF16),
            shape(part, BF16),
            shape(part, BF16),
            shape(part, BF16),
            shape((width, ff), BF16),
            shape((width, hw), BF16),
            shape((8, width), F32),
            shape((8, width), F32),
        ],
        compiler_params=pltpu.CompilerParams(
            vmem_limit_bytes=63 << 20, collective_id=1, has_side_effects=True
        ),
        cost_estimate=cost(37e9, 40e6, 6 * rows * rows),
        name="first_half",
    )(lengths, x, rand, bq, bv, wq, wk, wv, gout, *vectors, w_o, w_in, w_out)


PIECES = ("A1", "A2", "A3", "B1", "B2", "B3", "WO", "C0", "C1", "C2", "C3")


def piece_plan(dp_size, width, ff):
    x, y, z = bit_orders(dp_size)
    third, pw = ff // 3, 2 * HD
    return (
        (x, third), (y, third), (z, third), (x, third), (y, third), (z, third), (y, width // 2),
        (x, 3 * pw), (y, 3 * pw), (x, 2 * pw), (y, pw),
    )


def back_body(
    dp_size, q_i, k_i, v_i, ao, at, go, gt, vec, bi,
    xo_h, xt_h, p_h, gsum_h, wq, wk, wv, sa1, sa2, sa3, win, wo,
    ig_o, wq_o, wk_o, wv_o, wo_o, win_o, wout_o, vals_o, bi_o,
    xo, xt, p_s, gsum, g_s, gT, qT, dkT, dvT, dqkv, wcat, xT, acc, ig_s, ig_r, wsrc, gots, kepts,
    tb, tb_m, ts, trs, send, recv, lsem, vsend, vrecv, wsem,
):
    half, width = ig_o.shape
    rows = 2 * half
    pw = 2 * HD
    tile = 256
    p = pl.program_id(0)
    me = lax.axis_index("mp")
    dev = lax.axis_index("dp")
    nb = dp_size.bit_length() - 1
    sems = (send, recv, lsem)
    chunks = [slice(None)] * (nb + 1)
    third = sa1.shape[-1]

    def columns(ref, a, b):
        return ref.at[tuple(chunks + [slice(a, b)])]

    srcs = [sa1, sa2, sa3] + [columns(win, i * third, (i + 1) * third) for i in range(3)] + [wo]
    srcs += [wsrc.at[0], wsrc.at[1], columns(wsrc.at[2], 0, 2 * pw), columns(wsrc.at[2], 2 * pw, 3 * pw)]
    P = {}
    for i, (name, src) in enumerate(zip(PIECES, srcs)):
        bits = piece_plan(dp_size, width, win.shape[-1])[i][0]
        s0 = 1 if name[0] == "A" else 0
        P[name] = Piece(bits, sems, i * nb, src, gots[i], kepts[i], s0)
    from_hbm = PIECES[:7]
    x_loads = [
        pltpu.make_async_copy(s, d, wsem.at[5 + i])
        for i, (s, d) in enumerate(((xo_h, xo), (xt_h, xt), (gsum_h, gsum)))
    ]

    def p_load(j):
        return pltpu.make_async_copy(p_h.at[2 * j : 2 * j + 2], p_s.at[j % 2], wsem.at[3 + j % 2])

    ig_copy = partner_copy(ig_s, ig_r, vsend.at[0], vrecv.at[0], me)
    tb_copy = partner_copy(tb, tb_m, vsend.at[1], vrecv.at[1], me)
    t_copies = [
        pltpu.make_async_remote_copy(
            src_ref=ts[k], dst_ref=trs[k], send_sem=vsend.at[2 + k], recv_sem=vrecv.at[2 + k],
            device_id={"dp": P["C0"].peer(k)}, device_id_type=pl.DeviceIdType.MESH,
        )
        for k in range(nb)
    ]

    @pl.when(p == 0)
    def _():
        barrier = pltpu.get_barrier_semaphore()
        everyone = [{"mp": 1 - me}] + [{"dp": P["C0"].peer(k)} for k in range(nb)]
        for device in everyone:
            pl.semaphore_signal(
                barrier, inc=1, device_id=device, device_id_type=pl.DeviceIdType.MESH
            )
        for name in from_hbm:
            P[name].load_own().start()
        pl.semaphore_wait(barrier, len(everyone))
        for name in from_hbm:
            P[name].copy(P[name].stage0).start()
        for c in x_loads[:2]:
            c.start()
        p_load(0).start()
        p_load(1).start()
        x_loads[2].start()
        for c in x_loads[:2]:
            c.wait()
        xT[:, :half] = xo[...].T
        xT[:, half:] = xt[...].T
        tb[...] = jnp.zeros_like(tb)

    for j in range(HEADS // 4):

        @pl.when(p == j)
        def _(j=j):
            if j == 1:
                p_load(2).start()
            p_load(j).wait()

    slot = p % 2
    c_off = pl.multiple_of(me * (width // 2) + p * pw, pw)
    w_copies = [
        pltpu.make_async_copy(
            w.at[:, pl.ds(c_off, pw)], wcat.at[:, i * pw : (i + 1) * pw], wsem.at[i]
        )
        for i, w in enumerate((wq, wk, wv))
    ]
    for c in w_copies:
        c.start()
    g_s[:half, :] = go[...]
    g_s[half:, :] = gt[...]
    gT[...] = g_s[...].T
    qT[...] = q_i[...].T
    dkT[...] = jnp.zeros_like(dkT)
    dvT[...] = jnp.zeros_like(dvT)
    lane = lax.broadcasted_iota(jnp.int32, (tile, pw), 1)
    low = lane < HD

    def forward(k, *names):
        for name in names:
            x = P[name]
            loaded = name in from_hbm and k == x.stage0
            if loaded:
                x.load_own().wait()
            x.forward(k, loaded)

    def at_tile(t):
        if t == 1:

            @pl.when(p == 2)
            def _():
                forward(0, "WO")
                forward(2, "A3")

        if t == 3:

            @pl.when(p == 0)
            def _():
                forward(1, "A1", "A2")

            @pl.when(p == 1)
            def _():
                forward(0, "B1", "B2", "B3")
                forward(1, "A3")
                forward(2, "A1", "A2")

            @pl.when(p == 2)
            def _():
                forward(1, "B1", "B2")
                forward(0, "C0")

    for t in range(rows // tile):
        rs = slice(t * tile, (t + 1) * tile)
        a_ref = ao if t * tile < half else at
        as_ = slice(t * tile % half, t * tile % half + tile)
        g = g_s[rs, :]
        ga = g.astype(F32) * a_ref[as_, :].astype(F32)
        outs = []
        for h in range(2):
            mine = low if h == 0 else ~low
            hs = slice(h * HD, (h + 1) * HD)
            dp = mm(jnp.where(mine, g, BF16(0)), v_i[...], NT)
            delta = jnp.sum(jnp.where(mine, ga, 0.0), axis=-1, keepdims=True)
            pr = p_s[slot, h, rs, :]
            ds = (pr.astype(F32) * (dp - delta)).astype(BF16)
            outs.append(mm(ds, k_i[...]))
            dvT[hs, :] += mm(gT[hs, rs], pr)
            dkT[hs, :] += mm(qT[hs, rs], ds)
        dq = jnp.where(low, outs[0], outs[1]) * HD**-0.5
        dqkv[rs, 0:pw] = dq.astype(BF16)

        at_tile(t)

    dqkv[:, pw : 2 * pw] = (dkT[...].T * HD**-0.5).astype(BF16)
    dqkv[:, 2 * pw : 3 * pw] = dvT[...].T.astype(BF16)
    d = dqkv[...]
    wg = mm(xT[...], d).astype(BF16).reshape(wsrc.shape[1:])
    wsrc[p] = wg
    tb[0:1, pl.ds(c_off, pw)] = jnp.sum(d[:, 0:pw].astype(F32), axis=0, keepdims=True)
    tb[1:2, pl.ds(c_off, pw)] = jnp.sum(d[:, 2 * pw :].astype(F32), axis=0, keepdims=True)

    @pl.when(p == 0)
    def _():
        P["C0"].copy(0).start()

    @pl.when(p == 1)
    def _():
        P["C1"].copy(0).start()

    @pl.when(p == 2)
    def _():
        P["C2"].copy(0).start()
        P["C3"].copy(0).start()
        tb_copy.start()

    for c in w_copies:
        c.wait()
    part = mm(d, wcat[...], NT)

    @pl.when(p == 0)
    def _():
        acc[...] = part

    @pl.when(p == 1)
    def _():
        acc[...] += part

    @pl.when(p == 2)
    def _():
        ig_s[...] = (acc[half:, :] + part[half:]).astype(BF16)
        ig_copy.start()
        acc[:half, :] += part[:half]

        def next_table(k):
            t_copies[k].wait_recv()
            ts[k + 1][...] = ts[k][...] + trs[k][...]
            if k + 1 < nb:
                t_copies[k + 1].start()

        tb_copy.wait_recv()
        ts[0][0:8, :] = tb[...] + tb_m[...] + vec[...]
        ts[0][8:16, :] = bi[...]
        t_copies[0].start()
        forward(1, "B3")
        forward(2, "B1", "B2")
        forward(0, "C1")
        forward(1, "WO")
        next_table(0)
        forward(1, "C0")
        forward(0, "C2", "C3")
        ig_copy.wait_recv()
        x_loads[2].wait()
        ig_o[...] = gsum[...] + (acc[:half, :] + ig_r[...].astype(F32))
        next_table(1)
        forward(2, "B3")
        forward(1, "C1")
        forward(2, "WO", "C0")
        for k in range(2, nb - 1):
            next_table(k)
        forward(1, "C2", "C3")
        forward(2, "C1")
        for i in range(3):
            wout_o[:, i * third : (i + 1) * third] = P["A%d" % (i + 1)].result()
            win_o[:, i * third : (i + 1) * third] = P["B%d" % (i + 1)].result()
        forward(2, "C2", "C3")
        wo_o[...] = P["WO"].result()
        next_table(nb - 1)
        table = ts[nb][...]
        n = width // dp_size
        m = bi_o.shape[1]
        vals = table[0:8, 0:n]
        biv = table[8:9, 0:m]
        for j in range(1, dp_size):
            vals = jnp.where(dev == j, table[0:8, j * n : (j + 1) * n], vals)
            r = 8 + (j * m) // width
            k = (j * m) % width
            biv = jnp.where(dev == j, table[r : r + 1, k : k + m], biv)
        vals_o[...] = vals
        bi_o[...] = biv
        for j in range(3):
            cs = slice(j * pw, (j + 1) * pw)
            v = P["C%d" % j].result()
            wq_o[:, cs] = v[:, :pw]
            wk_o[:, cs] = v[:, pw : 2 * pw]
            wv_o[:, cs] = v[:, 2 * pw :] if j < 2 else P["C3"].result()

        for name in PIECES:
            P[name].drain()
        ig_copy.wait_send()
        tb_copy.wait_send()
        for c in t_copies:
            c.wait_send()


def back(dp_size, xo, xt, wq, wk, wv, q, k, v, probs, ao, at, go, gt, gsum, vec, bi, sa, win, wo):
    half, width = xo.shape
    rows = 2 * half
    pairs = HEADS // 4
    pw = 2 * HD
    ff = win.shape[1]
    nb = dp_size.bit_length() - 1
    n = width // dp_size
    split = lambda a: a.reshape((2,) * nb + (n, a.shape[-1]))
    whole = lambda a: pl.BlockSpec(
        a.shape, lambda p: (0,) * a.ndim, pipeline_mode=pl.Buffered(1)
    )
    col = lambda r, w: pl.BlockSpec((r, w), lambda p: (0, p))
    hbm = pl.BlockSpec(memory_space=pl.ANY)
    vm = pl.BlockSpec(memory_space=pltpu.VMEM)
    V = pltpu.VMEM
    plan = piece_plan(dp_size, width, ff)

    def stages(last):
        return tuple(
            tuple(
                V((2,) * (nb - 1 - k) + (n, w), BF16) if k < nb - last else V((16, 128), BF16)
                for k in range(nb)
            )
            for _, w in plan
        )

    table = lambda: V((16, width), F32)
    sem = pltpu.SemaphoreType.DMA
    return pl.pallas_call(
        functools.partial(back_body, dp_size),
        grid_spec=pltpu.PrefetchScalarGridSpec(
            num_scalar_prefetch=0,
            grid=(pairs,),
            in_specs=[col(rows, pw)] * 3 + [col(half, pw)] * 4 + [whole(vec), whole(bi)] + [hbm] * 12,
            out_specs=[vm] * 9,
            scratch_shapes=[
                V((half, width), BF16),
                V((half, width), BF16),
                V((2, 2, rows, rows), BF16),
                V((half, width), F32),
                V((rows, pw), BF16),
                V((pw, rows), BF16),
                V((pw, rows), BF16),
                V((pw, rows), F32),
                V((pw, rows), F32),
                V((rows, 3 * pw), BF16),
                V((width, 3 * pw), BF16),
                V((width, rows), BF16),
                V((rows, width), F32),
                V((half, width), BF16),
                V((half, width), BF16),
                V((pairs,) + (2,) * nb + (n, 3 * pw), BF16),
                stages(0),
                stages(1),
                V((8, width), F32),
                V((8, width), F32),
                tuple(table() for _ in range(nb + 1)),
                tuple(table() for _ in range(nb)),
                sem((len(plan) * nb,)),
                sem((len(plan) * nb,)),
                sem((len(plan),)),
                sem((2 + nb,)),
                sem((2 + nb,)),
                sem((8,)),
            ],
        ),
        out_shape=[shape((half, width), F32)]
        + [shape((n, width // 2), F32)] * 4
        + [shape((n, ff), F32)] * 2
        + [shape((8, n), F32), shape((1, 2 * ff // dp_size), F32)],
        compiler_params=pltpu.CompilerParams(
            vmem_limit_bytes=60 << 20, collective_id=2, has_side_effects=True
        ),
        cost_estimate=cost(40e9, 20e6),
        name="back",
    )(q, k, v, ao, at, go, gt, vec, bi, xo, xt, probs, gsum, wq, wk, wv, *sa, split(win), split(wo))


def emit_body(big, *refs):
    ins, outs = refs[: big + 2], refs[big + 2 :]
    for i in range(big):
        outs[i][...] = ins[i][...]
    vals = ins[big][...]
    for j in range(8):
        outs[big + j][...] = vals[j]
    outs[big + 8][...] = ins[big + 1][0]


def emit(arrays, vals, bi):
    vm = pl.BlockSpec(memory_space=pltpu.VMEM)
    return pl.pallas_call(
        functools.partial(emit_body, len(arrays)),
        in_specs=[vm] * (len(arrays) + 2),
        out_specs=[vm] * (len(arrays) + 9),
        out_shape=[shape(a.shape, a.dtype) for a in arrays]
        + [shape((vals.shape[1],), F32)] * 8
        + [shape((bi.shape[1],), F32)],
        compiler_params=params(60),
        name="emit",
    )(*arrays, vals, bi)


def local_pair(
    dp_size, inputs, grad_out, lengths, rand_blocks, w_query, b_query, w_key, w_value, b_value,
    w_output, b_output, gain_one, shift_one, w_in, b_in, w_out, b_out, gain_two, shift_two,
):
    x = inputs[0]
    (
        x_got, a_own, a_oth, q, k, v, probs, out, gsum, ga0, ga_got, sa1, sa2, sa3, w_in_g,
        w_output_g, vec_g, bi_g,
    ) = first_half(
        dp_size, lengths, x, rand_blocks.transpose(2, 0, 1), b_query, b_value, w_query, w_key,
        w_value, grad_out[0],
        (b_output, gain_one, shift_one, b_in, b_out, gain_two, shift_two), w_output, w_in, w_out,
    )
    *mats, vals, bi = back(
        dp_size, x, x_got, w_query, w_key, w_value, q, k, v, probs, a_own, a_oth, ga0, ga_got,
        gsum, vec_g, bi_g, (sa1, sa2, sa3), w_in_g, w_output_g,
    )
    (
        out, input_grad, wq_p, wk_p, wv_p, wo_p, in_part, out_part, bq_p, bv_p, bo_p, g1_p, s1_p,
        b2_p, g2_p, s2_p, bi_p,
    ) = emit([out] + mats, vals, bi)
    return (
        out[None], input_grad[None], wq_p, bq_p, wk_p, wv_p, bv_p, wo_p, bo_p, g1_p, s1_p,
        in_part, bi_p, out_part, b2_p, g2_p, s2_p,
    )


def layer_norm(features, norm_gain, norm_shift):
    row_mean = jnp.mean(features, axis=-1, keepdims=True)
    centered = features - row_mean
    variance = jnp.mean(centered * centered, axis=-1, keepdims=True)
    return centered * lax.rsqrt(variance + norm_epsilon) * norm_gain + norm_shift


def gelu_tanh(features):
    return jax.nn.gelu(features, approximate=True)


def slot_table_ids(block_ids, rand_rows, length):
    valid_blocks = (length + BLK - 1) // BLK
    column = block_ids[:, None]
    columns = jnp.concatenate(
        [
            column - 1,
            column,
            column + 1,
            rand_rows,
            jnp.zeros_like(column),
            jnp.zeros_like(column) + valid_blocks - 1,
        ],
        axis=1,
    )
    in_range = (columns >= 0) & (columns < valid_blocks)
    slot_ids = jnp.arange(columns.shape[1], dtype=jnp.int32)
    earlier = slot_ids[None, :] < slot_ids[:, None]
    repeated = jnp.any(
        (columns[:, :, None] == columns[:, None, :]) & earlier[None, :, :] & in_range[:, None, :],
        axis=2,
    )
    return (jnp.clip(columns, 0, NB - 1), in_range & jnp.logical_not(repeated))


def slot_table(first_block, rand_rows, length):
    block_ids = first_block + jnp.arange(rand_rows.shape[0], dtype=jnp.int32)
    return slot_table_ids(block_ids, rand_rows, length)


def slot_mask(slot_blocks, slot_valid, length):
    positions = slot_blocks[:, :, None] * BLK + jnp.arange(BLK, dtype=jnp.int32)
    allowed = slot_valid[:, :, None] & (positions < length)
    return allowed.reshape(slot_blocks.shape[0], 1, 1, -1)


def gather_slots(whole_rows, slot_blocks):
    picked = whole_rows.reshape(NB, BLK, whole_rows.shape[1])[slot_blocks]
    return picked.reshape(slot_blocks.shape[0], slot_blocks.shape[1] * BLK, HEADS, HD)


def log_total(scores, allowed):
    masked = jnp.where(allowed, scores, negative_fill)
    top_score = jnp.max(masked, axis=-1, keepdims=True)
    return top_score + jnp.log(jnp.sum(jnp.exp(masked - top_score), axis=-1, keepdims=True))


def exp_probs(scores, allowed, totals):
    return jnp.exp(jnp.where(allowed, scores, negative_fill) - totals)


def global_targets(length, device, local_blocks):
    last_block = (length + BLK - 1) // BLK - 1
    targets = []
    for target_block in (jnp.zeros_like(last_block), last_block):
        is_owner = target_block // local_blocks == device
        local_block = jnp.clip(target_block - device * local_blocks, 0, local_blocks - 1)
        targets.append((is_owner, local_block))
    return targets


def global_scores(query_rows, key_one, length):
    scores = jnp.einsum(
        "qhd,khd->hqk",
        query_rows.reshape(BLK, HEADS, HD),
        key_one.reshape(-1, HEADS, HD),
        preferred_element_type=jnp.float32,
    ) * HD ** (-0.5)
    allowed = (jnp.arange(key_one.shape[0], dtype=jnp.int32) < length)[None, None, :]
    return (scores, allowed)


def global_forward(query_rows, key_one, value_one, length):
    scores, allowed = global_scores(query_rows, key_one, length)
    totals = log_total(scores, allowed)
    weighting = exp_probs(scores, allowed, totals).astype(jnp.bfloat16)
    out_rows = jnp.einsum(
        "hqk,khd->qhd",
        weighting,
        value_one.reshape(-1, HEADS, HD),
        preferred_element_type=jnp.float32,
    )
    return (out_rows.reshape(BLK, -1), totals)


def global_skip(query_rows, key_one, value_one, length):
    return (jnp.zeros((BLK, HEADS * HD), jnp.float32), jnp.zeros((HEADS, BLK, 1), jnp.float32))


def global_backward(query_rows, grad_rows, key_one, value_one, length, row_totals):
    score_scale = HD ** (-0.5)
    scores, allowed = global_scores(query_rows, key_one, length)
    exact_probs = exp_probs(scores, allowed, row_totals)
    grad_heads = grad_rows.reshape(BLK, HEADS, HD)
    grad_weights = jnp.einsum(
        "qhd,khd->hqk",
        grad_heads,
        value_one.reshape(-1, HEADS, HD),
        preferred_element_type=jnp.float32,
    )
    delta_sum = jnp.sum(exact_probs * grad_weights, axis=-1, keepdims=True)
    grad_scores = (exact_probs * (grad_weights - delta_sum)).astype(jnp.bfloat16)
    grad_query = (
        jnp.einsum(
            "hqk,khd->qhd",
            grad_scores,
            key_one.reshape(-1, HEADS, HD),
            preferred_element_type=jnp.float32,
        )
        * score_scale
    )
    grad_keys = (
        jnp.einsum(
            "hqk,qhd->khd",
            grad_scores,
            query_rows.reshape(BLK, HEADS, HD),
            preferred_element_type=jnp.float32,
        )
        * score_scale
    )
    grad_values = jnp.einsum(
        "hqk,qhd->khd",
        exact_probs.astype(jnp.bfloat16),
        grad_heads,
        preferred_element_type=jnp.float32,
    )
    return (
        grad_query.reshape(BLK, -1),
        grad_keys.reshape(key_one.shape[0], -1),
        grad_values.reshape(key_one.shape[0], -1),
    )


def global_back_skip(query_rows, grad_rows, key_one, value_one, length, row_totals):
    key_zeros = jnp.zeros(key_one.shape, jnp.float32)
    return (jnp.zeros((BLK, key_one.shape[1]), jnp.float32), key_zeros, key_zeros)


def attend_forward(query_one, key_one, value_one, length, rand_rows, device):
    local_blocks = rand_rows.shape[0]
    slot_blocks, slot_valid = slot_table(device * local_blocks, rand_rows, length)
    allowed = slot_mask(slot_blocks, slot_valid, length)
    query_blocks = query_one.reshape(local_blocks, BLK, HEADS, HD)
    scores = jnp.einsum(
        "nqhd,nkhd->nhqk",
        query_blocks,
        gather_slots(key_one, slot_blocks),
        preferred_element_type=jnp.float32,
    ) * HD ** (-0.5)
    totals = log_total(scores, allowed)
    weighting = exp_probs(scores, allowed, totals).astype(jnp.bfloat16)
    attended = jnp.einsum(
        "nhqk,nkhd->nqhd",
        weighting,
        gather_slots(value_one, slot_blocks),
        preferred_element_type=jnp.float32,
    ).reshape(query_one.shape[0], -1)
    global_totals = []
    for is_owner, local_block in global_targets(length, device, local_blocks):
        query_rows = lax.dynamic_slice_in_dim(query_one, local_block * BLK, BLK, 0)
        out_rows, row_totals = lax.cond(
            is_owner, global_forward, global_skip, query_rows, key_one, value_one, length
        )
        updated = lax.dynamic_update_slice_in_dim(attended, out_rows, local_block * BLK, 0)
        attended = jnp.where(is_owner, updated, attended)
        global_totals.append(row_totals)
    return (attended, totals, global_totals[0], global_totals[1])


def attend_backward(
    query_one,
    key_one,
    value_one,
    length,
    rand_rows,
    totals,
    first_totals,
    last_totals,
    grad_one,
    device,
):
    score_scale = HD ** (-0.5)
    local_blocks = rand_rows.shape[0]
    first_block = device * local_blocks
    slot_blocks, slot_valid = slot_table(first_block, rand_rows, length)
    allowed = slot_mask(slot_blocks, slot_valid, length)
    query_blocks = query_one.reshape(local_blocks, BLK, HEADS, HD)
    key_slots = gather_slots(key_one, slot_blocks)
    value_slots = gather_slots(value_one, slot_blocks)
    scores = (
        jnp.einsum("nqhd,nkhd->nhqk", query_blocks, key_slots, preferred_element_type=jnp.float32)
        * score_scale
    )
    exact_probs = exp_probs(scores, allowed, totals)
    last_block = (length + BLK - 1) // BLK - 1
    row_blocks = first_block + jnp.arange(query_one.shape[0], dtype=jnp.int32) // BLK
    is_global = (row_blocks == 0) | (row_blocks == last_block)
    grad_sparse = jnp.where(is_global[:, None], jnp.zeros_like(grad_one), grad_one)
    grad_heads = grad_sparse.reshape(local_blocks, BLK, HEADS, HD)
    grad_weights = jnp.einsum(
        "nqhd,nkhd->nhqk", grad_heads, value_slots, preferred_element_type=jnp.float32
    )
    delta_sum = jnp.sum(exact_probs * grad_weights, axis=-1, keepdims=True)
    grad_scores = (exact_probs * (grad_weights - delta_sum)).astype(jnp.bfloat16)
    grad_query = (
        jnp.einsum(
            "nhqk,nkhd->nqhd", grad_scores, key_slots, preferred_element_type=jnp.float32
        ).reshape(query_one.shape[0], -1)
        * score_scale
    )
    grad_key_slots = (
        jnp.einsum("nhqk,nqhd->nkhd", grad_scores, query_blocks, preferred_element_type=jnp.float32)
        * score_scale
    )
    grad_value_slots = jnp.einsum(
        "nhqk,nqhd->nkhd",
        exact_probs.astype(jnp.bfloat16),
        grad_heads,
        preferred_element_type=jnp.float32,
    )
    flat_ids = slot_blocks.reshape(-1)
    slot_width = BLK * query_one.shape[1]
    grad_keys = jax.ops.segment_sum(
        grad_key_slots.reshape(-1, slot_width), flat_ids, num_segments=NB
    ).reshape(-1, query_one.shape[1])
    grad_values = jax.ops.segment_sum(
        grad_value_slots.reshape(-1, slot_width), flat_ids, num_segments=NB
    ).reshape(-1, query_one.shape[1])
    for (is_owner, local_block), row_totals in zip(
        global_targets(length, device, local_blocks), (first_totals, last_totals)
    ):
        query_rows = lax.dynamic_slice_in_dim(query_one, local_block * BLK, BLK, 0)
        grad_rows = lax.dynamic_slice_in_dim(grad_one, local_block * BLK, BLK, 0)
        query_add, key_add, value_add = lax.cond(
            is_owner,
            global_backward,
            global_back_skip,
            query_rows,
            grad_rows,
            key_one,
            value_one,
            length,
            row_totals,
        )
        current = lax.dynamic_slice_in_dim(grad_query, local_block * BLK, BLK, 0)
        grad_query = lax.dynamic_update_slice_in_dim(
            grad_query, current + query_add, local_block * BLK, 0
        )
        grad_keys = grad_keys + key_add
        grad_values = grad_values + value_add
    return (grad_query, grad_keys, grad_values)


def local(
    inputs,
    grad_out,
    lengths,
    rand_blocks,
    w_query,
    b_query,
    w_key,
    w_value,
    b_value,
    w_output,
    b_output,
    gain_one,
    shift_one,
    w_in,
    b_in,
    w_out,
    b_out,
    gain_two,
    shift_two,
):
    device = lax.axis_index("mp")
    seq_count, local_rows, width = inputs.shape
    flat_in = inputs.reshape(-1, width)
    query = (jnp.dot(flat_in, w_query, preferred_element_type=jnp.float32) + b_query).astype(
        jnp.bfloat16
    )
    keys = jnp.dot(flat_in, w_key, preferred_element_type=jnp.float32).astype(jnp.bfloat16)
    values = (jnp.dot(flat_in, w_value, preferred_element_type=jnp.float32) + b_value).astype(
        jnp.bfloat16
    )
    key_all, value_all = (
        lax.all_gather(keys.reshape(seq_count, local_rows, width), "mp", axis=1, tiled=True),
        lax.all_gather(values.reshape(seq_count, local_rows, width), "mp", axis=1, tiled=True),
    )
    query_seq = query.reshape(seq_count, local_rows, width)

    def forward_item(seq_items):
        query_one, key_one, value_one, length, rand_rows = seq_items
        return attend_forward(query_one, key_one, value_one, length, rand_rows, device)

    attended, totals, first_totals, last_totals = lax.map(
        forward_item, (query_seq, key_all, value_all, lengths, rand_blocks)
    )
    attended_low = attended.reshape(-1, width).astype(jnp.bfloat16)
    summed_one = (
        flat_in.astype(jnp.float32)
        + jnp.dot(attended_low, w_output, preferred_element_type=jnp.float32)
        + b_output
    )
    first, norm_one_back = jax.vjp(
        layer_norm, summed_one, gain_one.astype(jnp.float32), shift_one.astype(jnp.float32)
    )
    first_low = first.astype(jnp.bfloat16)
    rows_all = lax.all_gather(first_low, "mp", axis=0, tiled=True)
    hidden = jnp.dot(rows_all, w_in, preferred_element_type=jnp.float32) + b_in
    active_full, gelu_back = jax.vjp(gelu_tanh, hidden)
    active = active_full.astype(jnp.bfloat16)
    feed = lax.psum_scatter(
        jnp.einsum(
            "rf,df->rd",
            lax.slice_in_dim(active, 0, first_low.shape[0] * lax.axis_size("mp"), axis=0),
            w_out,
            preferred_element_type=jnp.float32,
        ),
        "mp",
        scatter_dimension=0,
        tiled=True,
    )
    summed_two = first + feed + b_out
    output, norm_two_back = jax.vjp(
        layer_norm, summed_two, gain_two.astype(jnp.float32), shift_two.astype(jnp.float32)
    )
    grad_two, gain_two_grad, shift_two_grad = norm_two_back(
        grad_out.reshape(-1, width).astype(jnp.float32)
    )
    grad_feed = grad_two.astype(jnp.bfloat16)
    b_out_grad = jnp.sum(grad_feed, axis=0, dtype=jnp.float32)
    grads_all = lax.all_gather(grad_feed, "mp", axis=0, tiled=True)
    w_out_grad = jnp.einsum("rd,rf->df", grads_all, active, preferred_element_type=jnp.float32)
    grad_hidden = gelu_back(jnp.dot(grads_all, w_out, preferred_element_type=jnp.float32))[
        0
    ].astype(jnp.bfloat16)
    w_in_grad = jnp.einsum("rd,rf->df", rows_all, grad_hidden, preferred_element_type=jnp.float32)
    grad_first = grad_two + lax.psum_scatter(
        jnp.einsum(
            "rf,df->rd",
            lax.slice_in_dim(grad_hidden, 0, grad_feed.shape[0] * lax.axis_size("mp"), axis=0),
            w_in,
            preferred_element_type=jnp.float32,
        ),
        "mp",
        scatter_dimension=0,
        tiled=True,
    )
    b_in_grad = lax.dynamic_update_slice_in_dim(
        jnp.zeros((FF,), jnp.float32),
        jnp.sum(grad_hidden, axis=0, dtype=jnp.float32),
        device * w_in.shape[1],
        0,
    )
    grad_sum_one, gain_one_grad, shift_one_grad = norm_one_back(grad_first)
    grad_branch = grad_sum_one.astype(jnp.bfloat16)
    b_output_grad = jnp.sum(grad_branch, axis=0, dtype=jnp.float32)
    w_output_grad = jnp.einsum(
        "rd,re->de", attended_low, grad_branch, preferred_element_type=jnp.float32
    )
    grad_attended = (
        jnp.einsum("re,de->rd", grad_branch, w_output, preferred_element_type=jnp.float32)
        .astype(jnp.bfloat16)
        .reshape(seq_count, local_rows, width)
    )

    def backward_item(seq_items):
        (
            query_one,
            key_one,
            value_one,
            length,
            rand_rows,
            sparse_totals,
            first_one,
            last_one,
            grad_one,
        ) = seq_items
        return attend_backward(
            query_one,
            key_one,
            value_one,
            length,
            rand_rows,
            sparse_totals,
            first_one,
            last_one,
            grad_one,
            device,
        )

    grad_query, grad_keys, grad_values = lax.map(
        backward_item,
        (
            query_seq,
            key_all,
            value_all,
            lengths,
            rand_blocks,
            totals,
            first_totals,
            last_totals,
            grad_attended,
        ),
    )
    key_sums, value_sums = (
        lax.psum_scatter(
            grad_keys.astype(jnp.bfloat16), "mp", scatter_dimension=1, tiled=True
        ).astype(jnp.float32),
        lax.psum_scatter(
            grad_values.astype(jnp.bfloat16), "mp", scatter_dimension=1, tiled=True
        ).astype(jnp.float32),
    )
    grad_q_low = grad_query.reshape(-1, width).astype(jnp.bfloat16)
    grad_k_low = key_sums.reshape(-1, width).astype(jnp.bfloat16)
    grad_v_low = value_sums.reshape(-1, width).astype(jnp.bfloat16)
    input_grad = grad_sum_one + jnp.einsum(
        "re,de->rd", grad_q_low, w_query, preferred_element_type=jnp.float32
    )
    input_grad = input_grad + jnp.einsum(
        "re,de->rd", grad_k_low, w_key, preferred_element_type=jnp.float32
    )
    input_grad = input_grad + jnp.einsum(
        "re,de->rd", grad_v_low, w_value, preferred_element_type=jnp.float32
    )
    w_query_grad = jnp.einsum("rd,re->de", flat_in, grad_q_low, preferred_element_type=jnp.float32)
    w_key_grad = jnp.einsum("rd,re->de", flat_in, grad_k_low, preferred_element_type=jnp.float32)
    w_value_grad = jnp.einsum("rd,re->de", flat_in, grad_v_low, preferred_element_type=jnp.float32)
    b_query_grad = jnp.sum(grad_q_low, axis=0, dtype=jnp.float32)
    b_value_grad = jnp.sum(grad_v_low, axis=0, dtype=jnp.float32)
    reduced = (
        lax.psum_scatter(
            w_query_grad.astype(jnp.bfloat16), "dp", scatter_dimension=0, tiled=True
        ).astype(jnp.float32),
        lax.psum_scatter(
            w_key_grad.astype(jnp.bfloat16), "dp", scatter_dimension=0, tiled=True
        ).astype(jnp.float32),
        lax.psum_scatter(
            w_value_grad.astype(jnp.bfloat16), "dp", scatter_dimension=0, tiled=True
        ).astype(jnp.float32),
        lax.psum_scatter(
            w_output_grad.astype(jnp.bfloat16), "dp", scatter_dimension=0, tiled=True
        ).astype(jnp.float32),
        lax.psum_scatter(
            w_in_grad.astype(jnp.bfloat16), "dp", scatter_dimension=0, tiled=True
        ).astype(jnp.float32),
        lax.psum_scatter(
            w_out_grad.astype(jnp.bfloat16), "dp", scatter_dimension=0, tiled=True
        ).astype(jnp.float32),
        lax.psum_scatter(
            b_query_grad.astype(jnp.bfloat16), "dp", scatter_dimension=0, tiled=True
        ).astype(jnp.float32),
        lax.psum_scatter(
            b_value_grad.astype(jnp.bfloat16), "dp", scatter_dimension=0, tiled=True
        ).astype(jnp.float32),
        lax.psum_scatter(
            b_output_grad.astype(jnp.bfloat16), "dp", scatter_dimension=0, tiled=True
        ).astype(jnp.float32),
        lax.psum_scatter(
            gain_one_grad.astype(jnp.bfloat16), "dp", scatter_dimension=0, tiled=True
        ).astype(jnp.float32),
        lax.psum_scatter(
            shift_one_grad.astype(jnp.bfloat16), "dp", scatter_dimension=0, tiled=True
        ).astype(jnp.float32),
        lax.psum_scatter(
            b_in_grad.astype(jnp.bfloat16), "dp", scatter_dimension=0, tiled=True
        ).astype(jnp.float32),
        lax.psum_scatter(
            b_out_grad.astype(jnp.bfloat16), "dp", scatter_dimension=0, tiled=True
        ).astype(jnp.float32),
        lax.psum_scatter(
            gain_two_grad.astype(jnp.bfloat16), "dp", scatter_dimension=0, tiled=True
        ).astype(jnp.float32),
        lax.psum_scatter(
            shift_two_grad.astype(jnp.bfloat16), "dp", scatter_dimension=0, tiled=True
        ).astype(jnp.float32),
    )
    query_part, key_part_out, value_part, output_part = (
        lax.psum_scatter(
            reduced[0].astype(jnp.bfloat16), "mp", scatter_dimension=1, tiled=True
        ).astype(jnp.float32),
        lax.psum_scatter(
            reduced[1].astype(jnp.bfloat16), "mp", scatter_dimension=1, tiled=True
        ).astype(jnp.float32),
        lax.psum_scatter(
            reduced[2].astype(jnp.bfloat16), "mp", scatter_dimension=1, tiled=True
        ).astype(jnp.float32),
        lax.psum_scatter(
            reduced[3].astype(jnp.bfloat16), "mp", scatter_dimension=1, tiled=True
        ).astype(jnp.float32),
    )
    in_part = reduced[4]
    out_part = reduced[5]
    vectors = lax.psum(
        (
            reduced[6],
            reduced[7],
            reduced[8],
            reduced[9],
            reduced[10],
            reduced[11],
            reduced[12],
            reduced[13],
            reduced[14],
        ),
        "mp",
    )
    return (
        output.astype(jnp.bfloat16).reshape(seq_count, local_rows, width),
        input_grad.reshape(seq_count, local_rows, width),
        query_part,
        vectors[0],
        key_part_out,
        value_part,
        vectors[1],
        output_part,
        vectors[2],
        vectors[3],
        vectors[4],
        in_part,
        vectors[5],
        out_part,
        vectors[6],
        vectors[7],
        vectors[8],
    )


def solution(mesh):
    in_specs = (
        P("dp", "mp", None),
        P("dp", "mp", None),
        P("dp"),
        P("dp", "mp", None),
        P(),
        P(),
        P(),
        P(),
        P(),
        P(),
        P(),
        P(),
        P(),
        P(None, "mp"),
        P("mp"),
        P(None, "mp"),
        P(),
        P(),
        P(),
    )
    out_specs = (
        P("dp", "mp", None),
        P("dp", "mp", None),
        P("dp", "mp"),
        P("dp"),
        P("dp", "mp"),
        P("dp", "mp"),
        P("dp"),
        P("dp", "mp"),
        P("dp"),
        P("dp"),
        P("dp"),
        P("dp", "mp"),
        P("dp"),
        P("dp", "mp"),
        P("dp"),
        P("dp"),
        P("dp"),
    )
    sizes = dict(mesh.shape)
    if sizes["mp"] == 2 and sizes["dp"] == 16:
        local_fn = functools.partial(local_pair, sizes["dp"])
    else:
        local_fn = local
    return jax.shard_map(local_fn, mesh=mesh, in_specs=in_specs, out_specs=out_specs, check_vma=False)
```

```python
import functools

import jax
import jax.numpy as jnp
from jax import lax
from jax.experimental import pallas as pl
from jax.experimental.pallas import tpu as pltpu
from jax.sharding import PartitionSpec as P

HEADS = 12
HD = 64
FF = 3072
BLK = 64
NB = 16


negative_fill = -1000000000.0
norm_epsilon = 1e-12


F32 = jnp.float32
BF16 = jnp.bfloat16
NN = (((1,), (0,)), ((), ()))
NT = (((1,), (1,)), ((), ()))
TN = (((0,), (0,)), ((), ()))


def mm(a, b, dims=NN):
    return lax.dot_general(a, b, dims, preferred_element_type=F32)


def params(mib=56):
    return pltpu.CompilerParams(vmem_limit_bytes=mib << 20)


def cost(flops, nbytes, trans=0):
    return pl.CostEstimate(flops=int(flops), bytes_accessed=int(nbytes), transcendentals=int(trans))


def shape(dims, dtype):
    return jax.ShapeDtypeStruct(dims, dtype)


def row_stats(u):
    mean = jnp.mean(u, axis=-1, keepdims=True)
    cen = u - mean
    var = jnp.mean(cen * cen, axis=-1, keepdims=True)
    rs = lax.rsqrt(var + norm_epsilon)
    return cen * rs, rs


def partner_copy(src, dst, send, recv, me):
    return pltpu.make_async_remote_copy(
        src_ref=src, dst_ref=dst, send_sem=send, recv_sem=recv,
        device_id={"mp": 1 - me}, device_id_type=pl.DeviceIdType.MESH,
    )


def front_body(
    lengths, x, rand, bq, bv, wq, wk, wv,
    x_got, a_own, a_oth, q_o, k_o, v_o, p_h,
    later_loads, middle_part, xg_s, ag_s, p_s, w_s, b_s, rand_s, rand_r, bias, wsem, psem, send, recv,
):
    me = lax.axis_index("mp")
    p = pl.program_id(0)
    half, width = x.shape
    rows = 2 * half
    hw = width // 2
    pw = 2 * HD
    nb = rows // BLK
    tile = 256
    x_copy = partner_copy(x, xg_s, send.at[0], recv.at[0], me)
    rand_copy = partner_copy(rand_s, rand_r, send.at[1], recv.at[1], me)

    def w_loads(j):
        own = pl.ds(pl.multiple_of(me * hw + j * pw, pw), pw)
        return [
            pltpu.make_async_copy(
                w.at[:, own], w_s.at[j, :, i * pw : (i + 1) * pw], wsem.at[3 * j + i]
            )
            for i, w in enumerate((wq, wk, wv))
        ]

    slot = p % 2

    def p_store(slot_j, j, i):
        r0, h = units[i]
        return pltpu.make_async_copy(
            p_s.at[slot_j, h, r0 : r0 + tile], p_h.at[2 * j + h, r0 : r0 + tile],
            psem.at[slot_j, i],
        )

    order = [half + t * tile for t in range(half // tile)] + [t * tile for t in range(half // tile)]
    units = [(r0, h) for r0 in order for h in range(2)]

    @pl.when(p == 0)
    def _():
        barrier = pltpu.get_barrier_semaphore()
        dev = lax.axis_index("dp")
        everyone = [{"mp": 1 - me}]
        everyone += [{"dp": dev + 2**b * (1 - 2 * ((dev // 2**b) % 2))} for b in range(3)]
        for device in everyone:
            pl.semaphore_signal(
                barrier, inc=1, device_id=device, device_id_type=pl.DeviceIdType.MESH
            )
        for j in range(hw // pw):
            for c in w_loads(j):
                c.start()
        for c in later_loads:
            c.start()
        rand_s[...] = jnp.zeros_like(rand_s)
        for j in range(rand.shape[0]):
            rand_s[j : j + 1, : nb // 2] = rand[j]
        b_s[0:1, :] = bq[...].astype(F32)[None, :]
        b_s[1:2, :] = bv[...].astype(F32)[None, :]
        pl.semaphore_wait(barrier, len(everyone))
        x_copy.start()
        rand_copy.start()

    cols = pl.ds(pl.multiple_of(p * pw, pw), pw)
    bias_cols = pl.ds(pl.multiple_of(me * hw + p * pw, pw), pw)

    for j in range(hw // pw):

        @pl.when(p == j)
        def _(j=j):
            for c in w_loads(j):
                c.wait()
            if j == 2:
                for i in range(len(units)):
                    p_store(0, 0, i).wait()

    def project(i, xr):
        rs = slice(i * half, (i + 1) * half)
        qkv = mm(xr[...], w_s[p])
        q_o[rs, :] = (qkv[:, :pw] + b_s[0:1, bias_cols]).astype(BF16)
        k_o[rs, :] = qkv[:, pw : 2 * pw].astype(BF16)
        v_o[rs, :] = (qkv[:, 2 * pw :] + b_s[1:2, bias_cols]).astype(BF16)

    project(0, x)

    @pl.when(p == 0)
    def _():
        rand_copy.wait_recv()
        ln = lengths[0]
        last = (ln + BLK - 1) // BLK - 1
        lb = lax.broadcasted_iota(jnp.int32, (nb, rows), 0)
        kp = lax.broadcasted_iota(jnp.int32, (nb, rows), 1)
        qb = jnp.where(lb < nb // 2, lb + (nb // 2) * me, lb - (nb // 2) * me)
        kpos = jnp.where(kp < half, kp + half * me, kp - half * me)
        kb = kpos // BLK
        ok = (jnp.abs(kb - qb) <= 1) | (kb == 0) | (kb == last)
        listed = [r[...].astype(F32).T[: nb // 2] for r in (rand_s, rand_r)]
        both = jnp.concatenate(listed, axis=0).astype(jnp.int32)
        for j in range(rand.shape[0]):
            ok = ok | (kb == both[:, j : j + 1])
        ok = ok | (qb == 0) | (qb == last)
        ok = ok & (kpos < ln)
        table = jnp.where(ok, 0.0, -1e30).astype(F32)
        for b in range(nb):
            bias[b] = jnp.broadcast_to(table[b : b + 1, :], (8, rows))
        x_copy.wait_recv()
        x_got[...] = xg_s[...]

    project(1, xg_s)

    low = lax.broadcasted_iota(jnp.int32, (tile, pw), 1) < HD
    scores, probs, outs = {}, {}, {}

    def score(i):
        r0, h = units[i]
        q = q_o[r0 : r0 + tile, :] * BF16(HD**-0.5)
        s = mm(jnp.where(low if h == 0 else ~low, q, BF16(0)), k_o[...], NT)
        b0 = r0 // BLK
        s = s.reshape(tile // BLK, BLK // 8, 8, rows) + bias[b0 : b0 + tile // BLK][:, None]
        scores[i] = s.reshape(tile, rows)

    def attend(i):
        r0, h = units[i]
        outs[i] = mm(probs.pop(i), v_o[...])
        if h == 1:
            a = jnp.where(low, outs.pop(i - 1), outs.pop(i)).astype(BF16)
            if r0 < half:
                a_own[r0 : r0 + tile, cols] = a
            else:
                a_oth[r0 - half : r0 - half + tile, cols] = a
                if r0 + tile == rows:
                    partner_copy(
                        a_oth.at[:, cols], ag_s.at[:, cols], send.at[2 + p], recv.at[2 + p], me
                    ).start()

    score(0)
    for i, (r0, h) in enumerate(units):
        if i + 1 < len(units):
            score(i + 1)
        s = scores.pop(i)
        e = jnp.exp(s - jnp.max(s, axis=-1, keepdims=True))
        pr = (e * (1.0 / jnp.sum(e, axis=-1, keepdims=True))).astype(BF16)
        p_s[slot, h, r0 : r0 + tile, :] = pr
        p_store(slot, p, i).start()
        probs[i] = pr
        if i >= 1:
            attend(i - 1)
    attend(len(units) - 1)

    @pl.when(p == pl.num_programs(0) - 1)
    def _():
        x_copy.wait_send()
        rand_copy.wait_send()
        for j in range(hw // pw):
            cs = slice(j * pw, (j + 1) * pw)
            c = partner_copy(a_oth.at[:, cs], ag_s.at[:, cs], send.at[2 + j], recv.at[2 + j], me)
            c.wait_send()
            c.wait_recv()
        middle_part(ag_s)
        for j in range(1, hw // pw):
            for i in range(len(units)):
                p_store(j % 2, j, i).wait()


class Piece:
    def __init__(self, bits, sems, base, src, got, kept, stage0=0):
        self.bits = bits
        self.send, self.recv, self.load = sems
        self.base = base
        self.src, self.got, self.kept = src, got, kept
        self.stage0 = stage0
        self.dev = lax.axis_index("dp")

    def mine(self, k):
        return (self.dev // 2 ** self.bits[k]) % 2

    def peer(self, k):
        return self.dev + 2 ** self.bits[k] * (1 - 2 * self.mine(k))

    def side(self, k, bit, lead=None):
        left = sorted(self.bits[k:], reverse=True)
        where = left.index(self.bits[k])
        idx = [slice(None)] * len(left) if lead is None else list(lead[:where]) + [None] + list(lead[where:])
        idx[where] = bit
        return tuple(idx)

    def source(self, k):
        return self.src if k == self.stage0 else self.kept[k - 1]

    def copy(self, k):
        i = self.base + k
        return pltpu.make_async_remote_copy(
            src_ref=self.source(k).at[self.side(k, 1 - self.mine(k))], dst_ref=self.got[k],
            send_sem=self.send.at[i], recv_sem=self.recv.at[i],
            device_id={"dp": self.peer(k)}, device_id_type=pl.DeviceIdType.MESH,
        )

    def load_own(self):
        k = self.stage0
        return pltpu.make_async_copy(
            self.src.at[self.side(k, self.mine(k))], self.kept[k], self.load.at[self.base // len(self.bits)]
        )

    def total(self, k, lead, loaded):
        if loaded:
            own = self.kept[k][lead]
        else:
            own = self.source(k)[self.side(k, self.mine(k), lead)]
        return own.astype(F32) + self.got[k][lead].astype(F32)

    def add(self, k, loaded=False):
        free = len(self.bits) - 1 - k

        def step(i, carry):
            lead = tuple((i // 2 ** (free - 1 - j)) % 2 for j in range(free))
            self.kept[k][lead] = self.total(k, lead, loaded).astype(BF16)
            return carry

        lax.fori_loop(0, 2**free, step, 0)

    def forward(self, k, loaded=False):
        self.copy(k).wait_recv()
        self.add(k, loaded)
        self.copy(k + 1).start()

    def result(self):
        k = len(self.bits) - 1
        self.copy(k).wait_recv()
        return self.total(k, (), False)

    def drain(self):
        for k in range(self.stage0, len(self.bits)):
            self.copy(k).wait_send()


def bit_orders(dp_size):
    nb = dp_size.bit_length() - 1
    rest = list(range(2, nb))
    return [0, 1] + rest, [1, 0] + rest, rest + [0, 1]


def gelu_and_slope(v):
    k0 = 0.7978845608028654
    k1 = 0.044715
    v2 = v * v
    t = jnp.tanh(v * (k0 + (k0 * k1) * v2))
    hp = 0.5 * t + 0.5
    return v * hp, hp + (0.5 * v) * (1.0 - t * t) * (k0 + (3 * k0 * k1) * v2)


def norm_back(e, n, rs, gain):
    eg = e * gain
    return (eg - jnp.mean(eg, -1, keepdims=True) - n * jnp.mean(eg * n, -1, keepdims=True)) * rs


def middle_body(
    dp_size, loads, a_own, a_got, x, gout, b_output, gain1, shift1, b_in, b_out, gain2, shift2,
    out_h, gsum_h, ga_o, gat_o, sa1, sa2, sa3, win_h, wo_g, vec_o, bi_o,
    out_o, gsum_o, win_g, gat_r,
    fl, feed_s, feed_g, gf, part_s, part_g, gat_s, wo_s, wo_r, vec_s, vec_r, bi_s, bi_s2, bi_r, wout_g, got_a1, got_a2, got_a3,
    w_o, w_in, w_out, act, gh, u_s, first_s, own_s, gtwo_s,
    store_sem, send_sem, recv_sem, a_send_sem, a_recv_sem,
):
    me = lax.axis_index("mp")
    half, width = x.shape
    hw = width // 2
    tile = 256
    tiles = half // tile
    cut = sa1.shape[-1]
    nb = dp_size.bit_length() - 1
    sems = (a_send_sem, a_recv_sem, None)
    chunks = [slice(None)] * (nb + 1)
    outs_a = [
        Piece(
            bits, sems, i * nb, wout_g.at[tuple(chunks + [slice(i * cut, (i + 1) * cut)])],
            (g,), (s,),
        )
        for i, (bits, g, s) in enumerate(
            zip(bit_orders(dp_size), (got_a1, got_a2, got_a3), (sa1, sa2, sa3))
        )
    ]
    stores = [
        pltpu.make_async_copy(src, dst, store_sem.at[i])
        for i, (src, dst) in enumerate(((out_o, out_h), (win_g, win_h), (gsum_o, gsum_h)))
    ]
    def copy(src, dst, i):
        return partner_copy(src, dst, send_sem.at[i], recv_sem.at[i], me)

    for c in loads:
        c.wait()

    def rows(t):
        return pl.ds(pl.multiple_of(t * tile, tile), tile)

    def fl_copy(t):
        return copy(fl.at[0, rows(t)], fl.at[1, rows(t)], 1 + t)

    def feed_copy(t):
        return copy(feed_s.at[rows(t)], feed_g.at[rows(t)], 3 + t)

    def gf_copy(t):
        return copy(gf.at[0, rows(t)], gf.at[1, rows(t)], 5 + t)

    def part_copy(t):
        return copy(part_s.at[rows(t)], part_g.at[rows(t)], 7 + t)

    def ga_copy(t):
        return copy(gat_s.at[rows(t)], gat_r.at[rows(t)], 9 + t)

    own_o = pl.ds(pl.multiple_of(me * hw, hw), hw)
    got_o = pl.ds(pl.multiple_of((1 - me) * hw, hw), hw)

    def project(t, carry):
        r = rows(t)
        u = x[r, :].astype(F32) + (
            mm(a_own[r, :], w_o[own_o, :]) + mm(a_got[r, :], w_o[got_o, :])
        ) + b_output[...].astype(F32)[None, :]
        n, _ = row_stats(u)
        first = n * gain1[...].astype(F32)[None, :] + shift1[...].astype(F32)[None, :]
        u_s[r, :] = u
        first_s[r, :] = first
        fl[0, r, :] = first.astype(BF16)
        fl_copy(t).start()
        return carry

    lax.fori_loop(0, tiles, project, 0)

    def feed_forward(i, t):
        r = rows(t)
        v = mm(fl[i, r, :], w_in[...]) + b_in[...].astype(F32)[None, :]
        a, s = gelu_and_slope(v)
        a = a.astype(BF16)
        act[i, r, :] = a
        gh[i, r, :] = s.astype(BF16)
        return mm(a, w_out[...], NT)

    def forward_own(t, carry):
        own_s[rows(t), :] = feed_forward(0, t)
        return carry

    def forward_got(t, carry):
        fl_copy(t).wait_recv()
        feed_s[rows(t), :] = feed_forward(1, t).astype(BF16)
        feed_copy(t).start()
        return carry

    lax.fori_loop(0, tiles, forward_own, 0)
    lax.fori_loop(0, tiles, forward_got, 0)

    vec_s[...] = jnp.zeros_like(vec_s)

    def add_vec(i, value):
        vec_s[i : i + 1, :] += jnp.sum(value, 0, keepdims=True)

    def second_norm(t, carry):
        r = rows(t)
        feed_copy(t).wait_recv()
        u = first_s[r, :] + (own_s[r, :] + feed_g[r, :].astype(F32)) + b_out[...].astype(F32)[None, :]
        n, rs = row_stats(u)
        gain = gain2[...].astype(F32)[None, :]
        out_o[r, :] = (n * gain + shift2[...].astype(F32)[None, :]).astype(BF16)
        e = gout[r, :].astype(F32)
        d = norm_back(e, n, rs, gain)
        low = d.astype(BF16)
        gtwo_s[r, :] = d
        gf[0, r, :] = low
        gf_copy(t).start()
        add_vec(6, e * n)
        add_vec(7, e)
        add_vec(5, low.astype(F32))
        return carry

    lax.fori_loop(0, tiles, second_norm, 0)
    stores[0].start()
    bi_s[...] = jnp.zeros_like(bi_s)

    def feed_back(i, t):
        r = rows(t)
        g = (mm(gf[i, r, :], w_out[...]) * gh[i, r, :].astype(F32)).astype(BF16)
        gh[i, r, :] = g
        bi_s[0:1, :] += jnp.sum(g.astype(F32), 0, keepdims=True)
        return mm(g, w_in[...], NT)

    def back_own(t, carry):
        own_s[rows(t), :] = feed_back(0, t)
        return carry

    def wait_gf(t, carry):
        gf_copy(t).wait_recv()
        return carry

    def back_got(t, carry):
        part_s[rows(t), :] = feed_back(1, t).astype(BF16)
        part_copy(t).start()
        return carry

    lax.fori_loop(0, tiles, back_own, 0)
    lax.fori_loop(0, tiles, wait_gf, 0)

    def out_weights(j, carry):
        c = pl.ds(pl.multiple_of(j * hw, hw), hw)
        total = mm(gf[0, :, c], act[0], TN) + mm(gf[1, :, c], act[1], TN)
        wout_g[j] = total.astype(BF16).reshape(wout_g.shape[1:])
        return carry

    lax.fori_loop(0, 2, out_weights, 0)
    for a in outs_a:
        a.copy(0).start()
    lax.fori_loop(0, tiles, back_got, 0)

    def weights(out, lhs, rhs):
        def step(j, carry):
            c = pl.ds(pl.multiple_of(j * tile, tile), tile)
            out[c, :] = (
                mm(lhs[0, :, c], rhs[0], TN) + mm(lhs[1, :, c], rhs[1], TN)
            ).astype(BF16)
            return carry

        lax.fori_loop(0, width // tile, step, 0)

    weights(win_g, fl, gh)
    stores[1].start()

    def first_norm(t, carry):
        r = rows(t)
        part_copy(t).wait_recv()
        e = gtwo_s[r, :] + own_s[r, :] + part_g[r, :].astype(F32)
        n, rs = row_stats(u_s[r, :])
        d = norm_back(e, n, rs, gain1[...].astype(F32)[None, :])
        low = d.astype(BF16)
        gsum_o[r, :] = d
        gout[r, :] = low
        gat_s[r, :] = mm(low, w_o[got_o, :], NT).astype(BF16)
        ga_copy(t).start()
        ga_o[r, :] = mm(low, w_o[own_o, :], NT).astype(BF16)
        add_vec(3, e * n)
        add_vec(4, e)
        add_vec(2, low.astype(F32))
        return carry

    lax.fori_loop(0, tiles, first_norm, 0)
    stores[2].start()
    vec_copy = copy(vec_s, vec_r, 11)
    vec_copy.start()
    bi_s2[0:1, :] = bi_s[0:1, :width]
    bi_s2[1:2, :] = bi_s[0:1, width:]
    bi_copy = copy(bi_s2, bi_r, 12)
    bi_copy.start()
    cols_own = own_o
    cols_got = got_o
    wo_s[own_o, :] = mm(a_own[...], gout[:, cols_got], TN).astype(BF16)
    wo_s[got_o, :] = mm(a_got[...], gout[:, cols_got], TN).astype(BF16)
    wo_copy = copy(wo_s, wo_r, 13)
    wo_copy.start()
    own_part = mm(a_own[...], gout[:, cols_own], TN)
    got_part = mm(a_got[...], gout[:, cols_own], TN)
    wo_copy.wait_recv()
    wo_g[own_o, :] = (own_part + wo_r[own_o, :].astype(F32)).astype(BF16)
    wo_g[got_o, :] = (got_part + wo_r[got_o, :].astype(F32)).astype(BF16)
    vec_copy.wait_recv()
    vec_o[...] = vec_s[...] + vec_r[...]
    bi_copy.wait_recv()
    bi_o[...] = jnp.zeros_like(bi_o)
    first_core = me == 0
    bi_o[0:2, :] = jnp.where(first_core, bi_s2[0:2, :], bi_r[0:2, :])
    bi_o[2:4, :] = jnp.where(first_core, bi_r[0:2, :], bi_s2[0:2, :])
    for a in outs_a:
        a.copy(0).wait_recv()
        a.add(0)

    def finish(t, carry):
        ga_copy(t).wait_recv()
        fl_copy(t).wait_send()
        feed_copy(t).wait_send()
        gf_copy(t).wait_send()
        part_copy(t).wait_send()
        ga_copy(t).wait_send()
        return carry

    lax.fori_loop(0, tiles, finish, 0)
    gat_o[...] = gat_r[...]
    for c in stores:
        c.wait()
    for a in outs_a:
        a.copy(0).wait_send()
    vec_copy.wait_send()
    bi_copy.wait_send()
    wo_copy.wait_send()


def first_half_body(dp_size, *refs):
    ins, refs = refs[:19], refs[19:]
    outs, refs = refs[:18], refs[18:]
    mine, (gout, load_sem), rest = refs[:12], refs[12:14], refs[14:]
    lengths, x, rand, bq, bv, wq, wk, wv, gout_h = ins[:9]
    vectors, weights_h = ins[9:16], ins[16:]
    weights = [rest[i] for i in (22, 23, 24)]
    loads = [
        pltpu.make_async_copy(a, b, load_sem.at[i])
        for i, (a, b) in enumerate(zip((gout_h,) + tuple(weights_h), [gout] + weights))
    ]

    def middle_part(a_got):
        middle_body(
            dp_size, loads, outs[1], a_got, x, gout, *vectors, *outs[7:], *rest
        )

    front_body(lengths, x, rand, bq, bv, wq, wk, wv, *outs[:7], loads, middle_part, *mine)


def first_half(dp_size, lengths, x, rand, bq, bv, wq, wk, wv, gout, vectors, w_o, w_in, w_out):
    half, width = x.shape
    rows = 2 * half
    pairs = HEADS // 4
    pw = 2 * HD
    hw = width // 2
    ff = w_in.shape[1]
    nb = dp_size.bit_length() - 1
    n = width // dp_size
    part = (2,) * (nb - 1) + (n, ff // 3)
    vm = pl.BlockSpec(memory_space=pltpu.VMEM)
    hbm = pl.BlockSpec(memory_space=pl.ANY)
    col = pl.BlockSpec((rows, pw), lambda p: (0, p))
    V = pltpu.VMEM
    sem = pltpu.SemaphoreType.DMA
    return pl.pallas_call(
        functools.partial(first_half_body, dp_size),
        grid_spec=pltpu.PrefetchScalarGridSpec(
            num_scalar_prefetch=0,
            grid=(pairs,),
            in_specs=[pl.BlockSpec(memory_space=pltpu.SMEM)] + [vm] * 4 + [hbm] * 4 + [vm] * 7 + [hbm] * 3,
            out_specs=[vm] * 3 + [col] * 3 + [hbm] + [hbm] * 2 + [vm] * 5 + [hbm] + [vm] * 3,
            scratch_shapes=[
                V((half, width), BF16),
                V((half, hw), BF16),
                V((2, 2, rows, rows), BF16),
                V((pairs, width, 3 * pw), BF16),
                V((8, width), F32),
                V((8, 128), jnp.int32),
                V((8, 128), jnp.int32),
                V((rows // BLK, 8, rows), F32),
                sem((3 * pairs,)),
                sem((2, 8)),
                sem((2 + pairs,)),
                sem((2 + pairs,)),
                V((half, width), BF16),
                sem((4,)),
                V((half, width), BF16),
                V((half, width), F32),
                V((width, ff), BF16),
                V((half, hw), BF16),
                V((2, half, width), BF16),
                V((half, width), BF16),
                V((half, width), BF16),
                V((2, half, width), BF16),
                V((half, width), BF16),
                V((half, width), BF16),
                V((half, hw), BF16),
                V((width, hw), BF16),
                V((width, hw), BF16),
                V((8, width), F32),
                V((8, width), F32),
                V((8, ff), F32),
                V((8, width), F32),
                V((8, width), F32),
                V((2,) * nb + (n, ff), BF16),
                V(part, BF16),
                V(part, BF16),
                V(part, BF16),
                V((width, width), BF16),
                V((width, ff), BF16),
                V((width, ff), BF16),
                V((2, half, ff), BF16),
                V((2, half, ff), BF16),
                V((half, width), F32),
                V((half, width), F32),
                V((half, width), F32),
                V((half, width), F32),
                pltpu.SemaphoreType.DMA((3,)),
                pltpu.SemaphoreType.DMA((14,)),
                pltpu.SemaphoreType.DMA((14,)),
                pltpu.SemaphoreType.DMA((3 * nb,)),
                pltpu.SemaphoreType.DMA((3 * nb,)),
            ],
        ),
        out_shape=[shape((half, width), BF16)]
        + [shape((half, hw), BF16)] * 2
        + [shape((rows, hw), BF16)] * 3
        + [shape((2 * pairs, rows, rows), BF16)]
        + [
            shape((half, width), BF16),
            shape((half, width), F32),
            shape((half, hw), BF16),
            shape((half, hw), BF16),
            shape(part, BF16),
            shape(part, BF16),
            shape(part, BF16),
            shape((width, ff), BF16),
            shape((width, hw), BF16),
            shape((8, width), F32),
            shape((8, width), F32),
        ],
        compiler_params=pltpu.CompilerParams(
            vmem_limit_bytes=63 << 20, collective_id=1, has_side_effects=True
        ),
        cost_estimate=cost(37e9, 40e6, 6 * rows * rows),
        name="first_half",
    )(lengths, x, rand, bq, bv, wq, wk, wv, gout, *vectors, w_o, w_in, w_out)


PIECES = ("A1", "A2", "A3", "B1", "B2", "B3", "WO", "C0", "C1", "C2", "C3")


def piece_plan(dp_size, width, ff):
    x, y, z = bit_orders(dp_size)
    third, pw = ff // 3, 2 * HD
    return (
        (x, third), (y, third), (z, third), (x, third), (y, third), (z, third), (y, width // 2),
        (x, 3 * pw), (y, 3 * pw), (x, 2 * pw), (y, pw),
    )


def back_body(
    dp_size, q_i, k_i, v_i, ao, at, go, gt, vec, bi,
    xo_h, xt_h, p_h, gsum_h, wq, wk, wv, sa1, sa2, sa3, win, wo,
    ig_o, wq_o, wk_o, wv_o, wo_o, win_o, wout_o, vals_o, bi_o,
    xo, xt, p_s, gsum, g_s, gT, qT, dkT, dvT, dqkv, wcat, xT, acc, ig_s, ig_r, wsrc, gots, kepts,
    tb, tb_m, ts, trs, send, recv, lsem, vsend, vrecv, wsem,
):
    half, width = ig_o.shape
    rows = 2 * half
    pw = 2 * HD
    tile = 256
    p = pl.program_id(0)
    me = lax.axis_index("mp")
    dev = lax.axis_index("dp")
    nb = dp_size.bit_length() - 1
    sems = (send, recv, lsem)
    chunks = [slice(None)] * (nb + 1)
    third = sa1.shape[-1]

    def columns(ref, a, b):
        return ref.at[tuple(chunks + [slice(a, b)])]

    srcs = [sa1, sa2, sa3] + [columns(win, i * third, (i + 1) * third) for i in range(3)] + [wo]
    srcs += [wsrc.at[0], wsrc.at[1], columns(wsrc.at[2], 0, 2 * pw), columns(wsrc.at[2], 2 * pw, 3 * pw)]
    P = {}
    for i, (name, src) in enumerate(zip(PIECES, srcs)):
        bits = piece_plan(dp_size, width, win.shape[-1])[i][0]
        s0 = 1 if name[0] == "A" else 0
        P[name] = Piece(bits, sems, i * nb, src, gots[i], kepts[i], s0)
    from_hbm = PIECES[:7]
    x_loads = [
        pltpu.make_async_copy(s, d, wsem.at[5 + i])
        for i, (s, d) in enumerate(((xo_h, xo), (xt_h, xt), (gsum_h, gsum)))
    ]

    def p_load(j):
        return pltpu.make_async_copy(p_h.at[2 * j : 2 * j + 2], p_s.at[j % 2], wsem.at[3 + j % 2])

    ig_copy = partner_copy(ig_s, ig_r, vsend.at[0], vrecv.at[0], me)
    tb_copy = partner_copy(tb, tb_m, vsend.at[1], vrecv.at[1], me)
    t_copies = [
        pltpu.make_async_remote_copy(
            src_ref=ts[k], dst_ref=trs[k], send_sem=vsend.at[2 + k], recv_sem=vrecv.at[2 + k],
            device_id={"dp": P["C0"].peer(k)}, device_id_type=pl.DeviceIdType.MESH,
        )
        for k in range(nb)
    ]

    @pl.when(p == 0)
    def _():
        barrier = pltpu.get_barrier_semaphore()
        everyone = [{"mp": 1 - me}] + [{"dp": P["C0"].peer(k)} for k in range(nb)]
        for device in everyone:
            pl.semaphore_signal(
                barrier, inc=1, device_id=device, device_id_type=pl.DeviceIdType.MESH
            )
        for name in from_hbm:
            P[name].load_own().start()
        pl.semaphore_wait(barrier, len(everyone))
        for name in from_hbm:
            P[name].copy(P[name].stage0).start()
        for c in x_loads[:2]:
            c.start()
        p_load(0).start()
        p_load(1).start()
        x_loads[2].start()
        for c in x_loads[:2]:
            c.wait()
        xT[:, :half] = xo[...].T
        xT[:, half:] = xt[...].T
        tb[...] = jnp.zeros_like(tb)

    for j in range(HEADS // 4):

        @pl.when(p == j)
        def _(j=j):
            if j == 1:
                p_load(2).start()
            p_load(j).wait()

    slot = p % 2
    c_off = pl.multiple_of(me * (width // 2) + p * pw, pw)
    w_copies = [
        pltpu.make_async_copy(
            w.at[:, pl.ds(c_off, pw)], wcat.at[:, i * pw : (i + 1) * pw], wsem.at[i]
        )
        for i, w in enumerate((wq, wk, wv))
    ]
    for c in w_copies:
        c.start()
    g_s[:half, :] = go[...]
    g_s[half:, :] = gt[...]
    gT[...] = g_s[...].T
    qT[...] = q_i[...].T
    dkT[...] = jnp.zeros_like(dkT)
    dvT[...] = jnp.zeros_like(dvT)
    lane = lax.broadcasted_iota(jnp.int32, (tile, pw), 1)
    low = lane < HD

    def forward(k, *names):
        for name in names:
            x = P[name]
            loaded = name in from_hbm and k == x.stage0
            if loaded:
                x.load_own().wait()
            x.forward(k, loaded)

    def at_tile(t):
        if t == 1:

            @pl.when(p == 2)
            def _():
                forward(0, "WO")
                forward(2, "A3")

        if t == 3:

            @pl.when(p == 0)
            def _():
                forward(1, "A1", "A2")

            @pl.when(p == 1)
            def _():
                forward(0, "B1", "B2", "B3")
                forward(1, "A3")
                forward(2, "A1", "A2")

            @pl.when(p == 2)
            def _():
                forward(1, "B1", "B2")
                forward(0, "C0")

    for t in range(rows // tile):
        rs = slice(t * tile, (t + 1) * tile)
        a_ref = ao if t * tile < half else at
        as_ = slice(t * tile % half, t * tile % half + tile)
        g = g_s[rs, :]
        ga = g.astype(F32) * a_ref[as_, :].astype(F32)
        outs = []
        for h in range(2):
            mine = low if h == 0 else ~low
            hs = slice(h * HD, (h + 1) * HD)
            dp = mm(jnp.where(mine, g, BF16(0)), v_i[...], NT)
            delta = jnp.sum(jnp.where(mine, ga, 0.0), axis=-1, keepdims=True)
            pr = p_s[slot, h, rs, :]
            ds = (pr.astype(F32) * (dp - delta)).astype(BF16)
            outs.append(mm(ds, k_i[...]))
            dvT[hs, :] += mm(gT[hs, rs], pr)
            dkT[hs, :] += mm(qT[hs, rs], ds)
        dq = jnp.where(low, outs[0], outs[1]) * HD**-0.5
        dqkv[rs, 0:pw] = dq.astype(BF16)

        at_tile(t)

    dqkv[:, pw : 2 * pw] = (dkT[...].T * HD**-0.5).astype(BF16)
    dqkv[:, 2 * pw : 3 * pw] = dvT[...].T.astype(BF16)
    d = dqkv[...]
    wg = mm(xT[...], d).astype(BF16).reshape(wsrc.shape[1:])
    wsrc[p] = wg
    tb[0:1, pl.ds(c_off, pw)] = jnp.sum(d[:, 0:pw].astype(F32), axis=0, keepdims=True)
    tb[1:2, pl.ds(c_off, pw)] = jnp.sum(d[:, 2 * pw :].astype(F32), axis=0, keepdims=True)

    @pl.when(p == 0)
    def _():
        P["C0"].copy(0).start()

    @pl.when(p == 1)
    def _():
        P["C1"].copy(0).start()

    @pl.when(p == 2)
    def _():
        P["C2"].copy(0).start()
        P["C3"].copy(0).start()
        tb_copy.start()

    for c in w_copies:
        c.wait()
    part = mm(d, wcat[...], NT)

    @pl.when(p == 0)
    def _():
        acc[...] = part

    @pl.when(p == 1)
    def _():
        acc[...] += part

    @pl.when(p == 2)
    def _():
        ig_s[...] = (acc[half:, :] + part[half:]).astype(BF16)
        ig_copy.start()
        acc[:half, :] += part[:half]

        def next_table(k):
            t_copies[k].wait_recv()
            ts[k + 1][...] = ts[k][...] + trs[k][...]
            if k + 1 < nb:
                t_copies[k + 1].start()

        tb_copy.wait_recv()
        ts[0][0:8, :] = tb[...] + tb_m[...] + vec[...]
        ts[0][8:16, :] = bi[...]
        t_copies[0].start()
        forward(1, "B3")
        forward(2, "B1", "B2")
        forward(0, "C1")
        forward(1, "WO")
        next_table(0)
        forward(1, "C0")
        forward(0, "C2", "C3")
        ig_copy.wait_recv()
        x_loads[2].wait()
        ig_o[...] = gsum[...] + (acc[:half, :] + ig_r[...].astype(F32))
        next_table(1)
        forward(2, "B3")
        forward(1, "C1")
        forward(2, "WO", "C0")
        for k in range(2, nb - 1):
            next_table(k)
        forward(1, "C2", "C3")
        forward(2, "C1")
        for i in range(3):
            wout_o[:, i * third : (i + 1) * third] = P["A%d" % (i + 1)].result()
        forward(2, "C2", "C3")
        for i in range(3):
            win_o[:, i * third : (i + 1) * third] = P["B%d" % (i + 1)].result()
        wo_o[...] = P["WO"].result()
        next_table(nb - 1)
        table = ts[nb][...]
        n = width // dp_size
        m = bi_o.shape[1]
        vals = table[0:8, 0:n]
        biv = table[8:9, 0:m]
        for j in range(1, dp_size):
            vals = jnp.where(dev == j, table[0:8, j * n : (j + 1) * n], vals)
            r = 8 + (j * m) // width
            k = (j * m) % width
            biv = jnp.where(dev == j, table[r : r + 1, k : k + m], biv)
        vals_o[...] = vals
        bi_o[...] = biv
        for j in range(3):
            cs = slice(j * pw, (j + 1) * pw)
            v = P["C%d" % j].result()
            wq_o[:, cs] = v[:, :pw]
            wk_o[:, cs] = v[:, pw : 2 * pw]
            wv_o[:, cs] = v[:, 2 * pw :] if j < 2 else P["C3"].result()

        for name in PIECES:
            P[name].drain()
        ig_copy.wait_send()
        tb_copy.wait_send()
        for c in t_copies:
            c.wait_send()


def back(dp_size, xo, xt, wq, wk, wv, q, k, v, probs, ao, at, go, gt, gsum, vec, bi, sa, win, wo):
    half, width = xo.shape
    rows = 2 * half
    pairs = HEADS // 4
    pw = 2 * HD
    ff = win.shape[1]
    nb = dp_size.bit_length() - 1
    n = width // dp_size
    split = lambda a: a.reshape((2,) * nb + (n, a.shape[-1]))
    whole = lambda a: pl.BlockSpec(
        a.shape, lambda p: (0,) * a.ndim, pipeline_mode=pl.Buffered(1)
    )
    col = lambda r, w: pl.BlockSpec((r, w), lambda p: (0, p))
    hbm = pl.BlockSpec(memory_space=pl.ANY)
    vm = pl.BlockSpec(memory_space=pltpu.VMEM)
    V = pltpu.VMEM
    plan = piece_plan(dp_size, width, ff)

    def stages(last):
        return tuple(
            tuple(
                V((2,) * (nb - 1 - k) + (n, w), BF16) if k < nb - last else V((16, 128), BF16)
                for k in range(nb)
            )
            for _, w in plan
        )

    table = lambda: V((16, width), F32)
    sem = pltpu.SemaphoreType.DMA
    return pl.pallas_call(
        functools.partial(back_body, dp_size),
        grid_spec=pltpu.PrefetchScalarGridSpec(
            num_scalar_prefetch=0,
            grid=(pairs,),
            in_specs=[col(rows, pw)] * 3 + [col(half, pw)] * 4 + [whole(vec), whole(bi)] + [hbm] * 12,
            out_specs=[vm] * 9,
            scratch_shapes=[
                V((half, width), BF16),
                V((half, width), BF16),
                V((2, 2, rows, rows), BF16),
                V((half, width), F32),
                V((rows, pw), BF16),
                V((pw, rows), BF16),
                V((pw, rows), BF16),
                V((pw, rows), F32),
                V((pw, rows), F32),
                V((rows, 3 * pw), BF16),
                V((width, 3 * pw), BF16),
                V((width, rows), BF16),
                V((rows, width), F32),
                V((half, width), BF16),
                V((half, width), BF16),
                V((pairs,) + (2,) * nb + (n, 3 * pw), BF16),
                stages(0),
                stages(1),
                V((8, width), F32),
                V((8, width), F32),
                tuple(table() for _ in range(nb + 1)),
                tuple(table() for _ in range(nb)),
                sem((len(plan) * nb,)),
                sem((len(plan) * nb,)),
                sem((len(plan),)),
                sem((2 + nb,)),
                sem((2 + nb,)),
                sem((8,)),
            ],
        ),
        out_shape=[shape((half, width), F32)]
        + [shape((n, width // 2), F32)] * 4
        + [shape((n, ff), F32)] * 2
        + [shape((8, n), F32), shape((1, 2 * ff // dp_size), F32)],
        compiler_params=pltpu.CompilerParams(
            vmem_limit_bytes=60 << 20, collective_id=2, has_side_effects=True
        ),
        cost_estimate=cost(40e9, 20e6),
        name="back",
    )(q, k, v, ao, at, go, gt, vec, bi, xo, xt, probs, gsum, wq, wk, wv, *sa, split(win), split(wo))


def emit_body(big, *refs):
    ins, outs = refs[: big + 2], refs[big + 2 :]
    for i in range(big):
        outs[i][...] = ins[i][...]
    vals = ins[big][...]
    for j in range(8):
        outs[big + j][...] = vals[j]
    outs[big + 8][...] = ins[big + 1][0]


def emit(arrays, vals, bi):
    vm = pl.BlockSpec(memory_space=pltpu.VMEM)
    return pl.pallas_call(
        functools.partial(emit_body, len(arrays)),
        in_specs=[vm] * (len(arrays) + 2),
        out_specs=[vm] * (len(arrays) + 9),
        out_shape=[shape(a.shape, a.dtype) for a in arrays]
        + [shape((vals.shape[1],), F32)] * 8
        + [shape((bi.shape[1],), F32)],
        compiler_params=params(60),
        name="emit",
    )(*arrays, vals, bi)


def local_pair(
    dp_size, inputs, grad_out, lengths, rand_blocks, w_query, b_query, w_key, w_value, b_value,
    w_output, b_output, gain_one, shift_one, w_in, b_in, w_out, b_out, gain_two, shift_two,
):
    x = inputs[0]
    (
        x_got, a_own, a_oth, q, k, v, probs, out, gsum, ga0, ga_got, sa1, sa2, sa3, w_in_g,
        w_output_g, vec_g, bi_g,
    ) = first_half(
        dp_size, lengths, x, rand_blocks.transpose(2, 0, 1), b_query, b_value, w_query, w_key,
        w_value, grad_out[0],
        (b_output, gain_one, shift_one, b_in, b_out, gain_two, shift_two), w_output, w_in, w_out,
    )
    *mats, vals, bi = back(
        dp_size, x, x_got, w_query, w_key, w_value, q, k, v, probs, a_own, a_oth, ga0, ga_got,
        gsum, vec_g, bi_g, (sa1, sa2, sa3), w_in_g, w_output_g,
    )
    (
        out, input_grad, wq_p, wk_p, wv_p, wo_p, in_part, out_part, bq_p, bv_p, bo_p, g1_p, s1_p,
        b2_p, g2_p, s2_p, bi_p,
    ) = emit([out] + mats, vals, bi)
    return (
        out[None], input_grad[None], wq_p, bq_p, wk_p, wv_p, bv_p, wo_p, bo_p, g1_p, s1_p,
        in_part, bi_p, out_part, b2_p, g2_p, s2_p,
    )


def layer_norm(features, norm_gain, norm_shift):
    row_mean = jnp.mean(features, axis=-1, keepdims=True)
    centered = features - row_mean
    variance = jnp.mean(centered * centered, axis=-1, keepdims=True)
    return centered * lax.rsqrt(variance + norm_epsilon) * norm_gain + norm_shift


def gelu_tanh(features):
    return jax.nn.gelu(features, approximate=True)


def slot_table_ids(block_ids, rand_rows, length):
    valid_blocks = (length + BLK - 1) // BLK
    column = block_ids[:, None]
    columns = jnp.concatenate(
        [
            column - 1,
            column,
            column + 1,
            rand_rows,
            jnp.zeros_like(column),
            jnp.zeros_like(column) + valid_blocks - 1,
        ],
        axis=1,
    )
    in_range = (columns >= 0) & (columns < valid_blocks)
    slot_ids = jnp.arange(columns.shape[1], dtype=jnp.int32)
    earlier = slot_ids[None, :] < slot_ids[:, None]
    repeated = jnp.any(
        (columns[:, :, None] == columns[:, None, :]) & earlier[None, :, :] & in_range[:, None, :],
        axis=2,
    )
    return (jnp.clip(columns, 0, NB - 1), in_range & jnp.logical_not(repeated))


def slot_table(first_block, rand_rows, length):
    block_ids = first_block + jnp.arange(rand_rows.shape[0], dtype=jnp.int32)
    return slot_table_ids(block_ids, rand_rows, length)


def slot_mask(slot_blocks, slot_valid, length):
    positions = slot_blocks[:, :, None] * BLK + jnp.arange(BLK, dtype=jnp.int32)
    allowed = slot_valid[:, :, None] & (positions < length)
    return allowed.reshape(slot_blocks.shape[0], 1, 1, -1)


def gather_slots(whole_rows, slot_blocks):
    picked = whole_rows.reshape(NB, BLK, whole_rows.shape[1])[slot_blocks]
    return picked.reshape(slot_blocks.shape[0], slot_blocks.shape[1] * BLK, HEADS, HD)


def log_total(scores, allowed):
    masked = jnp.where(allowed, scores, negative_fill)
    top_score = jnp.max(masked, axis=-1, keepdims=True)
    return top_score + jnp.log(jnp.sum(jnp.exp(masked - top_score), axis=-1, keepdims=True))


def exp_probs(scores, allowed, totals):
    return jnp.exp(jnp.where(allowed, scores, negative_fill) - totals)


def global_targets(length, device, local_blocks):
    last_block = (length + BLK - 1) // BLK - 1
    targets = []
    for target_block in (jnp.zeros_like(last_block), last_block):
        is_owner = target_block // local_blocks == device
        local_block = jnp.clip(target_block - device * local_blocks, 0, local_blocks - 1)
        targets.append((is_owner, local_block))
    return targets


def global_scores(query_rows, key_one, length):
    scores = jnp.einsum(
        "qhd,khd->hqk",
        query_rows.reshape(BLK, HEADS, HD),
        key_one.reshape(-1, HEADS, HD),
        preferred_element_type=jnp.float32,
    ) * HD ** (-0.5)
    allowed = (jnp.arange(key_one.shape[0], dtype=jnp.int32) < length)[None, None, :]
    return (scores, allowed)


def global_forward(query_rows, key_one, value_one, length):
    scores, allowed = global_scores(query_rows, key_one, length)
    totals = log_total(scores, allowed)
    weighting = exp_probs(scores, allowed, totals).astype(jnp.bfloat16)
    out_rows = jnp.einsum(
        "hqk,khd->qhd",
        weighting,
        value_one.reshape(-1, HEADS, HD),
        preferred_element_type=jnp.float32,
    )
    return (out_rows.reshape(BLK, -1), totals)


def global_skip(query_rows, key_one, value_one, length):
    return (jnp.zeros((BLK, HEADS * HD), jnp.float32), jnp.zeros((HEADS, BLK, 1), jnp.float32))


def global_backward(query_rows, grad_rows, key_one, value_one, length, row_totals):
    score_scale = HD ** (-0.5)
    scores, allowed = global_scores(query_rows, key_one, length)
    exact_probs = exp_probs(scores, allowed, row_totals)
    grad_heads = grad_rows.reshape(BLK, HEADS, HD)
    grad_weights = jnp.einsum(
        "qhd,khd->hqk",
        grad_heads,
        value_one.reshape(-1, HEADS, HD),
        preferred_element_type=jnp.float32,
    )
    delta_sum = jnp.sum(exact_probs * grad_weights, axis=-1, keepdims=True)
    grad_scores = (exact_probs * (grad_weights - delta_sum)).astype(jnp.bfloat16)
    grad_query = (
        jnp.einsum(
            "hqk,khd->qhd",
            grad_scores,
            key_one.reshape(-1, HEADS, HD),
            preferred_element_type=jnp.float32,
        )
        * score_scale
    )
    grad_keys = (
        jnp.einsum(
            "hqk,qhd->khd",
            grad_scores,
            query_rows.reshape(BLK, HEADS, HD),
            preferred_element_type=jnp.float32,
        )
        * score_scale
    )
    grad_values = jnp.einsum(
        "hqk,qhd->khd",
        exact_probs.astype(jnp.bfloat16),
        grad_heads,
        preferred_element_type=jnp.float32,
    )
    return (
        grad_query.reshape(BLK, -1),
        grad_keys.reshape(key_one.shape[0], -1),
        grad_values.reshape(key_one.shape[0], -1),
    )


def global_back_skip(query_rows, grad_rows, key_one, value_one, length, row_totals):
    key_zeros = jnp.zeros(key_one.shape, jnp.float32)
    return (jnp.zeros((BLK, key_one.shape[1]), jnp.float32), key_zeros, key_zeros)


def attend_forward(query_one, key_one, value_one, length, rand_rows, device):
    local_blocks = rand_rows.shape[0]
    slot_blocks, slot_valid = slot_table(device * local_blocks, rand_rows, length)
    allowed = slot_mask(slot_blocks, slot_valid, length)
    query_blocks = query_one.reshape(local_blocks, BLK, HEADS, HD)
    scores = jnp.einsum(
        "nqhd,nkhd->nhqk",
        query_blocks,
        gather_slots(key_one, slot_blocks),
        preferred_element_type=jnp.float32,
    ) * HD ** (-0.5)
    totals = log_total(scores, allowed)
    weighting = exp_probs(scores, allowed, totals).astype(jnp.bfloat16)
    attended = jnp.einsum(
        "nhqk,nkhd->nqhd",
        weighting,
        gather_slots(value_one, slot_blocks),
        preferred_element_type=jnp.float32,
    ).reshape(query_one.shape[0], -1)
    global_totals = []
    for is_owner, local_block in global_targets(length, device, local_blocks):
        query_rows = lax.dynamic_slice_in_dim(query_one, local_block * BLK, BLK, 0)
        out_rows, row_totals = lax.cond(
            is_owner, global_forward, global_skip, query_rows, key_one, value_one, length
        )
        updated = lax.dynamic_update_slice_in_dim(attended, out_rows, local_block * BLK, 0)
        attended = jnp.where(is_owner, updated, attended)
        global_totals.append(row_totals)
    return (attended, totals, global_totals[0], global_totals[1])


def attend_backward(
    query_one,
    key_one,
    value_one,
    length,
    rand_rows,
    totals,
    first_totals,
    last_totals,
    grad_one,
    device,
):
    score_scale = HD ** (-0.5)
    local_blocks = rand_rows.shape[0]
    first_block = device * local_blocks
    slot_blocks, slot_valid = slot_table(first_block, rand_rows, length)
    allowed = slot_mask(slot_blocks, slot_valid, length)
    query_blocks = query_one.reshape(local_blocks, BLK, HEADS, HD)
    key_slots = gather_slots(key_one, slot_blocks)
    value_slots = gather_slots(value_one, slot_blocks)
    scores = (
        jnp.einsum("nqhd,nkhd->nhqk", query_blocks, key_slots, preferred_element_type=jnp.float32)
        * score_scale
    )
    exact_probs = exp_probs(scores, allowed, totals)
    last_block = (length + BLK - 1) // BLK - 1
    row_blocks = first_block + jnp.arange(query_one.shape[0], dtype=jnp.int32) // BLK
    is_global = (row_blocks == 0) | (row_blocks == last_block)
    grad_sparse = jnp.where(is_global[:, None], jnp.zeros_like(grad_one), grad_one)
    grad_heads = grad_sparse.reshape(local_blocks, BLK, HEADS, HD)
    grad_weights = jnp.einsum(
        "nqhd,nkhd->nhqk", grad_heads, value_slots, preferred_element_type=jnp.float32
    )
    delta_sum = jnp.sum(exact_probs * grad_weights, axis=-1, keepdims=True)
    grad_scores = (exact_probs * (grad_weights - delta_sum)).astype(jnp.bfloat16)
    grad_query = (
        jnp.einsum(
            "nhqk,nkhd->nqhd", grad_scores, key_slots, preferred_element_type=jnp.float32
        ).reshape(query_one.shape[0], -1)
        * score_scale
    )
    grad_key_slots = (
        jnp.einsum("nhqk,nqhd->nkhd", grad_scores, query_blocks, preferred_element_type=jnp.float32)
        * score_scale
    )
    grad_value_slots = jnp.einsum(
        "nhqk,nqhd->nkhd",
        exact_probs.astype(jnp.bfloat16),
        grad_heads,
        preferred_element_type=jnp.float32,
    )
    flat_ids = slot_blocks.reshape(-1)
    slot_width = BLK * query_one.shape[1]
    grad_keys = jax.ops.segment_sum(
        grad_key_slots.reshape(-1, slot_width), flat_ids, num_segments=NB
    ).reshape(-1, query_one.shape[1])
    grad_values = jax.ops.segment_sum(
        grad_value_slots.reshape(-1, slot_width), flat_ids, num_segments=NB
    ).reshape(-1, query_one.shape[1])
    for (is_owner, local_block), row_totals in zip(
        global_targets(length, device, local_blocks), (first_totals, last_totals)
    ):
        query_rows = lax.dynamic_slice_in_dim(query_one, local_block * BLK, BLK, 0)
        grad_rows = lax.dynamic_slice_in_dim(grad_one, local_block * BLK, BLK, 0)
        query_add, key_add, value_add = lax.cond(
            is_owner,
            global_backward,
            global_back_skip,
            query_rows,
            grad_rows,
            key_one,
            value_one,
            length,
            row_totals,
        )
        current = lax.dynamic_slice_in_dim(grad_query, local_block * BLK, BLK, 0)
        grad_query = lax.dynamic_update_slice_in_dim(
            grad_query, current + query_add, local_block * BLK, 0
        )
        grad_keys = grad_keys + key_add
        grad_values = grad_values + value_add
    return (grad_query, grad_keys, grad_values)


def local(
    inputs,
    grad_out,
    lengths,
    rand_blocks,
    w_query,
    b_query,
    w_key,
    w_value,
    b_value,
    w_output,
    b_output,
    gain_one,
    shift_one,
    w_in,
    b_in,
    w_out,
    b_out,
    gain_two,
    shift_two,
):
    device = lax.axis_index("mp")
    seq_count, local_rows, width = inputs.shape
    flat_in = inputs.reshape(-1, width)
    query = (jnp.dot(flat_in, w_query, preferred_element_type=jnp.float32) + b_query).astype(
        jnp.bfloat16
    )
    keys = jnp.dot(flat_in, w_key, preferred_element_type=jnp.float32).astype(jnp.bfloat16)
    values = (jnp.dot(flat_in, w_value, preferred_element_type=jnp.float32) + b_value).astype(
        jnp.bfloat16
    )
    key_all, value_all = (
        lax.all_gather(keys.reshape(seq_count, local_rows, width), "mp", axis=1, tiled=True),
        lax.all_gather(values.reshape(seq_count, local_rows, width), "mp", axis=1, tiled=True),
    )
    query_seq = query.reshape(seq_count, local_rows, width)

    def forward_item(seq_items):
        query_one, key_one, value_one, length, rand_rows = seq_items
        return attend_forward(query_one, key_one, value_one, length, rand_rows, device)

    attended, totals, first_totals, last_totals = lax.map(
        forward_item, (query_seq, key_all, value_all, lengths, rand_blocks)
    )
    attended_low = attended.reshape(-1, width).astype(jnp.bfloat16)
    summed_one = (
        flat_in.astype(jnp.float32)
        + jnp.dot(attended_low, w_output, preferred_element_type=jnp.float32)
        + b_output
    )
    first, norm_one_back = jax.vjp(
        layer_norm, summed_one, gain_one.astype(jnp.float32), shift_one.astype(jnp.float32)
    )
    first_low = first.astype(jnp.bfloat16)
    rows_all = lax.all_gather(first_low, "mp", axis=0, tiled=True)
    hidden = jnp.dot(rows_all, w_in, preferred_element_type=jnp.float32) + b_in
    active_full, gelu_back = jax.vjp(gelu_tanh, hidden)
    active = active_full.astype(jnp.bfloat16)
    feed = lax.psum_scatter(
        jnp.einsum(
            "rf,df->rd",
            lax.slice_in_dim(active, 0, first_low.shape[0] * lax.axis_size("mp"), axis=0),
            w_out,
            preferred_element_type=jnp.float32,
        ),
        "mp",
        scatter_dimension=0,
        tiled=True,
    )
    summed_two = first + feed + b_out
    output, norm_two_back = jax.vjp(
        layer_norm, summed_two, gain_two.astype(jnp.float32), shift_two.astype(jnp.float32)
    )
    grad_two, gain_two_grad, shift_two_grad = norm_two_back(
        grad_out.reshape(-1, width).astype(jnp.float32)
    )
    grad_feed = grad_two.astype(jnp.bfloat16)
    b_out_grad = jnp.sum(grad_feed, axis=0, dtype=jnp.float32)
    grads_all = lax.all_gather(grad_feed, "mp", axis=0, tiled=True)
    w_out_grad = jnp.einsum("rd,rf->df", grads_all, active, preferred_element_type=jnp.float32)
    grad_hidden = gelu_back(jnp.dot(grads_all, w_out, preferred_element_type=jnp.float32))[
        0
    ].astype(jnp.bfloat16)
    w_in_grad = jnp.einsum("rd,rf->df", rows_all, grad_hidden, preferred_element_type=jnp.float32)
    grad_first = grad_two + lax.psum_scatter(
        jnp.einsum(
            "rf,df->rd",
            lax.slice_in_dim(grad_hidden, 0, grad_feed.shape[0] * lax.axis_size("mp"), axis=0),
            w_in,
            preferred_element_type=jnp.float32,
        ),
        "mp",
        scatter_dimension=0,
        tiled=True,
    )
    b_in_grad = lax.dynamic_update_slice_in_dim(
        jnp.zeros((FF,), jnp.float32),
        jnp.sum(grad_hidden, axis=0, dtype=jnp.float32),
        device * w_in.shape[1],
        0,
    )
    grad_sum_one, gain_one_grad, shift_one_grad = norm_one_back(grad_first)
    grad_branch = grad_sum_one.astype(jnp.bfloat16)
    b_output_grad = jnp.sum(grad_branch, axis=0, dtype=jnp.float32)
    w_output_grad = jnp.einsum(
        "rd,re->de", attended_low, grad_branch, preferred_element_type=jnp.float32
    )
    grad_attended = (
        jnp.einsum("re,de->rd", grad_branch, w_output, preferred_element_type=jnp.float32)
        .astype(jnp.bfloat16)
        .reshape(seq_count, local_rows, width)
    )

    def backward_item(seq_items):
        (
            query_one,
            key_one,
            value_one,
            length,
            rand_rows,
            sparse_totals,
            first_one,
            last_one,
            grad_one,
        ) = seq_items
        return attend_backward(
            query_one,
            key_one,
            value_one,
            length,
            rand_rows,
            sparse_totals,
            first_one,
            last_one,
            grad_one,
            device,
        )

    grad_query, grad_keys, grad_values = lax.map(
        backward_item,
        (
            query_seq,
            key_all,
            value_all,
            lengths,
            rand_blocks,
            totals,
            first_totals,
            last_totals,
            grad_attended,
        ),
    )
    key_sums, value_sums = (
        lax.psum_scatter(
            grad_keys.astype(jnp.bfloat16), "mp", scatter_dimension=1, tiled=True
        ).astype(jnp.float32),
        lax.psum_scatter(
            grad_values.astype(jnp.bfloat16), "mp", scatter_dimension=1, tiled=True
        ).astype(jnp.float32),
    )
    grad_q_low = grad_query.reshape(-1, width).astype(jnp.bfloat16)
    grad_k_low = key_sums.reshape(-1, width).astype(jnp.bfloat16)
    grad_v_low = value_sums.reshape(-1, width).astype(jnp.bfloat16)
    input_grad = grad_sum_one + jnp.einsum(
        "re,de->rd", grad_q_low, w_query, preferred_element_type=jnp.float32
    )
    input_grad = input_grad + jnp.einsum(
        "re,de->rd", grad_k_low, w_key, preferred_element_type=jnp.float32
    )
    input_grad = input_grad + jnp.einsum(
        "re,de->rd", grad_v_low, w_value, preferred_element_type=jnp.float32
    )
    w_query_grad = jnp.einsum("rd,re->de", flat_in, grad_q_low, preferred_element_type=jnp.float32)
    w_key_grad = jnp.einsum("rd,re->de", flat_in, grad_k_low, preferred_element_type=jnp.float32)
    w_value_grad = jnp.einsum("rd,re->de", flat_in, grad_v_low, preferred_element_type=jnp.float32)
    b_query_grad = jnp.sum(grad_q_low, axis=0, dtype=jnp.float32)
    b_value_grad = jnp.sum(grad_v_low, axis=0, dtype=jnp.float32)
    reduced = (
        lax.psum_scatter(
            w_query_grad.astype(jnp.bfloat16), "dp", scatter_dimension=0, tiled=True
        ).astype(jnp.float32),
        lax.psum_scatter(
            w_key_grad.astype(jnp.bfloat16), "dp", scatter_dimension=0, tiled=True
        ).astype(jnp.float32),
        lax.psum_scatter(
            w_value_grad.astype(jnp.bfloat16), "dp", scatter_dimension=0, tiled=True
        ).astype(jnp.float32),
        lax.psum_scatter(
            w_output_grad.astype(jnp.bfloat16), "dp", scatter_dimension=0, tiled=True
        ).astype(jnp.float32),
        lax.psum_scatter(
            w_in_grad.astype(jnp.bfloat16), "dp", scatter_dimension=0, tiled=True
        ).astype(jnp.float32),
        lax.psum_scatter(
            w_out_grad.astype(jnp.bfloat16), "dp", scatter_dimension=0, tiled=True
        ).astype(jnp.float32),
        lax.psum_scatter(
            b_query_grad.astype(jnp.bfloat16), "dp", scatter_dimension=0, tiled=True
        ).astype(jnp.float32),
        lax.psum_scatter(
            b_value_grad.astype(jnp.bfloat16), "dp", scatter_dimension=0, tiled=True
        ).astype(jnp.float32),
        lax.psum_scatter(
            b_output_grad.astype(jnp.bfloat16), "dp", scatter_dimension=0, tiled=True
        ).astype(jnp.float32),
        lax.psum_scatter(
            gain_one_grad.astype(jnp.bfloat16), "dp", scatter_dimension=0, tiled=True
        ).astype(jnp.float32),
        lax.psum_scatter(
            shift_one_grad.astype(jnp.bfloat16), "dp", scatter_dimension=0, tiled=True
        ).astype(jnp.float32),
        lax.psum_scatter(
            b_in_grad.astype(jnp.bfloat16), "dp", scatter_dimension=0, tiled=True
        ).astype(jnp.float32),
        lax.psum_scatter(
            b_out_grad.astype(jnp.bfloat16), "dp", scatter_dimension=0, tiled=True
        ).astype(jnp.float32),
        lax.psum_scatter(
            gain_two_grad.astype(jnp.bfloat16), "dp", scatter_dimension=0, tiled=True
        ).astype(jnp.float32),
        lax.psum_scatter(
            shift_two_grad.astype(jnp.bfloat16), "dp", scatter_dimension=0, tiled=True
        ).astype(jnp.float32),
    )
    query_part, key_part_out, value_part, output_part = (
        lax.psum_scatter(
            reduced[0].astype(jnp.bfloat16), "mp", scatter_dimension=1, tiled=True
        ).astype(jnp.float32),
        lax.psum_scatter(
            reduced[1].astype(jnp.bfloat16), "mp", scatter_dimension=1, tiled=True
        ).astype(jnp.float32),
        lax.psum_scatter(
            reduced[2].astype(jnp.bfloat16), "mp", scatter_dimension=1, tiled=True
        ).astype(jnp.float32),
        lax.psum_scatter(
            reduced[3].astype(jnp.bfloat16), "mp", scatter_dimension=1, tiled=True
        ).astype(jnp.float32),
    )
    in_part = reduced[4]
    out_part = reduced[5]
    vectors = lax.psum(
        (
            reduced[6],
            reduced[7],
            reduced[8],
            reduced[9],
            reduced[10],
            reduced[11],
            reduced[12],
            reduced[13],
            reduced[14],
        ),
        "mp",
    )
    return (
        output.astype(jnp.bfloat16).reshape(seq_count, local_rows, width),
        input_grad.reshape(seq_count, local_rows, width),
        query_part,
        vectors[0],
        key_part_out,
        value_part,
        vectors[1],
        output_part,
        vectors[2],
        vectors[3],
        vectors[4],
        in_part,
        vectors[5],
        out_part,
        vectors[6],
        vectors[7],
        vectors[8],
    )


def solution(mesh):
    in_specs = (
        P("dp", "mp", None),
        P("dp", "mp", None),
        P("dp"),
        P("dp", "mp", None),
        P(),
        P(),
        P(),
        P(),
        P(),
        P(),
        P(),
        P(),
        P(),
        P(None, "mp"),
        P("mp"),
        P(None, "mp"),
        P(),
        P(),
        P(),
    )
    out_specs = (
        P("dp", "mp", None),
        P("dp", "mp", None),
        P("dp", "mp"),
        P("dp"),
        P("dp", "mp"),
        P("dp", "mp"),
        P("dp"),
        P("dp", "mp"),
        P("dp"),
        P("dp"),
        P("dp"),
        P("dp", "mp"),
        P("dp"),
        P("dp", "mp"),
        P("dp"),
        P("dp"),
        P("dp"),
    )
    sizes = dict(mesh.shape)
    if sizes["mp"] == 2 and sizes["dp"] == 16:
        local_fn = functools.partial(local_pair, sizes["dp"])
    else:
        local_fn = local
    return jax.shard_map(local_fn, mesh=mesh, in_specs=in_specs, out_specs=out_specs, check_vma=False)
```
